32 devices in a mesh: sub: 8 (over z, x), layer: 4 (over y, core).
Axes of the slice: x: 2, y: 2, z: 4, core: 2. Of those that a mesh axis runs over, the one named last changes fastest.
Arguments:
- geometry: float32 [10, 4, 12288], P(None, 'layer', 'sub'), may hold values from -2 to 2, as said below
- dest_slot: int32 [4, 12288], P('layer', 'sub'), may hold values from 0 to 12287, as said below
- pairs: int32 [2, 4, 12288], P(None, 'layer', 'sub'), may hold values from 0 to 767, as said below
- colors: int32 [4, 96], P('layer', 'sub'), may hold values from 0 to 3
- free_vel: float32 [6, 4, 4096], P(None, 'layer', 'sub'), may hold values from -6 to 6
- inertia: float32 [4, 4, 4096], P(None, 'layer', 'sub'), may hold values from 0.5 to 3
- exports: int32 [4, 4, 512], P(None, 'layer', 'sub'), may hold values from 0 to 511, as said below
Outputs:
- impulse: float32 [3, 4, 12288], P(None, 'layer', 'sub')
- velocity: float32 [6, 4, 4096], P(None, 'layer', 'sub')
The draws below stay inside these ranges and needn't reach their ends.
Inputs may be any that keep to these rules, and one draw needn't show every extreme that they name: Within each layer dest_slot is a permutation of 0 to 12287; the owner of a detected contact lies in the same aligned group of 4 sub indices as the device that holds it. At most 768 contacts of one device go to one owner, and in every group some device hands exactly 768 to one owner. pairs[0] is an own block, 0 to 511. pairs[1] is another own block, or 512 + d * 64 + i, the copy of the i-th block that the neighbour in direction d (0 lower sub index, 1 higher, 2 lower layer, 3 higher layer) lists toward this subdomain; only directions with a neighbour appear. `exports`: each subdomain's list for one direction holds 64 distinct own blocks. `geometry`: rows 0 and 1 lie in -1 to 1 and row 2 in 0.5 to 1.5 (the normal before normalizing); rows 3 to 8 are lever arms, row 9 the gap rate within -1 to 1.
All inputs are finite; a program needn't handle non-finite values.
Results may differ from the reference program's by a relative error of at most 0.0003.
Values sent between devices are 32-bit elements; how exact they have to be, the bound alone decides.
No kernel may reach another device: no remote copies, remote signals or barrier semaphores. Data moves between devices by JAX's collectives and lax.ppermute only.
A program may use at most 64 MiB of HBM per device.

```python
import math
import jax
import jax.numpy as jnp
from jax import lax

NB = 512
WIN = 4
SWEEPS = 3
NCOLOR = 4
TILE = 128
CO = 1536
NI = 64
CAP = 768
CL = 12288
BL = 4096
TL = 96
N_SUB = 8
N_LAYER = 4


def shuffled(perm_key):
    return jax.random.permutation(perm_key, CO).astype(jnp.int32)


def relay_group(group_key):
    key_cut, key_big, key_src, key_dst = jax.random.split(group_key, 4)
    remainder = CO - CAP
    cut_points = jnp.sort(jax.random.randint(key_cut, (WIN - 2,), 0, remainder + 1)).astype(jnp.int32)
    cut_edges = jnp.concatenate([jnp.zeros((1,), jnp.int32), cut_points, jnp.full((1,), remainder, jnp.int32)])
    pieces = cut_edges[1:] - cut_edges[:-1]
    largest = jax.random.randint(key_big, (), 0, WIN)
    position = jnp.arange(WIN, dtype=jnp.int32)
    shifted = jnp.clip(jnp.where(position < largest, position, position - 1), 0, WIN - 2)
    circle = jnp.where(position == largest, CAP, pieces[shifted]).astype(jnp.int32)
    counts = circle[(position[None, :] - position[:, None]) % WIN]
    send_start = jnp.cumsum(counts, axis=1) - counts
    recv_start = jnp.cumsum(counts, axis=0) - counts
    src_order = jax.vmap(shuffled)(jax.random.split(key_src, WIN))
    dst_order = jax.vmap(shuffled)(jax.random.split(key_dst, WIN))
    flat_index = jnp.arange(WIN * CO, dtype=jnp.int32)
    source = flat_index // CO
    within = flat_index % CO
    span_ends = (send_start + counts)[source]
    target = jnp.sum((within[:, None] >= span_ends).astype(jnp.int32), axis=1)
    placed = within - send_start[source, target]
    landing = recv_start[source, target] + placed
    src_rows = source * CO + src_order[source, within]
    dst_slots = target * CO + dst_order[target, landing]
    return jnp.zeros((WIN * CO,), jnp.int32).at[src_rows].set(dst_slots)


def draw_dest_slot(key, part):
    groups = N_SUB // WIN
    group_keys = jax.random.split(jax.random.fold_in(key, 11), N_LAYER * groups)
    tables = jax.vmap(relay_group)(group_keys).reshape(N_LAYER, groups, WIN * CO)
    group_base = (jnp.arange(groups, dtype=jnp.int32) * (WIN * CO))[None, :, None]
    return (tables + group_base).reshape(N_LAYER, N_SUB * CO).astype(jnp.int32)


def draw_pairs(key, part):
    key_first, key_other, key_dir, key_which, key_remote = jax.random.split(jax.random.fold_in(key, 23), 5)
    grid_shape = (N_LAYER, N_SUB, CO)
    first = jax.random.randint(key_first, grid_shape, 0, NB)
    other = (first + 1 + jax.random.randint(key_other, grid_shape, 0, NB - 1)) % NB
    direction = jax.random.randint(key_dir, grid_shape, 0, 4)
    which = jax.random.randint(key_which, grid_shape, 0, NI)
    remote = jax.random.randint(key_remote, grid_shape, 0, 4) == 0
    sub_pos = jnp.arange(N_SUB, dtype=jnp.int32)[None, :, None]
    layer_pos = jnp.arange(N_LAYER, dtype=jnp.int32)[:, None, None]
    exists = jnp.where(direction == 0, sub_pos > 0, jnp.where(direction == 1, sub_pos < N_SUB - 1, jnp.where(direction == 2, layer_pos > 0, layer_pos < N_LAYER - 1)))
    second = jnp.where(remote & exists, NB + direction * NI + which, other)
    return jnp.stack([first, second]).reshape(2, N_LAYER, N_SUB * CO).astype(jnp.int32)


def pick_listed(perm_key):
    return jax.random.permutation(perm_key, NB)[:NI].astype(jnp.int32)


def draw_exports(key, part):
    list_keys = jax.random.split(jax.random.fold_in(key, 37), 4 * N_LAYER * N_SUB)
    listed = jax.vmap(pick_listed)(list_keys)
    return listed.reshape(4, N_LAYER, N_SUB * NI).astype(jnp.int32)


def draw_geometry(key, part):
    key_flat, key_up, key_arm, key_gap = jax.random.split(jax.random.fold_in(key, 41), 4)
    grid_shape = (N_LAYER, N_SUB * CO)
    flat_part = jax.random.uniform(key_flat, (2,) + grid_shape, jnp.float32, -1.0, 1.0)
    upward = jax.random.uniform(key_up, (1,) + grid_shape, jnp.float32, 0.5, 1.5)
    arms = 0.5 * jax.random.truncated_normal(key_arm, -4.0, 4.0, (6,) + grid_shape, jnp.float32)
    gap_rate = 0.5 * jax.random.truncated_normal(key_gap, -2.0, 2.0, (1,) + grid_shape, jnp.float32)
    return jnp.concatenate([flat_part, upward, arms, gap_rate], axis=0).astype(jnp.float32)


def place_ends(drawn, key, low, high):
    shape = drawn.shape
    index_at = [jax.random.randint(jax.random.fold_in(key, axis), (), 0, shape[axis]) for axis in range(len(shape))]
    drawn = drawn.at[tuple(index_at)].set(low)
    longest = shape.index(max(shape))
    index_at[longest] = (index_at[longest] + 1) % shape[longest]
    return drawn.at[tuple(index_at)].set(high)


def steps_of(key, dims, cuts, smallest, top_value):
    def one(dim, shards_of):
        heights = jax.random.uniform(jax.random.fold_in(jax.random.fold_in(key, 6), dim), (shards_of,), jnp.float32, smallest / len(cuts), top_value / len(cuts))
        return jnp.repeat(jnp.exp(heights), dims[dim] // shards_of).reshape((-1,) + (1,) * (len(dims) - dim - 1))

    level = one(*cuts[0])
    for cut in cuts[1:]:
        level = level * one(*cut)
    return level


def normal_values(stream_key, shape, spread, reach, cuts=(), kind=jnp.bfloat16):
    result = jax.random.normal(stream_key, shape, jnp.float32) * spread
    if len(cuts) > 0:
        result = steps_of(stream_key, shape, cuts, -0.22, 0.18) * result
    return jnp.clip(result, min=-reach, max=reach).astype(kind)


def setup_inputs(seed: int = 0) -> dict:
    key_of = jax.random.split(jax.random.key(seed), 8)
    geometry = draw_geometry(jax.random.fold_in(key_of[7], 71), 0)
    dest_slot = draw_dest_slot(jax.random.fold_in(key_of[7], 71), 0)
    pairs = draw_pairs(jax.random.fold_in(key_of[7], 71), 0)
    colors = place_ends(jax.random.randint(key_of[3], (N_LAYER, TL), 0, NCOLOR), jax.random.fold_in(key_of[3], 1), 0, NCOLOR - 1).astype(jnp.int32)
    free_vel = normal_values(key_of[4], (6, N_LAYER, BL), 1.0, 6.0, ((1, 4), (2, 8)), jnp.float32)
    inertia = jnp.clip(jnp.exp(math.log(3.0) - 1.7917595 * jax.random.uniform(key_of[5], (4, N_LAYER, BL), jnp.float32) ** steps_of(key_of[5], (4, N_LAYER, BL), ((1, 4), (2, 8)), -0.2, 0.2)), 0.5, 3.0)
    exports = draw_exports(jax.random.fold_in(key_of[7], 71), 0)
    return {"geometry": geometry, "dest_slot": dest_slot, "pairs": pairs, "colors": colors, "free_vel": free_vel, "inertia": inertia, "exports": exports}


relaxation = 0.7
friction = 0.6
tangent_floor = 0.1

def cross_rows(first_vec, second_vec):
    return jnp.stack([first_vec[1] * second_vec[2] - first_vec[2] * second_vec[1], first_vec[2] * second_vec[0] - first_vec[0] * second_vec[2], first_vec[0] * second_vec[1] - first_vec[1] * second_vec[0]])

def arm_block(lever_arm, spin_inv):
    return jnp.stack([spin_inv[1] * lever_arm[2] * lever_arm[2] + spin_inv[2] * lever_arm[1] * lever_arm[1], spin_inv[0] * lever_arm[2] * lever_arm[2] + spin_inv[2] * lever_arm[0] * lever_arm[0], spin_inv[0] * lever_arm[1] * lever_arm[1] + spin_inv[1] * lever_arm[0] * lever_arm[0], -spin_inv[2] * lever_arm[0] * lever_arm[1], -spin_inv[1] * lever_arm[0] * lever_arm[2], -spin_inv[0] * lever_arm[1] * lever_arm[2]])

def contact_setup(geometry, props_first, props_second):
    raw_normal = geometry[0:3]
    normal = raw_normal / jnp.sqrt(lax.optimization_barrier(jnp.sum(raw_normal * raw_normal, axis=0)))
    side_norm = jnp.sqrt(normal[1] * normal[1] + normal[2] * normal[2])
    tangent_one = jnp.stack([jnp.zeros_like(side_norm), normal[2] / side_norm, -normal[1] / side_norm])
    tangent_two = cross_rows(normal, tangent_one)
    frames = jnp.stack([normal, tangent_one, tangent_two])
    entries = arm_block(geometry[3:6], props_first[1:4]) + arm_block(geometry[6:9], props_second[1:4])
    masses = props_first[0] + props_second[0]
    entry_xx = masses + entries[0]
    entry_yy = masses + entries[1]
    entry_zz = masses + entries[2]
    entry_xy = entries[3]
    entry_xz = entries[4]
    entry_yz = entries[5]
    cofactor_xx = entry_yy * entry_zz - entry_yz * entry_yz
    cofactor_xy = entry_xz * entry_yz - entry_xy * entry_zz
    cofactor_xz = entry_xy * entry_yz - entry_xz * entry_yy
    cofactor_yy = entry_xx * entry_zz - entry_xz * entry_xz
    cofactor_yz = entry_xy * entry_xz - entry_xx * entry_yz
    cofactor_zz = entry_xx * entry_yy - entry_xy * entry_xy
    determinant = entry_xx * cofactor_xx + entry_xy * cofactor_xy + entry_xz * cofactor_xz
    inverse = jnp.stack([cofactor_xx, cofactor_yy, cofactor_zz, cofactor_xy, cofactor_xz, cofactor_yz]) / determinant
    return (frames, inverse)

def contact_pass(impulse, vel_table, first_idx, second_idx, frames, geometry, inverse, props_first, props_second, active):
    first_vel = vel_table[:, first_idx]
    second_vel = vel_table[:, second_idx]
    arm_first = geometry[3:6]
    arm_second = geometry[6:9]
    relative = first_vel[0:3] + cross_rows(first_vel[3:6], arm_first) - second_vel[0:3] - cross_rows(second_vel[3:6], arm_second)
    target = relative + geometry[9] * frames[0]
    solved = jnp.stack([inverse[0] * target[0] + inverse[3] * target[1] + inverse[4] * target[2], inverse[3] * target[0] + inverse[1] * target[1] + inverse[5] * target[2], inverse[4] * target[0] + inverse[5] * target[1] + inverse[2] * target[2]])
    trial_impulse = impulse - relaxation * lax.optimization_barrier(jnp.sum(frames * solved[None], axis=1))
    normal_part = jnp.maximum(trial_impulse[0], 0.0)
    slide_norm = jnp.sqrt(trial_impulse[1] * trial_impulse[1] + trial_impulse[2] * trial_impulse[2])
    factor = jnp.minimum(1.0, friction * normal_part / jnp.maximum(slide_norm, tangent_floor))
    projected = jnp.stack([normal_part, trial_impulse[1] * factor, trial_impulse[2] * factor])
    updated = jnp.where(active[None], projected, impulse)
    change = updated - impulse
    push_world = lax.optimization_barrier(jnp.sum(frames * change[:, None], axis=0))
    first_push = jnp.concatenate([props_first[0:1] * push_world, props_first[1:4] * cross_rows(arm_first, push_world)])
    second_push = -jnp.concatenate([props_second[0:1] * push_world, props_second[1:4] * cross_rows(arm_second, push_world)])
    vel_table = vel_table.at[:, first_idx].add(first_push).at[:, second_idx].add(second_push)
    return (updated, vel_table)

def gather_exports(values, export_list):
    index = jnp.transpose(export_list, (1, 2, 0, 3)).reshape(N_LAYER, N_SUB, 4 * NI)
    picked = jnp.take_along_axis(values, jnp.broadcast_to(index[None], (values.shape[0],) + index.shape), axis=3)
    picked = picked.reshape(values.shape[0], N_LAYER, N_SUB, 4, NI)
    return jnp.transpose(picked, (0, 3, 1, 2, 4))

def neighbour_trade(outbound):
    rows_here = outbound.shape[0]
    zero_sub = jnp.zeros((rows_here, N_LAYER, 1, NI), jnp.float32)
    zero_layer = jnp.zeros((rows_here, 1, N_SUB, NI), jnp.float32)
    from_lower = jnp.concatenate([zero_sub, outbound[:, 1, :, :-1]], axis=2)
    from_upper = jnp.concatenate([outbound[:, 0, :, 1:], zero_sub], axis=2)
    from_below = jnp.concatenate([zero_layer, outbound[:, 3, :-1]], axis=1)
    from_above = jnp.concatenate([outbound[:, 2, 1:], zero_layer], axis=1)
    return jnp.stack([from_lower, from_upper, from_below, from_above], axis=3)

def add_into(values_in, index):
    return jnp.zeros((values_in.shape[0], NB), jnp.float32).at[:, index].add(values_in)

def scatter_exports(arrived, export_list):
    rows_here = arrived.shape[0]
    moved = jnp.transpose(arrived, (1, 2, 0, 3, 4)).reshape(N_LAYER * N_SUB, rows_here, 4 * NI)
    index = jnp.transpose(export_list, (1, 2, 0, 3)).reshape(N_LAYER * N_SUB, 4 * NI)
    summed = jax.vmap(add_into)(moved, index)
    return jnp.transpose(summed.reshape(N_LAYER, N_SUB, rows_here, NB), (2, 0, 1, 3))

def place_layer(geo_layer, slot_layer):
    return jnp.zeros_like(geo_layer).at[:, slot_layer].set(geo_layer)

def reference(geometry, dest_slot, pairs, colors, free_vel, inertia, exports):
    devices = N_LAYER * N_SUB
    table_len = NB + 4 * NI
    owner_geo = jax.vmap(place_layer, in_axes=(1, 0), out_axes=1)(geometry, dest_slot).reshape(10, devices * CO)
    table_base = (jnp.arange(devices, dtype=jnp.int32) * table_len)[:, None]
    first_idx = (pairs[0].reshape(devices, CO) + table_base).reshape(-1)
    second_idx = (pairs[1].reshape(devices, CO) + table_base).reshape(-1)
    tile_color = jnp.repeat(colors.reshape(devices, CO // TILE), TILE, axis=1).reshape(-1)
    own_vel = free_vel.reshape(6, N_LAYER, N_SUB, NB)
    own_props = inertia.reshape(4, N_LAYER, N_SUB, NB)
    export_list = exports.reshape(4, N_LAYER, N_SUB, NI)
    sub_pos = jnp.arange(N_SUB, dtype=jnp.int32)[None, :]
    layer_pos = jnp.arange(N_LAYER, dtype=jnp.int32)[:, None]
    grid_shape = (N_LAYER, N_SUB)
    has_neighbour = jnp.stack([jnp.broadcast_to(sub_pos > 0, grid_shape), jnp.broadcast_to(sub_pos < N_SUB - 1, grid_shape), jnp.broadcast_to(layer_pos > 0, grid_shape), jnp.broadcast_to(layer_pos < N_LAYER - 1, grid_shape)]).astype(jnp.float32)
    listed = jnp.broadcast_to(jnp.transpose(has_neighbour, (1, 2, 0))[None, :, :, :, None], (1, N_LAYER, N_SUB, 4, NI))
    multiplicity = 1.0 + scatter_exports(listed, export_list)[0]

    def make_table(values):
        ghosts = neighbour_trade(gather_exports(values, export_list))
        ghosts = ghosts.reshape(values.shape[0], N_LAYER, N_SUB, 4 * NI)
        return jnp.concatenate([values, ghosts], axis=3).reshape(values.shape[0], -1)
    prop_table = make_table(own_props)
    vel_table = make_table(own_vel)
    props_first = prop_table[:, first_idx]
    props_second = prop_table[:, second_idx]
    frames, inverse = contact_setup(owner_geo, props_first, props_second)
    impulse = jnp.zeros((3, devices * CO), jnp.float32)
    for sweep_step in range(SWEEPS):
        start_table = vel_table
        for color_now in range(NCOLOR):
            impulse, vel_table = contact_pass(impulse, vel_table, first_idx, second_idx, frames, owner_geo, inverse, props_first, props_second, tile_color == color_now)
        change = (vel_table - start_table).reshape(6, N_LAYER, N_SUB, table_len)
        ghost_change = jnp.transpose(change[..., NB:].reshape(6, N_LAYER, N_SUB, 4, NI), (0, 3, 1, 2, 4))
        incoming = scatter_exports(neighbour_trade(ghost_change), export_list)
        own_vel = own_vel + (change[..., :NB] + incoming) / multiplicity
        if sweep_step + 1 < SWEEPS:
            vel_table = make_table(own_vel)
    return (impulse.reshape(3, N_LAYER, CL), own_vel.reshape(6, N_LAYER, BL))
```

```python
import jax
import jax.numpy as jnp
from jax import lax
from jax.experimental import pallas as pl
from jax.experimental.pallas import tpu as pltpu
from jax.sharding import PartitionSpec as P

WIN = 4
SWEEPS = 3
NCOLOR = 4
TILE = 128
LANES = 128
CHUNK = 4

relaxation = 0.7
friction = 0.6
tangent_floor = 0.1

AXES = ("sub", "layer")
F32 = jnp.float32
BF16 = jnp.bfloat16
VMEM_SPEC = pl.BlockSpec(memory_space=pltpu.VMEM)
SMEM_SPEC = pl.BlockSpec(memory_space=pltpu.SMEM)


def neighbour_matchings(subs, layers):
    assert subs % 2 == 0 and layers % 2 == 0

    def shifted(i):
        return i - 1 if i % 2 == 0 else i + 1

    def partner(match, s, y):
        if match == 0:
            return s ^ 1, y
        if match == 1:
            return (s, y ^ 1) if s in (0, subs - 1) else (shifted(s), y)
        if match == 2:
            return s, y ^ 1
        return (s ^ 1, y) if y in (0, layers - 1) else (s, shifted(y))

    out = []
    for match in range(4):
        pairs = []
        for s in range(subs):
            for y in range(layers):
                ps, py = partner(match, s, y)
                pairs.append((s * layers + y, ps * layers + py))
        out.append(pairs)
    return out


def relay_shuffle(subs, layers, k):
    return [
        (s * layers + y, (s ^ k) * layers + y) for s in range(subs) for y in range(layers)
    ]


def lane_iota():
    return lax.broadcasted_iota(jnp.int32, (8, LANES), 1)


def pick(tables, index):
    low = jnp.bitwise_and(index, LANES - 1)
    high = jnp.right_shift(index, 7)
    out = jnp.take_along_axis(tables[0], low, axis=1)
    for h in range(1, len(tables)):
        out = jnp.where(high == h, jnp.take_along_axis(tables[h], low, axis=1), out)
    return out


def three_parts(value):
    first = value.astype(BF16).astype(F32)
    rest = value - first
    second = rest.astype(BF16).astype(F32)
    return [first, second, rest - second]


def masked_rows(value, index, highs):
    parts = three_parts(value)
    high = jnp.right_shift(index, 7)
    rows = []
    for h in highs:
        hit = high == h
        rows.extend([jnp.where(hit, part, 0.0) for part in parts])
    return jnp.concatenate(rows, axis=0).astype(BF16)


def low_onehot(index_row):
    low = jnp.bitwise_and(index_row, LANES - 1)
    rows = lax.broadcasted_iota(jnp.int32, (LANES, LANES), 0)
    return jnp.where(rows == low, 1.0, 0.0).astype(BF16)


def contract_lanes(lhs, rhs):
    return lax.dot_general(
        lhs, rhs, (((1,), (1,)), ((), ())), preferred_element_type=F32
    )


def sum_parts(block, h):
    base = 24 * h
    return (block[base : base + 8] + block[base + 8 : base + 16]) + block[base + 16 : base + 24]


def cross(u, v):
    return [
        u[1] * v[2] - u[2] * v[1],
        u[2] * v[0] - u[0] * v[2],
        u[0] * v[1] - u[1] * v[0],
    ]


def dot3(u, v):
    return u[0] * v[0] + u[1] * v[1] + u[2] * v[2]


def halves(low, high, half):
    return jnp.where(lane_iota() < half, low, high)


def prepare_kernel(
    subs, layers, geo, dest, pairs, colors, vel, inertia, exports,
    place0, place1, place2, place3, start_own, index_out, export_index, mult, out0, out1, order,
    listed, lhs, hot,
):
    count = geo.shape[2]
    tiles = count // TILE
    slots = place0.shape[0] // 10
    bodies = vel.shape[2]
    interface = exports.shape[2]
    sub = lax.axis_index("sub")
    layer = lax.axis_index("layer")
    sub_even = lax.rem(sub, 2) == 0
    layer_even = lax.rem(layer, 2) == 0
    member = lax.rem(sub, WIN)
    filled = jnp.int32(0)
    for k in range(NCOLOR):
        order[16 + k] = filled
        for t in range(tiles):
            hit = colors[0, t] == k
            place = jnp.where(hit, filled, 31)
            order[place] = t
            filled = filled + jnp.where(hit, 1, 0)
    order[16 + NCOLOR] = filled
    for t in range(tiles, 16):
        order[t] = tiles
    start_own[...] = jnp.zeros_like(start_own)
    for r in range(6):
        start_own[r : r + 1, :] = vel[r]
    for r in range(4):
        start_own[8 + r : 9 + r, :] = inertia[r]
    listed[0:1, 0:interface] = exports[0]
    listed[0:1, interface : 2 * interface] = exports[1]
    listed[1:2, 0:interface] = exports[1]
    listed[1:2, interface : 2 * interface] = exports[0]
    listed[2:3, 0:interface] = exports[2]
    listed[2:3, interface : 2 * interface] = exports[3]
    listed[3:4, 0:interface] = exports[3]
    listed[3:4, interface : 2 * interface] = exports[2]
    row0 = jnp.where(sub_even, listed[1:2, :], listed[0:1, :])
    row1 = jnp.where(layer_even, listed[3:4, :], listed[2:3, :])
    idx0 = jnp.broadcast_to(row0, (8, LANES))
    idx1 = jnp.broadcast_to(row1, (8, LANES))
    export_index[0:8, :] = idx0
    export_index[8:16, :] = idx1
    blocks = bodies // LANES
    for base in (0, 8):
        tables = [
            start_own[base : base + 8, h * LANES : (h + 1) * LANES] for h in range(blocks)
        ]
        out0[base : base + 8, :] = pick(tables, idx0)
        out1[base : base + 8, :] = pick(tables, idx1)
    inner_sub = jnp.where(jnp.logical_and(sub > 0, sub < subs - 1), 1.0, 0.0)
    inner_layer = jnp.where(jnp.logical_and(layer > 0, layer < layers - 1), 1.0, 0.0)
    lane = lane_iota()
    weight0 = jnp.where(lane < interface, 1.0, inner_sub)
    weight1 = jnp.where(lane < interface, 1.0, inner_layer)
    for h in range(blocks):
        left = jnp.concatenate(
            [
                jnp.where(jnp.right_shift(idx0, 7) == h, weight0, 0.0),
                jnp.where(jnp.right_shift(idx1, 7) == h, weight1, 0.0),
            ],
            axis=1,
        ).astype(BF16)
        right = jnp.concatenate([low_onehot(row0), low_onehot(row1)], axis=1)
        mult[:, h * LANES : (h + 1) * LANES] = 1.0 + contract_lanes(left, right)
    index_out[...] = jnp.zeros_like(index_out)
    flip_sub = jnp.where(sub_even, interface, 0)
    flip_layer = jnp.where(layer_even, interface, 0)
    for t in range(tiles):
        span = pl.ds(t * TILE, TILE)
        index_out[t : t + 1, :] = pairs[0, :, span]
        other = pairs[1, :, span]
        ghost = other - bodies
        turned = jnp.where(
            ghost < 2 * interface,
            jnp.bitwise_xor(ghost, flip_sub),
            jnp.bitwise_xor(ghost, flip_layer),
        )
        index_out[16 + t : 17 + t, :] = jnp.where(ghost < 0, other, bodies + turned)
        index_out[32 + t : 33 + t, :] = jnp.full((1, TILE), colors[0, t], jnp.int32)
    for t in range(tiles, 16):
        index_out[32 + t : 33 + t, :] = jnp.full((1, TILE), -1, jnp.int32)
    slot = dest[...] - (sub - member) * count
    target = jnp.zeros_like(slot)
    for m in range(1, WIN):
        target = target + jnp.where(slot >= m * count, 1, 0)
    within = slot - target * count
    row_id = jnp.bitwise_xor(target, member) * slots + jnp.right_shift(within, 7)
    low = jnp.bitwise_and(within, LANES - 1)
    for t in range(tiles):
        span = pl.ds(t * TILE, TILE)
        hot[:, span] = low_onehot(low[:, t * TILE : (t + 1) * TILE])
    outs = (place0, place1, place2, place3)
    for k in range(WIN):
        rows = lax.broadcasted_iota(jnp.int32, (slots, count), 0) + k * slots
        hit = rows == row_id
        for p in range(3):
            for r in range(10):
                part = three_parts(geo[r])[p]
                lhs[p, r * slots : (r + 1) * slots, :] = jnp.where(hit, part, 0.0).astype(BF16)
        total = contract_lanes(lhs[0], hot[...])
        total = total + contract_lanes(lhs[1], hot[...])
        outs[k][...] = total + contract_lanes(lhs[2], hot[...])


STATE = 34


def contact_state(geo, first, second):
    raw = geo[0:3]
    length = jnp.sqrt(dot3(raw, raw))
    normal = [x / length for x in raw]
    side = jnp.sqrt(normal[1] * normal[1] + normal[2] * normal[2])
    tan_y = normal[2] / side
    tan_z = -normal[1] / side
    two = [
        normal[1] * tan_z - normal[2] * tan_y,
        -normal[0] * tan_z,
        normal[0] * tan_y,
    ]

    def arm(p, spin):
        return [
            spin[1] * p[2] * p[2] + spin[2] * p[1] * p[1],
            spin[0] * p[2] * p[2] + spin[2] * p[0] * p[0],
            spin[0] * p[1] * p[1] + spin[1] * p[0] * p[0],
            -spin[2] * p[0] * p[1],
            -spin[1] * p[0] * p[2],
            -spin[0] * p[1] * p[2],
        ]

    arm_a, arm_b = geo[3:6], geo[6:9]
    e = [x + y for x, y in zip(arm(arm_a, first[1:4]), arm(arm_b, second[1:4]))]
    mass = first[0] + second[0]
    xx, yy, zz = mass + e[0], mass + e[1], mass + e[2]
    xy, xz, yz = e[3], e[4], e[5]
    c_xx = yy * zz - yz * yz
    c_xy = xz * yz - xy * zz
    c_xz = xy * yz - xz * yy
    c_yy = xx * zz - xz * xz
    c_yz = xy * xz - xx * yz
    c_zz = xx * yy - xy * xy
    det = xx * c_xx + xy * c_xy + xz * c_xz
    inv = [
        [c_xx / det, c_xy / det, c_xz / det],
        [c_xy / det, c_yy / det, c_yz / det],
        [c_xz / det, c_yz / det, c_zz / det],
    ]
    solve = []
    for row in (normal, None, two):
        for j in range(3):
            if row is None:
                value = tan_y * inv[1][j] + tan_z * inv[2][j]
            else:
                value = row[0] * inv[0][j] + row[1] * inv[1][j] + row[2] * inv[2][j]
            solve.append(relaxation * value)
    bias = [geo[9] * dot3(solve[3 * i : 3 * i + 3], normal) for i in range(3)]
    return (
        solve + bias + normal + [tan_y, tan_z] + two + arm_a + arm_b + list(first) + list(second)
    )


def sweep_kernel(bodies, interface, first_sweep, last_sweep, *refs):
    refs = list(refs)
    order, index = refs[0], refs[1]
    refs = refs[2:]
    if first_sweep:
        own, r0, r1, r2, r3, g0, g1, g2, g3 = refs[:9]
        refs = refs[9:]
    else:
        own, r0, r1, r2, r3, state, impulse_in = refs[:7]
        refs = refs[7:]
    if first_sweep:
        state = refs.pop(0)
    impulse, own_change, ghost0, ghost1 = refs[:4]
    refs = refs[4:]
    got_a, got_b, push_a, push_b, hot, acc, table, imp = refs
    slots = 16
    tiles = hot.shape[1] // (2 * TILE) - 1
    blocks = bodies // LANES
    ghosts = (4 * interface) // LANES
    total = blocks + ghosts
    tile_rows = [pl.ds(c, slots, stride=8) for c in range(8)]

    def ghost_blocks(base):
        return [
            halves(r0[base : base + 8, :], r1[base : base + 8, :], interface),
            halves(r2[base : base + 8, :], r3[base : base + 8, :], interface),
        ]

    start = [own[0:8, h * LANES : (h + 1) * LANES] for h in range(blocks)] + ghost_blocks(0)
    for h in range(total):
        table[8 * h : 8 * h + 8, :] = start[h]

    for t in range(tiles):
        hot[:, 2 * t * TILE : (2 * t + 1) * TILE] = low_onehot(index[t : t + 1, :])
        hot[:, (2 * t + 1) * TILE : (2 * t + 2) * TILE] = low_onehot(index[16 + t : 17 + t, :])
    hot[:, 2 * tiles * TILE :] = jnp.zeros((LANES, 2 * TILE), BF16)

    push_a[...] = jnp.zeros_like(push_a)
    push_b[...] = jnp.zeros_like(push_b)

    if first_sweep:
        props = [own[8:16, h * LANES : (h + 1) * LANES] for h in range(blocks)] + ghost_blocks(8)
        got_a[...] = jnp.ones_like(got_a)
        got_b[...] = jnp.ones_like(got_b)
        for t in range(tiles):
            ia = jnp.broadcast_to(index[t : t + 1, :], (8, LANES))
            ib = jnp.broadcast_to(index[16 + t : 17 + t, :], (8, LANES))
            got_a[8 * t : 8 * t + 8, :] = pick(props[:blocks], ia)
            got_b[8 * t : 8 * t + 8, :] = pick(props, ib)
        first = [got_a[tile_rows[c], :] for c in range(4)]
        second = [got_b[tile_rows[c], :] for c in range(4)]
        real = lax.broadcasted_iota(jnp.int32, (slots, LANES), 0) < tiles
        geo = []
        for c in range(10):
            span = slice(c * slots, (c + 1) * slots)
            value = (g0[span, :] + g1[span, :]) + (g2[span, :] + g3[span, :])
            geo.append(jnp.where(real, value, 1.0))
        for c, value in enumerate(contact_state(geo, first, second)):
            state[c * slots : (c + 1) * slots, :] = value
        imp[...] = jnp.zeros_like(imp)
    else:
        imp[...] = impulse_in[...]

    def held(c):
        return state[c * slots : (c + 1) * slots, :]

    def color_pass(k, carry):
        begin = order[16 + k]
        chunks = lax.div(order[17 + k] - begin + (CHUNK - 1), CHUNK)
        now = [table[8 * h : 8 * h + 8, :] for h in range(total)]

        def gather(i, c):
            for j in range(CHUNK):
                t = order[jnp.minimum(begin + i * CHUNK + j, 15)]
                ia = jnp.broadcast_to(index[pl.ds(t, 1), :], (8, LANES))
                ib = jnp.broadcast_to(index[pl.ds(16 + t, 1), :], (8, LANES))
                at = pl.ds(pl.multiple_of(8 * t, 8), 8)
                got_a[at, :] = pick(now[:blocks], ia)
                got_b[at, :] = pick(now, ib)
            return c

        lax.fori_loop(0, chunks, gather, 0)
        va = [got_a[tile_rows[c], :] for c in range(6)]
        vb = [got_b[tile_rows[c], :] for c in range(6)]
        arm_a = [held(20 + c) for c in range(3)]
        arm_b = [held(23 + c) for c in range(3)]
        turn_a = cross(va[3:6], arm_a)
        turn_b = cross(vb[3:6], arm_b)
        rel = [((va[c] + turn_a[c]) - vb[c]) - turn_b[c] for c in range(3)]
        old = [imp[c * slots : (c + 1) * slots, :] for c in range(3)]
        trial = [
            old[c] - (dot3([held(3 * c + j) for j in range(3)], rel) + held(9 + c))
            for c in range(3)
        ]
        normal_part = jnp.maximum(trial[0], 0.0)
        slide = jnp.sqrt(trial[1] * trial[1] + trial[2] * trial[2])
        factor = jnp.minimum(1.0, friction * normal_part / jnp.maximum(slide, tangent_floor))
        active = index[32:48, :] == k
        new = [
            jnp.where(active, normal_part, old[0]),
            jnp.where(active, trial[1] * factor, old[1]),
            jnp.where(active, trial[2] * factor, old[2]),
        ]
        change = [new[c] - old[c] for c in range(3)]
        for c in range(3):
            imp[c * slots : (c + 1) * slots, :] = new[c]
        force = [
            held(12) * change[0] + held(17) * change[2],
            held(13) * change[0] + held(15) * change[1] + held(18) * change[2],
            held(14) * change[0] + held(16) * change[1] + held(19) * change[2],
        ]
        spin_a = cross(arm_a, force)
        spin_b = cross(arm_b, force)
        for c in range(3):
            push_a[tile_rows[c], :] = held(26) * force[c]
            push_a[tile_rows[3 + c], :] = held(27 + c) * spin_a[c]
            push_b[tile_rows[c], :] = -(held(30) * force[c])
            push_b[tile_rows[3 + c], :] = -(held(31 + c) * spin_b[c])
        acc[...] = jnp.zeros_like(acc)

        def scatter(i, c):
            own_left, own_right, ghost_left, ghost_right = [], [], [], []
            for j in range(CHUNK):
                t = order[jnp.minimum(begin + i * CHUNK + j, 15)]
                at = pl.ds(pl.multiple_of(8 * t, 8), 8)
                ia = jnp.broadcast_to(index[pl.ds(t, 1), :], (8, LANES))
                ib = jnp.broadcast_to(index[pl.ds(16 + t, 1), :], (8, LANES))
                all_b = masked_rows(push_b[at, :], ib, range(total))
                own_left.append(masked_rows(push_a[at, :], ia, range(blocks)))
                own_left.append(all_b[: 24 * blocks])
                ghost_left.append(all_b[24 * blocks :])
                at_hot = pl.multiple_of(2 * TILE * t, 2 * TILE)
                own_right.append(hot[:, pl.ds(at_hot, 2 * TILE)])
                ghost_right.append(
                    hot[:, pl.ds(pl.multiple_of(at_hot + TILE, TILE), TILE)]
                )
            acc[: 24 * blocks, :] += contract_lanes(
                jnp.concatenate(own_left, axis=1), jnp.concatenate(own_right, axis=1)
            )
            acc[24 * blocks :, :] += contract_lanes(
                jnp.concatenate(ghost_left, axis=1), jnp.concatenate(ghost_right, axis=1)
            )
            return c

        lax.fori_loop(0, chunks, scatter, 0)
        for h in range(total):
            table[8 * h : 8 * h + 8, :] = now[h] + sum_parts(acc, h)
        return carry

    lax.fori_loop(0, NCOLOR, color_pass, 0)
    for h in range(blocks):
        own_change[:, h * LANES : (h + 1) * LANES] = table[8 * h : 8 * h + 8, :] - start[h]
    ghost0[...] = table[8 * blocks : 8 * blocks + 8, :] - start[blocks]
    ghost1[...] = table[8 * blocks + 8 : 8 * blocks + 16, :] - start[blocks + 1]
    if last_sweep:
        for c in range(3):
            for t in range(tiles):
                impulse[c, :, t * TILE : (t + 1) * TILE] = imp[c * slots + t : c * slots + t + 1, :]
    else:
        impulse[...] = imp[...]


def merge_kernel(interface, last_sweep, own, change, c0, c1, c2, c3, mult, export_index, *outs):
    blocks = own.shape[1] // LANES
    idx = [export_index[0:8, :], export_index[8:16, :]]
    came = [halves(c0[...], c1[...], interface), halves(c2[...], c3[...], interface)]
    left = jnp.concatenate(
        [masked_rows(came[i], idx[i], range(blocks)) for i in range(2)], axis=1
    )
    right = jnp.concatenate(
        [low_onehot(export_index[8 * i : 8 * i + 1, :]) for i in range(2)], axis=1
    )
    incoming = contract_lanes(left, right)
    fresh = []
    for h in range(blocks):
        span = slice(h * LANES, (h + 1) * LANES)
        fresh.append(
            own[0:8, span] + (change[:, span] + sum_parts(incoming, h)) / mult[:, span]
        )
    if last_sweep:
        for r in range(6):
            for h in range(blocks):
                outs[0][r, :, h * LANES : (h + 1) * LANES] = fresh[h][r : r + 1, :]
    else:
        for h in range(blocks):
            outs[0][:, h * LANES : (h + 1) * LANES] = fresh[h]
        outs[1][...] = pick(fresh, idx[0])
        outs[2][...] = pick(fresh, idx[1])


def shape(dims, dtype=F32):
    return jax.ShapeDtypeStruct(dims, dtype)


def make(subs, layers):
    matchings = neighbour_matchings(subs, layers)
    shuffles = [relay_shuffle(subs, layers, k) for k in range(1, WIN)]

    def trade(low, high):
        return [
            lax.ppermute(low if m < 2 else high, AXES, matchings[m]) for m in range(4)
        ]

    def on_device(geometry, dest_slot, pairs, colors, free_vel, inertia, exports):
        count = geometry.shape[2]
        bodies = free_vel.shape[2]
        interface = exports.shape[2]
        tiles = count // TILE
        slots = 16
        assert count % TILE == 0 and tiles < slots and 2 * interface == LANES
        assert bodies % LANES == 0
        blocks = bodies // LANES
        total = blocks + 2

        def prepare(*refs):
            prepare_kernel(subs, layers, *refs)

        place = shape((10 * slots, LANES))
        prepared = pl.pallas_call(
            prepare,
            out_shape=(
                place, place, place, place,
                shape((16, bodies)),
                shape((48, LANES), jnp.int32),
                shape((16, LANES), jnp.int32),
                shape((8, bodies)),
                shape((16, LANES)),
                shape((16, LANES)),
                shape((32,), jnp.int32),
            ),
            in_specs=[VMEM_SPEC] * 3 + [SMEM_SPEC] + [VMEM_SPEC] * 3,
            out_specs=(VMEM_SPEC,) * 10 + (SMEM_SPEC,),
            scratch_shapes=[
                pltpu.VMEM((8, LANES), jnp.int32),
                pltpu.VMEM((3, 10 * slots, count), BF16),
                pltpu.VMEM((LANES, count), BF16),
            ],
            name="prepare",
        )(geometry, dest_slot, pairs, colors, free_vel, inertia, exports)
        placed = prepared[:4]
        own, index, export_index, mult, out0, out1, order = prepared[4:]
        came = trade(out0, out1)
        placed = [placed[0]] + [
            lax.ppermute(placed[k], AXES, shuffles[k - 1]) for k in range(1, WIN)
        ]

        state = impulse = None
        for sweep in range(SWEEPS):
            first, last = sweep == 0, sweep == SWEEPS - 1

            def run(*refs, first=first, last=last):
                sweep_kernel(bodies, interface, first, last, *refs)

            outs = [
                shape((3, 1, count)) if last else shape((3 * slots, LANES)),
                shape((8, bodies)),
                shape((8, LANES)),
                shape((8, LANES)),
            ]
            if first:
                outs = [shape((STATE * slots, LANES))] + outs
                operands = [order, index, own, *came, *placed]
            else:
                operands = [order, index, own, *came, state, impulse]
            result = pl.pallas_call(
                run,
                out_shape=tuple(outs),
                in_specs=[SMEM_SPEC] + [VMEM_SPEC] * (len(operands) - 1),
                out_specs=(VMEM_SPEC,) * len(outs),
                scratch_shapes=[
                    pltpu.VMEM((8 * slots, LANES), F32),
                    pltpu.VMEM((8 * slots, LANES), F32),
                    pltpu.VMEM((8 * slots, LANES), F32),
                    pltpu.VMEM((8 * slots, LANES), F32),
                    pltpu.VMEM((LANES, 2 * TILE * (tiles + 1)), BF16),
                    pltpu.VMEM((24 * total, LANES), F32),
                    pltpu.VMEM((8 * total, LANES), F32),
                    pltpu.VMEM((3 * slots, LANES), F32),
                ],
                name="sweep",
            )(*operands)
            if first:
                state, result = result[0], result[1:]
            impulse, change, ghost0, ghost1 = result
            sums = trade(ghost0, ghost1)

            def merge(*refs, last=last):
                merge_kernel(interface, last, *refs)

            outs = (
                (shape((6, 1, bodies)),)
                if last
                else (shape((8, bodies)), shape((8, LANES)), shape((8, LANES)))
            )
            merged = pl.pallas_call(
                merge,
                out_shape=outs,
                in_specs=[VMEM_SPEC] * 8,
                out_specs=(VMEM_SPEC,) * len(outs),
                name="merge",
            )(own, change, *sums, mult, export_index)
            own = merged[0]
            if not last:
                came = trade(merged[1], merged[2])
        return impulse, own

    return on_device


def solution(mesh):
    placed = (
        P(None, "layer", "sub"),
        P("layer", "sub"),
        P(None, "layer", "sub"),
        P("layer", "sub"),
        P(None, "layer", "sub"),
        P(None, "layer", "sub"),
        P(None, "layer", "sub"),
    )
    return jax.shard_map(
        make(mesh.shape["sub"], mesh.shape["layer"]),
        mesh=mesh,
        in_specs=placed,
        out_specs=(P(None, "layer", "sub"), P(None, "layer", "sub")),
        check_vma=False,
    )
```

```python
import jax
import jax.numpy as jnp
from jax import lax
from jax.experimental import pallas as pl
from jax.experimental.pallas import tpu as pltpu
from jax.sharding import PartitionSpec as P

WIN = 4
SWEEPS = 3
NCOLOR = 4
TILE = 128
LANES = 128
CHUNK = 4

relaxation = 0.7
friction = 0.6
tangent_floor = 0.1

AXES = ("sub", "layer")
F32 = jnp.float32
BF16 = jnp.bfloat16
VMEM_SPEC = pl.BlockSpec(memory_space=pltpu.VMEM)
SMEM_SPEC = pl.BlockSpec(memory_space=pltpu.SMEM)
PARAMS = pltpu.CompilerParams(vmem_limit_bytes=16 << 20)


def neighbour_matchings(subs, layers):
    assert subs % 2 == 0 and layers % 2 == 0

    def shifted(i):
        return i - 1 if i % 2 == 0 else i + 1

    def partner(match, s, y):
        if match == 0:
            return s ^ 1, y
        if match == 1:
            return (s, y ^ 1) if s in (0, subs - 1) else (shifted(s), y)
        if match == 2:
            return s, y ^ 1
        return (s ^ 1, y) if y in (0, layers - 1) else (s, shifted(y))

    out = []
    for match in range(4):
        pairs = []
        for s in range(subs):
            for y in range(layers):
                ps, py = partner(match, s, y)
                pairs.append((s * layers + y, ps * layers + py))
        out.append(pairs)
    return out


def relay_shuffle(subs, layers, k):
    return [
        (s * layers + y, (s ^ k) * layers + y) for s in range(subs) for y in range(layers)
    ]


def lane_iota():
    return lax.broadcasted_iota(jnp.int32, (8, LANES), 1)


def pick(tables, index):
    low = jnp.bitwise_and(index, LANES - 1)
    high = jnp.right_shift(index, 7)
    out = jnp.take_along_axis(tables[0], low, axis=1)
    for h in range(1, len(tables)):
        out = jnp.where(high == h, jnp.take_along_axis(tables[h], low, axis=1), out)
    return out


def three_parts(value):
    first = value.astype(BF16).astype(F32)
    rest = value - first
    second = rest.astype(BF16).astype(F32)
    return [first, second, rest - second]


def masked_rows(value, index, highs):
    parts = three_parts(value)
    high = jnp.right_shift(index, 7)
    rows = []
    for h in highs:
        hit = high == h
        rows.extend([jnp.where(hit, part, 0.0) for part in parts])
    return jnp.concatenate(rows, axis=0).astype(BF16)


def low_onehot(index_row):
    low = jnp.bitwise_and(index_row, LANES - 1)
    rows = lax.broadcasted_iota(jnp.int32, (LANES, LANES), 0)
    return jnp.where(rows == low, 1.0, 0.0).astype(BF16)


def contract_lanes(lhs, rhs):
    return lax.dot_general(
        lhs, rhs, (((1,), (1,)), ((), ())), preferred_element_type=F32
    )


def sum_parts(block, h):
    base = 24 * h
    return (block[base : base + 8] + block[base + 8 : base + 16]) + block[base + 16 : base + 24]


def cross(u, v):
    return [
        u[1] * v[2] - u[2] * v[1],
        u[2] * v[0] - u[0] * v[2],
        u[0] * v[1] - u[1] * v[0],
    ]


def dot3(u, v):
    return u[0] * v[0] + u[1] * v[1] + u[2] * v[2]


def halves(low, high, half):
    return jnp.where(lane_iota() < half, low, high)


def prepare_kernel(
    subs, layers, geo, dest, pairs, colors, vel, inertia, exports,
    place0, place1, place2, place3, start_own, index_out, export_index, mult, out0, out1, order,
    listed, lhs, hot,
):
    count = geo.shape[2]
    tiles = count // TILE
    slots = place0.shape[0] // 10
    bodies = vel.shape[2]
    interface = exports.shape[2]
    sub = lax.axis_index("sub")
    layer = lax.axis_index("layer")
    sub_even = lax.rem(sub, 2) == 0
    layer_even = lax.rem(layer, 2) == 0
    member = lax.rem(sub, WIN)
    filled = jnp.int32(0)
    for k in range(NCOLOR):
        order[16 + k] = filled
        for t in range(tiles):
            hit = colors[0, t] == k
            place = jnp.where(hit, filled, 31)
            order[place] = t
            filled = filled + jnp.where(hit, 1, 0)
    order[16 + NCOLOR] = filled
    for t in range(tiles, 16):
        order[t] = tiles
    start_own[...] = jnp.zeros_like(start_own)
    for r in range(6):
        start_own[r : r + 1, :] = vel[r]
    for r in range(4):
        start_own[8 + r : 9 + r, :] = inertia[r]
    listed[0:1, 0:interface] = exports[0]
    listed[0:1, interface : 2 * interface] = exports[1]
    listed[1:2, 0:interface] = exports[1]
    listed[1:2, interface : 2 * interface] = exports[0]
    listed[2:3, 0:interface] = exports[2]
    listed[2:3, interface : 2 * interface] = exports[3]
    listed[3:4, 0:interface] = exports[3]
    listed[3:4, interface : 2 * interface] = exports[2]
    row0 = jnp.where(sub_even, listed[1:2, :], listed[0:1, :])
    row1 = jnp.where(layer_even, listed[3:4, :], listed[2:3, :])
    idx0 = jnp.broadcast_to(row0, (8, LANES))
    idx1 = jnp.broadcast_to(row1, (8, LANES))
    export_index[0:8, :] = idx0
    export_index[8:16, :] = idx1
    blocks = bodies // LANES
    for base in (0, 8):
        tables = [
            start_own[base : base + 8, h * LANES : (h + 1) * LANES] for h in range(blocks)
        ]
        out0[base : base + 8, :] = pick(tables, idx0)
        out1[base : base + 8, :] = pick(tables, idx1)
    inner_sub = jnp.where(jnp.logical_and(sub > 0, sub < subs - 1), 1.0, 0.0)
    inner_layer = jnp.where(jnp.logical_and(layer > 0, layer < layers - 1), 1.0, 0.0)
    lane = lane_iota()
    weight0 = jnp.where(lane < interface, 1.0, inner_sub)
    weight1 = jnp.where(lane < interface, 1.0, inner_layer)
    for h in range(blocks):
        left = jnp.concatenate(
            [
                jnp.where(jnp.right_shift(idx0, 7) == h, weight0, 0.0),
                jnp.where(jnp.right_shift(idx1, 7) == h, weight1, 0.0),
            ],
            axis=1,
        ).astype(BF16)
        right = jnp.concatenate([low_onehot(row0), low_onehot(row1)], axis=1)
        mult[:, h * LANES : (h + 1) * LANES] = 1.0 + contract_lanes(left, right)
    index_out[...] = jnp.zeros_like(index_out)
    flip_sub = jnp.where(sub_even, interface, 0)
    flip_layer = jnp.where(layer_even, interface, 0)
    for t in range(tiles):
        span = pl.ds(t * TILE, TILE)
        index_out[t : t + 1, :] = pairs[0, :, span]
        other = pairs[1, :, span]
        ghost = other - bodies
        turned = jnp.where(
            ghost < 2 * interface,
            jnp.bitwise_xor(ghost, flip_sub),
            jnp.bitwise_xor(ghost, flip_layer),
        )
        index_out[16 + t : 17 + t, :] = jnp.where(ghost < 0, other, bodies + turned)
        index_out[32 + t : 33 + t, :] = jnp.full((1, TILE), colors[0, t], jnp.int32)
    for t in range(tiles, 16):
        index_out[32 + t : 33 + t, :] = jnp.full((1, TILE), -1, jnp.int32)
    slot = dest[...] - (sub - member) * count
    target = jnp.zeros_like(slot)
    for m in range(1, WIN):
        target = target + jnp.where(slot >= m * count, 1, 0)
    within = slot - target * count
    row_id = jnp.bitwise_xor(target, member) * slots + jnp.right_shift(within, 7)
    low = jnp.bitwise_and(within, LANES - 1)
    for t in range(tiles):
        span = pl.ds(t * TILE, TILE)
        hot[:, span] = low_onehot(low[:, t * TILE : (t + 1) * TILE])
    outs = (place0, place1, place2, place3)
    for k in range(WIN):
        rows = lax.broadcasted_iota(jnp.int32, (slots, count), 0) + k * slots
        hit = rows == row_id
        for p in range(3):
            for r in range(10):
                part = three_parts(geo[r])[p]
                lhs[p, r * slots : (r + 1) * slots, :] = jnp.where(hit, part, 0.0).astype(BF16)
        total = contract_lanes(lhs[0], hot[...])
        total = total + contract_lanes(lhs[1], hot[...])
        outs[k][...] = total + contract_lanes(lhs[2], hot[...])


STATE = 34


def contact_state(geo, first, second):
    raw = geo[0:3]
    length = jnp.sqrt(dot3(raw, raw))
    normal = [x / length for x in raw]
    side = jnp.sqrt(normal[1] * normal[1] + normal[2] * normal[2])
    tan_y = normal[2] / side
    tan_z = -normal[1] / side
    two = [
        normal[1] * tan_z - normal[2] * tan_y,
        -normal[0] * tan_z,
        normal[0] * tan_y,
    ]

    def arm(p, spin):
        return [
            spin[1] * p[2] * p[2] + spin[2] * p[1] * p[1],
            spin[0] * p[2] * p[2] + spin[2] * p[0] * p[0],
            spin[0] * p[1] * p[1] + spin[1] * p[0] * p[0],
            -spin[2] * p[0] * p[1],
            -spin[1] * p[0] * p[2],
            -spin[0] * p[1] * p[2],
        ]

    arm_a, arm_b = geo[3:6], geo[6:9]
    e = [x + y for x, y in zip(arm(arm_a, first[1:4]), arm(arm_b, second[1:4]))]
    mass = first[0] + second[0]
    xx, yy, zz = mass + e[0], mass + e[1], mass + e[2]
    xy, xz, yz = e[3], e[4], e[5]
    c_xx = yy * zz - yz * yz
    c_xy = xz * yz - xy * zz
    c_xz = xy * yz - xz * yy
    c_yy = xx * zz - xz * xz
    c_yz = xy * xz - xx * yz
    c_zz = xx * yy - xy * xy
    det = xx * c_xx + xy * c_xy + xz * c_xz
    inv = [
        [c_xx / det, c_xy / det, c_xz / det],
        [c_xy / det, c_yy / det, c_yz / det],
        [c_xz / det, c_yz / det, c_zz / det],
    ]
    solve = []
    for row in (normal, None, two):
        for j in range(3):
            if row is None:
                value = tan_y * inv[1][j] + tan_z * inv[2][j]
            else:
                value = row[0] * inv[0][j] + row[1] * inv[1][j] + row[2] * inv[2][j]
            solve.append(relaxation * value)
    bias = [geo[9] * dot3(solve[3 * i : 3 * i + 3], normal) for i in range(3)]
    return (
        solve + bias + normal + [tan_y, tan_z] + two + arm_a + arm_b + list(first) + list(second)
    )


def sweep_kernel(bodies, interface, first_sweep, last_sweep, *refs):
    refs = list(refs)
    order, index = refs[0], refs[1]
    refs = refs[2:]
    if first_sweep:
        own, r0, r1, r2, r3, g0, g1, g2, g3 = refs[:9]
        refs = refs[9:]
    else:
        own, r0, r1, r2, r3, state, impulse_in = refs[:7]
        refs = refs[7:]
    if first_sweep:
        state = refs.pop(0)
    impulse, own_change, ghost0, ghost1 = refs[:4]
    refs = refs[4:]
    got_a, got_b, push_a, push_b, hot, acc, table, imp = refs
    slots = 16
    tiles = hot.shape[1] // (2 * TILE) - 1
    blocks = bodies // LANES
    ghosts = (4 * interface) // LANES
    total = blocks + ghosts
    tile_rows = [pl.ds(c, slots, stride=8) for c in range(8)]

    def ghost_blocks(base):
        return [
            halves(r0[base : base + 8, :], r1[base : base + 8, :], interface),
            halves(r2[base : base + 8, :], r3[base : base + 8, :], interface),
        ]

    start = [own[0:8, h * LANES : (h + 1) * LANES] for h in range(blocks)] + ghost_blocks(0)
    for h in range(total):
        table[8 * h : 8 * h + 8, :] = start[h]

    for t in range(tiles):
        hot[:, 2 * t * TILE : (2 * t + 1) * TILE] = low_onehot(index[t : t + 1, :])
        hot[:, (2 * t + 1) * TILE : (2 * t + 2) * TILE] = low_onehot(index[16 + t : 17 + t, :])
    hot[:, 2 * tiles * TILE :] = jnp.zeros((LANES, 2 * TILE), BF16)

    push_a[...] = jnp.zeros_like(push_a)
    push_b[...] = jnp.zeros_like(push_b)

    if first_sweep:
        props = [own[8:16, h * LANES : (h + 1) * LANES] for h in range(blocks)] + ghost_blocks(8)
        got_a[...] = jnp.ones_like(got_a)
        got_b[...] = jnp.ones_like(got_b)
        for t in range(tiles):
            ia = jnp.broadcast_to(index[t : t + 1, :], (8, LANES))
            ib = jnp.broadcast_to(index[16 + t : 17 + t, :], (8, LANES))
            got_a[8 * t : 8 * t + 8, :] = pick(props[:blocks], ia)
            got_b[8 * t : 8 * t + 8, :] = pick(props, ib)
        first = [got_a[tile_rows[c], :] for c in range(4)]
        second = [got_b[tile_rows[c], :] for c in range(4)]
        real = lax.broadcasted_iota(jnp.int32, (slots, LANES), 0) < tiles
        geo = []
        for c in range(10):
            span = slice(c * slots, (c + 1) * slots)
            value = (g0[span, :] + g1[span, :]) + (g2[span, :] + g3[span, :])
            geo.append(jnp.where(real, value, 1.0))
        for c, value in enumerate(contact_state(geo, first, second)):
            state[c * slots : (c + 1) * slots, :] = value
        imp[...] = jnp.zeros_like(imp)
    else:
        imp[...] = impulse_in[...]

    def held(c):
        return state[c * slots : (c + 1) * slots, :]

    def color_pass(k, carry):
        begin = order[16 + k]
        chunks = lax.div(order[17 + k] - begin + (CHUNK - 1), CHUNK)
        now = [table[8 * h : 8 * h + 8, :] for h in range(total)]

        def gather(i, c):
            for j in range(CHUNK):
                t = order[jnp.minimum(begin + i * CHUNK + j, 15)]
                ia = jnp.broadcast_to(index[pl.ds(t, 1), :], (8, LANES))
                ib = jnp.broadcast_to(index[pl.ds(16 + t, 1), :], (8, LANES))
                at = pl.ds(pl.multiple_of(8 * t, 8), 8)
                got_a[at, :] = pick(now[:blocks], ia)
                got_b[at, :] = pick(now, ib)
            return c

        lax.fori_loop(0, chunks, gather, 0)
        va = [got_a[tile_rows[c], :] for c in range(6)]
        vb = [got_b[tile_rows[c], :] for c in range(6)]
        arm_a = [held(20 + c) for c in range(3)]
        arm_b = [held(23 + c) for c in range(3)]
        turn_a = cross(va[3:6], arm_a)
        turn_b = cross(vb[3:6], arm_b)
        rel = [((va[c] + turn_a[c]) - vb[c]) - turn_b[c] for c in range(3)]
        old = [imp[c * slots : (c + 1) * slots, :] for c in range(3)]
        trial = [
            old[c] - (dot3([held(3 * c + j) for j in range(3)], rel) + held(9 + c))
            for c in range(3)
        ]
        normal_part = jnp.maximum(trial[0], 0.0)
        slide = jnp.sqrt(trial[1] * trial[1] + trial[2] * trial[2])
        factor = jnp.minimum(1.0, friction * normal_part / jnp.maximum(slide, tangent_floor))
        active = index[32:48, :] == k
        new = [
            jnp.where(active, normal_part, old[0]),
            jnp.where(active, trial[1] * factor, old[1]),
            jnp.where(active, trial[2] * factor, old[2]),
        ]
        change = [new[c] - old[c] for c in range(3)]
        for c in range(3):
            imp[c * slots : (c + 1) * slots, :] = new[c]
        force = [
            held(12) * change[0] + held(17) * change[2],
            held(13) * change[0] + held(15) * change[1] + held(18) * change[2],
            held(14) * change[0] + held(16) * change[1] + held(19) * change[2],
        ]
        spin_a = cross(arm_a, force)
        spin_b = cross(arm_b, force)
        for c in range(3):
            push_a[tile_rows[c], :] = held(26) * force[c]
            push_a[tile_rows[3 + c], :] = held(27 + c) * spin_a[c]
            push_b[tile_rows[c], :] = -(held(30) * force[c])
            push_b[tile_rows[3 + c], :] = -(held(31 + c) * spin_b[c])
        acc[...] = jnp.zeros_like(acc)

        def scatter(i, c):
            own_left, own_right, ghost_left, ghost_right = [], [], [], []
            for j in range(CHUNK):
                t = order[jnp.minimum(begin + i * CHUNK + j, 15)]
                at = pl.ds(pl.multiple_of(8 * t, 8), 8)
                ia = jnp.broadcast_to(index[pl.ds(t, 1), :], (8, LANES))
                ib = jnp.broadcast_to(index[pl.ds(16 + t, 1), :], (8, LANES))
                all_b = masked_rows(push_b[at, :], ib, range(total))
                own_left.append(masked_rows(push_a[at, :], ia, range(blocks)))
                own_left.append(all_b[: 24 * blocks])
                ghost_left.append(all_b[24 * blocks :])
                at_hot = pl.multiple_of(2 * TILE * t, 2 * TILE)
                own_right.append(hot[:, pl.ds(at_hot, 2 * TILE)])
                ghost_right.append(
                    hot[:, pl.ds(pl.multiple_of(at_hot + TILE, TILE), TILE)]
                )
            acc[: 24 * blocks, :] += contract_lanes(
                jnp.concatenate(own_left, axis=1), jnp.concatenate(own_right, axis=1)
            )
            acc[24 * blocks :, :] += contract_lanes(
                jnp.concatenate(ghost_left, axis=1), jnp.concatenate(ghost_right, axis=1)
            )
            return c

        lax.fori_loop(0, chunks, scatter, 0)
        for h in range(total):
            table[8 * h : 8 * h + 8, :] = now[h] + sum_parts(acc, h)
        return carry

    lax.fori_loop(0, NCOLOR, color_pass, 0)
    for h in range(blocks):
        own_change[:, h * LANES : (h + 1) * LANES] = table[8 * h : 8 * h + 8, :] - start[h]
    ghost0[...] = table[8 * blocks : 8 * blocks + 8, :] - start[blocks]
    ghost1[...] = table[8 * blocks + 8 : 8 * blocks + 16, :] - start[blocks + 1]
    if last_sweep:
        for c in range(3):
            for t in range(tiles):
                impulse[c, :, t * TILE : (t + 1) * TILE] = imp[c * slots + t : c * slots + t + 1, :]
    else:
        impulse[...] = imp[...]


def merge_kernel(interface, last_sweep, own, change, c0, c1, c2, c3, mult, export_index, *outs):
    blocks = own.shape[1] // LANES
    idx = [export_index[0:8, :], export_index[8:16, :]]
    came = [halves(c0[...], c1[...], interface), halves(c2[...], c3[...], interface)]
    left = jnp.concatenate(
        [masked_rows(came[i], idx[i], range(blocks)) for i in range(2)], axis=1
    )
    right = jnp.concatenate(
        [low_onehot(export_index[8 * i : 8 * i + 1, :]) for i in range(2)], axis=1
    )
    incoming = contract_lanes(left, right)
    fresh = []
    for h in range(blocks):
        span = slice(h * LANES, (h + 1) * LANES)
        fresh.append(
            own[0:8, span] + (change[:, span] + sum_parts(incoming, h)) / mult[:, span]
        )
    if last_sweep:
        for r in range(6):
            for h in range(blocks):
                outs[0][r, :, h * LANES : (h + 1) * LANES] = fresh[h][r : r + 1, :]
    else:
        for h in range(blocks):
            outs[0][:, h * LANES : (h + 1) * LANES] = fresh[h]
        outs[1][...] = pick(fresh, idx[0])
        outs[2][...] = pick(fresh, idx[1])


def shape(dims, dtype=F32):
    return jax.ShapeDtypeStruct(dims, dtype)


def make(subs, layers):
    matchings = neighbour_matchings(subs, layers)
    shuffles = [relay_shuffle(subs, layers, k) for k in range(1, WIN)]

    def trade(low, high):
        return [
            lax.ppermute(low if m < 2 else high, AXES, matchings[m]) for m in range(4)
        ]

    def on_device(geometry, dest_slot, pairs, colors, free_vel, inertia, exports):
        count = geometry.shape[2]
        bodies = free_vel.shape[2]
        interface = exports.shape[2]
        tiles = count // TILE
        slots = 16
        assert count % TILE == 0 and tiles < slots and 2 * interface == LANES
        assert bodies % LANES == 0
        blocks = bodies // LANES
        total = blocks + 2

        def prepare(*refs):
            prepare_kernel(subs, layers, *refs)

        place = shape((10 * slots, LANES))
        prepared = pl.pallas_call(
            prepare,
            out_shape=(
                place, place, place, place,
                shape((16, bodies)),
                shape((48, LANES), jnp.int32),
                shape((16, LANES), jnp.int32),
                shape((8, bodies)),
                shape((16, LANES)),
                shape((16, LANES)),
                shape((32,), jnp.int32),
            ),
            in_specs=[VMEM_SPEC] * 3 + [SMEM_SPEC] + [VMEM_SPEC] * 3,
            out_specs=(VMEM_SPEC,) * 10 + (SMEM_SPEC,),
            scratch_shapes=[
                pltpu.VMEM((8, LANES), jnp.int32),
                pltpu.VMEM((3, 10 * slots, count), BF16),
                pltpu.VMEM((LANES, count), BF16),
            ],
            compiler_params=PARAMS,
            name="prepare",
        )(geometry, dest_slot, pairs, colors, free_vel, inertia, exports)
        placed = prepared[:4]
        own, index, export_index, mult, out0, out1, order = prepared[4:]
        came = trade(out0, out1)
        placed = [placed[0]] + [
            lax.ppermute(placed[k], AXES, shuffles[k - 1]) for k in range(1, WIN)
        ]

        state = impulse = None
        for sweep in range(SWEEPS):
            first, last = sweep == 0, sweep == SWEEPS - 1

            def run(*refs, first=first, last=last):
                sweep_kernel(bodies, interface, first, last, *refs)

            outs = [
                shape((3, 1, count)) if last else shape((3 * slots, LANES)),
                shape((8, bodies)),
                shape((8, LANES)),
                shape((8, LANES)),
            ]
            if first:
                outs = [shape((STATE * slots, LANES))] + outs
                operands = [order, index, own, *came, *placed]
            else:
                operands = [order, index, own, *came, state, impulse]
            result = pl.pallas_call(
                run,
                out_shape=tuple(outs),
                in_specs=[SMEM_SPEC] + [VMEM_SPEC] * (len(operands) - 1),
                out_specs=(VMEM_SPEC,) * len(outs),
                scratch_shapes=[
                    pltpu.VMEM((8 * slots, LANES), F32),
                    pltpu.VMEM((8 * slots, LANES), F32),
                    pltpu.VMEM((8 * slots, LANES), F32),
                    pltpu.VMEM((8 * slots, LANES), F32),
                    pltpu.VMEM((LANES, 2 * TILE * (tiles + 1)), BF16),
                    pltpu.VMEM((24 * total, LANES), F32),
                    pltpu.VMEM((8 * total, LANES), F32),
                    pltpu.VMEM((3 * slots, LANES), F32),
                ],
                compiler_params=PARAMS,
                name="sweep",
            )(*operands)
            if first:
                state, result = result[0], result[1:]
            impulse, change, ghost0, ghost1 = result
            sums = trade(ghost0, ghost1)

            def merge(*refs, last=last):
                merge_kernel(interface, last, *refs)

            outs = (
                (shape((6, 1, bodies)),)
                if last
                else (shape((8, bodies)), shape((8, LANES)), shape((8, LANES)))
            )
            merged = pl.pallas_call(
                merge,
                out_shape=outs,
                in_specs=[VMEM_SPEC] * 8,
                out_specs=(VMEM_SPEC,) * len(outs),
                compiler_params=PARAMS,
                name="merge",
            )(own, change, *sums, mult, export_index)
            own = merged[0]
            if not last:
                came = trade(merged[1], merged[2])
        return impulse, own

    return on_device


def solution(mesh):
    placed = (
        P(None, "layer", "sub"),
        P("layer", "sub"),
        P(None, "layer", "sub"),
        P("layer", "sub"),
        P(None, "layer", "sub"),
        P(None, "layer", "sub"),
        P(None, "layer", "sub"),
    )
    return jax.shard_map(
        make(mesh.shape["sub"], mesh.shape["layer"]),
        mesh=mesh,
        in_specs=placed,
        out_specs=(P(None, "layer", "sub"), P(None, "layer", "sub")),
        check_vma=False,
    )
```

```python
import jax
import jax.numpy as jnp
from jax import lax
from jax.experimental import pallas as pl
from jax.experimental.pallas import tpu as pltpu
from jax.sharding import PartitionSpec as P

WIN = 4
SWEEPS = 3
NCOLOR = 4
TILE = 128
LANES = 128
CHUNK = 4

relaxation = 0.7
friction = 0.6
tangent_floor = 0.1

AXES = ("sub", "layer")
F32 = jnp.float32
BF16 = jnp.bfloat16
VMEM_SPEC = pl.BlockSpec(memory_space=pltpu.VMEM)
SMEM_SPEC = pl.BlockSpec(memory_space=pltpu.SMEM)
PARAMS = pltpu.CompilerParams(vmem_limit_bytes=16 << 20)


def neighbour_matchings(subs, layers):
    assert subs % 2 == 0 and layers % 2 == 0

    def shifted(i):
        return i - 1 if i % 2 == 0 else i + 1

    def partner(match, s, y):
        if match == 0:
            return s ^ 1, y
        if match == 1:
            return (s, y ^ 1) if s in (0, subs - 1) else (shifted(s), y)
        if match == 2:
            return s, y ^ 1
        return (s ^ 1, y) if y in (0, layers - 1) else (s, shifted(y))

    out = []
    for match in range(4):
        pairs = []
        for s in range(subs):
            for y in range(layers):
                ps, py = partner(match, s, y)
                pairs.append((s * layers + y, ps * layers + py))
        out.append(pairs)
    return out


def relay_shuffle(subs, layers, k):
    return [
        (s * layers + y, (s ^ k) * layers + y) for s in range(subs) for y in range(layers)
    ]


def lane_iota():
    return lax.broadcasted_iota(jnp.int32, (8, LANES), 1)


def pick(tables, index):
    low = jnp.bitwise_and(index, LANES - 1)
    high = jnp.right_shift(index, 7)
    out = jnp.take_along_axis(tables[0], low, axis=1)
    for h in range(1, len(tables)):
        out = jnp.where(high == h, jnp.take_along_axis(tables[h], low, axis=1), out)
    return out


def two_parts(value):
    first = value.astype(BF16).astype(F32)
    return jnp.concatenate([first, value - first], axis=0).astype(BF16)


def high_masks(index_row, highs):
    high = jnp.broadcast_to(jnp.right_shift(index_row, 7), (16, LANES))
    return jnp.concatenate(
        [jnp.where(high == h, 1.0, 0.0) for h in range(highs)], axis=0
    ).astype(BF16)


def low_onehot(index_row):
    low = jnp.bitwise_and(index_row, LANES - 1)
    rows = lax.broadcasted_iota(jnp.int32, (LANES, LANES), 0)
    return jnp.where(rows == low, 1.0, 0.0).astype(BF16)


def contract_lanes(lhs, rhs):
    return lax.dot_general(
        lhs, rhs, (((1,), (1,)), ((), ())), preferred_element_type=F32
    )


def sum_parts(block, h):
    return block[16 * h : 16 * h + 8] + block[16 * h + 8 : 16 * h + 16]


def cross(u, v):
    return [
        u[1] * v[2] - u[2] * v[1],
        u[2] * v[0] - u[0] * v[2],
        u[0] * v[1] - u[1] * v[0],
    ]


def dot3(u, v):
    return u[0] * v[0] + u[1] * v[1] + u[2] * v[2]


def halves(low, high, half):
    return jnp.where(lane_iota() < half, low, high)


def parities():
    sub = lax.axis_index("sub")
    layer = lax.axis_index("layer")
    return sub, layer, lax.rem(sub, 2) == 0, lax.rem(layer, 2) == 0


def prepare_kernel(
    geo_hbm, dest_hbm, vel_hbm, inertia_hbm, exports_hbm,
    place0, send0, place2, place3, out0, out1, start_own, export_index,
    geo, dest, vel, inertia, exports, listed, dense, mask, lhs, hot, sems,
):
    copies = [
        pltpu.make_async_copy(src, dst, sems.at[i])
        for i, (src, dst) in enumerate(
            [
                (exports_hbm, exports),
                (vel_hbm, vel),
                (inertia_hbm, inertia),
                (dest_hbm, dest),
                (geo_hbm, geo),
            ]
        )
    ]
    for copy in copies:
        copy.start()
    count = geo.shape[2]
    tiles = count // TILE
    slots = place0.shape[0] // 10
    bodies = vel.shape[2]
    interface = exports.shape[2]
    sub, layer, sub_even, layer_even = parities()
    member = lax.rem(sub, WIN)
    start_own[...] = jnp.zeros_like(start_own)
    dense[...] = jnp.zeros_like(dense)
    for copy in copies[:4]:
        copy.wait()
    for r in range(6):
        start_own[r : r + 1, :] = vel[r]
    for r in range(4):
        start_own[8 + r : 9 + r, :] = inertia[r]
    listed[0:1, 0:interface] = exports[0]
    listed[0:1, interface : 2 * interface] = exports[1]
    listed[1:2, 0:interface] = exports[1]
    listed[1:2, interface : 2 * interface] = exports[0]
    listed[2:3, 0:interface] = exports[2]
    listed[2:3, interface : 2 * interface] = exports[3]
    listed[3:4, 0:interface] = exports[3]
    listed[3:4, interface : 2 * interface] = exports[2]
    row0 = jnp.where(sub_even, listed[1:2, :], listed[0:1, :])
    row1 = jnp.where(layer_even, listed[3:4, :], listed[2:3, :])
    idx0 = jnp.broadcast_to(row0, (8, LANES))
    idx1 = jnp.broadcast_to(row1, (8, LANES))
    export_index[0:8, :] = idx0
    export_index[8:16, :] = idx1
    blocks = bodies // LANES
    for base in (0, 8):
        tables = [
            start_own[base : base + 8, h * LANES : (h + 1) * LANES] for h in range(blocks)
        ]
        picked = pick(tables, idx0)
        out0[base : base + 8, :] = picked
        send0[10 * slots + base : 10 * slots + base + 8, :] = picked
        out1[base : base + 8, :] = pick(tables, idx1)
    slot = dest[...] - (sub - member) * count
    target = jnp.zeros_like(slot)
    for m in range(1, WIN):
        target = target + jnp.where(slot >= m * count, 1, 0)
    within = slot - target * count
    row_id = jnp.bitwise_xor(target, member) * slots + jnp.right_shift(within, 7)
    low = jnp.bitwise_and(within, LANES - 1)
    rows = lax.broadcasted_iota(jnp.int32, (WIN * slots, TILE), 0)
    for t in range(tiles):
        span = slice(t * TILE, (t + 1) * TILE)
        hot[:, span] = low_onehot(low[:, span])
        mask[:, span] = jnp.where(rows == row_id[:, span], 1.0, 0.0).astype(BF16)
    copies[4].wait()
    for r in range(10):
        dense[r : r + 1, :] = geo[r]
    value = dense[...]
    first = value.astype(BF16).astype(F32)
    parts = [first, value - first]
    for p in range(2):
        for r in range(10):
            row = jnp.broadcast_to(parts[p][r : r + 1, :], (slots, count)).astype(BF16)
            for k in range(WIN):
                at = (10 * k + r) * slots
                lhs[p, at : at + slots, :] = mask[k * slots : (k + 1) * slots, :] * row
    outs = (place0, send0, place2, place3)
    for k in range(WIN):
        span = slice(10 * slots * k, 10 * slots * (k + 1))
        total = contract_lanes(lhs[0, span, :], hot[...])
        total = total + contract_lanes(lhs[1, span, :], hot[...])
        outs[k][0 : 10 * slots, :] = total


def index_kernel(
    subs, layers, interface, bodies, pairs, colors, export_index,
    index_out, hot, masks, export_hot, export_masks, mult, order,
):
    count = pairs.shape[2]
    tiles = count // TILE
    blocks = bodies // LANES
    total = blocks + 4 * interface // LANES
    sub, layer, sub_even, layer_even = parities()
    filled = jnp.int32(0)
    for k in range(NCOLOR):
        order[16 + k] = filled
        for t in range(tiles):
            hit = colors[0, t] == k
            place = jnp.where(hit, filled, 31)
            order[place] = t
            filled = filled + jnp.where(hit, 1, 0)
    order[16 + NCOLOR] = filled
    for t in range(tiles, 16):
        order[t] = tiles
    index_out[...] = jnp.zeros_like(index_out)
    flip_sub = jnp.where(sub_even, interface, 0)
    flip_layer = jnp.where(layer_even, interface, 0)
    for t in range(tiles):
        span = slice(t * TILE, (t + 1) * TILE)
        first = pairs[0, :, span]
        other = pairs[1, :, span]
        ghost = other - bodies
        turned = jnp.where(
            ghost < 2 * interface,
            jnp.bitwise_xor(ghost, flip_sub),
            jnp.bitwise_xor(ghost, flip_layer),
        )
        second = jnp.where(ghost < 0, other, bodies + turned)
        index_out[t : t + 1, :] = first
        index_out[16 + t : 17 + t, :] = second
        index_out[32 + t : 33 + t, :] = jnp.full((1, TILE), colors[0, t], jnp.int32)
        hot[:, 2 * t * TILE : (2 * t + 1) * TILE] = low_onehot(first)
        hot[:, (2 * t + 1) * TILE : (2 * t + 2) * TILE] = low_onehot(second)
        masks[t, : 16 * blocks, :] = high_masks(first, blocks)
        masks[t, 16 * blocks :, :] = high_masks(second, total)
    for t in range(tiles, 16):
        index_out[32 + t : 33 + t, :] = jnp.full((1, TILE), -1, jnp.int32)
    hot[:, 2 * tiles * TILE :] = jnp.zeros((LANES, 2 * TILE), BF16)
    masks[tiles] = jnp.zeros_like(masks[tiles])
    inner_sub = jnp.where(jnp.logical_and(sub > 0, sub < subs - 1), 1.0, 0.0)
    inner_layer = jnp.where(jnp.logical_and(layer > 0, layer < layers - 1), 1.0, 0.0)
    lane = lane_iota()
    weights = [
        jnp.where(lane < interface, 1.0, inner_sub),
        jnp.where(lane < interface, 1.0, inner_layer),
    ]
    left = []
    for i in range(2):
        row = export_index[8 * i : 8 * i + 1, :]
        export_hot[:, i * LANES : (i + 1) * LANES] = low_onehot(row)
        chosen = high_masks(row, blocks)
        export_masks[i] = chosen
        weight = jnp.concatenate([weights[i], jnp.zeros_like(weights[i])], axis=0).astype(BF16)
        left.append(jnp.concatenate([weight] * blocks, axis=0) * chosen)
    listed = contract_lanes(jnp.concatenate(left, axis=1), export_hot[...])
    for h in range(blocks):
        mult[:, h * LANES : (h + 1) * LANES] = 1.0 + listed[16 * h : 16 * h + 8]


STATE = 34


def contact_state(geo, first, second):
    raw = geo[0:3]
    length = jnp.sqrt(dot3(raw, raw))
    normal = [x / length for x in raw]
    side = jnp.sqrt(normal[1] * normal[1] + normal[2] * normal[2])
    tan_y = normal[2] / side
    tan_z = -normal[1] / side
    two = [
        normal[1] * tan_z - normal[2] * tan_y,
        -normal[0] * tan_z,
        normal[0] * tan_y,
    ]

    def arm(p, spin):
        return [
            spin[1] * p[2] * p[2] + spin[2] * p[1] * p[1],
            spin[0] * p[2] * p[2] + spin[2] * p[0] * p[0],
            spin[0] * p[1] * p[1] + spin[1] * p[0] * p[0],
            -spin[2] * p[0] * p[1],
            -spin[1] * p[0] * p[2],
            -spin[0] * p[1] * p[2],
        ]

    arm_a, arm_b = geo[3:6], geo[6:9]
    e = [x + y for x, y in zip(arm(arm_a, first[1:4]), arm(arm_b, second[1:4]))]
    mass = first[0] + second[0]
    xx, yy, zz = mass + e[0], mass + e[1], mass + e[2]
    xy, xz, yz = e[3], e[4], e[5]
    c_xx = yy * zz - yz * yz
    c_xy = xz * yz - xy * zz
    c_xz = xy * yz - xz * yy
    c_yy = xx * zz - xz * xz
    c_yz = xy * xz - xx * yz
    c_zz = xx * yy - xy * xy
    det = xx * c_xx + xy * c_xy + xz * c_xz
    inv = [
        [c_xx / det, c_xy / det, c_xz / det],
        [c_xy / det, c_yy / det, c_yz / det],
        [c_xz / det, c_yz / det, c_zz / det],
    ]
    solve = []
    for row in (normal, None, two):
        for j in range(3):
            if row is None:
                value = tan_y * inv[1][j] + tan_z * inv[2][j]
            else:
                value = row[0] * inv[0][j] + row[1] * inv[1][j] + row[2] * inv[2][j]
            solve.append(relaxation * value)
    bias = [geo[9] * dot3(solve[3 * i : 3 * i + 3], normal) for i in range(3)]
    return (
        solve + bias + normal + [tan_y, tan_z] + two + arm_a + arm_b + list(first) + list(second)
    )


def sweep_kernel(bodies, interface, first_sweep, *refs):
    refs = list(refs)
    order, index, hot, masks = refs[:4]
    refs = refs[4:]
    if first_sweep:
        own, g1, r1, r2, r3, g0, g2, g3 = refs[:8]
        refs = refs[8:]
        r0 = g1.at[pl.ds(g0.shape[0], 16), :]
    else:
        own, r0, r1, r2, r3, state, impulse_in = refs[:7]
        refs = refs[7:]
    if first_sweep:
        state = refs.pop(0)
    impulse, own_change, ghost0, ghost1 = refs[:4]
    refs = refs[4:]
    got_a, got_b, push_a, push_b, acc, table, imp = refs
    slots = 16
    tiles = masks.shape[0] - 1
    blocks = bodies // LANES
    ghosts = (4 * interface) // LANES
    total = blocks + ghosts
    tile_rows = [pl.ds(c, slots, stride=8) for c in range(8)]

    def ghost_blocks(base):
        return [
            halves(r0[base : base + 8, :], r1[base : base + 8, :], interface),
            halves(r2[base : base + 8, :], r3[base : base + 8, :], interface),
        ]

    start = [own[0:8, h * LANES : (h + 1) * LANES] for h in range(blocks)] + ghost_blocks(0)
    for h in range(total):
        table[8 * h : 8 * h + 8, :] = start[h]

    push_a[...] = jnp.zeros_like(push_a)
    push_b[...] = jnp.zeros_like(push_b)

    if first_sweep:
        props = [own[8:16, h * LANES : (h + 1) * LANES] for h in range(blocks)] + ghost_blocks(8)
        got_a[...] = jnp.ones_like(got_a)
        got_b[...] = jnp.ones_like(got_b)
        for t in range(tiles):
            ia = jnp.broadcast_to(index[t : t + 1, :], (8, LANES))
            ib = jnp.broadcast_to(index[16 + t : 17 + t, :], (8, LANES))
            got_a[8 * t : 8 * t + 8, :] = pick(props[:blocks], ia)
            got_b[8 * t : 8 * t + 8, :] = pick(props, ib)
        first = [got_a[tile_rows[c], :] for c in range(4)]
        second = [got_b[tile_rows[c], :] for c in range(4)]
        real = lax.broadcasted_iota(jnp.int32, (slots, LANES), 0) < tiles
        geo = []
        for c in range(10):
            span = slice(c * slots, (c + 1) * slots)
            value = (g0[span, :] + g1[span, :]) + (g2[span, :] + g3[span, :])
            geo.append(jnp.where(real, value, 1.0))
        for c, value in enumerate(contact_state(geo, first, second)):
            state[c * slots : (c + 1) * slots, :] = value
        imp[...] = jnp.zeros_like(imp)
    else:
        imp[...] = impulse_in[...]

    def held(c):
        return state[c * slots : (c + 1) * slots, :]

    def color_pass(k, carry):
        begin = order[16 + k]
        chunks = lax.div(order[17 + k] - begin + (CHUNK - 1), CHUNK)
        now = [table[8 * h : 8 * h + 8, :] for h in range(total)]

        def gather(i, c):
            for j in range(CHUNK):
                t = order[jnp.minimum(begin + i * CHUNK + j, 15)]
                ia = jnp.broadcast_to(index[pl.ds(t, 1), :], (8, LANES))
                ib = jnp.broadcast_to(index[pl.ds(16 + t, 1), :], (8, LANES))
                at = pl.ds(pl.multiple_of(8 * t, 8), 8)
                got_a[at, :] = pick(now[:blocks], ia)
                got_b[at, :] = pick(now, ib)
            return c

        lax.fori_loop(0, chunks, gather, 0)
        va = [got_a[tile_rows[c], :] for c in range(6)]
        vb = [got_b[tile_rows[c], :] for c in range(6)]
        arm_a = [held(20 + c) for c in range(3)]
        arm_b = [held(23 + c) for c in range(3)]
        turn_a = cross(va[3:6], arm_a)
        turn_b = cross(vb[3:6], arm_b)
        rel = [((va[c] + turn_a[c]) - vb[c]) - turn_b[c] for c in range(3)]
        old = [imp[c * slots : (c + 1) * slots, :] for c in range(3)]
        trial = [
            old[c] - (dot3([held(3 * c + j) for j in range(3)], rel) + held(9 + c))
            for c in range(3)
        ]
        normal_part = jnp.maximum(trial[0], 0.0)
        slide = jnp.sqrt(trial[1] * trial[1] + trial[2] * trial[2])
        factor = jnp.minimum(1.0, friction * normal_part / jnp.maximum(slide, tangent_floor))
        active = index[32:48, :] == k
        new = [
            jnp.where(active, normal_part, old[0]),
            jnp.where(active, trial[1] * factor, old[1]),
            jnp.where(active, trial[2] * factor, old[2]),
        ]
        change = [new[c] - old[c] for c in range(3)]
        for c in range(3):
            imp[c * slots : (c + 1) * slots, :] = new[c]
        force = [
            held(12) * change[0] + held(17) * change[2],
            held(13) * change[0] + held(15) * change[1] + held(18) * change[2],
            held(14) * change[0] + held(16) * change[1] + held(19) * change[2],
        ]
        spin_a = cross(arm_a, force)
        spin_b = cross(arm_b, force)
        for c in range(3):
            push_a[tile_rows[c], :] = held(26) * force[c]
            push_a[tile_rows[3 + c], :] = held(27 + c) * spin_a[c]
            push_b[tile_rows[c], :] = -(held(30) * force[c])
            push_b[tile_rows[3 + c], :] = -(held(31 + c) * spin_b[c])
        acc[...] = jnp.zeros_like(acc)

        def scatter(i, c):
            own_left, own_right, ghost_left, ghost_right = [], [], [], []
            for j in range(CHUNK):
                t = order[jnp.minimum(begin + i * CHUNK + j, 15)]
                at = pl.ds(pl.multiple_of(8 * t, 8), 8)
                first = two_parts(push_a[at, :])
                second = two_parts(push_b[at, :])
                rows = [masks[t, 16 * m : 16 * m + 16, :] for m in range(blocks + total)]
                own_left.append(jnp.concatenate([first * m for m in rows[:blocks]], axis=0))
                own_left.append(
                    jnp.concatenate([second * m for m in rows[blocks : 2 * blocks]], axis=0)
                )
                ghost_left.append(
                    jnp.concatenate([second * m for m in rows[2 * blocks :]], axis=0)
                )
                at_hot = pl.multiple_of(2 * TILE * t, 2 * TILE)
                own_right.append(hot[:, pl.ds(at_hot, 2 * TILE)])
                ghost_right.append(
                    hot[:, pl.ds(pl.multiple_of(at_hot + TILE, TILE), TILE)]
                )
            acc[: 16 * blocks, :] += contract_lanes(
                jnp.concatenate(own_left, axis=1), jnp.concatenate(own_right, axis=1)
            )
            acc[16 * blocks :, :] += contract_lanes(
                jnp.concatenate(ghost_left, axis=1), jnp.concatenate(ghost_right, axis=1)
            )
            return c

        lax.fori_loop(0, chunks, scatter, 0)
        for h in range(total):
            table[8 * h : 8 * h + 8, :] = now[h] + sum_parts(acc, h)
        return carry

    lax.fori_loop(0, NCOLOR, color_pass, 0)
    for h in range(blocks):
        own_change[:, h * LANES : (h + 1) * LANES] = table[8 * h : 8 * h + 8, :] - start[h]
    ghost0[...] = table[8 * blocks : 8 * blocks + 8, :] - start[blocks]
    ghost1[...] = table[8 * blocks + 8 : 8 * blocks + 16, :] - start[blocks + 1]
    impulse[...] = imp[...]


def merge_kernel(
    interface, last_sweep, own, change, c0, c1, c2, c3, mult, export_index, export_hot,
    export_masks, *refs,
):
    blocks = own.shape[1] // LANES
    came = [halves(c0[...], c1[...], interface), halves(c2[...], c3[...], interface)]
    left = jnp.concatenate(
        [
            jnp.concatenate([two_parts(came[i])] * blocks, axis=0) * export_masks[i]
            for i in range(2)
        ],
        axis=1,
    )
    incoming = contract_lanes(left, export_hot[...])
    fresh = []
    for h in range(blocks):
        span = slice(h * LANES, (h + 1) * LANES)
        fresh.append(
            own[0:8, span] + (change[:, span] + sum_parts(incoming, h)) / mult[:, span]
        )
    if last_sweep:
        imp, impulse, velocity = refs
        slots = imp.shape[0] // 3
        for c in range(3):
            for t in range(impulse.shape[2] // TILE):
                row = c * slots + t
                impulse[c, :, t * TILE : (t + 1) * TILE] = imp[row : row + 1, :]
        for r in range(6):
            for h in range(blocks):
                velocity[r, :, h * LANES : (h + 1) * LANES] = fresh[h][r : r + 1, :]
    else:
        fresh_own, out0, out1 = refs
        for h in range(blocks):
            fresh_own[:, h * LANES : (h + 1) * LANES] = fresh[h]
        out0[...] = pick(fresh, export_index[0:8, :])
        out1[...] = pick(fresh, export_index[8:16, :])


def shape(dims, dtype=F32):
    return jax.ShapeDtypeStruct(dims, dtype)


def make(subs, layers):
    matchings = neighbour_matchings(subs, layers)
    shuffles = [relay_shuffle(subs, layers, k) for k in range(WIN)]

    def trade(low, high):
        return [
            lax.ppermute(low if m < 2 else high, AXES, matchings[m]) for m in range(4)
        ]

    def on_device(geometry, dest_slot, pairs, colors, free_vel, inertia, exports):
        count = geometry.shape[2]
        bodies = free_vel.shape[2]
        interface = exports.shape[2]
        tiles = count // TILE
        slots = 16
        assert count % TILE == 0 and tiles < slots and 2 * interface == LANES
        assert bodies % LANES == 0
        blocks = bodies // LANES
        total = blocks + 2
        place = shape((10 * slots, LANES))
        small = shape((16, LANES))
        place0, send0, place2, place3, out0, out1, own, export_index = pl.pallas_call(
            prepare_kernel,
            out_shape=(
                place, shape((10 * slots + 16, LANES)), place, place, small, small,
                shape((16, bodies)),
                shape((16, LANES), jnp.int32),
            ),
            in_specs=[pl.BlockSpec(memory_space=pl.ANY)] * 5,
            out_specs=(VMEM_SPEC,) * 8,
            scratch_shapes=[
                pltpu.VMEM(geometry.shape, F32),
                pltpu.VMEM(dest_slot.shape, jnp.int32),
                pltpu.VMEM(free_vel.shape, F32),
                pltpu.VMEM(inertia.shape, F32),
                pltpu.VMEM(exports.shape, jnp.int32),
                pltpu.VMEM((8, LANES), jnp.int32),
                pltpu.VMEM((16, count), F32),
                pltpu.VMEM((WIN * slots, count), BF16),
                pltpu.VMEM((2, 10 * WIN * slots, count), BF16),
                pltpu.VMEM((LANES, count), BF16),
                pltpu.SemaphoreType.DMA((5,)),
            ],
            compiler_params=PARAMS,
            name="prepare",
        )(geometry, dest_slot, free_vel, inertia, exports)
        came = [lax.ppermute(send0, AXES, matchings[0])]
        came.append(lax.ppermute(out0, AXES, matchings[1]))
        came.append(lax.ppermute(out1, AXES, matchings[2]))
        came.append(lax.ppermute(out1, AXES, matchings[3]))
        placed = [place0]
        placed.append(lax.ppermute(place2, AXES, shuffles[2]))
        placed.append(lax.ppermute(place3, AXES, shuffles[3]))

        def indexing(*refs):
            index_kernel(subs, layers, interface, bodies, *refs)

        index, hot, masks, export_hot, export_masks, mult, order = pl.pallas_call(
            indexing,
            out_shape=(
                shape((48, LANES), jnp.int32),
                shape((LANES, 2 * TILE * (tiles + 1)), BF16),
                shape((tiles + 1, 16 * (blocks + total), LANES), BF16),
                shape((LANES, 2 * LANES), BF16),
                shape((2, 16 * blocks, LANES), BF16),
                shape((8, bodies)),
                shape((32,), jnp.int32),
            ),
            in_specs=[VMEM_SPEC, SMEM_SPEC, VMEM_SPEC],
            out_specs=(VMEM_SPEC,) * 6 + (SMEM_SPEC,),
            compiler_params=PARAMS,
            name="indexing",
        )(pairs, colors, export_index)

        state = impulse = None
        for sweep in range(SWEEPS):
            first, last = sweep == 0, sweep == SWEEPS - 1

            def run(*refs, first=first):
                sweep_kernel(bodies, interface, first, *refs)

            outs = [
                shape((3 * slots, LANES)),
                shape((8, bodies)),
                shape((8, LANES)),
                shape((8, LANES)),
            ]
            operands = [order, index, hot, masks, own, *came]
            if first:
                outs = [shape((STATE * slots, LANES))] + outs
                operands += placed
            else:
                operands += [state, impulse]
            result = pl.pallas_call(
                run,
                out_shape=tuple(outs),
                in_specs=[SMEM_SPEC] + [VMEM_SPEC] * (len(operands) - 1),
                out_specs=(VMEM_SPEC,) * len(outs),
                scratch_shapes=[
                    pltpu.VMEM((8 * slots, LANES), F32),
                    pltpu.VMEM((8 * slots, LANES), F32),
                    pltpu.VMEM((8 * slots, LANES), F32),
                    pltpu.VMEM((8 * slots, LANES), F32),
                    pltpu.VMEM((16 * total, LANES), F32),
                    pltpu.VMEM((8 * total, LANES), F32),
                    pltpu.VMEM((3 * slots, LANES), F32),
                ],
                compiler_params=PARAMS,
                name="sweep",
            )(*operands)
            if first:
                state, result = result[0], result[1:]
            impulse, change, ghost0, ghost1 = result
            sums = trade(ghost0, ghost1)

            def merge(*refs, last=last):
                merge_kernel(interface, last, *refs)

            operands = [own, change, *sums, mult, export_index, export_hot, export_masks]
            if last:
                operands.append(impulse)
                outs = (shape((3, 1, count)), shape((6, 1, bodies)))
            else:
                outs = (shape((8, bodies)), shape((8, LANES)), shape((8, LANES)))
            merged = pl.pallas_call(
                merge,
                out_shape=outs,
                in_specs=[VMEM_SPEC] * len(operands),
                out_specs=(VMEM_SPEC,) * len(outs),
                compiler_params=PARAMS,
                name="merge",
            )(*operands)
            if last:
                return merged
            own = merged[0]
            came = trade(merged[1], merged[2])

    return on_device


def solution(mesh):
    placed = (
        P(None, "layer", "sub"),
        P("layer", "sub"),
        P(None, "layer", "sub"),
        P("layer", "sub"),
        P(None, "layer", "sub"),
        P(None, "layer", "sub"),
        P(None, "layer", "sub"),
    )
    return jax.shard_map(
        make(mesh.shape["sub"], mesh.shape["layer"]),
        mesh=mesh,
        in_specs=placed,
        out_specs=(P(None, "layer", "sub"), P(None, "layer", "sub")),
        check_vma=False,
    )
```

```python
import jax
import jax.numpy as jnp
from jax import lax
from jax.experimental import pallas as pl
from jax.experimental.pallas import tpu as pltpu
from jax.sharding import PartitionSpec as P

WIN = 4
SWEEPS = 3
NCOLOR = 4
TILE = 128
LANES = 128
CHUNK = 4

relaxation = 0.7
friction = 0.6
tangent_floor = 0.1

AXES = ("sub", "layer")
F32 = jnp.float32
BF16 = jnp.bfloat16
VMEM_SPEC = pl.BlockSpec(memory_space=pltpu.VMEM)
SMEM_SPEC = pl.BlockSpec(memory_space=pltpu.SMEM)
PARAMS = pltpu.CompilerParams(vmem_limit_bytes=16 << 20)


def neighbour_matchings(subs, layers):
    assert subs % 2 == 0 and layers % 2 == 0

    def shifted(i):
        return i - 1 if i % 2 == 0 else i + 1

    def partner(match, s, y):
        if match == 0:
            return s ^ 1, y
        if match == 1:
            return (s, y ^ 1) if s in (0, subs - 1) else (shifted(s), y)
        if match == 2:
            return s, y ^ 1
        return (s ^ 1, y) if y in (0, layers - 1) else (s, shifted(y))

    out = []
    for match in range(4):
        pairs = []
        for s in range(subs):
            for y in range(layers):
                ps, py = partner(match, s, y)
                pairs.append((s * layers + y, ps * layers + py))
        out.append(pairs)
    return out


def relay_shuffle(subs, layers, k):
    return [
        (s * layers + y, (s ^ k) * layers + y) for s in range(subs) for y in range(layers)
    ]


def lane_iota():
    return lax.broadcasted_iota(jnp.int32, (8, LANES), 1)


def pick(tables, index):
    low = jnp.bitwise_and(index, LANES - 1)
    high = jnp.right_shift(index, 7)
    out = jnp.take_along_axis(tables[0], low, axis=1)
    for h in range(1, len(tables)):
        out = jnp.where(high == h, jnp.take_along_axis(tables[h], low, axis=1), out)
    return out


def two_parts(value):
    first = value.astype(BF16).astype(F32)
    return jnp.concatenate([first, value - first], axis=0).astype(BF16)


def high_masks(index_row, highs):
    high = jnp.broadcast_to(jnp.right_shift(index_row, 7), (16, LANES))
    return jnp.concatenate(
        [jnp.where(high == h, 1.0, 0.0) for h in range(highs)], axis=0
    ).astype(BF16)


def low_onehot(index_row):
    low = jnp.bitwise_and(index_row, LANES - 1)
    rows = lax.broadcasted_iota(jnp.int32, (LANES, LANES), 0)
    return jnp.where(rows == low, 1.0, 0.0).astype(BF16)


def contract_lanes(lhs, rhs):
    return lax.dot_general(
        lhs, rhs, (((1,), (1,)), ((), ())), preferred_element_type=F32
    )


def sum_parts(block, h):
    return block[16 * h : 16 * h + 8] + block[16 * h + 8 : 16 * h + 16]


def cross(u, v):
    return [
        u[1] * v[2] - u[2] * v[1],
        u[2] * v[0] - u[0] * v[2],
        u[0] * v[1] - u[1] * v[0],
    ]


def dot3(u, v):
    return u[0] * v[0] + u[1] * v[1] + u[2] * v[2]


def halves(low, high, half):
    return jnp.where(lane_iota() < half, low, high)


def parities():
    sub = lax.axis_index("sub")
    layer = lax.axis_index("layer")
    return sub, layer, lax.rem(sub, 2) == 0, lax.rem(layer, 2) == 0


def prepare_kernel(
    geo_hbm, dest_hbm, vel_hbm, inertia_hbm, exports_hbm,
    place0, send0, place2, place3, out0, out1, start_own, export_index,
    geo, dest, vel, inertia, exports, listed, dense, mask, lhs, hot, sems,
):
    copies = [
        pltpu.make_async_copy(src, dst, sems.at[i])
        for i, (src, dst) in enumerate(
            [
                (exports_hbm, exports),
                (vel_hbm, vel),
                (inertia_hbm, inertia),
                (dest_hbm, dest),
                (geo_hbm, geo),
            ]
        )
    ]
    for copy in copies:
        copy.start()
    count = geo.shape[2]
    tiles = count // TILE
    slots = place0.shape[0] // 10
    bodies = vel.shape[2]
    interface = exports.shape[2]
    sub, layer, sub_even, layer_even = parities()
    member = lax.rem(sub, WIN)
    start_own[...] = jnp.zeros_like(start_own)
    dense[...] = jnp.zeros_like(dense)
    for copy in copies[:4]:
        copy.wait()
    for r in range(6):
        start_own[r : r + 1, :] = vel[r]
    for r in range(4):
        start_own[8 + r : 9 + r, :] = inertia[r]
    listed[0:1, 0:interface] = exports[0]
    listed[0:1, interface : 2 * interface] = exports[1]
    listed[1:2, 0:interface] = exports[1]
    listed[1:2, interface : 2 * interface] = exports[0]
    listed[2:3, 0:interface] = exports[2]
    listed[2:3, interface : 2 * interface] = exports[3]
    listed[3:4, 0:interface] = exports[3]
    listed[3:4, interface : 2 * interface] = exports[2]
    row0 = jnp.where(sub_even, listed[1:2, :], listed[0:1, :])
    row1 = jnp.where(layer_even, listed[3:4, :], listed[2:3, :])
    idx0 = jnp.broadcast_to(row0, (8, LANES))
    idx1 = jnp.broadcast_to(row1, (8, LANES))
    export_index[0:8, :] = idx0
    export_index[8:16, :] = idx1
    blocks = bodies // LANES
    for base in (0, 8):
        tables = [
            start_own[base : base + 8, h * LANES : (h + 1) * LANES] for h in range(blocks)
        ]
        picked = pick(tables, idx0)
        out0[base : base + 8, :] = picked
        send0[10 * slots + base : 10 * slots + base + 8, :] = picked
        out1[base : base + 8, :] = pick(tables, idx1)
    slot = dest[...] - (sub - member) * count
    target = jnp.zeros_like(slot)
    for m in range(1, WIN):
        target = target + jnp.where(slot >= m * count, 1, 0)
    within = slot - target * count
    row_id = jnp.bitwise_xor(target, member) * slots + jnp.right_shift(within, 7)
    low = jnp.bitwise_and(within, LANES - 1)
    rows = lax.broadcasted_iota(jnp.int32, (WIN * slots, TILE), 0)
    for t in range(tiles):
        span = slice(t * TILE, (t + 1) * TILE)
        hot[:, span] = low_onehot(low[:, span])
        mask[:, span] = jnp.where(rows == row_id[:, span], 1.0, 0.0).astype(BF16)
    copies[4].wait()
    for r in range(10):
        dense[r : r + 1, :] = geo[r]
    value = dense[...]
    first = value.astype(BF16).astype(F32)
    parts = [first, value - first]
    for p in range(2):
        for r in range(10):
            row = jnp.broadcast_to(parts[p][r : r + 1, :], (slots, count)).astype(BF16)
            for k in range(WIN):
                at = (10 * k + r) * slots
                lhs[p, at : at + slots, :] = mask[k * slots : (k + 1) * slots, :] * row
    outs = (place0, send0, place2, place3)
    for k in range(WIN):
        span = slice(10 * slots * k, 10 * slots * (k + 1))
        total = contract_lanes(lhs[0, span, :], hot[...])
        total = total + contract_lanes(lhs[1, span, :], hot[...])
        outs[k][0 : 10 * slots, :] = total


def index_kernel(
    subs, layers, interface, bodies, pairs, colors, export_index,
    index_out, hot, masks, export_hot, export_masks, mult, order,
):
    count = pairs.shape[2]
    tiles = count // TILE
    blocks = bodies // LANES
    total = blocks + 4 * interface // LANES
    sub, layer, sub_even, layer_even = parities()
    filled = jnp.int32(0)
    for k in range(NCOLOR):
        order[16 + k] = filled
        for t in range(tiles):
            hit = colors[0, t] == k
            place = jnp.where(hit, filled, 31)
            order[place] = t
            filled = filled + jnp.where(hit, 1, 0)
    order[16 + NCOLOR] = filled
    for t in range(tiles, 16):
        order[t] = tiles
    index_out[...] = jnp.zeros_like(index_out)
    flip_sub = jnp.where(sub_even, interface, 0)
    flip_layer = jnp.where(layer_even, interface, 0)
    for t in range(tiles):
        span = slice(t * TILE, (t + 1) * TILE)
        first = pairs[0, :, span]
        other = pairs[1, :, span]
        ghost = other - bodies
        turned = jnp.where(
            ghost < 2 * interface,
            jnp.bitwise_xor(ghost, flip_sub),
            jnp.bitwise_xor(ghost, flip_layer),
        )
        second = jnp.where(ghost < 0, other, bodies + turned)
        index_out[t : t + 1, :] = first
        index_out[16 + t : 17 + t, :] = second
        index_out[32 + t : 33 + t, :] = jnp.full((1, TILE), colors[0, t], jnp.int32)
        hot[:, 2 * t * TILE : (2 * t + 1) * TILE] = low_onehot(first)
        hot[:, (2 * t + 1) * TILE : (2 * t + 2) * TILE] = low_onehot(second)
        masks[t, : 16 * blocks, :] = high_masks(first, blocks)
        masks[t, 16 * blocks :, :] = high_masks(second, total)
    for t in range(tiles, 16):
        index_out[32 + t : 33 + t, :] = jnp.full((1, TILE), -1, jnp.int32)
    hot[:, 2 * tiles * TILE :] = jnp.zeros((LANES, 2 * TILE), BF16)
    masks[tiles] = jnp.zeros_like(masks[tiles])
    inner_sub = jnp.where(jnp.logical_and(sub > 0, sub < subs - 1), 1.0, 0.0)
    inner_layer = jnp.where(jnp.logical_and(layer > 0, layer < layers - 1), 1.0, 0.0)
    lane = lane_iota()
    weights = [
        jnp.where(lane < interface, 1.0, inner_sub),
        jnp.where(lane < interface, 1.0, inner_layer),
    ]
    left = []
    for i in range(2):
        row = export_index[8 * i : 8 * i + 1, :]
        export_hot[:, i * LANES : (i + 1) * LANES] = low_onehot(row)
        chosen = high_masks(row, blocks)
        export_masks[i] = chosen
        weight = jnp.concatenate([weights[i], jnp.zeros_like(weights[i])], axis=0).astype(BF16)
        left.append(jnp.concatenate([weight] * blocks, axis=0) * chosen)
    listed = contract_lanes(jnp.concatenate(left, axis=1), export_hot[...])
    for h in range(blocks):
        mult[:, h * LANES : (h + 1) * LANES] = 1.0 + listed[16 * h : 16 * h + 8]


STATE = 34


def contact_state(geo, first, second):
    raw = geo[0:3]
    length = jnp.sqrt(dot3(raw, raw))
    normal = [x / length for x in raw]
    side = jnp.sqrt(normal[1] * normal[1] + normal[2] * normal[2])
    tan_y = normal[2] / side
    tan_z = -normal[1] / side
    two = [
        normal[1] * tan_z - normal[2] * tan_y,
        -normal[0] * tan_z,
        normal[0] * tan_y,
    ]

    def arm(p, spin):
        return [
            spin[1] * p[2] * p[2] + spin[2] * p[1] * p[1],
            spin[0] * p[2] * p[2] + spin[2] * p[0] * p[0],
            spin[0] * p[1] * p[1] + spin[1] * p[0] * p[0],
            -spin[2] * p[0] * p[1],
            -spin[1] * p[0] * p[2],
            -spin[0] * p[1] * p[2],
        ]

    arm_a, arm_b = geo[3:6], geo[6:9]
    e = [x + y for x, y in zip(arm(arm_a, first[1:4]), arm(arm_b, second[1:4]))]
    mass = first[0] + second[0]
    xx, yy, zz = mass + e[0], mass + e[1], mass + e[2]
    xy, xz, yz = e[3], e[4], e[5]
    c_xx = yy * zz - yz * yz
    c_xy = xz * yz - xy * zz
    c_xz = xy * yz - xz * yy
    c_yy = xx * zz - xz * xz
    c_yz = xy * xz - xx * yz
    c_zz = xx * yy - xy * xy
    det = xx * c_xx + xy * c_xy + xz * c_xz
    inv = [
        [c_xx / det, c_xy / det, c_xz / det],
        [c_xy / det, c_yy / det, c_yz / det],
        [c_xz / det, c_yz / det, c_zz / det],
    ]
    solve = []
    for row in (normal, None, two):
        for j in range(3):
            if row is None:
                value = tan_y * inv[1][j] + tan_z * inv[2][j]
            else:
                value = row[0] * inv[0][j] + row[1] * inv[1][j] + row[2] * inv[2][j]
            solve.append(relaxation * value)
    bias = [geo[9] * dot3(solve[3 * i : 3 * i + 3], normal) for i in range(3)]
    return (
        solve + bias + normal + [tan_y, tan_z] + two + arm_a + arm_b + list(first) + list(second)
    )


def sweep_kernel(bodies, interface, first_sweep, *refs):
    refs = list(refs)
    order, index, hot, masks = refs[:4]
    refs = refs[4:]
    if first_sweep:
        own, g1, r1, r2, r3, g0, g2, g3 = refs[:8]
        refs = refs[8:]
        r0 = g1.at[pl.ds(g0.shape[0], 16), :]
    else:
        own, r0, r1, r2, r3, state, impulse_in = refs[:7]
        refs = refs[7:]
    if first_sweep:
        state = refs.pop(0)
    impulse, own_change, ghost0, ghost1 = refs[:4]
    refs = refs[4:]
    got_a, got_b, push_a, push_b, acc, table, imp = refs
    slots = 16
    tiles = masks.shape[0] - 1
    blocks = bodies // LANES
    ghosts = (4 * interface) // LANES
    total = blocks + ghosts
    tile_rows = [pl.ds(c, slots, stride=8) for c in range(8)]

    def ghost_blocks(base):
        return [
            halves(r0[base : base + 8, :], r1[base : base + 8, :], interface),
            halves(r2[base : base + 8, :], r3[base : base + 8, :], interface),
        ]

    start = [own[0:8, h * LANES : (h + 1) * LANES] for h in range(blocks)] + ghost_blocks(0)
    for h in range(total):
        table[8 * h : 8 * h + 8, :] = start[h]

    push_a[...] = jnp.zeros_like(push_a)
    push_b[...] = jnp.zeros_like(push_b)

    if first_sweep:
        props = [own[8:16, h * LANES : (h + 1) * LANES] for h in range(blocks)] + ghost_blocks(8)
        got_a[...] = jnp.ones_like(got_a)
        got_b[...] = jnp.ones_like(got_b)
        for t in range(tiles):
            ia = jnp.broadcast_to(index[t : t + 1, :], (8, LANES))
            ib = jnp.broadcast_to(index[16 + t : 17 + t, :], (8, LANES))
            got_a[8 * t : 8 * t + 8, :] = pick(props[:blocks], ia)
            got_b[8 * t : 8 * t + 8, :] = pick(props, ib)
        first = [got_a[tile_rows[c], :] for c in range(4)]
        second = [got_b[tile_rows[c], :] for c in range(4)]
        real = lax.broadcasted_iota(jnp.int32, (slots, LANES), 0) < tiles
        geo = []
        for c in range(10):
            span = slice(c * slots, (c + 1) * slots)
            value = (g0[span, :] + g1[span, :]) + (g2[span, :] + g3[span, :])
            geo.append(jnp.where(real, value, 1.0))
        for c, value in enumerate(contact_state(geo, first, second)):
            state[c * slots : (c + 1) * slots, :] = value
        imp[...] = jnp.zeros_like(imp)
    else:
        imp[...] = impulse_in[...]

    def held(c):
        return state[c * slots : (c + 1) * slots, :]

    def color_pass(k, carry):
        begin = order[16 + k]
        chunks = lax.div(order[17 + k] - begin + (CHUNK - 1), CHUNK)
        now = [table[8 * h : 8 * h + 8, :] for h in range(total)]

        def gather(i, c):
            for j in range(CHUNK):
                t = order[jnp.minimum(begin + i * CHUNK + j, 15)]
                ia = jnp.broadcast_to(index[pl.ds(t, 1), :], (8, LANES))
                ib = jnp.broadcast_to(index[pl.ds(16 + t, 1), :], (8, LANES))
                at = pl.ds(pl.multiple_of(8 * t, 8), 8)
                got_a[at, :] = pick(now[:blocks], ia)
                got_b[at, :] = pick(now, ib)
            return c

        lax.fori_loop(0, chunks, gather, 0)
        va = [got_a[tile_rows[c], :] for c in range(6)]
        vb = [got_b[tile_rows[c], :] for c in range(6)]
        arm_a = [held(20 + c) for c in range(3)]
        arm_b = [held(23 + c) for c in range(3)]
        turn_a = cross(va[3:6], arm_a)
        turn_b = cross(vb[3:6], arm_b)
        rel = [((va[c] + turn_a[c]) - vb[c]) - turn_b[c] for c in range(3)]
        old = [imp[c * slots : (c + 1) * slots, :] for c in range(3)]
        trial = [
            old[c] - (dot3([held(3 * c + j) for j in range(3)], rel) + held(9 + c))
            for c in range(3)
        ]
        normal_part = jnp.maximum(trial[0], 0.0)
        slide = jnp.sqrt(trial[1] * trial[1] + trial[2] * trial[2])
        factor = jnp.minimum(1.0, friction * normal_part / jnp.maximum(slide, tangent_floor))
        active = index[32:48, :] == k
        new = [
            jnp.where(active, normal_part, old[0]),
            jnp.where(active, trial[1] * factor, old[1]),
            jnp.where(active, trial[2] * factor, old[2]),
        ]
        change = [new[c] - old[c] for c in range(3)]
        for c in range(3):
            imp[c * slots : (c + 1) * slots, :] = new[c]
        force = [
            held(12) * change[0] + held(17) * change[2],
            held(13) * change[0] + held(15) * change[1] + held(18) * change[2],
            held(14) * change[0] + held(16) * change[1] + held(19) * change[2],
        ]
        spin_a = cross(arm_a, force)
        spin_b = cross(arm_b, force)
        for c in range(3):
            push_a[tile_rows[c], :] = held(26) * force[c]
            push_a[tile_rows[3 + c], :] = held(27 + c) * spin_a[c]
            push_b[tile_rows[c], :] = -(held(30) * force[c])
            push_b[tile_rows[3 + c], :] = -(held(31 + c) * spin_b[c])
        acc[...] = jnp.zeros_like(acc)

        def scatter(i, c):
            own_left, own_right, ghost_left, ghost_right = [], [], [], []
            for j in range(CHUNK):
                t = order[jnp.minimum(begin + i * CHUNK + j, 15)]
                at = pl.ds(pl.multiple_of(8 * t, 8), 8)
                first = two_parts(push_a[at, :])
                second = two_parts(push_b[at, :])
                rows = [masks[t, 16 * m : 16 * m + 16, :] for m in range(blocks + total)]
                own_left.append(jnp.concatenate([first * m for m in rows[:blocks]], axis=0))
                own_left.append(
                    jnp.concatenate([second * m for m in rows[blocks : 2 * blocks]], axis=0)
                )
                ghost_left.append(
                    jnp.concatenate([second * m for m in rows[2 * blocks :]], axis=0)
                )
                at_hot = pl.multiple_of(2 * TILE * t, 2 * TILE)
                own_right.append(hot[:, pl.ds(at_hot, 2 * TILE)])
                ghost_right.append(
                    hot[:, pl.ds(pl.multiple_of(at_hot + TILE, TILE), TILE)]
                )
            acc[: 16 * blocks, :] += contract_lanes(
                jnp.concatenate(own_left, axis=1), jnp.concatenate(own_right, axis=1)
            )
            acc[16 * blocks :, :] += contract_lanes(
                jnp.concatenate(ghost_left, axis=1), jnp.concatenate(ghost_right, axis=1)
            )
            return c

        lax.fori_loop(0, chunks, scatter, 0)
        for h in range(total):
            table[8 * h : 8 * h + 8, :] = now[h] + sum_parts(acc, h)
        return carry

    lax.fori_loop(0, NCOLOR, color_pass, 0)
    for h in range(blocks):
        own_change[:, h * LANES : (h + 1) * LANES] = table[8 * h : 8 * h + 8, :] - start[h]
    ghost0[...] = table[8 * blocks : 8 * blocks + 8, :] - start[blocks]
    ghost1[...] = table[8 * blocks + 8 : 8 * blocks + 16, :] - start[blocks + 1]
    impulse[...] = imp[...]


def merge_kernel(
    interface, last_sweep, own, change, c0, c1, c2, c3, mult, export_index, export_hot,
    export_masks, *refs,
):
    blocks = own.shape[1] // LANES
    came = [halves(c0[...], c1[...], interface), halves(c2[...], c3[...], interface)]
    left = jnp.concatenate(
        [
            jnp.concatenate([two_parts(came[i])] * blocks, axis=0) * export_masks[i]
            for i in range(2)
        ],
        axis=1,
    )
    incoming = contract_lanes(left, export_hot[...])
    fresh = []
    for h in range(blocks):
        span = slice(h * LANES, (h + 1) * LANES)
        fresh.append(
            own[0:8, span] + (change[:, span] + sum_parts(incoming, h)) / mult[:, span]
        )
    if last_sweep:
        imp, impulse, velocity = refs
        slots = imp.shape[0] // 3
        for c in range(3):
            for t in range(impulse.shape[2] // TILE):
                row = c * slots + t
                impulse[c, :, t * TILE : (t + 1) * TILE] = imp[row : row + 1, :]
        for r in range(6):
            for h in range(blocks):
                velocity[r, :, h * LANES : (h + 1) * LANES] = fresh[h][r : r + 1, :]
    else:
        fresh_own, out0, out1 = refs
        for h in range(blocks):
            fresh_own[:, h * LANES : (h + 1) * LANES] = fresh[h]
        out0[...] = pick(fresh, export_index[0:8, :])
        out1[...] = pick(fresh, export_index[8:16, :])


def in_hbm(array):
    return pltpu.with_memory_space_constraint(array, pltpu.HBM)


def shape(dims, dtype=F32):
    return jax.ShapeDtypeStruct(dims, dtype)


def make(subs, layers):
    matchings = neighbour_matchings(subs, layers)
    shuffles = [relay_shuffle(subs, layers, k) for k in range(WIN)]

    def trade(low, high):
        return [
            lax.ppermute(low if m < 2 else high, AXES, matchings[m]) for m in range(4)
        ]

    def on_device(geometry, dest_slot, pairs, colors, free_vel, inertia, exports):
        count = geometry.shape[2]
        bodies = free_vel.shape[2]
        interface = exports.shape[2]
        tiles = count // TILE
        slots = 16
        assert count % TILE == 0 and tiles < slots and 2 * interface == LANES
        assert bodies % LANES == 0
        blocks = bodies // LANES
        total = blocks + 2
        place = shape((10 * slots, LANES))
        small = shape((16, LANES))
        place0, send0, place2, place3, out0, out1, own, export_index = pl.pallas_call(
            prepare_kernel,
            out_shape=(
                place, shape((10 * slots + 16, LANES)), place, place, small, small,
                shape((16, bodies)),
                shape((16, LANES), jnp.int32),
            ),
            in_specs=[pl.BlockSpec(memory_space=pltpu.HBM)] * 5,
            out_specs=(VMEM_SPEC,) * 8,
            scratch_shapes=[
                pltpu.VMEM(geometry.shape, F32),
                pltpu.VMEM(dest_slot.shape, jnp.int32),
                pltpu.VMEM(free_vel.shape, F32),
                pltpu.VMEM(inertia.shape, F32),
                pltpu.VMEM(exports.shape, jnp.int32),
                pltpu.VMEM((8, LANES), jnp.int32),
                pltpu.VMEM((16, count), F32),
                pltpu.VMEM((WIN * slots, count), BF16),
                pltpu.VMEM((2, 10 * WIN * slots, count), BF16),
                pltpu.VMEM((LANES, count), BF16),
                pltpu.SemaphoreType.DMA((5,)),
            ],
            compiler_params=PARAMS,
            name="prepare",
        )(*[in_hbm(x) for x in (geometry, dest_slot, free_vel, inertia, exports)])
        came = [lax.ppermute(send0, AXES, matchings[0])]
        came.append(lax.ppermute(out0, AXES, matchings[1]))
        came.append(lax.ppermute(out1, AXES, matchings[2]))
        came.append(lax.ppermute(out1, AXES, matchings[3]))
        placed = [place0]
        placed.append(lax.ppermute(place2, AXES, shuffles[2]))
        placed.append(lax.ppermute(place3, AXES, shuffles[3]))

        def indexing(*refs):
            index_kernel(subs, layers, interface, bodies, *refs)

        index, hot, masks, export_hot, export_masks, mult, order = pl.pallas_call(
            indexing,
            out_shape=(
                shape((48, LANES), jnp.int32),
                shape((LANES, 2 * TILE * (tiles + 1)), BF16),
                shape((tiles + 1, 16 * (blocks + total), LANES), BF16),
                shape((LANES, 2 * LANES), BF16),
                shape((2, 16 * blocks, LANES), BF16),
                shape((8, bodies)),
                shape((32,), jnp.int32),
            ),
            in_specs=[VMEM_SPEC, SMEM_SPEC, VMEM_SPEC],
            out_specs=(VMEM_SPEC,) * 6 + (SMEM_SPEC,),
            compiler_params=PARAMS,
            name="indexing",
        )(pairs, colors, export_index)

        state = impulse = None
        for sweep in range(SWEEPS):
            first, last = sweep == 0, sweep == SWEEPS - 1

            def run(*refs, first=first):
                sweep_kernel(bodies, interface, first, *refs)

            outs = [
                shape((3 * slots, LANES)),
                shape((8, bodies)),
                shape((8, LANES)),
                shape((8, LANES)),
            ]
            operands = [order, index, hot, masks, own, *came]
            if first:
                outs = [shape((STATE * slots, LANES))] + outs
                operands += placed
            else:
                operands += [state, impulse]
            result = pl.pallas_call(
                run,
                out_shape=tuple(outs),
                in_specs=[SMEM_SPEC] + [VMEM_SPEC] * (len(operands) - 1),
                out_specs=(VMEM_SPEC,) * len(outs),
                scratch_shapes=[
                    pltpu.VMEM((8 * slots, LANES), F32),
                    pltpu.VMEM((8 * slots, LANES), F32),
                    pltpu.VMEM((8 * slots, LANES), F32),
                    pltpu.VMEM((8 * slots, LANES), F32),
                    pltpu.VMEM((16 * total, LANES), F32),
                    pltpu.VMEM((8 * total, LANES), F32),
                    pltpu.VMEM((3 * slots, LANES), F32),
                ],
                compiler_params=PARAMS,
                name="sweep",
            )(*operands)
            if first:
                state, result = result[0], result[1:]
            impulse, change, ghost0, ghost1 = result
            sums = trade(ghost0, ghost1)

            def merge(*refs, last=last):
                merge_kernel(interface, last, *refs)

            operands = [own, change, *sums, mult, export_index, export_hot, export_masks]
            if last:
                operands.append(impulse)
                outs = (shape((3, 1, count)), shape((6, 1, bodies)))
            else:
                outs = (shape((8, bodies)), shape((8, LANES)), shape((8, LANES)))
            merged = pl.pallas_call(
                merge,
                out_shape=outs,
                in_specs=[VMEM_SPEC] * len(operands),
                out_specs=(VMEM_SPEC,) * len(outs),
                compiler_params=PARAMS,
                name="merge",
            )(*operands)
            if last:
                return merged
            own = merged[0]
            came = trade(merged[1], merged[2])

    return on_device


def solution(mesh):
    placed = (
        P(None, "layer", "sub"),
        P("layer", "sub"),
        P(None, "layer", "sub"),
        P("layer", "sub"),
        P(None, "layer", "sub"),
        P(None, "layer", "sub"),
        P(None, "layer", "sub"),
    )
    return jax.shard_map(
        make(mesh.shape["sub"], mesh.shape["layer"]),
        mesh=mesh,
        in_specs=placed,
        out_specs=(P(None, "layer", "sub"), P(None, "layer", "sub")),
        check_vma=False,
    )
```

```python
import jax
import jax.numpy as jnp
from jax import lax
from jax.experimental import pallas as pl
from jax.experimental.pallas import tpu as pltpu
from jax.sharding import PartitionSpec as P

WIN = 4
SWEEPS = 3
NCOLOR = 4
TILE = 128
LANES = 128
CHUNK = 4

relaxation = 0.7
friction = 0.6
tangent_floor = 0.1

AXES = ("sub", "layer")
F32 = jnp.float32
BF16 = jnp.bfloat16
VMEM_SPEC = pl.BlockSpec(memory_space=pltpu.VMEM)
SMEM_SPEC = pl.BlockSpec(memory_space=pltpu.SMEM)
PARAMS = pltpu.CompilerParams(vmem_limit_bytes=16 << 20)


def neighbour_matchings(subs, layers):
    assert subs % 2 == 0 and layers % 2 == 0

    def shifted(i):
        return i - 1 if i % 2 == 0 else i + 1

    def partner(match, s, y):
        if match == 0:
            return s ^ 1, y
        if match == 1:
            return (s, y ^ 1) if s in (0, subs - 1) else (shifted(s), y)
        if match == 2:
            return s, y ^ 1
        return (s ^ 1, y) if y in (0, layers - 1) else (s, shifted(y))

    out = []
    for match in range(4):
        pairs = []
        for s in range(subs):
            for y in range(layers):
                ps, py = partner(match, s, y)
                pairs.append((s * layers + y, ps * layers + py))
        out.append(pairs)
    return out


def relay_shuffle(subs, layers, k):
    return [
        (s * layers + y, (s ^ k) * layers + y) for s in range(subs) for y in range(layers)
    ]


def lane_iota():
    return lax.broadcasted_iota(jnp.int32, (8, LANES), 1)


def pick(tables, index):
    low = jnp.bitwise_and(index, LANES - 1)
    high = jnp.right_shift(index, 7)
    out = jnp.take_along_axis(tables[0], low, axis=1)
    for h in range(1, len(tables)):
        out = jnp.where(high == h, jnp.take_along_axis(tables[h], low, axis=1), out)
    return out


def two_parts(value):
    first = value.astype(BF16).astype(F32)
    return jnp.concatenate([first, value - first], axis=0).astype(BF16)


def high_masks(index_row, highs):
    high = jnp.broadcast_to(jnp.right_shift(index_row, 7), (16, LANES))
    return jnp.concatenate(
        [jnp.where(high == h, 1.0, 0.0) for h in range(highs)], axis=0
    ).astype(BF16)


def low_onehot(index_row):
    low = jnp.bitwise_and(index_row, LANES - 1)
    rows = lax.broadcasted_iota(jnp.int32, (LANES, LANES), 0)
    return jnp.where(rows == low, 1.0, 0.0).astype(BF16)


def contract_lanes(lhs, rhs):
    return lax.dot_general(
        lhs, rhs, (((1,), (1,)), ((), ())), preferred_element_type=F32
    )


def sum_parts(block, h):
    return block[16 * h : 16 * h + 8] + block[16 * h + 8 : 16 * h + 16]


def cross(u, v):
    return [
        u[1] * v[2] - u[2] * v[1],
        u[2] * v[0] - u[0] * v[2],
        u[0] * v[1] - u[1] * v[0],
    ]


def dot3(u, v):
    return u[0] * v[0] + u[1] * v[1] + u[2] * v[2]


def halves(low, high, half):
    return jnp.where(lane_iota() < half, low, high)


def parities():
    sub = lax.axis_index("sub")
    layer = lax.axis_index("layer")
    return sub, layer, lax.rem(sub, 2) == 0, lax.rem(layer, 2) == 0


def prepare_kernel(
    geo_hbm, dest_hbm, vel_hbm, inertia_hbm, exports_hbm,
    place0, send0, place2, place3, out0, out1, start_own, export_index,
    geo, dest, vel, inertia, exports, listed, dense, mask, lhs, hot, sems,
):
    copies = [
        pltpu.make_async_copy(src, dst, sems.at[i])
        for i, (src, dst) in enumerate(
            [
                (exports_hbm, exports),
                (vel_hbm, vel),
                (inertia_hbm, inertia),
                (dest_hbm, dest),
                (geo_hbm, geo),
            ]
        )
    ]
    for copy in copies:
        copy.start()
    count = geo.shape[2]
    tiles = count // TILE
    slots = place0.shape[0] // 10
    bodies = vel.shape[2]
    interface = exports.shape[2]
    sub, layer, sub_even, layer_even = parities()
    member = lax.rem(sub, WIN)
    start_own[...] = jnp.zeros_like(start_own)
    dense[...] = jnp.zeros_like(dense)
    for copy in copies[:4]:
        copy.wait()
    for r in range(6):
        start_own[r : r + 1, :] = vel[r]
    for r in range(4):
        start_own[8 + r : 9 + r, :] = inertia[r]
    listed[0:1, 0:interface] = exports[0]
    listed[0:1, interface : 2 * interface] = exports[1]
    listed[1:2, 0:interface] = exports[1]
    listed[1:2, interface : 2 * interface] = exports[0]
    listed[2:3, 0:interface] = exports[2]
    listed[2:3, interface : 2 * interface] = exports[3]
    listed[3:4, 0:interface] = exports[3]
    listed[3:4, interface : 2 * interface] = exports[2]
    row0 = jnp.where(sub_even, listed[1:2, :], listed[0:1, :])
    row1 = jnp.where(layer_even, listed[3:4, :], listed[2:3, :])
    idx0 = jnp.broadcast_to(row0, (8, LANES))
    idx1 = jnp.broadcast_to(row1, (8, LANES))
    export_index[0:8, :] = idx0
    export_index[8:16, :] = idx1
    blocks = bodies // LANES
    for base in (0, 8):
        tables = [
            start_own[base : base + 8, h * LANES : (h + 1) * LANES] for h in range(blocks)
        ]
        picked = pick(tables, idx0)
        out0[base : base + 8, :] = picked
        send0[10 * slots + base : 10 * slots + base + 8, :] = picked
        out1[base : base + 8, :] = pick(tables, idx1)
    slot = dest[...] - (sub - member) * count
    target = jnp.zeros_like(slot)
    for m in range(1, WIN):
        target = target + jnp.where(slot >= m * count, 1, 0)
    within = slot - target * count
    row_id = jnp.bitwise_xor(target, member) * slots + jnp.right_shift(within, 7)
    low = jnp.bitwise_and(within, LANES - 1)
    rows = lax.broadcasted_iota(jnp.int32, (WIN * slots, TILE), 0)
    for t in range(tiles):
        span = slice(t * TILE, (t + 1) * TILE)
        hot[:, span] = low_onehot(low[:, span])
        mask[:, span] = jnp.where(rows == row_id[:, span], 1.0, 0.0).astype(BF16)
    copies[4].wait()
    for r in range(10):
        dense[r : r + 1, :] = geo[r]
    value = dense[...]
    first = value.astype(BF16).astype(F32)
    parts = [first, value - first]
    for p in range(2):
        for r in range(10):
            row = jnp.broadcast_to(parts[p][r : r + 1, :], (slots, count)).astype(BF16)
            for k in range(WIN):
                at = (10 * k + r) * slots
                lhs[p, at : at + slots, :] = mask[k * slots : (k + 1) * slots, :] * row
    outs = (place0, send0, place2, place3)
    for k in range(WIN):
        span = slice(10 * slots * k, 10 * slots * (k + 1))
        total = contract_lanes(lhs[0, span, :], hot[...])
        total = total + contract_lanes(lhs[1, span, :], hot[...])
        outs[k][0 : 10 * slots, :] = total


def index_kernel(
    subs, layers, interface, bodies, pairs, colors, export_index,
    index_out, hot, masks, export_hot, export_masks, mult, order,
):
    count = pairs.shape[2]
    tiles = count // TILE
    blocks = bodies // LANES
    total = blocks + 4 * interface // LANES
    sub, layer, sub_even, layer_even = parities()
    filled = jnp.int32(0)
    for k in range(NCOLOR):
        order[16 + k] = filled
        for t in range(tiles):
            hit = colors[0, t] == k
            place = jnp.where(hit, filled, 31)
            order[place] = t
            filled = filled + jnp.where(hit, 1, 0)
    order[16 + NCOLOR] = filled
    for t in range(tiles, 16):
        order[t] = tiles
    index_out[...] = jnp.zeros_like(index_out)
    flip_sub = jnp.where(sub_even, interface, 0)
    flip_layer = jnp.where(layer_even, interface, 0)
    for t in range(tiles):
        span = slice(t * TILE, (t + 1) * TILE)
        first = pairs[0, :, span]
        other = pairs[1, :, span]
        ghost = other - bodies
        turned = jnp.where(
            ghost < 2 * interface,
            jnp.bitwise_xor(ghost, flip_sub),
            jnp.bitwise_xor(ghost, flip_layer),
        )
        second = jnp.where(ghost < 0, other, bodies + turned)
        index_out[t : t + 1, :] = first
        index_out[16 + t : 17 + t, :] = second
        index_out[32 + t : 33 + t, :] = jnp.full((1, TILE), colors[0, t], jnp.int32)
        hot[:, 2 * t * TILE : (2 * t + 1) * TILE] = low_onehot(first)
        hot[:, (2 * t + 1) * TILE : (2 * t + 2) * TILE] = low_onehot(second)
        masks[t, : 16 * blocks, :] = high_masks(first, blocks)
        masks[t, 16 * blocks :, :] = high_masks(second, total)
    for t in range(tiles, 16):
        index_out[32 + t : 33 + t, :] = jnp.full((1, TILE), -1, jnp.int32)
    hot[:, 2 * tiles * TILE :] = jnp.zeros((LANES, 2 * TILE), BF16)
    masks[tiles] = jnp.zeros_like(masks[tiles])
    inner_sub = jnp.where(jnp.logical_and(sub > 0, sub < subs - 1), 1.0, 0.0)
    inner_layer = jnp.where(jnp.logical_and(layer > 0, layer < layers - 1), 1.0, 0.0)
    lane = lane_iota()
    weights = [
        jnp.where(lane < interface, 1.0, inner_sub),
        jnp.where(lane < interface, 1.0, inner_layer),
    ]
    left = []
    for i in range(2):
        row = export_index[8 * i : 8 * i + 1, :]
        export_hot[:, i * LANES : (i + 1) * LANES] = low_onehot(row)
        chosen = high_masks(row, blocks)
        export_masks[i] = chosen
        weight = jnp.concatenate([weights[i], jnp.zeros_like(weights[i])], axis=0).astype(BF16)
        left.append(jnp.concatenate([weight] * blocks, axis=0) * chosen)
    listed = contract_lanes(jnp.concatenate(left, axis=1), export_hot[...])
    for h in range(blocks):
        mult[:, h * LANES : (h + 1) * LANES] = 1.0 + listed[16 * h : 16 * h + 8]


STATE = 34


def contact_state(geo, first, second):
    raw = geo[0:3]
    length = jnp.sqrt(dot3(raw, raw))
    normal = [x / length for x in raw]
    side = jnp.sqrt(normal[1] * normal[1] + normal[2] * normal[2])
    tan_y = normal[2] / side
    tan_z = -normal[1] / side
    two = [
        normal[1] * tan_z - normal[2] * tan_y,
        -normal[0] * tan_z,
        normal[0] * tan_y,
    ]

    def arm(p, spin):
        return [
            spin[1] * p[2] * p[2] + spin[2] * p[1] * p[1],
            spin[0] * p[2] * p[2] + spin[2] * p[0] * p[0],
            spin[0] * p[1] * p[1] + spin[1] * p[0] * p[0],
            -spin[2] * p[0] * p[1],
            -spin[1] * p[0] * p[2],
            -spin[0] * p[1] * p[2],
        ]

    arm_a, arm_b = geo[3:6], geo[6:9]
    e = [x + y for x, y in zip(arm(arm_a, first[1:4]), arm(arm_b, second[1:4]))]
    mass = first[0] + second[0]
    xx, yy, zz = mass + e[0], mass + e[1], mass + e[2]
    xy, xz, yz = e[3], e[4], e[5]
    c_xx = yy * zz - yz * yz
    c_xy = xz * yz - xy * zz
    c_xz = xy * yz - xz * yy
    c_yy = xx * zz - xz * xz
    c_yz = xy * xz - xx * yz
    c_zz = xx * yy - xy * xy
    det = xx * c_xx + xy * c_xy + xz * c_xz
    inv = [
        [c_xx / det, c_xy / det, c_xz / det],
        [c_xy / det, c_yy / det, c_yz / det],
        [c_xz / det, c_yz / det, c_zz / det],
    ]
    solve = []
    for row in (normal, None, two):
        for j in range(3):
            if row is None:
                value = tan_y * inv[1][j] + tan_z * inv[2][j]
            else:
                value = row[0] * inv[0][j] + row[1] * inv[1][j] + row[2] * inv[2][j]
            solve.append(relaxation * value)
    bias = [geo[9] * dot3(solve[3 * i : 3 * i + 3], normal) for i in range(3)]
    return (
        solve + bias + normal + [tan_y, tan_z] + two + arm_a + arm_b + list(first) + list(second)
    )


def sweep_kernel(bodies, interface, first_sweep, *refs):
    refs = list(refs)
    order, index, hot, masks = refs[:4]
    refs = refs[4:]
    if first_sweep:
        own, g1, r1, r2, r3, g0, g2, g3 = refs[:8]
        refs = refs[8:]
        r0 = g1.at[pl.ds(g0.shape[0], 16), :]
    else:
        own, r0, r1, r2, r3, state, impulse_in = refs[:7]
        refs = refs[7:]
    if first_sweep:
        state = refs.pop(0)
    impulse, own_change, ghost0, ghost1 = refs[:4]
    refs = refs[4:]
    got_a, got_b, push_a, push_b, acc, table, imp = refs
    slots = 16
    tiles = masks.shape[0] - 1
    blocks = bodies // LANES
    ghosts = (4 * interface) // LANES
    total = blocks + ghosts
    tile_rows = [pl.ds(c, slots, stride=8) for c in range(8)]

    def ghost_blocks(base):
        return [
            halves(r0[base : base + 8, :], r1[base : base + 8, :], interface),
            halves(r2[base : base + 8, :], r3[base : base + 8, :], interface),
        ]

    start = [own[0:8, h * LANES : (h + 1) * LANES] for h in range(blocks)] + ghost_blocks(0)
    for h in range(total):
        table[8 * h : 8 * h + 8, :] = start[h]

    push_a[...] = jnp.zeros_like(push_a)
    push_b[...] = jnp.zeros_like(push_b)

    if first_sweep:
        props = [own[8:16, h * LANES : (h + 1) * LANES] for h in range(blocks)] + ghost_blocks(8)
        got_a[...] = jnp.ones_like(got_a)
        got_b[...] = jnp.ones_like(got_b)
        for t in range(tiles):
            ia = jnp.broadcast_to(index[t : t + 1, :], (8, LANES))
            ib = jnp.broadcast_to(index[16 + t : 17 + t, :], (8, LANES))
            got_a[8 * t : 8 * t + 8, :] = pick(props[:blocks], ia)
            got_b[8 * t : 8 * t + 8, :] = pick(props, ib)
        first = [got_a[tile_rows[c], :] for c in range(4)]
        second = [got_b[tile_rows[c], :] for c in range(4)]
        real = lax.broadcasted_iota(jnp.int32, (slots, LANES), 0) < tiles
        geo = []
        for c in range(10):
            span = slice(c * slots, (c + 1) * slots)
            value = (g0[span, :] + g1[span, :]) + (g2[span, :] + g3[span, :])
            geo.append(jnp.where(real, value, 1.0))
        for c, value in enumerate(contact_state(geo, first, second)):
            state[c * slots : (c + 1) * slots, :] = value
        imp[...] = jnp.zeros_like(imp)
    else:
        imp[...] = impulse_in[...]

    def held(c):
        return state[c * slots : (c + 1) * slots, :]

    def color_pass(k, carry):
        begin = order[16 + k]
        chunks = lax.div(order[17 + k] - begin + (CHUNK - 1), CHUNK)
        now = [table[8 * h : 8 * h + 8, :] for h in range(total)]

        def gather(i, c):
            for j in range(CHUNK):
                t = order[begin + i * CHUNK + j]
                ia = jnp.broadcast_to(index[pl.ds(t, 1), :], (8, LANES))
                ib = jnp.broadcast_to(index[pl.ds(16 + t, 1), :], (8, LANES))
                at = pl.ds(pl.multiple_of(8 * t, 8), 8)
                got_a[at, :] = pick(now[:blocks], ia)
                got_b[at, :] = pick(now, ib)
            return c

        lax.fori_loop(1, chunks, gather, 0)
        gather(0, 0)
        va = [got_a[tile_rows[c], :] for c in range(6)]
        vb = [got_b[tile_rows[c], :] for c in range(6)]
        arm_a = [held(20 + c) for c in range(3)]
        arm_b = [held(23 + c) for c in range(3)]
        turn_a = cross(va[3:6], arm_a)
        turn_b = cross(vb[3:6], arm_b)
        rel = [((va[c] + turn_a[c]) - vb[c]) - turn_b[c] for c in range(3)]
        old = [imp[c * slots : (c + 1) * slots, :] for c in range(3)]
        trial = [
            old[c] - (dot3([held(3 * c + j) for j in range(3)], rel) + held(9 + c))
            for c in range(3)
        ]
        normal_part = jnp.maximum(trial[0], 0.0)
        slide = trial[1] * trial[1] + trial[2] * trial[2]
        shrink = lax.rsqrt(jnp.maximum(slide, tangent_floor * tangent_floor))
        factor = jnp.minimum(1.0, friction * normal_part * shrink)
        active = index[32:48, :] == k
        new = [
            jnp.where(active, normal_part, old[0]),
            jnp.where(active, trial[1] * factor, old[1]),
            jnp.where(active, trial[2] * factor, old[2]),
        ]
        change = [new[c] - old[c] for c in range(3)]
        for c in range(3):
            imp[c * slots : (c + 1) * slots, :] = new[c]
        force = [
            held(12) * change[0] + held(17) * change[2],
            held(13) * change[0] + held(15) * change[1] + held(18) * change[2],
            held(14) * change[0] + held(16) * change[1] + held(19) * change[2],
        ]
        spin_a = cross(arm_a, force)
        spin_b = cross(arm_b, force)
        for c in range(3):
            push_a[tile_rows[c], :] = held(26) * force[c]
            push_a[tile_rows[3 + c], :] = held(27 + c) * spin_a[c]
            push_b[tile_rows[c], :] = -(held(30) * force[c])
            push_b[tile_rows[3 + c], :] = -(held(31 + c) * spin_b[c])

        def spread(i):
            left, right = [], []
            empty = jnp.zeros((16 * (total - blocks), LANES), BF16)
            for j in range(CHUNK):
                t = order[begin + i * CHUNK + j]
                at = pl.ds(pl.multiple_of(8 * t, 8), 8)
                first = two_parts(push_a[at, :])
                second = two_parts(push_b[at, :])
                rows = [masks[t, 16 * m : 16 * m + 16, :] for m in range(blocks + total)]
                left.append(jnp.concatenate([first * m for m in rows[:blocks]] + [empty], axis=0))
                left.append(jnp.concatenate([second * m for m in rows[blocks:]], axis=0))
                at_hot = pl.multiple_of(2 * TILE * t, 2 * TILE)
                right.append(hot[:, pl.ds(at_hot, 2 * TILE)])
            return contract_lanes(
                jnp.concatenate(left, axis=1), jnp.concatenate(right, axis=1)
            )

        def scatter(i, c):
            acc[...] += spread(i)
            return c

        acc[...] = spread(0)
        lax.fori_loop(1, chunks, scatter, 0)
        for h in range(total):
            table[8 * h : 8 * h + 8, :] = now[h] + sum_parts(acc, h)
        return carry

    lax.fori_loop(0, NCOLOR, color_pass, 0)
    for h in range(blocks):
        own_change[:, h * LANES : (h + 1) * LANES] = table[8 * h : 8 * h + 8, :] - start[h]
    ghost0[...] = table[8 * blocks : 8 * blocks + 8, :] - start[blocks]
    ghost1[...] = table[8 * blocks + 8 : 8 * blocks + 16, :] - start[blocks + 1]
    impulse[...] = imp[...]


def merge_kernel(
    interface, last_sweep, own, change, c0, c1, c2, c3, mult, export_index, export_hot,
    export_masks, *refs,
):
    blocks = own.shape[1] // LANES
    came = [halves(c0[...], c1[...], interface), halves(c2[...], c3[...], interface)]
    left = jnp.concatenate(
        [
            jnp.concatenate([two_parts(came[i])] * blocks, axis=0) * export_masks[i]
            for i in range(2)
        ],
        axis=1,
    )
    incoming = contract_lanes(left, export_hot[...])
    fresh = []
    for h in range(blocks):
        span = slice(h * LANES, (h + 1) * LANES)
        fresh.append(
            own[0:8, span] + (change[:, span] + sum_parts(incoming, h)) / mult[:, span]
        )
    if last_sweep:
        imp, impulse, velocity = refs
        slots = imp.shape[0] // 3
        for c in range(3):
            for t in range(impulse.shape[2] // TILE):
                row = c * slots + t
                impulse[c, :, t * TILE : (t + 1) * TILE] = imp[row : row + 1, :]
        for r in range(6):
            for h in range(blocks):
                velocity[r, :, h * LANES : (h + 1) * LANES] = fresh[h][r : r + 1, :]
    else:
        fresh_own, out0, out1 = refs
        for h in range(blocks):
            fresh_own[:, h * LANES : (h + 1) * LANES] = fresh[h]
        out0[...] = pick(fresh, export_index[0:8, :])
        out1[...] = pick(fresh, export_index[8:16, :])


def in_hbm(array):
    return pltpu.with_memory_space_constraint(array, pltpu.HBM)


def shape(dims, dtype=F32):
    return jax.ShapeDtypeStruct(dims, dtype)


def make(subs, layers):
    matchings = neighbour_matchings(subs, layers)
    shuffles = [relay_shuffle(subs, layers, k) for k in range(WIN)]

    def trade(low, high):
        return [
            lax.ppermute(low if m < 2 else high, AXES, matchings[m]) for m in range(4)
        ]

    def on_device(geometry, dest_slot, pairs, colors, free_vel, inertia, exports):
        count = geometry.shape[2]
        bodies = free_vel.shape[2]
        interface = exports.shape[2]
        tiles = count // TILE
        slots = 16
        assert count % TILE == 0 and tiles < slots and 2 * interface == LANES
        assert bodies % LANES == 0
        blocks = bodies // LANES
        total = blocks + 2
        place = shape((10 * slots, LANES))
        small = shape((16, LANES))
        place0, send0, place2, place3, out0, out1, own, export_index = pl.pallas_call(
            prepare_kernel,
            out_shape=(
                place, shape((10 * slots + 16, LANES)), place, place, small, small,
                shape((16, bodies)),
                shape((16, LANES), jnp.int32),
            ),
            in_specs=[pl.BlockSpec(memory_space=pltpu.HBM)] * 5,
            out_specs=(VMEM_SPEC,) * 8,
            scratch_shapes=[
                pltpu.VMEM(geometry.shape, F32),
                pltpu.VMEM(dest_slot.shape, jnp.int32),
                pltpu.VMEM(free_vel.shape, F32),
                pltpu.VMEM(inertia.shape, F32),
                pltpu.VMEM(exports.shape, jnp.int32),
                pltpu.VMEM((8, LANES), jnp.int32),
                pltpu.VMEM((16, count), F32),
                pltpu.VMEM((WIN * slots, count), BF16),
                pltpu.VMEM((2, 10 * WIN * slots, count), BF16),
                pltpu.VMEM((LANES, count), BF16),
                pltpu.SemaphoreType.DMA((5,)),
            ],
            compiler_params=PARAMS,
            name="prepare",
        )(*[in_hbm(x) for x in (geometry, dest_slot, free_vel, inertia, exports)])
        came = [lax.ppermute(send0, AXES, matchings[0])]
        came.append(lax.ppermute(out0, AXES, matchings[1]))
        came.append(lax.ppermute(out1, AXES, matchings[2]))
        came.append(lax.ppermute(out1, AXES, matchings[3]))
        placed = [place0]
        placed.append(lax.ppermute(place2, AXES, shuffles[2]))
        placed.append(lax.ppermute(place3, AXES, shuffles[3]))

        def indexing(*refs):
            index_kernel(subs, layers, interface, bodies, *refs)

        index, hot, masks, export_hot, export_masks, mult, order = pl.pallas_call(
            indexing,
            out_shape=(
                shape((48, LANES), jnp.int32),
                shape((LANES, 2 * TILE * (tiles + 1)), BF16),
                shape((tiles + 1, 16 * (blocks + total), LANES), BF16),
                shape((LANES, 2 * LANES), BF16),
                shape((2, 16 * blocks, LANES), BF16),
                shape((8, bodies)),
                shape((32,), jnp.int32),
            ),
            in_specs=[VMEM_SPEC, SMEM_SPEC, VMEM_SPEC],
            out_specs=(VMEM_SPEC,) * 6 + (SMEM_SPEC,),
            compiler_params=PARAMS,
            name="indexing",
        )(pairs, colors, export_index)

        state = impulse = None
        for sweep in range(SWEEPS):
            first, last = sweep == 0, sweep == SWEEPS - 1

            def run(*refs, first=first):
                sweep_kernel(bodies, interface, first, *refs)

            outs = [
                shape((3 * slots, LANES)),
                shape((8, bodies)),
                shape((8, LANES)),
                shape((8, LANES)),
            ]
            operands = [order, index, hot, masks, own, *came]
            if first:
                outs = [shape((STATE * slots, LANES))] + outs
                operands += placed
            else:
                operands += [state, impulse]
            result = pl.pallas_call(
                run,
                out_shape=tuple(outs),
                in_specs=[SMEM_SPEC] + [VMEM_SPEC] * (len(operands) - 1),
                out_specs=(VMEM_SPEC,) * len(outs),
                scratch_shapes=[
                    pltpu.VMEM((8 * slots, LANES), F32),
                    pltpu.VMEM((8 * slots, LANES), F32),
                    pltpu.VMEM((8 * slots, LANES), F32),
                    pltpu.VMEM((8 * slots, LANES), F32),
                    pltpu.VMEM((16 * total, LANES), F32),
                    pltpu.VMEM((8 * total, LANES), F32),
                    pltpu.VMEM((3 * slots, LANES), F32),
                ],
                compiler_params=PARAMS,
                name="sweep",
            )(*operands)
            if first:
                state, result = result[0], result[1:]
            impulse, change, ghost0, ghost1 = result
            sums = trade(ghost0, ghost1)

            def merge(*refs, last=last):
                merge_kernel(interface, last, *refs)

            operands = [own, change, *sums, mult, export_index, export_hot, export_masks]
            if last:
                operands.append(impulse)
                outs = (shape((3, 1, count)), shape((6, 1, bodies)))
            else:
                outs = (shape((8, bodies)), shape((8, LANES)), shape((8, LANES)))
            merged = pl.pallas_call(
                merge,
                out_shape=outs,
                in_specs=[VMEM_SPEC] * len(operands),
                out_specs=(VMEM_SPEC,) * len(outs),
                compiler_params=PARAMS,
                name="merge",
            )(*operands)
            if last:
                return merged
            own = merged[0]
            came = trade(merged[1], merged[2])

    return on_device


def solution(mesh):
    placed = (
        P(None, "layer", "sub"),
        P("layer", "sub"),
        P(None, "layer", "sub"),
        P("layer", "sub"),
        P(None, "layer", "sub"),
        P(None, "layer", "sub"),
        P(None, "layer", "sub"),
    )
    return jax.shard_map(
        make(mesh.shape["sub"], mesh.shape["layer"]),
        mesh=mesh,
        in_specs=placed,
        out_specs=(P(None, "layer", "sub"), P(None, "layer", "sub")),
        check_vma=False,
    )
```

```python
import jax
import jax.numpy as jnp
from jax import lax
from jax.experimental import pallas as pl
from jax.experimental.pallas import tpu as pltpu
from jax.sharding import PartitionSpec as P

WIN = 4
SWEEPS = 3
NCOLOR = 4
TILE = 128
LANES = 128
GROUP = 4

relaxation = 0.7
friction = 0.6
tangent_floor = 0.1

AXES = ("sub", "layer")
F32 = jnp.float32
BF16 = jnp.bfloat16
VMEM_SPEC = pl.BlockSpec(memory_space=pltpu.VMEM)
SMEM_SPEC = pl.BlockSpec(memory_space=pltpu.SMEM)
PARAMS = pltpu.CompilerParams(vmem_limit_bytes=16 << 20)


def neighbour_matchings(subs, layers):
    assert subs % 2 == 0 and layers % 2 == 0

    def shifted(i):
        return i - 1 if i % 2 == 0 else i + 1

    def partner(match, s, y):
        if match == 0:
            return s ^ 1, y
        if match == 1:
            return (s, y ^ 1) if s in (0, subs - 1) else (shifted(s), y)
        if match == 2:
            return s, y ^ 1
        return (s ^ 1, y) if y in (0, layers - 1) else (s, shifted(y))

    out = []
    for match in range(4):
        pairs = []
        for s in range(subs):
            for y in range(layers):
                ps, py = partner(match, s, y)
                pairs.append((s * layers + y, ps * layers + py))
        out.append(pairs)
    return out


def relay_shuffle(subs, layers, k):
    return [
        (s * layers + y, (s ^ k) * layers + y) for s in range(subs) for y in range(layers)
    ]


def lane_iota():
    return lax.broadcasted_iota(jnp.int32, (8, LANES), 1)


def pick(tables, index):
    low = jnp.bitwise_and(index, LANES - 1)
    high = jnp.right_shift(index, 7)
    out = jnp.take_along_axis(tables[0], low, axis=1)
    for h in range(1, len(tables)):
        out = jnp.where(high == h, jnp.take_along_axis(tables[h], low, axis=1), out)
    return out


def two_parts(value):
    first = value.astype(BF16).astype(F32)
    return jnp.concatenate([first, value - first], axis=0).astype(BF16)


def high_masks(index_row, highs):
    high = jnp.broadcast_to(jnp.right_shift(index_row, 7), (16, LANES))
    return jnp.concatenate(
        [jnp.where(high == h, 1.0, 0.0) for h in range(highs)], axis=0
    ).astype(BF16)


def low_onehot(index_row):
    low = jnp.bitwise_and(index_row, LANES - 1)
    rows = lax.broadcasted_iota(jnp.int32, (LANES, LANES), 0)
    return jnp.where(rows == low, 1.0, 0.0).astype(BF16)


def contract_lanes(lhs, rhs):
    return lax.dot_general(
        lhs, rhs, (((1,), (1,)), ((), ())), preferred_element_type=F32
    )


def sum_parts(block, h):
    return block[16 * h : 16 * h + 8] + block[16 * h + 8 : 16 * h + 16]


def cross(u, v):
    return [
        u[1] * v[2] - u[2] * v[1],
        u[2] * v[0] - u[0] * v[2],
        u[0] * v[1] - u[1] * v[0],
    ]


def dot3(u, v):
    return u[0] * v[0] + u[1] * v[1] + u[2] * v[2]


def halves(low, high, half):
    return jnp.where(lane_iota() < half, low, high)


def parities():
    sub = lax.axis_index("sub")
    layer = lax.axis_index("layer")
    return sub, layer, lax.rem(sub, 2) == 0, lax.rem(layer, 2) == 0


def prepare_kernel(
    geo_hbm, dest_hbm, vel_hbm, inertia_hbm, exports_hbm,
    place0, send0, place2, place3, out0, out1, start_own, export_index,
    geo, dest, vel, inertia, exports, listed, dense, mask, lhs, hot, sems,
):
    copies = [
        pltpu.make_async_copy(src, dst, sems.at[i])
        for i, (src, dst) in enumerate(
            [
                (exports_hbm, exports),
                (vel_hbm, vel),
                (inertia_hbm, inertia),
                (dest_hbm, dest),
                (geo_hbm, geo),
            ]
        )
    ]
    for copy in copies:
        copy.start()
    count = geo.shape[2]
    tiles = count // TILE
    slots = place0.shape[0] // 10
    bodies = vel.shape[2]
    interface = exports.shape[2]
    sub, layer, sub_even, layer_even = parities()
    member = lax.rem(sub, WIN)
    start_own[...] = jnp.zeros_like(start_own)
    dense[...] = jnp.zeros_like(dense)
    for copy in copies[:4]:
        copy.wait()
    for r in range(6):
        start_own[r : r + 1, :] = vel[r]
    for r in range(4):
        start_own[8 + r : 9 + r, :] = inertia[r]
    listed[0:1, 0:interface] = exports[0]
    listed[0:1, interface : 2 * interface] = exports[1]
    listed[1:2, 0:interface] = exports[1]
    listed[1:2, interface : 2 * interface] = exports[0]
    listed[2:3, 0:interface] = exports[2]
    listed[2:3, interface : 2 * interface] = exports[3]
    listed[3:4, 0:interface] = exports[3]
    listed[3:4, interface : 2 * interface] = exports[2]
    row0 = jnp.where(sub_even, listed[1:2, :], listed[0:1, :])
    row1 = jnp.where(layer_even, listed[3:4, :], listed[2:3, :])
    idx0 = jnp.broadcast_to(row0, (8, LANES))
    idx1 = jnp.broadcast_to(row1, (8, LANES))
    export_index[0:8, :] = idx0
    export_index[8:16, :] = idx1
    blocks = bodies // LANES
    for base in (0, 8):
        tables = [
            start_own[base : base + 8, h * LANES : (h + 1) * LANES] for h in range(blocks)
        ]
        picked = pick(tables, idx0)
        out0[base : base + 8, :] = picked
        send0[10 * slots + base : 10 * slots + base + 8, :] = picked
        out1[base : base + 8, :] = pick(tables, idx1)
    slot = dest[...] - (sub - member) * count
    target = jnp.zeros_like(slot)
    for m in range(1, WIN):
        target = target + jnp.where(slot >= m * count, 1, 0)
    within = slot - target * count
    row_id = jnp.bitwise_xor(target, member) * slots + jnp.right_shift(within, 7)
    low = jnp.bitwise_and(within, LANES - 1)
    rows = lax.broadcasted_iota(jnp.int32, (WIN * slots, TILE), 0)
    for t in range(tiles):
        span = slice(t * TILE, (t + 1) * TILE)
        hot[:, span] = low_onehot(low[:, span])
        mask[:, span] = jnp.where(rows == row_id[:, span], 1.0, 0.0).astype(BF16)
    copies[4].wait()
    for r in range(10):
        dense[r : r + 1, :] = geo[r]
    value = dense[...]
    first = value.astype(BF16).astype(F32)
    parts = [first, value - first]
    for p in range(2):
        for r in range(10):
            row = jnp.broadcast_to(parts[p][r : r + 1, :], (slots, count)).astype(BF16)
            for k in range(WIN):
                at = (10 * k + r) * slots
                lhs[p, at : at + slots, :] = mask[k * slots : (k + 1) * slots, :] * row
    outs = (place0, send0, place2, place3)
    for k in range(WIN):
        span = slice(10 * slots * k, 10 * slots * (k + 1))
        total = contract_lanes(lhs[0, span, :], hot[...])
        total = total + contract_lanes(lhs[1, span, :], hot[...])
        outs[k][0 : 10 * slots, :] = total


TILE_SLOT, OVER_FROM, OVER_TO, UNUSED = 32, 48, 56, 63


def overflow_groups(tiles):
    most = 0
    for busy in range(1, NCOLOR + 1):
        spare = tiles - busy * (GROUP + 1)
        if spare >= 0:
            most = max(most, busy + spare // GROUP)
    return most


def slot_count(tiles):
    return -(-GROUP * (NCOLOR + overflow_groups(tiles)) // 8) * 8


def index_kernel(
    subs, layers, interface, bodies, pairs, colors, export_index,
    index_out, used, hot, masks, export_hot, export_masks, mult, scalars,
):
    count = pairs.shape[2]
    tiles = count // TILE
    slots = used.shape[0]
    blocks = bodies // LANES
    total = blocks + 4 * interface // LANES
    sub, layer, sub_even, layer_even = parities()
    for i in range(slots):
        scalars[i] = tiles
    place = [jnp.int32(0)] * tiles
    over = jnp.int32(0)
    for k in range(NCOLOR):
        filled = jnp.int32(0)
        base = (NCOLOR + over) * GROUP - GROUP
        for t in range(tiles):
            hit = colors[0, t] == k
            at = jnp.where(filled < GROUP, GROUP * k, base) + filled
            place[t] = jnp.where(hit, at, place[t])
            scalars[jnp.where(hit, at, UNUSED)] = t
            filled = filled + jnp.where(hit, 1, 0)
        scalars[OVER_FROM + k] = over
        over = over + lax.div(jnp.maximum(filled - 1, GROUP - 1), GROUP)
        scalars[OVER_TO + k] = over
    index_out[...] = jnp.zeros_like(index_out)
    used[...] = jnp.zeros_like(used)
    flip_sub = jnp.where(sub_even, interface, 0)
    flip_layer = jnp.where(layer_even, interface, 0)
    for t in range(tiles):
        span = slice(t * TILE, (t + 1) * TILE)
        first = pairs[0, :, span]
        other = pairs[1, :, span]
        ghost = other - bodies
        turned = jnp.where(
            ghost < 2 * interface,
            jnp.bitwise_xor(ghost, flip_sub),
            jnp.bitwise_xor(ghost, flip_layer),
        )
        second = jnp.where(ghost < 0, other, bodies + turned)
        scalars[TILE_SLOT + t] = place[t]
        index_out[pl.ds(place[t], 1), :] = first
        index_out[pl.ds(slots + place[t], 1), :] = second
        used[pl.ds(place[t], 1), :] = jnp.ones((1, LANES), F32)
        hot[:, 2 * t * TILE : (2 * t + 1) * TILE] = low_onehot(first)
        hot[:, (2 * t + 1) * TILE : (2 * t + 2) * TILE] = low_onehot(second)
        masks[t, : 16 * blocks, :] = high_masks(first, blocks)
        masks[t, 16 * blocks :, :] = high_masks(second, total)
    hot[:, 2 * tiles * TILE :] = jnp.zeros((LANES, 2 * TILE), BF16)
    masks[tiles] = jnp.zeros_like(masks[tiles])
    inner_sub = jnp.where(jnp.logical_and(sub > 0, sub < subs - 1), 1.0, 0.0)
    inner_layer = jnp.where(jnp.logical_and(layer > 0, layer < layers - 1), 1.0, 0.0)
    lane = lane_iota()
    weights = [
        jnp.where(lane < interface, 1.0, inner_sub),
        jnp.where(lane < interface, 1.0, inner_layer),
    ]
    left = []
    for i in range(2):
        row = export_index[8 * i : 8 * i + 1, :]
        export_hot[:, i * LANES : (i + 1) * LANES] = low_onehot(row)
        chosen = high_masks(row, blocks)
        export_masks[i] = chosen
        weight = jnp.concatenate([weights[i], jnp.zeros_like(weights[i])], axis=0).astype(BF16)
        left.append(jnp.concatenate([weight] * blocks, axis=0) * chosen)
    listed = contract_lanes(jnp.concatenate(left, axis=1), export_hot[...])
    for h in range(blocks):
        mult[:, h * LANES : (h + 1) * LANES] = 1.0 + listed[16 * h : 16 * h + 8]


STATE = 34


def contact_state(geo, first, second):
    raw = geo[0:3]
    length = jnp.sqrt(dot3(raw, raw))
    normal = [x / length for x in raw]
    side = jnp.sqrt(normal[1] * normal[1] + normal[2] * normal[2])
    tan_y = normal[2] / side
    tan_z = -normal[1] / side
    two = [
        normal[1] * tan_z - normal[2] * tan_y,
        -normal[0] * tan_z,
        normal[0] * tan_y,
    ]

    def arm(p, spin):
        return [
            spin[1] * p[2] * p[2] + spin[2] * p[1] * p[1],
            spin[0] * p[2] * p[2] + spin[2] * p[0] * p[0],
            spin[0] * p[1] * p[1] + spin[1] * p[0] * p[0],
            -spin[2] * p[0] * p[1],
            -spin[1] * p[0] * p[2],
            -spin[0] * p[1] * p[2],
        ]

    arm_a, arm_b = geo[3:6], geo[6:9]
    e = [x + y for x, y in zip(arm(arm_a, first[1:4]), arm(arm_b, second[1:4]))]
    mass = first[0] + second[0]
    xx, yy, zz = mass + e[0], mass + e[1], mass + e[2]
    xy, xz, yz = e[3], e[4], e[5]
    c_xx = yy * zz - yz * yz
    c_xy = xz * yz - xy * zz
    c_xz = xy * yz - xz * yy
    c_yy = xx * zz - xz * xz
    c_yz = xy * xz - xx * yz
    c_zz = xx * yy - xy * xy
    det = xx * c_xx + xy * c_xy + xz * c_xz
    inv = [
        [c_xx / det, c_xy / det, c_xz / det],
        [c_xy / det, c_yy / det, c_yz / det],
        [c_xz / det, c_yz / det, c_zz / det],
    ]
    solve = []
    for row in (normal, None, two):
        for j in range(3):
            if row is None:
                value = tan_y * inv[1][j] + tan_z * inv[2][j]
            else:
                value = row[0] * inv[0][j] + row[1] * inv[1][j] + row[2] * inv[2][j]
            solve.append(relaxation * value)
    bias = [geo[9] * dot3(solve[3 * i : 3 * i + 3], normal) for i in range(3)]
    return (
        solve + bias + normal + [tan_y, tan_z] + two + arm_a + arm_b + list(first) + list(second)
    )


def sweep_kernel(bodies, interface, first_sweep, *refs):
    scalars_in, index, used, hot, masks = refs[:5]
    refs = refs[5:]
    if first_sweep:
        own, g1, r1, r2, r3, g0, g2, g3, state = refs[:9]
        refs = refs[9:]
        r0 = g1.at[pl.ds(g0.shape[0], 16), :]
    else:
        own, r0, r1, r2, r3, state, impulse_in = refs[:7]
        refs = refs[7:]
    impulse, own_change, ghost0, ghost1 = refs[:4]
    got_a, got_b, push_a, push_b, acc, table, all_a, all_b, gathered, placed, scalars, sem = refs[4:]
    slots = used.shape[0]
    tiles = masks.shape[0] - 1
    blocks = bodies // LANES
    total = blocks + (4 * interface) // LANES
    fetch = pltpu.make_async_copy(scalars_in, scalars, sem)
    fetch.start()

    def ghost_blocks(base):
        return [
            halves(r0[base : base + 8, :], r1[base : base + 8, :], interface),
            halves(r2[base : base + 8, :], r3[base : base + 8, :], interface),
        ]

    start = [own[0:8, h * LANES : (h + 1) * LANES] for h in range(blocks)] + ghost_blocks(0)
    for h in range(total):
        table[8 * h : 8 * h + 8, :] = start[h]
    push_a[...] = jnp.zeros_like(push_a)
    push_b[...] = jnp.zeros_like(push_b)

    if first_sweep:
        props = [own[8:16, h * LANES : (h + 1) * LANES] for h in range(blocks)] + ghost_blocks(8)
        for t in range(slots):
            ia = jnp.broadcast_to(index[t : t + 1, :], (8, LANES))
            ib = jnp.broadcast_to(index[slots + t : slots + t + 1, :], (8, LANES))
            all_a[8 * t : 8 * t + 8, :] = pick(props[:blocks], ia)
            all_b[8 * t : 8 * t + 8, :] = pick(props, ib)
        gathered[...] = (g0[...] + g1[0 : g0.shape[0], :]) + (g2[...] + g3[...])
        placed[...] = jnp.ones_like(placed)
        fetch.wait()
        rows = g0.shape[0] // 10
        for t in range(tiles):
            slot = scalars[TILE_SLOT + t]
            for c in range(10):
                placed[pl.ds(c * slots + slot, 1), :] = gathered[c * rows + t : c * rows + t + 1, :]
        first = [all_a[pl.ds(c, slots, stride=8), :] for c in range(4)]
        second = [all_b[pl.ds(c, slots, stride=8), :] for c in range(4)]
        geo = [placed[c * slots : (c + 1) * slots, :] for c in range(10)]
        for c, value in enumerate(contact_state(geo, first, second)):
            state[c * slots : (c + 1) * slots, :] = value
        impulse[...] = jnp.zeros_like(impulse)
    else:
        impulse[...] = impulse_in[...]

    def group(base, now, before):
        def held(c):
            return state[pl.ds(c * slots + base, GROUP), :]

        for j in range(GROUP):
            ia = jnp.broadcast_to(index[pl.ds(base + j, 1), :], (8, LANES))
            ib = jnp.broadcast_to(index[pl.ds(slots + base + j, 1), :], (8, LANES))
            got_a[8 * j : 8 * j + 8, :] = pick(now[:blocks], ia)
            got_b[8 * j : 8 * j + 8, :] = pick(now, ib)
        tile_rows = [pl.ds(c, GROUP, stride=8) for c in range(6)]
        va = [got_a[tile_rows[c], :] for c in range(6)]
        vb = [got_b[tile_rows[c], :] for c in range(6)]
        arm_a = [held(20 + c) for c in range(3)]
        arm_b = [held(23 + c) for c in range(3)]
        turn_a = cross(va[3:6], arm_a)
        turn_b = cross(vb[3:6], arm_b)
        rel = [((va[c] + turn_a[c]) - vb[c]) - turn_b[c] for c in range(3)]
        old = [impulse[pl.ds(c * slots + base, GROUP), :] for c in range(3)]
        trial = [
            old[c] - (dot3([held(3 * c + j) for j in range(3)], rel) + held(9 + c))
            for c in range(3)
        ]
        normal_part = jnp.maximum(trial[0], 0.0)
        slide = trial[1] * trial[1] + trial[2] * trial[2]
        shrink = lax.rsqrt(jnp.maximum(slide, tangent_floor * tangent_floor))
        factor = jnp.minimum(1.0, friction * normal_part * shrink)
        active = used[pl.ds(base, GROUP), :] > 0.5
        new = [
            jnp.where(active, normal_part, old[0]),
            jnp.where(active, trial[1] * factor, old[1]),
            jnp.where(active, trial[2] * factor, old[2]),
        ]
        change = [new[c] - old[c] for c in range(3)]
        for c in range(3):
            impulse[pl.ds(c * slots + base, GROUP), :] = new[c]
        force = [
            held(12) * change[0] + held(17) * change[2],
            held(13) * change[0] + held(15) * change[1] + held(18) * change[2],
            held(14) * change[0] + held(16) * change[1] + held(19) * change[2],
        ]
        spin_a = cross(arm_a, force)
        spin_b = cross(arm_b, force)
        for c in range(3):
            push_a[tile_rows[c], :] = held(26) * force[c]
            push_a[tile_rows[3 + c], :] = held(27 + c) * spin_a[c]
            push_b[tile_rows[c], :] = -(held(30) * force[c])
            push_b[tile_rows[3 + c], :] = -(held(31 + c) * spin_b[c])
        if before is not None:
            before()
        left, right = [], []
        empty = jnp.zeros((16 * (total - blocks), LANES), BF16)
        for j in range(GROUP):
            t = scalars[base + j]
            first = two_parts(push_a[8 * j : 8 * j + 8, :])
            second = two_parts(push_b[8 * j : 8 * j + 8, :])
            rows = [masks[t, 16 * m : 16 * m + 16, :] for m in range(blocks + total)]
            left.append(jnp.concatenate([first * m for m in rows[:blocks]] + [empty], axis=0))
            left.append(jnp.concatenate([second * m for m in rows[blocks:]], axis=0))
            right.append(hot[:, pl.ds(pl.multiple_of(2 * TILE * t, 2 * TILE), 2 * TILE)])
        return contract_lanes(jnp.concatenate(left, axis=1), jnp.concatenate(right, axis=1))

    def color_pass(k, before=None):
        now = [table[8 * h : 8 * h + 8, :] for h in range(total)]
        acc[...] = group(pl.multiple_of(GROUP * k, GROUP), now, before)

        def more(g, c):
            acc[...] += group(pl.multiple_of(GROUP * (NCOLOR + g), GROUP), now, None)
            return c

        lax.fori_loop(scalars[OVER_FROM + k], scalars[OVER_TO + k], more, 0)
        for h in range(total):
            table[8 * h : 8 * h + 8, :] = now[h] + sum_parts(acc, h)

    def later_pass(k, carry):
        color_pass(k)
        return carry

    color_pass(0, None if first_sweep else fetch.wait)
    lax.fori_loop(1, NCOLOR, later_pass, 0)
    for h in range(blocks):
        own_change[:, h * LANES : (h + 1) * LANES] = table[8 * h : 8 * h + 8, :] - start[h]
    ghost0[...] = table[8 * blocks : 8 * blocks + 8, :] - start[blocks]
    ghost1[...] = table[8 * blocks + 8 : 8 * blocks + 16, :] - start[blocks + 1]


def impulse_kernel(scalars, held, impulse):
    slots = held.shape[0] // 3
    for t in range(impulse.shape[2] // TILE):
        slot = scalars[TILE_SLOT + t]
        for c in range(3):
            impulse[c, :, t * TILE : (t + 1) * TILE] = held[pl.ds(c * slots + slot, 1), :]


def merge_kernel(
    interface, last_sweep, own, change, c0, c1, c2, c3, mult, export_index, export_hot,
    export_masks, *refs,
):
    blocks = own.shape[1] // LANES
    came = [halves(c0[...], c1[...], interface), halves(c2[...], c3[...], interface)]
    left = jnp.concatenate(
        [
            jnp.concatenate([two_parts(came[i])] * blocks, axis=0) * export_masks[i]
            for i in range(2)
        ],
        axis=1,
    )
    incoming = contract_lanes(left, export_hot[...])
    fresh = []
    for h in range(blocks):
        span = slice(h * LANES, (h + 1) * LANES)
        fresh.append(
            own[0:8, span] + (change[:, span] + sum_parts(incoming, h)) / mult[:, span]
        )
    if last_sweep:
        (velocity,) = refs
        for r in range(6):
            for h in range(blocks):
                velocity[r, :, h * LANES : (h + 1) * LANES] = fresh[h][r : r + 1, :]
    else:
        fresh_own, out0, out1 = refs
        for h in range(blocks):
            fresh_own[:, h * LANES : (h + 1) * LANES] = fresh[h]
        out0[...] = pick(fresh, export_index[0:8, :])
        out1[...] = pick(fresh, export_index[8:16, :])


def in_hbm(array):
    return pltpu.with_memory_space_constraint(array, pltpu.HBM)


def shape(dims, dtype=F32):
    return jax.ShapeDtypeStruct(dims, dtype)


def make(subs, layers):
    matchings = neighbour_matchings(subs, layers)
    shuffles = [relay_shuffle(subs, layers, k) for k in range(WIN)]

    def trade(low, high):
        return [
            lax.ppermute(low if m < 2 else high, AXES, matchings[m]) for m in range(4)
        ]

    def on_device(geometry, dest_slot, pairs, colors, free_vel, inertia, exports):
        count = geometry.shape[2]
        bodies = free_vel.shape[2]
        interface = exports.shape[2]
        tiles = count // TILE
        slots = 16
        assert count % TILE == 0 and tiles < slots and 2 * interface == LANES
        assert bodies % LANES == 0
        blocks = bodies // LANES
        total = blocks + 2
        place = shape((10 * slots, LANES))
        small = shape((16, LANES))
        place0, send0, place2, place3, out0, out1, own, export_index = pl.pallas_call(
            prepare_kernel,
            out_shape=(
                place, shape((10 * slots + 16, LANES)), place, place, small, small,
                shape((16, bodies)),
                shape((16, LANES), jnp.int32),
            ),
            in_specs=[pl.BlockSpec(memory_space=pltpu.HBM)] * 5,
            out_specs=(VMEM_SPEC,) * 8,
            scratch_shapes=[
                pltpu.VMEM(geometry.shape, F32),
                pltpu.VMEM(dest_slot.shape, jnp.int32),
                pltpu.VMEM(free_vel.shape, F32),
                pltpu.VMEM(inertia.shape, F32),
                pltpu.VMEM(exports.shape, jnp.int32),
                pltpu.VMEM((8, LANES), jnp.int32),
                pltpu.VMEM((16, count), F32),
                pltpu.VMEM((WIN * slots, count), BF16),
                pltpu.VMEM((2, 10 * WIN * slots, count), BF16),
                pltpu.VMEM((LANES, count), BF16),
                pltpu.SemaphoreType.DMA((5,)),
            ],
            compiler_params=PARAMS,
            name="prepare",
        )(*[in_hbm(x) for x in (geometry, dest_slot, free_vel, inertia, exports)])
        came = [lax.ppermute(send0, AXES, matchings[0])]
        came.append(lax.ppermute(out0, AXES, matchings[1]))
        came.append(lax.ppermute(out1, AXES, matchings[2]))
        came.append(lax.ppermute(out1, AXES, matchings[3]))
        placed = [place0]
        placed.append(lax.ppermute(place2, AXES, shuffles[2]))
        placed.append(lax.ppermute(place3, AXES, shuffles[3]))

        def indexing(*refs):
            index_kernel(subs, layers, interface, bodies, *refs)

        rows = slot_count(tiles)
        assert rows <= TILE_SLOT
        index, used, hot, masks, export_hot, export_masks, mult, scalars = pl.pallas_call(
            indexing,
            out_shape=(
                shape((2 * rows, LANES), jnp.int32),
                shape((rows, LANES)),
                shape((LANES, 2 * TILE * (tiles + 1)), BF16),
                shape((tiles + 1, 16 * (blocks + total), LANES), BF16),
                shape((LANES, 2 * LANES), BF16),
                shape((2, 16 * blocks, LANES), BF16),
                shape((8, bodies)),
                shape((64,), jnp.int32),
            ),
            in_specs=[VMEM_SPEC, SMEM_SPEC, VMEM_SPEC],
            out_specs=(VMEM_SPEC,) * 7 + (SMEM_SPEC,),
            compiler_params=PARAMS,
            name="indexing",
        )(pairs, colors, export_index)

        state = impulse = None
        for sweep in range(SWEEPS):
            first, last = sweep == 0, sweep == SWEEPS - 1

            def run(*refs, first=first):
                sweep_kernel(bodies, interface, first, *refs)

            outs = [
                shape((3 * rows, LANES)),
                shape((8, bodies)),
                shape((8, LANES)),
                shape((8, LANES)),
            ]
            operands = [scalars, index, used, hot, masks, own, *came]
            if first:
                outs = [shape((STATE * rows, LANES))] + outs
                operands += placed
            else:
                operands += [state, impulse]
            result = pl.pallas_call(
                run,
                out_shape=tuple(outs),
                in_specs=[VMEM_SPEC] * len(operands),
                out_specs=(VMEM_SPEC,) * len(outs),
                scratch_shapes=[
                    pltpu.VMEM((8 * GROUP, LANES), F32),
                    pltpu.VMEM((8 * GROUP, LANES), F32),
                    pltpu.VMEM((8 * GROUP, LANES), F32),
                    pltpu.VMEM((8 * GROUP, LANES), F32),
                    pltpu.VMEM((16 * total, LANES), F32),
                    pltpu.VMEM((8 * total, LANES), F32),
                    pltpu.VMEM((8 * rows, LANES), F32),
                    pltpu.VMEM((8 * rows, LANES), F32),
                    pltpu.VMEM((10 * slots, LANES), F32),
                    pltpu.VMEM((10 * rows, LANES), F32),
                    pltpu.SMEM((64,), jnp.int32),
                    pltpu.SemaphoreType.DMA,
                ],
                compiler_params=PARAMS,
                name="sweep",
            )(*operands)
            if first:
                state, result = result[0], result[1:]
            impulse, change, ghost0, ghost1 = result
            sums = trade(ghost0, ghost1)

            def merge(*refs, last=last):
                merge_kernel(interface, last, *refs)

            operands = [own, change, *sums, mult, export_index, export_hot, export_masks]
            if last:
                outs = (shape((6, 1, bodies)),)
            else:
                outs = (shape((8, bodies)), shape((8, LANES)), shape((8, LANES)))
            merged = pl.pallas_call(
                merge,
                out_shape=outs,
                in_specs=[VMEM_SPEC] * len(operands),
                out_specs=(VMEM_SPEC,) * len(outs),
                compiler_params=PARAMS,
                name="merge",
            )(*operands)
            if last:
                in_order = pl.pallas_call(
                    impulse_kernel,
                    out_shape=shape((3, 1, count)),
                    in_specs=[SMEM_SPEC, VMEM_SPEC],
                    out_specs=VMEM_SPEC,
                    compiler_params=PARAMS,
                    name="impulse",
                )(scalars, impulse)
                return in_order, merged[0]
            own = merged[0]
            came = trade(merged[1], merged[2])

    return on_device


def solution(mesh):
    placed = (
        P(None, "layer", "sub"),
        P("layer", "sub"),
        P(None, "layer", "sub"),
        P("layer", "sub"),
        P(None, "layer", "sub"),
        P(None, "layer", "sub"),
        P(None, "layer", "sub"),
    )
    return jax.shard_map(
        make(mesh.shape["sub"], mesh.shape["layer"]),
        mesh=mesh,
        in_specs=placed,
        out_specs=(P(None, "layer", "sub"), P(None, "layer", "sub")),
        check_vma=False,
    )
```

```python
import jax
import jax.numpy as jnp
from jax import lax
from jax.experimental import pallas as pl
from jax.experimental.pallas import tpu as pltpu
from jax.sharding import PartitionSpec as P

WIN = 4
SWEEPS = 3
NCOLOR = 4
TILE = 128
LANES = 128
WIDE = 256
GROUP = 4

relaxation = 0.7
friction = 0.6
tangent_floor = 0.1

AXES = ("sub", "layer")
F32 = jnp.float32
BF16 = jnp.bfloat16
VMEM_SPEC = pl.BlockSpec(memory_space=pltpu.VMEM)
SMEM_SPEC = pl.BlockSpec(memory_space=pltpu.SMEM)
PARAMS = pltpu.CompilerParams(vmem_limit_bytes=16 << 20)


def neighbour_matchings(subs, layers):
    assert subs % 2 == 0 and layers % 2 == 0

    def shifted(i):
        return i - 1 if i % 2 == 0 else i + 1

    def partner(match, s, y):
        if match == 0:
            return s ^ 1, y
        if match == 1:
            return (s, y ^ 1) if s in (0, subs - 1) else (shifted(s), y)
        if match == 2:
            return s, y ^ 1
        return (s ^ 1, y) if y in (0, layers - 1) else (s, shifted(y))

    out = []
    for match in range(4):
        pairs = []
        for s in range(subs):
            for y in range(layers):
                ps, py = partner(match, s, y)
                pairs.append((s * layers + y, ps * layers + py))
        out.append(pairs)
    return out


def relay_shuffle(subs, layers, k):
    return [
        (s * layers + y, (s ^ k) * layers + y) for s in range(subs) for y in range(layers)
    ]


def lane_iota():
    return lax.broadcasted_iota(jnp.int32, (8, LANES), 1)


def pick(tables, index):
    low = jnp.bitwise_and(index, LANES - 1)
    high = jnp.right_shift(index, 7)
    out = jnp.take_along_axis(tables[0], low, axis=1)
    for h in range(1, len(tables)):
        out = jnp.where(high == h, jnp.take_along_axis(tables[h], low, axis=1), out)
    return out


def two_parts(value):
    first = value.astype(BF16).astype(F32)
    return jnp.concatenate([first, value - first], axis=0).astype(BF16)


def equal_rows(row, count):
    shape = (count, row.shape[1])
    ids = lax.broadcasted_iota(jnp.int32, shape, 0).astype(F32).astype(BF16)
    here = jnp.broadcast_to(row.astype(F32), shape).astype(BF16)
    return jnp.where(ids == here, jnp.ones(shape, BF16), jnp.zeros(shape, BF16))


def high_masks(index_row, highs):
    shape = (16, LANES)
    high = jnp.broadcast_to(jnp.right_shift(index_row, 7).astype(F32), shape).astype(BF16)
    one, zero = jnp.ones(shape, BF16), jnp.zeros(shape, BF16)
    return jnp.concatenate(
        [jnp.where(high == jnp.full(shape, h, BF16), one, zero) for h in range(highs)], axis=0
    )


def low_onehot(index_row):
    return equal_rows(jnp.bitwise_and(index_row, LANES - 1), LANES)


def contract_lanes(lhs, rhs):
    return lax.dot_general(
        lhs, rhs, (((1,), (1,)), ((), ())), preferred_element_type=F32
    )


def sum_parts(block, h):
    return block[16 * h : 16 * h + 8] + block[16 * h + 8 : 16 * h + 16]


def cross(u, v):
    return [
        u[1] * v[2] - u[2] * v[1],
        u[2] * v[0] - u[0] * v[2],
        u[0] * v[1] - u[1] * v[0],
    ]


def dot3(u, v):
    return u[0] * v[0] + u[1] * v[1] + u[2] * v[2]


def halves(low, high, half):
    return jnp.where(lane_iota() < half, low, high)


def parities():
    sub = lax.axis_index("sub")
    layer = lax.axis_index("layer")
    return sub, layer, lax.rem(sub, 2) == 0, lax.rem(layer, 2) == 0


def prepare_kernel(
    geo_hbm, dest_hbm, vel_hbm, inertia_hbm, exports_hbm,
    send0, place2, place3, out0, out1, start_own, export_index, hot, own_mask, tall,
    geo, dest, vel, inertia, exports, listed, dense, mask, lhs, sems,
):
    copies = [
        pltpu.make_async_copy(src, dst, sems.at[i])
        for i, (src, dst) in enumerate(
            [
                (exports_hbm, exports),
                (vel_hbm, vel),
                (inertia_hbm, inertia),
                (dest_hbm, dest),
                (geo_hbm, geo),
            ]
        )
    ]
    for copy in copies:
        copy.start()
    count = geo.shape[2]
    tiles = count // TILE
    slots = place2.shape[0] // 10
    bodies = vel.shape[2]
    interface = exports.shape[2]
    sub, layer, sub_even, layer_even = parities()
    member = lax.rem(sub, WIN)
    start_own[...] = jnp.zeros_like(start_own)
    dense[...] = jnp.zeros_like(dense)
    for copy in copies[:4]:
        copy.wait()
    for r in range(6):
        start_own[r : r + 1, :] = vel[r]
    for r in range(4):
        start_own[8 + r : 9 + r, :] = inertia[r]
    listed[0:1, 0:interface] = exports[0]
    listed[0:1, interface : 2 * interface] = exports[1]
    listed[1:2, 0:interface] = exports[1]
    listed[1:2, interface : 2 * interface] = exports[0]
    listed[2:3, 0:interface] = exports[2]
    listed[2:3, interface : 2 * interface] = exports[3]
    listed[3:4, 0:interface] = exports[3]
    listed[3:4, interface : 2 * interface] = exports[2]
    row0 = jnp.where(sub_even, listed[1:2, :], listed[0:1, :])
    row1 = jnp.where(layer_even, listed[3:4, :], listed[2:3, :])
    idx0 = jnp.broadcast_to(row0, (8, LANES))
    idx1 = jnp.broadcast_to(row1, (8, LANES))
    export_index[0:8, :] = idx0
    export_index[8:16, :] = idx1
    blocks = bodies // LANES
    for base in (0, 8):
        tables = [
            start_own[base : base + 8, h * LANES : (h + 1) * LANES] for h in range(blocks)
        ]
        picked = pick(tables, idx0)
        out0[base : base + 8, :] = picked
        send0[10 * slots + base : 10 * slots + base + 8, :] = picked
        out1[base : base + 8, :] = pick(tables, idx1)
    slot = dest[...] - (sub - member) * count
    target = jnp.zeros_like(slot)
    for m in range(1, WIN):
        target = target + jnp.where(slot >= m * count, 1, 0)
    within = slot - target * count
    row_id = jnp.bitwise_xor(target, member) * 8 + jnp.right_shift(within, 8)
    low = jnp.bitwise_and(within, WIDE - 1)
    paired = (16, TILE)
    ids = lax.broadcasted_iota(jnp.int32, paired, 0)
    ids = jnp.bitwise_and(ids, 7).astype(F32)
    one, zero = jnp.ones(paired, BF16), jnp.zeros(paired, BF16)
    for t in range(tiles):
        span = slice(t * TILE, (t + 1) * TILE)
        hot[:, span] = equal_rows(low[:, span], WIDE)
        here = jnp.broadcast_to(row_id[:, span].astype(F32), paired).astype(BF16)
        for k in range(WIN):
            chosen = jnp.where(here == (ids + 8.0 * k).astype(BF16), one, zero)
            if k == 0:
                own_mask[:, span] = chosen
            else:
                mask[16 * k - 16 : 16 * k, span] = chosen
    copies[4].wait()
    for r in range(10):
        dense[r : r + 1, :] = geo[r]
    value = dense[...]
    first = value.astype(BF16).astype(F32)
    parts = [first, value - first]
    for p in range(2):
        for i in range(5):
            pair = jnp.concatenate(
                [jnp.broadcast_to(parts[p][r : r + 1, :], (8, count)) for r in (2 * i, 2 * i + 1)],
                axis=0,
            ).astype(BF16)
            tall[p, 16 * i : 16 * i + 16, :] = pair
            for k in range(1, WIN):
                at = 80 * (k - 1) + 16 * i
                lhs[p, at : at + 16, :] = mask[16 * k - 16 : 16 * k, :] * pair
    total = contract_lanes(lhs[0], hot[...]) + contract_lanes(lhs[1], hot[...])
    for k, out in enumerate((send0, place2, place3)):
        store_placed(out, total[80 * k : 80 * k + 80, :])


def store_placed(out, total):
    for r in range(10):
        for side in range(2):
            out[16 * r + 8 * side : 16 * r + 8 * side + 8, :] = total[
                8 * r : 8 * r + 8, side * LANES : (side + 1) * LANES
            ]


def place_kernel(tall, own_mask, hot, out):
    left = [jnp.concatenate([own_mask[...]] * 5, axis=0) * tall[p] for p in range(2)]
    store_placed(out, contract_lanes(left[0], hot[...]) + contract_lanes(left[1], hot[...]))


TILE_SLOT, OVER_FROM, OVER_TO, UNUSED = 32, 48, 56, 63


def overflow_groups(tiles):
    most = 0
    for busy in range(1, NCOLOR + 1):
        spare = tiles - busy * (GROUP + 1)
        if spare >= 0:
            most = max(most, busy + spare // GROUP)
    return most


def slot_count(tiles):
    return -(-GROUP * (NCOLOR + overflow_groups(tiles)) // 8) * 8


def index_kernel(
    subs, layers, interface, bodies, pairs, colors, export_index,
    index_out, used, hot, masks, export_hot, export_masks, mult, scalars,
):
    count = pairs.shape[2]
    tiles = count // TILE
    slots = used.shape[0]
    blocks = bodies // LANES
    total = blocks + 4 * interface // LANES
    sub, layer, sub_even, layer_even = parities()
    for i in range(slots):
        scalars[i] = tiles
    place = [jnp.int32(0)] * tiles
    over = jnp.int32(0)
    for k in range(NCOLOR):
        filled = jnp.int32(0)
        base = (NCOLOR + over) * GROUP - GROUP
        for t in range(tiles):
            hit = colors[0, t] == k
            at = jnp.where(filled < GROUP, GROUP * k, base) + filled
            place[t] = jnp.where(hit, at, place[t])
            scalars[jnp.where(hit, at, UNUSED)] = t
            filled = filled + jnp.where(hit, 1, 0)
        scalars[OVER_FROM + k] = over
        over = over + lax.div(jnp.maximum(filled - 1, GROUP - 1), GROUP)
        scalars[OVER_TO + k] = over
    index_out[...] = jnp.zeros_like(index_out)
    used[...] = jnp.zeros_like(used)
    flip_sub = jnp.where(sub_even, interface, 0)
    flip_layer = jnp.where(layer_even, interface, 0)
    for t in range(tiles):
        span = slice(t * TILE, (t + 1) * TILE)
        first = pairs[0, :, span]
        other = pairs[1, :, span]
        ghost = other - bodies
        turned = jnp.where(
            ghost < 2 * interface,
            jnp.bitwise_xor(ghost, flip_sub),
            jnp.bitwise_xor(ghost, flip_layer),
        )
        second = jnp.where(ghost < 0, other, bodies + turned)
        scalars[TILE_SLOT + t] = place[t]
        index_out[pl.ds(place[t], 1), :] = first
        index_out[pl.ds(slots + place[t], 1), :] = second
        used[pl.ds(place[t], 1), :] = jnp.ones((1, LANES), F32)
        hot[:, 2 * t * TILE : (2 * t + 1) * TILE] = low_onehot(first)
        hot[:, (2 * t + 1) * TILE : (2 * t + 2) * TILE] = low_onehot(second)
        masks[t, : 16 * blocks, :] = high_masks(first, blocks)
        masks[t, 16 * blocks :, :] = high_masks(second, total)
    hot[:, 2 * tiles * TILE :] = jnp.zeros((LANES, 2 * TILE), BF16)
    masks[tiles] = jnp.zeros_like(masks[tiles])
    inner_sub = jnp.where(jnp.logical_and(sub > 0, sub < subs - 1), 1.0, 0.0)
    inner_layer = jnp.where(jnp.logical_and(layer > 0, layer < layers - 1), 1.0, 0.0)
    lane = lane_iota()
    weights = [
        jnp.where(lane < interface, 1.0, inner_sub),
        jnp.where(lane < interface, 1.0, inner_layer),
    ]
    left = []
    for i in range(2):
        row = export_index[8 * i : 8 * i + 1, :]
        export_hot[:, i * LANES : (i + 1) * LANES] = low_onehot(row)
        chosen = high_masks(row, blocks)
        export_masks[i] = chosen
        weight = jnp.concatenate([weights[i], jnp.zeros_like(weights[i])], axis=0).astype(BF16)
        left.append(jnp.concatenate([weight] * blocks, axis=0) * chosen)
    listed = contract_lanes(jnp.concatenate(left, axis=1), export_hot[...])
    for h in range(blocks):
        mult[:, h * LANES : (h + 1) * LANES] = 1.0 + listed[16 * h : 16 * h + 8]


STATE = 34


def contact_state(geo, first, second):
    raw = geo[0:3]
    length = jnp.sqrt(dot3(raw, raw))
    normal = [x / length for x in raw]
    side = jnp.sqrt(normal[1] * normal[1] + normal[2] * normal[2])
    tan_y = normal[2] / side
    tan_z = -normal[1] / side
    two = [
        normal[1] * tan_z - normal[2] * tan_y,
        -normal[0] * tan_z,
        normal[0] * tan_y,
    ]

    def arm(p, spin):
        return [
            spin[1] * p[2] * p[2] + spin[2] * p[1] * p[1],
            spin[0] * p[2] * p[2] + spin[2] * p[0] * p[0],
            spin[0] * p[1] * p[1] + spin[1] * p[0] * p[0],
            -spin[2] * p[0] * p[1],
            -spin[1] * p[0] * p[2],
            -spin[0] * p[1] * p[2],
        ]

    arm_a, arm_b = geo[3:6], geo[6:9]
    e = [x + y for x, y in zip(arm(arm_a, first[1:4]), arm(arm_b, second[1:4]))]
    mass = first[0] + second[0]
    xx, yy, zz = mass + e[0], mass + e[1], mass + e[2]
    xy, xz, yz = e[3], e[4], e[5]
    c_xx = yy * zz - yz * yz
    c_xy = xz * yz - xy * zz
    c_xz = xy * yz - xz * yy
    c_yy = xx * zz - xz * xz
    c_yz = xy * xz - xx * yz
    c_zz = xx * yy - xy * xy
    det = xx * c_xx + xy * c_xy + xz * c_xz
    inv = [
        [c_xx / det, c_xy / det, c_xz / det],
        [c_xy / det, c_yy / det, c_yz / det],
        [c_xz / det, c_yz / det, c_zz / det],
    ]
    solve = []
    for row in (normal, None, two):
        for j in range(3):
            if row is None:
                value = tan_y * inv[1][j] + tan_z * inv[2][j]
            else:
                value = row[0] * inv[0][j] + row[1] * inv[1][j] + row[2] * inv[2][j]
            solve.append(relaxation * value)
    bias = [geo[9] * dot3(solve[3 * i : 3 * i + 3], normal) for i in range(3)]
    return (
        solve + bias + normal + [tan_y, tan_z] + two + arm_a + arm_b + list(first) + list(second)
    )


def sweep_kernel(bodies, interface, first_sweep, *refs):
    scalars_in, index, used, hot, masks = refs[:5]
    refs = refs[5:]
    if first_sweep:
        own, g1, r1, r2, r3, g0, g2, g3, state = refs[:9]
        refs = refs[9:]
        r0 = g1.at[pl.ds(g0.shape[0], 16), :]
    else:
        own, r0, r1, r2, r3, state, impulse_in = refs[:7]
        refs = refs[7:]
    impulse, own_change, ghost0, ghost1 = refs[:4]
    got_a, got_b, push_a, push_b, acc, table, all_a, all_b, gathered, placed, scalars, sem = refs[4:]
    slots = used.shape[0]
    tiles = masks.shape[0] - 1
    blocks = bodies // LANES
    total = blocks + (4 * interface) // LANES
    fetch = pltpu.make_async_copy(scalars_in, scalars, sem)
    fetch.start()

    def ghost_blocks(base):
        return [
            halves(r0[base : base + 8, :], r1[base : base + 8, :], interface),
            halves(r2[base : base + 8, :], r3[base : base + 8, :], interface),
        ]

    start = [own[0:8, h * LANES : (h + 1) * LANES] for h in range(blocks)] + ghost_blocks(0)
    for h in range(total):
        table[8 * h : 8 * h + 8, :] = start[h]
    push_a[...] = jnp.zeros_like(push_a)
    push_b[...] = jnp.zeros_like(push_b)

    if first_sweep:
        props = [own[8:16, h * LANES : (h + 1) * LANES] for h in range(blocks)] + ghost_blocks(8)

        def props_of(t):
            ia = jnp.broadcast_to(index[pl.ds(t, 1), :], (8, LANES))
            ib = jnp.broadcast_to(index[pl.ds(slots + t, 1), :], (8, LANES))
            at = pl.ds(8 * t, 8) if isinstance(t, int) else pl.ds(pl.multiple_of(8 * t, 8), 8)
            all_a[at, :] = pick(props[:blocks], ia)
            all_b[at, :] = pick(props, ib)

        for t in range(GROUP * NCOLOR):
            props_of(t)
        spare = GROUP * NCOLOR
        all_a[8 * spare :, :] = jnp.ones((8 * (slots - spare), LANES), F32)
        all_b[8 * spare :, :] = jnp.ones((8 * (slots - spare), LANES), F32)
        gathered[...] = (g0[...] + g1[0 : g0.shape[0], :]) + (g2[...] + g3[...])
        placed[...] = jnp.ones_like(placed)
        fetch.wait()

        def more_props(g, c):
            for j in range(GROUP):
                props_of(GROUP * g + j)
            return c

        lax.fori_loop(NCOLOR, NCOLOR + scalars[OVER_TO + NCOLOR - 1], more_props, 0)
        rows = g0.shape[0] // 10
        for t in range(tiles):
            slot = scalars[TILE_SLOT + t]
            at = 8 * (t % 2) + t // 2
            for c in range(10):
                row = c * rows + at
                placed[pl.ds(c * slots + slot, 1), :] = gathered[row : row + 1, :]
        first = [all_a[pl.ds(c, slots, stride=8), :] for c in range(4)]
        second = [all_b[pl.ds(c, slots, stride=8), :] for c in range(4)]
        geo = [placed[c * slots : (c + 1) * slots, :] for c in range(10)]
        for c, value in enumerate(contact_state(geo, first, second)):
            state[c * slots : (c + 1) * slots, :] = value
        impulse[...] = jnp.zeros_like(impulse)
    else:
        impulse[...] = impulse_in[...]

    def group(base, now, before):
        def held(c):
            return state[pl.ds(c * slots + base, GROUP), :]

        for j in range(GROUP):
            ia = jnp.broadcast_to(index[pl.ds(base + j, 1), :], (8, LANES))
            ib = jnp.broadcast_to(index[pl.ds(slots + base + j, 1), :], (8, LANES))
            got_a[8 * j : 8 * j + 8, :] = pick(now[:blocks], ia)
            got_b[8 * j : 8 * j + 8, :] = pick(now, ib)
        tile_rows = [pl.ds(c, GROUP, stride=8) for c in range(6)]
        va = [got_a[tile_rows[c], :] for c in range(6)]
        vb = [got_b[tile_rows[c], :] for c in range(6)]
        arm_a = [held(20 + c) for c in range(3)]
        arm_b = [held(23 + c) for c in range(3)]
        turn_a = cross(va[3:6], arm_a)
        turn_b = cross(vb[3:6], arm_b)
        rel = [((va[c] + turn_a[c]) - vb[c]) - turn_b[c] for c in range(3)]
        old = [impulse[pl.ds(c * slots + base, GROUP), :] for c in range(3)]
        trial = [
            old[c] - (dot3([held(3 * c + j) for j in range(3)], rel) + held(9 + c))
            for c in range(3)
        ]
        normal_part = jnp.maximum(trial[0], 0.0)
        slide = trial[1] * trial[1] + trial[2] * trial[2]
        shrink = lax.rsqrt(jnp.maximum(slide, tangent_floor * tangent_floor))
        factor = jnp.minimum(1.0, friction * normal_part * shrink)
        active = used[pl.ds(base, GROUP), :] > 0.5
        new = [
            jnp.where(active, normal_part, old[0]),
            jnp.where(active, trial[1] * factor, old[1]),
            jnp.where(active, trial[2] * factor, old[2]),
        ]
        change = [new[c] - old[c] for c in range(3)]
        for c in range(3):
            impulse[pl.ds(c * slots + base, GROUP), :] = new[c]
        force = [
            held(12) * change[0] + held(17) * change[2],
            held(13) * change[0] + held(15) * change[1] + held(18) * change[2],
            held(14) * change[0] + held(16) * change[1] + held(19) * change[2],
        ]
        spin_a = cross(arm_a, force)
        spin_b = cross(arm_b, force)
        for c in range(3):
            push_a[tile_rows[c], :] = held(26) * force[c]
            push_a[tile_rows[3 + c], :] = held(27 + c) * spin_a[c]
            push_b[tile_rows[c], :] = -(held(30) * force[c])
            push_b[tile_rows[3 + c], :] = -(held(31 + c) * spin_b[c])
        if before is not None:
            before()
        left, right = [], []
        empty = jnp.zeros((16 * (total - blocks), LANES), BF16)
        for j in range(GROUP):
            t = scalars[base + j]
            first = two_parts(push_a[8 * j : 8 * j + 8, :])
            second = two_parts(push_b[8 * j : 8 * j + 8, :])
            rows = [masks[t, 16 * m : 16 * m + 16, :] for m in range(blocks + total)]
            left.append(jnp.concatenate([first * m for m in rows[:blocks]] + [empty], axis=0))
            left.append(jnp.concatenate([second * m for m in rows[blocks:]], axis=0))
            right.append(hot[:, pl.ds(pl.multiple_of(2 * TILE * t, 2 * TILE), 2 * TILE)])
        return contract_lanes(jnp.concatenate(left, axis=1), jnp.concatenate(right, axis=1))

    def color_pass(k, before=None):
        now = [table[8 * h : 8 * h + 8, :] for h in range(total)]
        acc[...] = group(pl.multiple_of(GROUP * k, GROUP), now, before)

        def more(g, c):
            acc[...] += group(pl.multiple_of(GROUP * (NCOLOR + g), GROUP), now, None)
            return c

        lax.fori_loop(scalars[OVER_FROM + k], scalars[OVER_TO + k], more, 0)
        for h in range(total):
            table[8 * h : 8 * h + 8, :] = now[h] + sum_parts(acc, h)

    def later_pass(k, carry):
        color_pass(k)
        return carry

    color_pass(0, None if first_sweep else fetch.wait)
    lax.fori_loop(1, NCOLOR, later_pass, 0)
    for h in range(blocks):
        own_change[:, h * LANES : (h + 1) * LANES] = table[8 * h : 8 * h + 8, :] - start[h]
    ghost0[...] = table[8 * blocks : 8 * blocks + 8, :] - start[blocks]
    ghost1[...] = table[8 * blocks + 8 : 8 * blocks + 16, :] - start[blocks + 1]


def impulse_kernel(scalars, held, impulse):
    slots = held.shape[0] // 3
    for t in range(impulse.shape[2] // TILE):
        slot = scalars[TILE_SLOT + t]
        for c in range(3):
            impulse[c, :, t * TILE : (t + 1) * TILE] = held[pl.ds(c * slots + slot, 1), :]


def merge_kernel(
    interface, last_sweep, own, change, c0, c1, c2, c3, mult, export_index, export_hot,
    export_masks, *refs,
):
    blocks = own.shape[1] // LANES
    came = [halves(c0[...], c1[...], interface), halves(c2[...], c3[...], interface)]
    left = jnp.concatenate(
        [
            jnp.concatenate([two_parts(came[i])] * blocks, axis=0) * export_masks[i]
            for i in range(2)
        ],
        axis=1,
    )
    incoming = contract_lanes(left, export_hot[...])
    fresh = []
    for h in range(blocks):
        span = slice(h * LANES, (h + 1) * LANES)
        fresh.append(
            own[0:8, span] + (change[:, span] + sum_parts(incoming, h)) / mult[:, span]
        )
    if last_sweep:
        (velocity,) = refs
        for r in range(6):
            for h in range(blocks):
                velocity[r, :, h * LANES : (h + 1) * LANES] = fresh[h][r : r + 1, :]
    else:
        fresh_own, out0, out1 = refs
        for h in range(blocks):
            fresh_own[:, h * LANES : (h + 1) * LANES] = fresh[h]
        out0[...] = pick(fresh, export_index[0:8, :])
        out1[...] = pick(fresh, export_index[8:16, :])


def in_hbm(array):
    return pltpu.with_memory_space_constraint(array, pltpu.HBM)


def shape(dims, dtype=F32):
    return jax.ShapeDtypeStruct(dims, dtype)


def make(subs, layers):
    matchings = neighbour_matchings(subs, layers)
    shuffles = [relay_shuffle(subs, layers, k) for k in range(WIN)]

    def trade(low, high):
        return [
            lax.ppermute(low if m < 2 else high, AXES, matchings[m]) for m in range(4)
        ]

    def on_device(geometry, dest_slot, pairs, colors, free_vel, inertia, exports):
        count = geometry.shape[2]
        bodies = free_vel.shape[2]
        interface = exports.shape[2]
        tiles = count // TILE
        slots = 16
        assert count % TILE == 0 and tiles < slots and 2 * interface == LANES
        assert bodies % LANES == 0
        blocks = bodies // LANES
        total = blocks + 2
        place = shape((10 * slots, LANES))
        small = shape((16, LANES))
        prepared = pl.pallas_call(
            prepare_kernel,
            out_shape=(
                shape((10 * slots + 16, LANES)), place, place, small, small,
                shape((16, bodies)),
                shape((16, LANES), jnp.int32),
                shape((WIDE, count), BF16),
                shape((16, count), BF16),
                shape((2, 80, count), BF16),
            ),
            in_specs=[pl.BlockSpec(memory_space=pltpu.HBM)] * 5,
            out_specs=(VMEM_SPEC,) * 10,
            scratch_shapes=[
                pltpu.VMEM(geometry.shape, F32),
                pltpu.VMEM(dest_slot.shape, jnp.int32),
                pltpu.VMEM(free_vel.shape, F32),
                pltpu.VMEM(inertia.shape, F32),
                pltpu.VMEM(exports.shape, jnp.int32),
                pltpu.VMEM((8, LANES), jnp.int32),
                pltpu.VMEM((16, count), F32),
                pltpu.VMEM((16 * (WIN - 1), count), BF16),
                pltpu.VMEM((2, 80 * (WIN - 1), count), BF16),
                pltpu.SemaphoreType.DMA((5,)),
            ],
            compiler_params=PARAMS,
            name="prepare",
        )(*[in_hbm(x) for x in (geometry, dest_slot, free_vel, inertia, exports)])
        send0, place2, place3, out0, out1, own, export_index, wide_hot, own_mask, tall = prepared
        came = [lax.ppermute(send0, AXES, matchings[0])]
        came.append(lax.ppermute(out0, AXES, matchings[1]))
        came.append(lax.ppermute(out1, AXES, matchings[2]))
        came.append(lax.ppermute(out1, AXES, matchings[3]))
        place0 = pl.pallas_call(
            place_kernel,
            out_shape=place,
            in_specs=[VMEM_SPEC] * 3,
            out_specs=VMEM_SPEC,
            compiler_params=PARAMS,
            name="place",
        )(tall, own_mask, wide_hot)
        placed = [place0]
        placed.append(lax.ppermute(place2, AXES, shuffles[2]))
        placed.append(lax.ppermute(place3, AXES, shuffles[3]))

        def indexing(*refs):
            index_kernel(subs, layers, interface, bodies, *refs)

        rows = slot_count(tiles)
        assert rows <= TILE_SLOT
        index, used, hot, masks, export_hot, export_masks, mult, scalars = pl.pallas_call(
            indexing,
            out_shape=(
                shape((2 * rows, LANES), jnp.int32),
                shape((rows, LANES)),
                shape((LANES, 2 * TILE * (tiles + 1)), BF16),
                shape((tiles + 1, 16 * (blocks + total), LANES), BF16),
                shape((LANES, 2 * LANES), BF16),
                shape((2, 16 * blocks, LANES), BF16),
                shape((8, bodies)),
                shape((64,), jnp.int32),
            ),
            in_specs=[VMEM_SPEC, SMEM_SPEC, VMEM_SPEC],
            out_specs=(VMEM_SPEC,) * 7 + (SMEM_SPEC,),
            compiler_params=PARAMS,
            name="indexing",
        )(pairs, colors, export_index)

        state = impulse = None
        for sweep in range(SWEEPS):
            first, last = sweep == 0, sweep == SWEEPS - 1

            def run(*refs, first=first):
                sweep_kernel(bodies, interface, first, *refs)

            outs = [
                shape((3 * rows, LANES)),
                shape((8, bodies)),
                shape((8, LANES)),
                shape((8, LANES)),
            ]
            operands = [scalars, index, used, hot, masks, own, *came]
            if first:
                outs = [shape((STATE * rows, LANES))] + outs
                operands += placed
            else:
                operands += [state, impulse]
            result = pl.pallas_call(
                run,
                out_shape=tuple(outs),
                in_specs=[VMEM_SPEC] * len(operands),
                out_specs=(VMEM_SPEC,) * len(outs),
                scratch_shapes=[
                    pltpu.VMEM((8 * GROUP, LANES), F32),
                    pltpu.VMEM((8 * GROUP, LANES), F32),
                    pltpu.VMEM((8 * GROUP, LANES), F32),
                    pltpu.VMEM((8 * GROUP, LANES), F32),
                    pltpu.VMEM((16 * total, LANES), F32),
                    pltpu.VMEM((8 * total, LANES), F32),
                    pltpu.VMEM((8 * rows, LANES), F32),
                    pltpu.VMEM((8 * rows, LANES), F32),
                    pltpu.VMEM((10 * slots, LANES), F32),
                    pltpu.VMEM((10 * rows, LANES), F32),
                    pltpu.SMEM((64,), jnp.int32),
                    pltpu.SemaphoreType.DMA,
                ],
                compiler_params=PARAMS,
                name="sweep",
            )(*operands)
            if first:
                state, result = result[0], result[1:]
            impulse, change, ghost0, ghost1 = result
            sums = trade(ghost0, ghost1)

            def merge(*refs, last=last):
                merge_kernel(interface, last, *refs)

            operands = [own, change, *sums, mult, export_index, export_hot, export_masks]
            if last:
                outs = (shape((6, 1, bodies)),)
            else:
                outs = (shape((8, bodies)), shape((8, LANES)), shape((8, LANES)))
            merged = pl.pallas_call(
                merge,
                out_shape=outs,
                in_specs=[VMEM_SPEC] * len(operands),
                out_specs=(VMEM_SPEC,) * len(outs),
                compiler_params=PARAMS,
                name="merge",
            )(*operands)
            if last:
                in_order = pl.pallas_call(
                    impulse_kernel,
                    out_shape=shape((3, 1, count)),
                    in_specs=[SMEM_SPEC, VMEM_SPEC],
                    out_specs=VMEM_SPEC,
                    compiler_params=PARAMS,
                    name="impulse",
                )(scalars, impulse)
                return in_order, merged[0]
            own = merged[0]
            came = trade(merged[1], merged[2])

    return on_device


def solution(mesh):
    placed = (
        P(None, "layer", "sub"),
        P("layer", "sub"),
        P(None, "layer", "sub"),
        P("layer", "sub"),
        P(None, "layer", "sub"),
        P(None, "layer", "sub"),
        P(None, "layer", "sub"),
    )
    return jax.shard_map(
        make(mesh.shape["sub"], mesh.shape["layer"]),
        mesh=mesh,
        in_specs=placed,
        out_specs=(P(None, "layer", "sub"), P(None, "layer", "sub")),
        check_vma=False,
    )
```

```python
import jax
import jax.numpy as jnp
from jax import lax
from jax.experimental import pallas as pl
from jax.experimental.pallas import tpu as pltpu
from jax.sharding import PartitionSpec as P

WIN = 4
SWEEPS = 3
NCOLOR = 4
TILE = 128
LANES = 128
WIDE = 256
GROUP = 4

relaxation = 0.7
friction = 0.6
tangent_floor = 0.1

AXES = ("sub", "layer")
F32 = jnp.float32
BF16 = jnp.bfloat16
VMEM_SPEC = pl.BlockSpec(memory_space=pltpu.VMEM)
SMEM_SPEC = pl.BlockSpec(memory_space=pltpu.SMEM)
PARAMS = pltpu.CompilerParams(vmem_limit_bytes=16 << 20)


def neighbour_matchings(subs, layers):
    assert subs % 2 == 0 and layers % 2 == 0

    def shifted(i):
        return i - 1 if i % 2 == 0 else i + 1

    def partner(match, s, y):
        if match == 0:
            return s ^ 1, y
        if match == 1:
            return (s, y ^ 1) if s in (0, subs - 1) else (shifted(s), y)
        if match == 2:
            return s, y ^ 1
        return (s ^ 1, y) if y in (0, layers - 1) else (s, shifted(y))

    out = []
    for match in range(4):
        pairs = []
        for s in range(subs):
            for y in range(layers):
                ps, py = partner(match, s, y)
                pairs.append((s * layers + y, ps * layers + py))
        out.append(pairs)
    return out


def relay_shuffle(subs, layers, k):
    return [
        (s * layers + y, (s ^ k) * layers + y) for s in range(subs) for y in range(layers)
    ]


def lane_iota():
    return lax.broadcasted_iota(jnp.int32, (8, LANES), 1)


def pick(tables, index):
    low = jnp.bitwise_and(index, LANES - 1)
    high = jnp.right_shift(index, 7)
    out = jnp.take_along_axis(tables[0], low, axis=1)
    for h in range(1, len(tables)):
        out = jnp.where(high == h, jnp.take_along_axis(tables[h], low, axis=1), out)
    return out


def two_parts(value):
    first = value.astype(BF16).astype(F32)
    return jnp.concatenate([first, value - first], axis=0).astype(BF16)


def equal_rows(row, count):
    shape = (count, row.shape[1])
    ids = lax.broadcasted_iota(jnp.int32, shape, 0).astype(F32).astype(BF16)
    here = jnp.broadcast_to(row.astype(F32), shape).astype(BF16)
    return jnp.where(ids == here, jnp.ones(shape, BF16), jnp.zeros(shape, BF16))


def high_masks(index_row, highs):
    shape = (16, LANES)
    high = jnp.broadcast_to(jnp.right_shift(index_row, 7).astype(F32), shape).astype(BF16)
    one, zero = jnp.ones(shape, BF16), jnp.zeros(shape, BF16)
    return jnp.concatenate(
        [jnp.where(high == jnp.full(shape, h, BF16), one, zero) for h in range(highs)], axis=0
    )


def low_onehot(index_row):
    return equal_rows(jnp.bitwise_and(index_row, LANES - 1), LANES)


def contract_lanes(lhs, rhs):
    return lax.dot_general(
        lhs, rhs, (((1,), (1,)), ((), ())), preferred_element_type=F32
    )


def sum_parts(block, h):
    return block[16 * h : 16 * h + 8] + block[16 * h + 8 : 16 * h + 16]


def cross(u, v):
    return [
        u[1] * v[2] - u[2] * v[1],
        u[2] * v[0] - u[0] * v[2],
        u[0] * v[1] - u[1] * v[0],
    ]


def dot3(u, v):
    return u[0] * v[0] + u[1] * v[1] + u[2] * v[2]


def halves(low, high, half):
    return jnp.where(lane_iota() < half, low, high)


def parities():
    sub = lax.axis_index("sub")
    layer = lax.axis_index("layer")
    return sub, layer, lax.rem(sub, 2) == 0, lax.rem(layer, 2) == 0


def prepare_kernel(
    geo_hbm, dest_hbm, vel_hbm, inertia_hbm, exports_hbm, pairs_hbm, colors_hbm,
    send0, place2, place3, out0, out1, start_own, export_index, hot, own_mask, tall,
    ordered, index_out, used, scalars_out,
    geo, dest, vel, inertia, exports, pairs, colors, scalars, listed, dense, mask, lhs, sems,
):
    copies = [
        pltpu.make_async_copy(src, dst, sems.at[i])
        for i, (src, dst) in enumerate(
            [
                (exports_hbm, exports),
                (vel_hbm, vel),
                (inertia_hbm, inertia),
                (dest_hbm, dest),
                (colors_hbm, colors),
                (pairs_hbm, pairs),
                (geo_hbm, geo),
            ]
        )
    ]
    for copy in copies:
        copy.start()
    count = geo.shape[2]
    tiles = count // TILE
    slots = place2.shape[0] // 10
    bodies = vel.shape[2]
    interface = exports.shape[2]
    sub, layer, sub_even, layer_even = parities()
    member = lax.rem(sub, WIN)
    start_own[...] = jnp.zeros_like(start_own)
    dense[...] = jnp.zeros_like(dense)
    for copy in copies[:6]:
        copy.wait()
    for r in range(6):
        start_own[r : r + 1, :] = vel[r]
    for r in range(4):
        start_own[8 + r : 9 + r, :] = inertia[r]
    listed[0:1, 0:interface] = exports[0]
    listed[0:1, interface : 2 * interface] = exports[1]
    listed[1:2, 0:interface] = exports[1]
    listed[1:2, interface : 2 * interface] = exports[0]
    listed[2:3, 0:interface] = exports[2]
    listed[2:3, interface : 2 * interface] = exports[3]
    listed[3:4, 0:interface] = exports[3]
    listed[3:4, interface : 2 * interface] = exports[2]
    row0 = jnp.where(sub_even, listed[1:2, :], listed[0:1, :])
    row1 = jnp.where(layer_even, listed[3:4, :], listed[2:3, :])
    idx0 = jnp.broadcast_to(row0, (8, LANES))
    idx1 = jnp.broadcast_to(row1, (8, LANES))
    export_index[0:8, :] = idx0
    export_index[8:16, :] = idx1
    blocks = bodies // LANES
    for base in (0, 8):
        tables = [
            start_own[base : base + 8, h * LANES : (h + 1) * LANES] for h in range(blocks)
        ]
        picked = pick(tables, idx0)
        out0[base : base + 8, :] = picked
        send0[10 * slots + base : 10 * slots + base + 8, :] = picked
        out1[base : base + 8, :] = pick(tables, idx1)
    rank = used.shape[0]
    for i in range(rank):
        scalars[i] = tiles
    place = [jnp.int32(0)] * tiles
    over = jnp.int32(0)
    for k in range(NCOLOR):
        filled = jnp.int32(0)
        base = (NCOLOR + over) * GROUP - GROUP
        for t in range(tiles):
            hit = colors[0, t] == k
            at = jnp.where(filled < GROUP, GROUP * k, base) + filled
            place[t] = jnp.where(hit, at, place[t])
            scalars[jnp.where(hit, at, UNUSED)] = t
            filled = filled + jnp.where(hit, 1, 0)
        scalars[OVER_FROM + k] = over
        over = over + lax.div(jnp.maximum(filled - 1, GROUP - 1), GROUP)
        scalars[OVER_TO + k] = over
    index_out[...] = jnp.zeros_like(index_out)
    used[...] = jnp.zeros_like(used)
    flip_sub = jnp.where(sub_even, interface, 0)
    flip_layer = jnp.where(layer_even, interface, 0)
    for t in range(tiles):
        span = slice(t * TILE, (t + 1) * TILE)
        nearer = pairs[0, :, span]
        other = pairs[1, :, span]
        ghost = other - bodies
        turned = jnp.where(
            ghost < 2 * interface,
            jnp.bitwise_xor(ghost, flip_sub),
            jnp.bitwise_xor(ghost, flip_layer),
        )
        farther = jnp.where(ghost < 0, other, bodies + turned)
        scalars[TILE_SLOT + t] = place[t]
        ordered[t : t + 1, :] = nearer
        ordered[16 + t : 17 + t, :] = farther
        index_out[pl.ds(place[t], 1), :] = nearer
        index_out[pl.ds(rank + place[t], 1), :] = farther
        used[pl.ds(place[t], 1), :] = jnp.ones((1, LANES), F32)
    slot = dest[...] - (sub - member) * count
    target = jnp.zeros_like(slot)
    for m in range(1, WIN):
        target = target + jnp.where(slot >= m * count, 1, 0)
    within = slot - target * count
    row_id = jnp.bitwise_xor(target, member) * 8 + jnp.right_shift(within, 8)
    low = jnp.bitwise_and(within, WIDE - 1)
    paired = (16, TILE)
    ids = lax.broadcasted_iota(jnp.int32, paired, 0)
    ids = jnp.bitwise_and(ids, 7).astype(F32)
    one, zero = jnp.ones(paired, BF16), jnp.zeros(paired, BF16)
    for t in range(tiles):
        span = slice(t * TILE, (t + 1) * TILE)
        hot[:, span] = equal_rows(low[:, span], WIDE)
        here = jnp.broadcast_to(row_id[:, span].astype(F32), paired).astype(BF16)
        for k in range(WIN):
            chosen = jnp.where(here == (ids + 8.0 * k).astype(BF16), one, zero)
            if k == 0:
                own_mask[:, span] = chosen
            else:
                mask[16 * k - 16 : 16 * k, span] = chosen
    give = pltpu.make_async_copy(scalars, scalars_out, sems.at[7])
    give.start()
    copies[6].wait()
    for r in range(10):
        dense[r : r + 1, :] = geo[r]
    value = dense[...]
    first = value.astype(BF16).astype(F32)
    parts = [first, value - first]
    for p in range(2):
        for i in range(5):
            pair = jnp.concatenate(
                [jnp.broadcast_to(parts[p][r : r + 1, :], (8, count)) for r in (2 * i, 2 * i + 1)],
                axis=0,
            ).astype(BF16)
            tall[p, 16 * i : 16 * i + 16, :] = pair
            for k in range(1, WIN):
                at = 80 * (k - 1) + 16 * i
                lhs[p, at : at + 16, :] = mask[16 * k - 16 : 16 * k, :] * pair
    total = contract_lanes(lhs[0], hot[...]) + contract_lanes(lhs[1], hot[...])
    for k, out in enumerate((send0, place2, place3)):
        store_placed(out, total[80 * k : 80 * k + 80, :])
    give.wait()


def store_placed(out, total):
    for r in range(10):
        for side in range(2):
            out[16 * r + 8 * side : 16 * r + 8 * side + 8, :] = total[
                8 * r : 8 * r + 8, side * LANES : (side + 1) * LANES
            ]


def place_kernel(tall, own_mask, hot, out):
    left = [jnp.concatenate([own_mask[...]] * 5, axis=0) * tall[p] for p in range(2)]
    store_placed(out, contract_lanes(left[0], hot[...]) + contract_lanes(left[1], hot[...]))


TILE_SLOT, OVER_FROM, OVER_TO, UNUSED = 32, 48, 56, 63


def overflow_groups(tiles):
    most = 0
    for busy in range(1, NCOLOR + 1):
        spare = tiles - busy * (GROUP + 1)
        if spare >= 0:
            most = max(most, busy + spare // GROUP)
    return most


def slot_count(tiles):
    return -(-GROUP * (NCOLOR + overflow_groups(tiles)) // 8) * 8


def index_kernel(
    subs, layers, interface, bodies, ordered, export_index,
    hot, masks, export_hot, export_masks, mult,
):
    tiles = masks.shape[0] - 1
    blocks = bodies // LANES
    total = blocks + 4 * interface // LANES
    sub, layer, sub_even, layer_even = parities()
    for t in range(tiles):
        first = ordered[t : t + 1, :]
        second = ordered[16 + t : 17 + t, :]
        hot[:, 2 * t * TILE : (2 * t + 1) * TILE] = low_onehot(first)
        hot[:, (2 * t + 1) * TILE : (2 * t + 2) * TILE] = low_onehot(second)
        masks[t, : 16 * blocks, :] = high_masks(first, blocks)
        masks[t, 16 * blocks :, :] = high_masks(second, total)
    hot[:, 2 * tiles * TILE :] = jnp.zeros((LANES, 2 * TILE), BF16)
    masks[tiles] = jnp.zeros_like(masks[tiles])
    inner_sub = jnp.where(jnp.logical_and(sub > 0, sub < subs - 1), 1.0, 0.0)
    inner_layer = jnp.where(jnp.logical_and(layer > 0, layer < layers - 1), 1.0, 0.0)
    lane = lane_iota()
    weights = [
        jnp.where(lane < interface, 1.0, inner_sub),
        jnp.where(lane < interface, 1.0, inner_layer),
    ]
    left = []
    for i in range(2):
        row = export_index[8 * i : 8 * i + 1, :]
        export_hot[:, i * LANES : (i + 1) * LANES] = low_onehot(row)
        chosen = high_masks(row, blocks)
        export_masks[i] = chosen
        weight = jnp.concatenate([weights[i], jnp.zeros_like(weights[i])], axis=0).astype(BF16)
        left.append(jnp.concatenate([weight] * blocks, axis=0) * chosen)
    listed = contract_lanes(jnp.concatenate(left, axis=1), export_hot[...])
    for h in range(blocks):
        mult[:, h * LANES : (h + 1) * LANES] = 1.0 + listed[16 * h : 16 * h + 8]


STATE = 34


def contact_state(geo, first, second):
    raw = geo[0:3]
    length = jnp.sqrt(dot3(raw, raw))
    normal = [x / length for x in raw]
    side = jnp.sqrt(normal[1] * normal[1] + normal[2] * normal[2])
    tan_y = normal[2] / side
    tan_z = -normal[1] / side
    two = [
        normal[1] * tan_z - normal[2] * tan_y,
        -normal[0] * tan_z,
        normal[0] * tan_y,
    ]

    def arm(p, spin):
        return [
            spin[1] * p[2] * p[2] + spin[2] * p[1] * p[1],
            spin[0] * p[2] * p[2] + spin[2] * p[0] * p[0],
            spin[0] * p[1] * p[1] + spin[1] * p[0] * p[0],
            -spin[2] * p[0] * p[1],
            -spin[1] * p[0] * p[2],
            -spin[0] * p[1] * p[2],
        ]

    arm_a, arm_b = geo[3:6], geo[6:9]
    e = [x + y for x, y in zip(arm(arm_a, first[1:4]), arm(arm_b, second[1:4]))]
    mass = first[0] + second[0]
    xx, yy, zz = mass + e[0], mass + e[1], mass + e[2]
    xy, xz, yz = e[3], e[4], e[5]
    c_xx = yy * zz - yz * yz
    c_xy = xz * yz - xy * zz
    c_xz = xy * yz - xz * yy
    c_yy = xx * zz - xz * xz
    c_yz = xy * xz - xx * yz
    c_zz = xx * yy - xy * xy
    det = xx * c_xx + xy * c_xy + xz * c_xz
    inv = [
        [c_xx / det, c_xy / det, c_xz / det],
        [c_xy / det, c_yy / det, c_yz / det],
        [c_xz / det, c_yz / det, c_zz / det],
    ]
    solve = []
    for row in (normal, None, two):
        for j in range(3):
            if row is None:
                value = tan_y * inv[1][j] + tan_z * inv[2][j]
            else:
                value = row[0] * inv[0][j] + row[1] * inv[1][j] + row[2] * inv[2][j]
            solve.append(relaxation * value)
    bias = [geo[9] * dot3(solve[3 * i : 3 * i + 3], normal) for i in range(3)]
    return (
        solve + bias + normal + [tan_y, tan_z] + two + arm_a + arm_b + list(first) + list(second)
    )


def sweep_kernel(bodies, interface, first_sweep, *refs):
    scalars_in, index, used, hot, masks = refs[:5]
    refs = refs[5:]
    if first_sweep:
        own, g1, r1, r2, r3, g0, g2, g3, state = refs[:9]
        refs = refs[9:]
        r0 = g1.at[pl.ds(g0.shape[0], 16), :]
    else:
        own, r0, r1, r2, r3, state, impulse_in = refs[:7]
        refs = refs[7:]
    impulse, own_change, ghost0, ghost1 = refs[:4]
    got_a, got_b, push_a, push_b, acc, table, all_a, all_b, gathered, placed, scalars, sem = refs[4:]
    slots = used.shape[0]
    tiles = masks.shape[0] - 1
    blocks = bodies // LANES
    total = blocks + (4 * interface) // LANES
    fetch = pltpu.make_async_copy(scalars_in, scalars, sem)
    fetch.start()

    def ghost_blocks(base):
        return [
            halves(r0[base : base + 8, :], r1[base : base + 8, :], interface),
            halves(r2[base : base + 8, :], r3[base : base + 8, :], interface),
        ]

    start = [own[0:8, h * LANES : (h + 1) * LANES] for h in range(blocks)] + ghost_blocks(0)
    for h in range(total):
        table[8 * h : 8 * h + 8, :] = start[h]
    push_a[...] = jnp.zeros_like(push_a)
    push_b[...] = jnp.zeros_like(push_b)

    if first_sweep:
        props = [own[8:16, h * LANES : (h + 1) * LANES] for h in range(blocks)] + ghost_blocks(8)
        for t in range(slots):
            ia = jnp.broadcast_to(index[t : t + 1, :], (8, LANES))
            ib = jnp.broadcast_to(index[slots + t : slots + t + 1, :], (8, LANES))
            all_a[8 * t : 8 * t + 8, :] = pick(props[:blocks], ia)
            all_b[8 * t : 8 * t + 8, :] = pick(props, ib)
        gathered[...] = (g0[...] + g1[0 : g0.shape[0], :]) + (g2[...] + g3[...])
        placed[...] = jnp.ones_like(placed)
        fetch.wait()
        rows = g0.shape[0] // 10
        for t in range(tiles):
            slot = scalars[TILE_SLOT + t]
            at = 8 * (t % 2) + t // 2
            for c in range(10):
                row = c * rows + at
                placed[pl.ds(c * slots + slot, 1), :] = gathered[row : row + 1, :]
        first = [all_a[pl.ds(c, slots, stride=8), :] for c in range(4)]
        second = [all_b[pl.ds(c, slots, stride=8), :] for c in range(4)]
        geo = [placed[c * slots : (c + 1) * slots, :] for c in range(10)]
        for c, value in enumerate(contact_state(geo, first, second)):
            state[c * slots : (c + 1) * slots, :] = value
        impulse[...] = jnp.zeros_like(impulse)
    else:
        impulse[...] = impulse_in[...]

    def group(base, now, before):
        def held(c):
            return state[pl.ds(c * slots + base, GROUP), :]

        for j in range(GROUP):
            ia = jnp.broadcast_to(index[pl.ds(base + j, 1), :], (8, LANES))
            ib = jnp.broadcast_to(index[pl.ds(slots + base + j, 1), :], (8, LANES))
            got_a[8 * j : 8 * j + 8, :] = pick(now[:blocks], ia)
            got_b[8 * j : 8 * j + 8, :] = pick(now, ib)
        tile_rows = [pl.ds(c, GROUP, stride=8) for c in range(6)]
        va = [got_a[tile_rows[c], :] for c in range(6)]
        vb = [got_b[tile_rows[c], :] for c in range(6)]
        arm_a = [held(20 + c) for c in range(3)]
        arm_b = [held(23 + c) for c in range(3)]
        turn_a = cross(va[3:6], arm_a)
        turn_b = cross(vb[3:6], arm_b)
        rel = [((va[c] + turn_a[c]) - vb[c]) - turn_b[c] for c in range(3)]
        old = [impulse[pl.ds(c * slots + base, GROUP), :] for c in range(3)]
        trial = [
            old[c] - (dot3([held(3 * c + j) for j in range(3)], rel) + held(9 + c))
            for c in range(3)
        ]
        normal_part = jnp.maximum(trial[0], 0.0)
        slide = trial[1] * trial[1] + trial[2] * trial[2]
        shrink = lax.rsqrt(jnp.maximum(slide, tangent_floor * tangent_floor))
        factor = jnp.minimum(1.0, friction * normal_part * shrink)
        active = used[pl.ds(base, GROUP), :] > 0.5
        new = [
            jnp.where(active, normal_part, old[0]),
            jnp.where(active, trial[1] * factor, old[1]),
            jnp.where(active, trial[2] * factor, old[2]),
        ]
        change = [new[c] - old[c] for c in range(3)]
        for c in range(3):
            impulse[pl.ds(c * slots + base, GROUP), :] = new[c]
        force = [
            held(12) * change[0] + held(17) * change[2],
            held(13) * change[0] + held(15) * change[1] + held(18) * change[2],
            held(14) * change[0] + held(16) * change[1] + held(19) * change[2],
        ]
        spin_a = cross(arm_a, force)
        spin_b = cross(arm_b, force)
        for c in range(3):
            push_a[tile_rows[c], :] = held(26) * force[c]
            push_a[tile_rows[3 + c], :] = held(27 + c) * spin_a[c]
            push_b[tile_rows[c], :] = -(held(30) * force[c])
            push_b[tile_rows[3 + c], :] = -(held(31 + c) * spin_b[c])
        if before is not None:
            before()
        left, right = [], []
        empty = jnp.zeros((16 * (total - blocks), LANES), BF16)
        for j in range(GROUP):
            t = scalars[base + j]
            first = two_parts(push_a[8 * j : 8 * j + 8, :])
            second = two_parts(push_b[8 * j : 8 * j + 8, :])
            rows = [masks[t, 16 * m : 16 * m + 16, :] for m in range(blocks + total)]
            left.append(jnp.concatenate([first * m for m in rows[:blocks]] + [empty], axis=0))
            left.append(jnp.concatenate([second * m for m in rows[blocks:]], axis=0))
            right.append(hot[:, pl.ds(pl.multiple_of(2 * TILE * t, 2 * TILE), 2 * TILE)])
        return contract_lanes(jnp.concatenate(left, axis=1), jnp.concatenate(right, axis=1))

    def color_pass(k, before=None):
        now = [table[8 * h : 8 * h + 8, :] for h in range(total)]
        acc[...] = group(pl.multiple_of(GROUP * k, GROUP), now, before)

        def more(g, c):
            acc[...] += group(pl.multiple_of(GROUP * (NCOLOR + g), GROUP), now, None)
            return c

        lax.fori_loop(scalars[OVER_FROM + k], scalars[OVER_TO + k], more, 0)
        for h in range(total):
            table[8 * h : 8 * h + 8, :] = now[h] + sum_parts(acc, h)

    def later_pass(k, carry):
        color_pass(k)
        return carry

    color_pass(0, None if first_sweep else fetch.wait)
    lax.fori_loop(1, NCOLOR, later_pass, 0)
    for h in range(blocks):
        own_change[:, h * LANES : (h + 1) * LANES] = table[8 * h : 8 * h + 8, :] - start[h]
    ghost0[...] = table[8 * blocks : 8 * blocks + 8, :] - start[blocks]
    ghost1[...] = table[8 * blocks + 8 : 8 * blocks + 16, :] - start[blocks + 1]


def impulse_kernel(scalars, held, impulse):
    slots = held.shape[0] // 3
    for t in range(impulse.shape[2] // TILE):
        slot = scalars[TILE_SLOT + t]
        for c in range(3):
            impulse[c, :, t * TILE : (t + 1) * TILE] = held[pl.ds(c * slots + slot, 1), :]


def merge_kernel(
    interface, last_sweep, own, change, c0, c1, c2, c3, mult, export_index, export_hot,
    export_masks, *refs,
):
    blocks = own.shape[1] // LANES
    came = [halves(c0[...], c1[...], interface), halves(c2[...], c3[...], interface)]
    left = jnp.concatenate(
        [
            jnp.concatenate([two_parts(came[i])] * blocks, axis=0) * export_masks[i]
            for i in range(2)
        ],
        axis=1,
    )
    incoming = contract_lanes(left, export_hot[...])
    fresh = []
    for h in range(blocks):
        span = slice(h * LANES, (h + 1) * LANES)
        fresh.append(
            own[0:8, span] + (change[:, span] + sum_parts(incoming, h)) / mult[:, span]
        )
    if last_sweep:
        (velocity,) = refs
        for r in range(6):
            for h in range(blocks):
                velocity[r, :, h * LANES : (h + 1) * LANES] = fresh[h][r : r + 1, :]
    else:
        fresh_own, out0, out1 = refs
        for h in range(blocks):
            fresh_own[:, h * LANES : (h + 1) * LANES] = fresh[h]
        out0[...] = pick(fresh, export_index[0:8, :])
        out1[...] = pick(fresh, export_index[8:16, :])


def in_hbm(array):
    return pltpu.with_memory_space_constraint(array, pltpu.HBM)


def shape(dims, dtype=F32):
    return jax.ShapeDtypeStruct(dims, dtype)


def make(subs, layers):
    matchings = neighbour_matchings(subs, layers)
    shuffles = [relay_shuffle(subs, layers, k) for k in range(WIN)]

    def trade(low, high):
        return [
            lax.ppermute(low if m < 2 else high, AXES, matchings[m]) for m in range(4)
        ]

    def on_device(geometry, dest_slot, pairs, colors, free_vel, inertia, exports):
        count = geometry.shape[2]
        bodies = free_vel.shape[2]
        interface = exports.shape[2]
        tiles = count // TILE
        slots = 16
        assert count % TILE == 0 and tiles < slots and 2 * interface == LANES
        assert bodies % LANES == 0
        blocks = bodies // LANES
        total = blocks + 2
        place = shape((10 * slots, LANES))
        small = shape((16, LANES))
        arguments = (geometry, dest_slot, free_vel, inertia, exports, pairs, colors)
        rows = slot_count(tiles)
        assert rows <= TILE_SLOT
        prepared = pl.pallas_call(
            prepare_kernel,
            out_shape=(
                shape((10 * slots + 16, LANES)), place, place, small, small,
                shape((16, bodies)),
                shape((16, LANES), jnp.int32),
                shape((WIDE, count), BF16),
                shape((16, count), BF16),
                shape((2, 80, count), BF16),
                shape((32, LANES), jnp.int32),
                shape((2 * rows, LANES), jnp.int32),
                shape((rows, LANES)),
                shape((64,), jnp.int32),
            ),
            in_specs=[pl.BlockSpec(memory_space=pltpu.HBM)] * 7,
            out_specs=(VMEM_SPEC,) * 14,
            scratch_shapes=[
                pltpu.VMEM(geometry.shape, F32),
                pltpu.VMEM(dest_slot.shape, jnp.int32),
                pltpu.VMEM(free_vel.shape, F32),
                pltpu.VMEM(inertia.shape, F32),
                pltpu.VMEM(exports.shape, jnp.int32),
                pltpu.VMEM(pairs.shape, jnp.int32),
                pltpu.SMEM(colors.shape, jnp.int32),
                pltpu.SMEM((64,), jnp.int32),
                pltpu.VMEM((8, LANES), jnp.int32),
                pltpu.VMEM((16, count), F32),
                pltpu.VMEM((16 * (WIN - 1), count), BF16),
                pltpu.VMEM((2, 80 * (WIN - 1), count), BF16),
                pltpu.SemaphoreType.DMA((8,)),
            ],
            compiler_params=PARAMS,
            name="prepare",
        )(*[in_hbm(x) for x in arguments])
        send0, place2, place3, out0, out1, own, export_index = prepared[:7]
        wide_hot, own_mask, tall, ordered, index, used, scalars = prepared[7:]
        came = [lax.ppermute(send0, AXES, matchings[0])]
        came.append(lax.ppermute(out0, AXES, matchings[1]))
        came.append(lax.ppermute(out1, AXES, matchings[2]))
        came.append(lax.ppermute(out1, AXES, matchings[3]))
        place0 = pl.pallas_call(
            place_kernel,
            out_shape=place,
            in_specs=[VMEM_SPEC] * 3,
            out_specs=VMEM_SPEC,
            compiler_params=PARAMS,
            name="place",
        )(tall, own_mask, wide_hot)
        placed = [place0]
        placed.append(lax.ppermute(place2, AXES, shuffles[2]))
        placed.append(lax.ppermute(place3, AXES, shuffles[3]))

        def indexing(*refs):
            index_kernel(subs, layers, interface, bodies, *refs)

        hot, masks, export_hot, export_masks, mult = pl.pallas_call(
            indexing,
            out_shape=(
                shape((LANES, 2 * TILE * (tiles + 1)), BF16),
                shape((tiles + 1, 16 * (blocks + total), LANES), BF16),
                shape((LANES, 2 * LANES), BF16),
                shape((2, 16 * blocks, LANES), BF16),
                shape((8, bodies)),
            ),
            in_specs=[VMEM_SPEC] * 2,
            out_specs=(VMEM_SPEC,) * 5,
            compiler_params=PARAMS,
            name="indexing",
        )(ordered, export_index)

        state = impulse = None
        for sweep in range(SWEEPS):
            first, last = sweep == 0, sweep == SWEEPS - 1

            def run(*refs, first=first):
                sweep_kernel(bodies, interface, first, *refs)

            outs = [
                shape((3 * rows, LANES)),
                shape((8, bodies)),
                shape((8, LANES)),
                shape((8, LANES)),
            ]
            operands = [scalars, index, used, hot, masks, own, *came]
            if first:
                outs = [shape((STATE * rows, LANES))] + outs
                operands += placed
            else:
                operands += [state, impulse]
            result = pl.pallas_call(
                run,
                out_shape=tuple(outs),
                in_specs=[VMEM_SPEC] * len(operands),
                out_specs=(VMEM_SPEC,) * len(outs),
                scratch_shapes=[
                    pltpu.VMEM((8 * GROUP, LANES), F32),
                    pltpu.VMEM((8 * GROUP, LANES), F32),
                    pltpu.VMEM((8 * GROUP, LANES), F32),
                    pltpu.VMEM((8 * GROUP, LANES), F32),
                    pltpu.VMEM((16 * total, LANES), F32),
                    pltpu.VMEM((8 * total, LANES), F32),
                    pltpu.VMEM((8 * rows, LANES), F32),
                    pltpu.VMEM((8 * rows, LANES), F32),
                    pltpu.VMEM((10 * slots, LANES), F32),
                    pltpu.VMEM((10 * rows, LANES), F32),
                    pltpu.SMEM((64,), jnp.int32),
                    pltpu.SemaphoreType.DMA,
                ],
                compiler_params=PARAMS,
                name="sweep",
            )(*operands)
            if first:
                state, result = result[0], result[1:]
            impulse, change, ghost0, ghost1 = result
            sums = trade(ghost0, ghost1)

            def merge(*refs, last=last):
                merge_kernel(interface, last, *refs)

            operands = [own, change, *sums, mult, export_index, export_hot, export_masks]
            if last:
                outs = (shape((6, 1, bodies)),)
            else:
                outs = (shape((8, bodies)), shape((8, LANES)), shape((8, LANES)))
            merged = pl.pallas_call(
                merge,
                out_shape=outs,
                in_specs=[VMEM_SPEC] * len(operands),
                out_specs=(VMEM_SPEC,) * len(outs),
                compiler_params=PARAMS,
                name="merge",
            )(*operands)
            if last:
                in_order = pl.pallas_call(
                    impulse_kernel,
                    out_shape=shape((3, 1, count)),
                    in_specs=[SMEM_SPEC, VMEM_SPEC],
                    out_specs=VMEM_SPEC,
                    compiler_params=PARAMS,
                    name="impulse",
                )(scalars, impulse)
                return in_order, merged[0]
            own = merged[0]
            came = trade(merged[1], merged[2])

    return on_device


def solution(mesh):
    placed = (
        P(None, "layer", "sub"),
        P("layer", "sub"),
        P(None, "layer", "sub"),
        P("layer", "sub"),
        P(None, "layer", "sub"),
        P(None, "layer", "sub"),
        P(None, "layer", "sub"),
    )
    return jax.shard_map(
        make(mesh.shape["sub"], mesh.shape["layer"]),
        mesh=mesh,
        in_specs=placed,
        out_specs=(P(None, "layer", "sub"), P(None, "layer", "sub")),
        check_vma=False,
    )
```

```python
import jax
import jax.numpy as jnp
from jax import lax
from jax.experimental import pallas as pl
from jax.experimental.pallas import tpu as pltpu
from jax.sharding import PartitionSpec as P

WIN = 4
SWEEPS = 3
NCOLOR = 4
TILE = 128
LANES = 128
WIDE = 256
GROUP = 4

relaxation = 0.7
friction = 0.6
tangent_floor = 0.1

AXES = ("sub", "layer")
F32 = jnp.float32
BF16 = jnp.bfloat16
VMEM_SPEC = pl.BlockSpec(memory_space=pltpu.VMEM)
SMEM_SPEC = pl.BlockSpec(memory_space=pltpu.SMEM)
PARAMS = pltpu.CompilerParams(vmem_limit_bytes=16 << 20)


def neighbour_matchings(subs, layers):
    assert subs % 2 == 0 and layers % 2 == 0

    def shifted(i):
        return i - 1 if i % 2 == 0 else i + 1

    def partner(match, s, y):
        if match == 0:
            return s ^ 1, y
        if match == 1:
            return (s, y ^ 1) if s in (0, subs - 1) else (shifted(s), y)
        if match == 2:
            return s, y ^ 1
        return (s ^ 1, y) if y in (0, layers - 1) else (s, shifted(y))

    out = []
    for match in range(4):
        pairs = []
        for s in range(subs):
            for y in range(layers):
                ps, py = partner(match, s, y)
                pairs.append((s * layers + y, ps * layers + py))
        out.append(pairs)
    return out


def relay_shuffle(subs, layers, k):
    return [
        (s * layers + y, (s ^ k) * layers + y) for s in range(subs) for y in range(layers)
    ]


def lane_iota():
    return lax.broadcasted_iota(jnp.int32, (8, LANES), 1)


def pick(tables, index):
    low = jnp.bitwise_and(index, LANES - 1)
    high = jnp.right_shift(index, 7)
    out = jnp.take_along_axis(tables[0], low, axis=1)
    for h in range(1, len(tables)):
        out = jnp.where(high == h, jnp.take_along_axis(tables[h], low, axis=1), out)
    return out


def two_parts(value):
    first = value.astype(BF16).astype(F32)
    return jnp.concatenate([first, value - first], axis=0).astype(BF16)


def equal_rows(row, count):
    shape = (count, row.shape[1])
    ids = lax.broadcasted_iota(jnp.int32, shape, 0).astype(F32).astype(BF16)
    here = jnp.broadcast_to(row.astype(F32), shape).astype(BF16)
    return jnp.where(ids == here, jnp.ones(shape, BF16), jnp.zeros(shape, BF16))


def high_masks(index_row, highs):
    shape = (16, LANES)
    high = jnp.broadcast_to(jnp.right_shift(index_row, 7).astype(F32), shape).astype(BF16)
    one, zero = jnp.ones(shape, BF16), jnp.zeros(shape, BF16)
    return jnp.concatenate(
        [jnp.where(high == jnp.full(shape, h, BF16), one, zero) for h in range(highs)], axis=0
    )


def low_onehot(index_row):
    return equal_rows(jnp.bitwise_and(index_row, LANES - 1), LANES)


def contract_lanes(lhs, rhs):
    return lax.dot_general(
        lhs, rhs, (((1,), (1,)), ((), ())), preferred_element_type=F32
    )


def sum_parts(block, h):
    return block[16 * h : 16 * h + 8] + block[16 * h + 8 : 16 * h + 16]


def cross(u, v):
    return [
        u[1] * v[2] - u[2] * v[1],
        u[2] * v[0] - u[0] * v[2],
        u[0] * v[1] - u[1] * v[0],
    ]


def dot3(u, v):
    return u[0] * v[0] + u[1] * v[1] + u[2] * v[2]


def halves(low, high, half):
    return jnp.where(lane_iota() < half, low, high)


def parities():
    sub = lax.axis_index("sub")
    layer = lax.axis_index("layer")
    return sub, layer, lax.rem(sub, 2) == 0, lax.rem(layer, 2) == 0


def prepare_kernel(
    geo_hbm, dest_hbm, vel_hbm, inertia_hbm, exports_hbm, pairs_hbm, colors_hbm,
    send0, place2, place3, out0, out1, start_own, export_index, hot, own_mask, tall,
    ordered, index_out, used, scalars_out,
    geo, dest, vel, inertia, exports, pairs, colors, scalars, listed, dense, mask, lhs, sems,
):
    copies = [
        pltpu.make_async_copy(src, dst, sems.at[i])
        for i, (src, dst) in enumerate(
            [
                (exports_hbm, exports),
                (vel_hbm, vel),
                (inertia_hbm, inertia),
                (dest_hbm, dest),
                (colors_hbm, colors),
                (pairs_hbm, pairs),
                (geo_hbm, geo),
            ]
        )
    ]
    for copy in copies:
        copy.start()
    count = geo.shape[2]
    tiles = count // TILE
    slots = place2.shape[0] // 10
    bodies = vel.shape[2]
    interface = exports.shape[2]
    sub, layer, sub_even, layer_even = parities()
    member = lax.rem(sub, WIN)
    start_own[...] = jnp.zeros_like(start_own)
    dense[...] = jnp.zeros_like(dense)
    for copy in copies[:6]:
        copy.wait()
    for r in range(6):
        start_own[r : r + 1, :] = vel[r]
    for r in range(4):
        start_own[8 + r : 9 + r, :] = inertia[r]
    listed[0:1, 0:interface] = exports[0]
    listed[0:1, interface : 2 * interface] = exports[1]
    listed[1:2, 0:interface] = exports[1]
    listed[1:2, interface : 2 * interface] = exports[0]
    listed[2:3, 0:interface] = exports[2]
    listed[2:3, interface : 2 * interface] = exports[3]
    listed[3:4, 0:interface] = exports[3]
    listed[3:4, interface : 2 * interface] = exports[2]
    row0 = jnp.where(sub_even, listed[1:2, :], listed[0:1, :])
    row1 = jnp.where(layer_even, listed[3:4, :], listed[2:3, :])
    idx0 = jnp.broadcast_to(row0, (8, LANES))
    idx1 = jnp.broadcast_to(row1, (8, LANES))
    export_index[0:8, :] = idx0
    export_index[8:16, :] = idx1
    blocks = bodies // LANES
    for base in (0, 8):
        tables = [
            start_own[base : base + 8, h * LANES : (h + 1) * LANES] for h in range(blocks)
        ]
        picked = pick(tables, idx0)
        out0[base : base + 8, :] = picked
        send0[10 * slots + base : 10 * slots + base + 8, :] = picked
        out1[base : base + 8, :] = pick(tables, idx1)
    rank = used.shape[0]
    for i in range(rank):
        scalars[i] = tiles
    place = [jnp.int32(0)] * tiles
    over = jnp.int32(0)
    for k in range(NCOLOR):
        filled = jnp.int32(0)
        base = (NCOLOR + over) * GROUP - GROUP
        for t in range(tiles):
            hit = colors[0, t] == k
            at = jnp.where(filled < GROUP, GROUP * k, base) + filled
            place[t] = jnp.where(hit, at, place[t])
            scalars[jnp.where(hit, at, UNUSED)] = t
            filled = filled + jnp.where(hit, 1, 0)
        scalars[OVER_FROM + k] = over
        over = over + lax.div(jnp.maximum(filled - 1, GROUP - 1), GROUP)
        scalars[OVER_TO + k] = over
    index_out[...] = jnp.zeros_like(index_out)
    used[...] = jnp.zeros_like(used)
    flip_sub = jnp.where(sub_even, interface, 0)
    flip_layer = jnp.where(layer_even, interface, 0)
    for t in range(tiles):
        span = slice(t * TILE, (t + 1) * TILE)
        nearer = pairs[0, :, span]
        other = pairs[1, :, span]
        ghost = other - bodies
        turned = jnp.where(
            ghost < 2 * interface,
            jnp.bitwise_xor(ghost, flip_sub),
            jnp.bitwise_xor(ghost, flip_layer),
        )
        farther = jnp.where(ghost < 0, other, bodies + turned)
        scalars[TILE_SLOT + t] = place[t]
        ordered[t : t + 1, :] = nearer
        ordered[16 + t : 17 + t, :] = farther
        index_out[pl.ds(place[t], 1), :] = nearer
        index_out[pl.ds(rank + place[t], 1), :] = farther
        used[pl.ds(place[t], 1), :] = jnp.ones((1, LANES), F32)
    slot = dest[...] - (sub - member) * count
    target = jnp.zeros_like(slot)
    for m in range(1, WIN):
        target = target + jnp.where(slot >= m * count, 1, 0)
    within = slot - target * count
    row_id = jnp.bitwise_xor(target, member) * 8 + jnp.right_shift(within, 8)
    low = jnp.bitwise_and(within, WIDE - 1)
    paired = (16, TILE)
    ids = lax.broadcasted_iota(jnp.int32, paired, 0)
    ids = jnp.bitwise_and(ids, 7).astype(F32)
    one, zero = jnp.ones(paired, BF16), jnp.zeros(paired, BF16)
    for t in range(tiles):
        span = slice(t * TILE, (t + 1) * TILE)
        hot[:, span] = equal_rows(low[:, span], WIDE)
        here = jnp.broadcast_to(row_id[:, span].astype(F32), paired).astype(BF16)
        for k in range(WIN):
            chosen = jnp.where(here == (ids + 8.0 * k).astype(BF16), one, zero)
            if k == 0:
                own_mask[:, span] = chosen
            else:
                mask[16 * k - 16 : 16 * k, span] = chosen
    give = pltpu.make_async_copy(scalars, scalars_out, sems.at[7])
    give.start()
    copies[6].wait()
    for r in range(10):
        dense[r : r + 1, :] = geo[r]
    value = dense[...]
    first = value.astype(BF16).astype(F32)
    parts = [first, value - first]
    for p in range(2):
        for i in range(5):
            pair = jnp.concatenate(
                [jnp.broadcast_to(parts[p][r : r + 1, :], (8, count)) for r in (2 * i, 2 * i + 1)],
                axis=0,
            ).astype(BF16)
            tall[p, 16 * i : 16 * i + 16, :] = pair
            for k in range(1, WIN):
                at = 80 * (k - 1) + 16 * i
                lhs[p, at : at + 16, :] = mask[16 * k - 16 : 16 * k, :] * pair
    total = contract_lanes(lhs[0], hot[...]) + contract_lanes(lhs[1], hot[...])
    for k, out in enumerate((send0, place2, place3)):
        store_placed(out, total[80 * k : 80 * k + 80, :])
    give.wait()


def store_placed(out, total):
    for r in range(10):
        for side in range(2):
            out[16 * r + 8 * side : 16 * r + 8 * side + 8, :] = total[
                8 * r : 8 * r + 8, side * LANES : (side + 1) * LANES
            ]


def place_kernel(tall, own_mask, hot, out):
    left = [jnp.concatenate([own_mask[...]] * 5, axis=0) * tall[p] for p in range(2)]
    store_placed(out, contract_lanes(left[0], hot[...]) + contract_lanes(left[1], hot[...]))


TILE_SLOT, OVER_FROM, OVER_TO, UNUSED = 32, 48, 56, 63


def overflow_groups(tiles):
    most = 0
    for busy in range(1, NCOLOR + 1):
        spare = tiles - busy * (GROUP + 1)
        if spare >= 0:
            most = max(most, busy + spare // GROUP)
    return most


def slot_count(tiles):
    return -(-GROUP * (NCOLOR + overflow_groups(tiles)) // 8) * 8


def index_kernel(
    subs, layers, interface, bodies, ordered, export_index,
    hot, masks, export_hot, export_masks, mult,
):
    tiles = masks.shape[0] - 1
    blocks = bodies // LANES
    total = blocks + 4 * interface // LANES
    sub, layer, sub_even, layer_even = parities()
    for t in range(tiles):
        first = ordered[t : t + 1, :]
        second = ordered[16 + t : 17 + t, :]
        hot[:, 2 * t * TILE : (2 * t + 1) * TILE] = low_onehot(first)
        hot[:, (2 * t + 1) * TILE : (2 * t + 2) * TILE] = low_onehot(second)
        masks[t, : 16 * blocks, :] = high_masks(first, blocks)
        masks[t, 16 * blocks :, :] = high_masks(second, total)
    hot[:, 2 * tiles * TILE :] = jnp.zeros((LANES, 2 * TILE), BF16)
    masks[tiles] = jnp.zeros_like(masks[tiles])
    inner_sub = jnp.where(jnp.logical_and(sub > 0, sub < subs - 1), 1.0, 0.0)
    inner_layer = jnp.where(jnp.logical_and(layer > 0, layer < layers - 1), 1.0, 0.0)
    lane = lane_iota()
    weights = [
        jnp.where(lane < interface, 1.0, inner_sub),
        jnp.where(lane < interface, 1.0, inner_layer),
    ]
    left = []
    for i in range(2):
        row = export_index[8 * i : 8 * i + 1, :]
        export_hot[:, i * LANES : (i + 1) * LANES] = low_onehot(row)
        chosen = high_masks(row, blocks)
        export_masks[i] = chosen
        weight = jnp.concatenate([weights[i], jnp.zeros_like(weights[i])], axis=0).astype(BF16)
        left.append(jnp.concatenate([weight] * blocks, axis=0) * chosen)
    listed = contract_lanes(jnp.concatenate(left, axis=1), export_hot[...])
    for h in range(blocks):
        mult[:, h * LANES : (h + 1) * LANES] = 1.0 + listed[16 * h : 16 * h + 8]


STATE = 34


def contact_state(geo, first, second):
    raw = geo[0:3]
    length = jnp.sqrt(dot3(raw, raw))
    normal = [x / length for x in raw]
    side = jnp.sqrt(normal[1] * normal[1] + normal[2] * normal[2])
    tan_y = normal[2] / side
    tan_z = -normal[1] / side
    two = [
        normal[1] * tan_z - normal[2] * tan_y,
        -normal[0] * tan_z,
        normal[0] * tan_y,
    ]

    def arm(p, spin):
        return [
            spin[1] * p[2] * p[2] + spin[2] * p[1] * p[1],
            spin[0] * p[2] * p[2] + spin[2] * p[0] * p[0],
            spin[0] * p[1] * p[1] + spin[1] * p[0] * p[0],
            -spin[2] * p[0] * p[1],
            -spin[1] * p[0] * p[2],
            -spin[0] * p[1] * p[2],
        ]

    arm_a, arm_b = geo[3:6], geo[6:9]
    e = [x + y for x, y in zip(arm(arm_a, first[1:4]), arm(arm_b, second[1:4]))]
    mass = first[0] + second[0]
    xx, yy, zz = mass + e[0], mass + e[1], mass + e[2]
    xy, xz, yz = e[3], e[4], e[5]
    c_xx = yy * zz - yz * yz
    c_xy = xz * yz - xy * zz
    c_xz = xy * yz - xz * yy
    c_yy = xx * zz - xz * xz
    c_yz = xy * xz - xx * yz
    c_zz = xx * yy - xy * xy
    det = xx * c_xx + xy * c_xy + xz * c_xz
    inv = [
        [c_xx / det, c_xy / det, c_xz / det],
        [c_xy / det, c_yy / det, c_yz / det],
        [c_xz / det, c_yz / det, c_zz / det],
    ]
    solve = []
    for row in (normal, None, two):
        for j in range(3):
            if row is None:
                value = tan_y * inv[1][j] + tan_z * inv[2][j]
            else:
                value = row[0] * inv[0][j] + row[1] * inv[1][j] + row[2] * inv[2][j]
            solve.append(relaxation * value)
    bias = [geo[9] * dot3(solve[3 * i : 3 * i + 3], normal) for i in range(3)]
    return (
        solve + bias + normal + [tan_y, tan_z] + two + arm_a + arm_b + list(first) + list(second)
    )


def sweep_kernel(bodies, interface, first_sweep, *refs):
    scalars_in, index, used, hot, masks = refs[:5]
    refs = refs[5:]
    if first_sweep:
        own, g1, r1, r2, r3, g0, g2, g3, state = refs[:9]
        refs = refs[9:]
        r0 = g1.at[pl.ds(g0.shape[0], 16), :]
    else:
        own, r0, r1, r2, r3, state, impulse_in = refs[:7]
        refs = refs[7:]
    impulse, own_change, ghost0, ghost1 = refs[:4]
    got_a, got_b, push_a, push_b, acc, table, all_a, all_b, gathered, placed, scalars, sem = refs[4:]
    slots = used.shape[0]
    tiles = masks.shape[0] - 1
    blocks = bodies // LANES
    total = blocks + (4 * interface) // LANES
    fetch = pltpu.make_async_copy(scalars_in, scalars, sem)
    fetch.start()

    def ghost_blocks(base):
        return [
            halves(r0[base : base + 8, :], r1[base : base + 8, :], interface),
            halves(r2[base : base + 8, :], r3[base : base + 8, :], interface),
        ]

    start = [own[0:8, h * LANES : (h + 1) * LANES] for h in range(blocks)] + ghost_blocks(0)
    for h in range(total):
        table[8 * h : 8 * h + 8, :] = start[h]
    push_a[...] = jnp.zeros_like(push_a)
    push_b[...] = jnp.zeros_like(push_b)

    if first_sweep:
        props = [own[8:16, h * LANES : (h + 1) * LANES] for h in range(blocks)] + ghost_blocks(8)
        for t in range(slots):
            ia = jnp.broadcast_to(index[t : t + 1, :], (8, LANES))
            ib = jnp.broadcast_to(index[slots + t : slots + t + 1, :], (8, LANES))
            all_a[8 * t : 8 * t + 8, :] = pick(props[:blocks], ia)
            all_b[8 * t : 8 * t + 8, :] = pick(props, ib)
        gathered[...] = (g0[...] + g1[0 : g0.shape[0], :]) + (g2[...] + g3[...])
        placed[...] = jnp.ones_like(placed)
        fetch.wait()
        rows = g0.shape[0] // 10
        for t in range(tiles):
            slot = scalars[TILE_SLOT + t]
            at = 8 * (t % 2) + t // 2
            for c in range(10):
                row = c * rows + at
                placed[pl.ds(c * slots + slot, 1), :] = gathered[row : row + 1, :]
        first = [all_a[pl.ds(c, slots, stride=8), :] for c in range(4)]
        second = [all_b[pl.ds(c, slots, stride=8), :] for c in range(4)]
        geo = [placed[c * slots : (c + 1) * slots, :] for c in range(10)]
        for c, value in enumerate(contact_state(geo, first, second)):
            state[c * slots : (c + 1) * slots, :] = value
        impulse[...] = jnp.zeros_like(impulse)
    else:
        impulse[...] = impulse_in[...]

    def held_at(base):
        return lambda c: state[pl.ds(c * slots + base, GROUP), :]

    def gather(base, room, now):
        for j in range(GROUP):
            ia = jnp.broadcast_to(index[pl.ds(base + j, 1), :], (8, LANES))
            ib = jnp.broadcast_to(index[pl.ds(slots + base + j, 1), :], (8, LANES))
            got_a[room + 8 * j : room + 8 * j + 8, :] = pick(now[:blocks], ia)
            got_b[room + 8 * j : room + 8 * j + 8, :] = pick(now, ib)

    def press(base, room):
        held = held_at(base)
        tile_rows = [pl.ds(room + c, GROUP, stride=8) for c in range(6)]
        va = [got_a[tile_rows[c], :] for c in range(6)]
        vb = [got_b[tile_rows[c], :] for c in range(6)]
        arm_a = [held(20 + c) for c in range(3)]
        arm_b = [held(23 + c) for c in range(3)]
        turn_a = cross(va[3:6], arm_a)
        turn_b = cross(vb[3:6], arm_b)
        rel = [((va[c] + turn_a[c]) - vb[c]) - turn_b[c] for c in range(3)]
        old = [impulse[pl.ds(c * slots + base, GROUP), :] for c in range(3)]
        trial = [
            old[c] - (dot3([held(3 * c + j) for j in range(3)], rel) + held(9 + c))
            for c in range(3)
        ]
        normal_part = jnp.maximum(trial[0], 0.0)
        slide = trial[1] * trial[1] + trial[2] * trial[2]
        shrink = lax.rsqrt(jnp.maximum(slide, tangent_floor * tangent_floor))
        factor = jnp.minimum(1.0, friction * normal_part * shrink)
        active = used[pl.ds(base, GROUP), :] > 0.5
        new = [
            jnp.where(active, normal_part, old[0]),
            jnp.where(active, trial[1] * factor, old[1]),
            jnp.where(active, trial[2] * factor, old[2]),
        ]
        change = [new[c] - old[c] for c in range(3)]
        for c in range(3):
            impulse[pl.ds(c * slots + base, GROUP), :] = new[c]
        force = [
            held(12) * change[0] + held(17) * change[2],
            held(13) * change[0] + held(15) * change[1] + held(18) * change[2],
            held(14) * change[0] + held(16) * change[1] + held(19) * change[2],
        ]
        spin_a = cross(arm_a, force)
        spin_b = cross(arm_b, force)
        for c in range(3):
            push_a[tile_rows[c], :] = held(26) * force[c]
            push_a[tile_rows[3 + c], :] = held(27 + c) * spin_a[c]
            push_b[tile_rows[c], :] = -(held(30) * force[c])
            push_b[tile_rows[3 + c], :] = -(held(31 + c) * spin_b[c])

    def sides(base, room):
        left, right = [], []
        empty = jnp.zeros((16 * (total - blocks), LANES), BF16)
        for j in range(GROUP):
            t = scalars[base + j]
            first = two_parts(push_a[room + 8 * j : room + 8 * j + 8, :])
            second = two_parts(push_b[room + 8 * j : room + 8 * j + 8, :])
            rows = [masks[t, 16 * m : 16 * m + 16, :] for m in range(blocks + total)]
            left.append(jnp.concatenate([first * m for m in rows[:blocks]] + [empty], axis=0))
            left.append(jnp.concatenate([second * m for m in rows[blocks:]], axis=0))
            right.append(hot[:, pl.ds(pl.multiple_of(2 * TILE * t, 2 * TILE), 2 * TILE)])
        return left, right

    def groups(bases, now, before=None):
        rooms = [8 * GROUP * i for i in range(len(bases))]
        for base, room in zip(bases, rooms):
            gather(base, room, now)
        for base, room in zip(bases, rooms):
            press(base, room)
        if before is not None:
            before()
        left, right = [], []
        for base, room in zip(bases, rooms):
            more_left, more_right = sides(base, room)
            left += more_left
            right += more_right
        return contract_lanes(jnp.concatenate(left, axis=1), jnp.concatenate(right, axis=1))

    def color_pass(k, before=None):
        now = [table[8 * h : 8 * h + 8, :] for h in range(total)]
        main = pl.multiple_of(GROUP * k, GROUP)

        def over(g):
            return pl.multiple_of(GROUP * (NCOLOR + g), GROUP)

        if before is not None:
            acc[...] = groups([main], now, before)
        begin, end = scalars[OVER_FROM + k], scalars[OVER_TO + k]
        if before is None:

            @pl.when(end > begin)
            def _():
                acc[...] = groups([main, over(begin)], now)

            @pl.when(end <= begin)
            def _():
                acc[...] = groups([main], now)

            begin = begin + 1

        def more(g, c):
            acc[...] += groups([over(g)], now)
            return c

        lax.fori_loop(begin, end, more, 0)
        for h in range(total):
            table[8 * h : 8 * h + 8, :] = now[h] + sum_parts(acc, h)

    def later_pass(k, carry):
        color_pass(k)
        return carry

    color_pass(0, None if first_sweep else fetch.wait)
    lax.fori_loop(1, NCOLOR, later_pass, 0)
    for h in range(blocks):
        own_change[:, h * LANES : (h + 1) * LANES] = table[8 * h : 8 * h + 8, :] - start[h]
    ghost0[...] = table[8 * blocks : 8 * blocks + 8, :] - start[blocks]
    ghost1[...] = table[8 * blocks + 8 : 8 * blocks + 16, :] - start[blocks + 1]


def impulse_kernel(scalars, held, impulse):
    slots = held.shape[0] // 3
    for t in range(impulse.shape[2] // TILE):
        slot = scalars[TILE_SLOT + t]
        for c in range(3):
            impulse[c, :, t * TILE : (t + 1) * TILE] = held[pl.ds(c * slots + slot, 1), :]


def merge_kernel(
    interface, last_sweep, own, change, c0, c1, c2, c3, mult, export_index, export_hot,
    export_masks, *refs,
):
    blocks = own.shape[1] // LANES
    came = [halves(c0[...], c1[...], interface), halves(c2[...], c3[...], interface)]
    left = jnp.concatenate(
        [
            jnp.concatenate([two_parts(came[i])] * blocks, axis=0) * export_masks[i]
            for i in range(2)
        ],
        axis=1,
    )
    incoming = contract_lanes(left, export_hot[...])
    fresh = []
    for h in range(blocks):
        span = slice(h * LANES, (h + 1) * LANES)
        fresh.append(
            own[0:8, span] + (change[:, span] + sum_parts(incoming, h)) / mult[:, span]
        )
    if last_sweep:
        (velocity,) = refs
        for r in range(6):
            for h in range(blocks):
                velocity[r, :, h * LANES : (h + 1) * LANES] = fresh[h][r : r + 1, :]
    else:
        fresh_own, out0, out1 = refs
        for h in range(blocks):
            fresh_own[:, h * LANES : (h + 1) * LANES] = fresh[h]
        out0[...] = pick(fresh, export_index[0:8, :])
        out1[...] = pick(fresh, export_index[8:16, :])


def in_hbm(array):
    return pltpu.with_memory_space_constraint(array, pltpu.HBM)


def shape(dims, dtype=F32):
    return jax.ShapeDtypeStruct(dims, dtype)


def make(subs, layers):
    matchings = neighbour_matchings(subs, layers)
    shuffles = [relay_shuffle(subs, layers, k) for k in range(WIN)]

    def trade(low, high):
        return [
            lax.ppermute(low if m < 2 else high, AXES, matchings[m]) for m in range(4)
        ]

    def on_device(geometry, dest_slot, pairs, colors, free_vel, inertia, exports):
        count = geometry.shape[2]
        bodies = free_vel.shape[2]
        interface = exports.shape[2]
        tiles = count // TILE
        slots = 16
        assert count % TILE == 0 and tiles < slots and 2 * interface == LANES
        assert bodies % LANES == 0
        blocks = bodies // LANES
        total = blocks + 2
        place = shape((10 * slots, LANES))
        small = shape((16, LANES))
        arguments = (geometry, dest_slot, free_vel, inertia, exports, pairs, colors)
        rows = slot_count(tiles)
        assert rows <= TILE_SLOT
        prepared = pl.pallas_call(
            prepare_kernel,
            out_shape=(
                shape((10 * slots + 16, LANES)), place, place, small, small,
                shape((16, bodies)),
                shape((16, LANES), jnp.int32),
                shape((WIDE, count), BF16),
                shape((16, count), BF16),
                shape((2, 80, count), BF16),
                shape((32, LANES), jnp.int32),
                shape((2 * rows, LANES), jnp.int32),
                shape((rows, LANES)),
                shape((64,), jnp.int32),
            ),
            in_specs=[pl.BlockSpec(memory_space=pltpu.HBM)] * 7,
            out_specs=(VMEM_SPEC,) * 14,
            scratch_shapes=[
                pltpu.VMEM(geometry.shape, F32),
                pltpu.VMEM(dest_slot.shape, jnp.int32),
                pltpu.VMEM(free_vel.shape, F32),
                pltpu.VMEM(inertia.shape, F32),
                pltpu.VMEM(exports.shape, jnp.int32),
                pltpu.VMEM(pairs.shape, jnp.int32),
                pltpu.SMEM(colors.shape, jnp.int32),
                pltpu.SMEM((64,), jnp.int32),
                pltpu.VMEM((8, LANES), jnp.int32),
                pltpu.VMEM((16, count), F32),
                pltpu.VMEM((16 * (WIN - 1), count), BF16),
                pltpu.VMEM((2, 80 * (WIN - 1), count), BF16),
                pltpu.SemaphoreType.DMA((8,)),
            ],
            compiler_params=PARAMS,
            name="prepare",
        )(*[in_hbm(x) for x in arguments])
        send0, place2, place3, out0, out1, own, export_index = prepared[:7]
        wide_hot, own_mask, tall, ordered, index, used, scalars = prepared[7:]
        came = [lax.ppermute(send0, AXES, matchings[0])]
        came.append(lax.ppermute(out0, AXES, matchings[1]))
        came.append(lax.ppermute(out1, AXES, matchings[2]))
        came.append(lax.ppermute(out1, AXES, matchings[3]))
        place0 = pl.pallas_call(
            place_kernel,
            out_shape=place,
            in_specs=[VMEM_SPEC] * 3,
            out_specs=VMEM_SPEC,
            compiler_params=PARAMS,
            name="place",
        )(tall, own_mask, wide_hot)
        placed = [place0]
        placed.append(lax.ppermute(place2, AXES, shuffles[2]))
        placed.append(lax.ppermute(place3, AXES, shuffles[3]))

        def indexing(*refs):
            index_kernel(subs, layers, interface, bodies, *refs)

        hot, masks, export_hot, export_masks, mult = pl.pallas_call(
            indexing,
            out_shape=(
                shape((LANES, 2 * TILE * (tiles + 1)), BF16),
                shape((tiles + 1, 16 * (blocks + total), LANES), BF16),
                shape((LANES, 2 * LANES), BF16),
                shape((2, 16 * blocks, LANES), BF16),
                shape((8, bodies)),
            ),
            in_specs=[VMEM_SPEC] * 2,
            out_specs=(VMEM_SPEC,) * 5,
            compiler_params=PARAMS,
            name="indexing",
        )(ordered, export_index)

        state = impulse = None
        for sweep in range(SWEEPS):
            first, last = sweep == 0, sweep == SWEEPS - 1

            def run(*refs, first=first):
                sweep_kernel(bodies, interface, first, *refs)

            outs = [
                shape((3 * rows, LANES)),
                shape((8, bodies)),
                shape((8, LANES)),
                shape((8, LANES)),
            ]
            operands = [scalars, index, used, hot, masks, own, *came]
            if first:
                outs = [shape((STATE * rows, LANES))] + outs
                operands += placed
            else:
                operands += [state, impulse]
            result = pl.pallas_call(
                run,
                out_shape=tuple(outs),
                in_specs=[VMEM_SPEC] * len(operands),
                out_specs=(VMEM_SPEC,) * len(outs),
                scratch_shapes=[
                    pltpu.VMEM((16 * GROUP, LANES), F32),
                    pltpu.VMEM((16 * GROUP, LANES), F32),
                    pltpu.VMEM((16 * GROUP, LANES), F32),
                    pltpu.VMEM((16 * GROUP, LANES), F32),
                    pltpu.VMEM((16 * total, LANES), F32),
                    pltpu.VMEM((8 * total, LANES), F32),
                    pltpu.VMEM((8 * rows, LANES), F32),
                    pltpu.VMEM((8 * rows, LANES), F32),
                    pltpu.VMEM((10 * slots, LANES), F32),
                    pltpu.VMEM((10 * rows, LANES), F32),
                    pltpu.SMEM((64,), jnp.int32),
                    pltpu.SemaphoreType.DMA,
                ],
                compiler_params=PARAMS,
                name="sweep",
            )(*operands)
            if first:
                state, result = result[0], result[1:]
            impulse, change, ghost0, ghost1 = result
            sums = trade(ghost0, ghost1)

            def merge(*refs, last=last):
                merge_kernel(interface, last, *refs)

            operands = [own, change, *sums, mult, export_index, export_hot, export_masks]
            if last:
                outs = (shape((6, 1, bodies)),)
            else:
                outs = (shape((8, bodies)), shape((8, LANES)), shape((8, LANES)))
            merged = pl.pallas_call(
                merge,
                out_shape=outs,
                in_specs=[VMEM_SPEC] * len(operands),
                out_specs=(VMEM_SPEC,) * len(outs),
                compiler_params=PARAMS,
                name="merge",
            )(*operands)
            if last:
                in_order = pl.pallas_call(
                    impulse_kernel,
                    out_shape=shape((3, 1, count)),
                    in_specs=[SMEM_SPEC, VMEM_SPEC],
                    out_specs=VMEM_SPEC,
                    compiler_params=PARAMS,
                    name="impulse",
                )(scalars, impulse)
                return in_order, merged[0]
            own = merged[0]
            came = trade(merged[1], merged[2])

    return on_device


def solution(mesh):
    placed = (
        P(None, "layer", "sub"),
        P("layer", "sub"),
        P(None, "layer", "sub"),
        P("layer", "sub"),
        P(None, "layer", "sub"),
        P(None, "layer", "sub"),
        P(None, "layer", "sub"),
    )
    return jax.shard_map(
        make(mesh.shape["sub"], mesh.shape["layer"]),
        mesh=mesh,
        in_specs=placed,
        out_specs=(P(None, "layer", "sub"), P(None, "layer", "sub")),
        check_vma=False,
    )
```

```python
import jax
import jax.numpy as jnp
from jax import lax
from jax.experimental import pallas as pl
from jax.experimental.pallas import tpu as pltpu
from jax.sharding import PartitionSpec as P

WIN = 4
SWEEPS = 3
NCOLOR = 4
TILE = 128
LANES = 128
WIDE = 256
GROUP = 4

relaxation = 0.7
friction = 0.6
tangent_floor = 0.1

AXES = ("sub", "layer")
F32 = jnp.float32
BF16 = jnp.bfloat16
VMEM_SPEC = pl.BlockSpec(memory_space=pltpu.VMEM)
SMEM_SPEC = pl.BlockSpec(memory_space=pltpu.SMEM)
PARAMS = pltpu.CompilerParams(vmem_limit_bytes=16 << 20)


def neighbour_matchings(subs, layers):
    assert subs % 2 == 0 and layers % 2 == 0

    def shifted(i):
        return i - 1 if i % 2 == 0 else i + 1

    def partner(match, s, y):
        if match == 0:
            return s ^ 1, y
        if match == 1:
            return (s, y ^ 1) if s in (0, subs - 1) else (shifted(s), y)
        if match == 2:
            return s, y ^ 1
        return (s ^ 1, y) if y in (0, layers - 1) else (s, shifted(y))

    out = []
    for match in range(4):
        pairs = []
        for s in range(subs):
            for y in range(layers):
                ps, py = partner(match, s, y)
                pairs.append((s * layers + y, ps * layers + py))
        out.append(pairs)
    return out


def relay_shuffle(subs, layers, k):
    return [
        (s * layers + y, (s ^ k) * layers + y) for s in range(subs) for y in range(layers)
    ]


def lane_iota():
    return lax.broadcasted_iota(jnp.int32, (8, LANES), 1)


def pick(tables, index):
    low = jnp.bitwise_and(index, LANES - 1)
    high = jnp.right_shift(index, 7)
    out = jnp.take_along_axis(tables[0], low, axis=1)
    for h in range(1, len(tables)):
        out = jnp.where(high == h, jnp.take_along_axis(tables[h], low, axis=1), out)
    return out


def two_parts(value):
    first = value.astype(BF16).astype(F32)
    return jnp.concatenate([first, value - first], axis=0).astype(BF16)


def equal_rows(row, count):
    shape = (count, row.shape[1])
    ids = lax.broadcasted_iota(jnp.int32, shape, 0).astype(F32).astype(BF16)
    here = jnp.broadcast_to(row.astype(F32), shape).astype(BF16)
    return jnp.where(ids == here, jnp.ones(shape, BF16), jnp.zeros(shape, BF16))


def high_masks(index_row, highs):
    shape = (16, LANES)
    high = jnp.broadcast_to(jnp.right_shift(index_row, 7).astype(F32), shape).astype(BF16)
    one, zero = jnp.ones(shape, BF16), jnp.zeros(shape, BF16)
    return jnp.concatenate(
        [jnp.where(high == jnp.full(shape, h, BF16), one, zero) for h in range(highs)], axis=0
    )


def low_onehot(index_row):
    return equal_rows(jnp.bitwise_and(index_row, LANES - 1), LANES)


def contract_lanes(lhs, rhs):
    return lax.dot_general(
        lhs, rhs, (((1,), (1,)), ((), ())), preferred_element_type=F32
    )


def sum_parts(block, h):
    return block[16 * h : 16 * h + 8] + block[16 * h + 8 : 16 * h + 16]


def cross(u, v):
    return [
        u[1] * v[2] - u[2] * v[1],
        u[2] * v[0] - u[0] * v[2],
        u[0] * v[1] - u[1] * v[0],
    ]


def dot3(u, v):
    return u[0] * v[0] + u[1] * v[1] + u[2] * v[2]


def halves(low, high, half):
    return jnp.where(lane_iota() < half, low, high)


def parities():
    sub = lax.axis_index("sub")
    layer = lax.axis_index("layer")
    return sub, layer, lax.rem(sub, 2) == 0, lax.rem(layer, 2) == 0


def prepare_kernel(
    geo_hbm, dest_hbm, vel_hbm, inertia_hbm, exports_hbm, pairs_hbm, colors_hbm,
    send0, place2, place3, out0, out1, start_own, export_index, hot, own_mask, tall,
    ordered, index_out, used, scalars_out,
    geo, dest, vel, inertia, exports, pairs, colors, scalars, listed, dense, mask, lhs, sems,
):
    copies = [
        pltpu.make_async_copy(src, dst, sems.at[i])
        for i, (src, dst) in enumerate(
            [
                (exports_hbm, exports),
                (vel_hbm, vel),
                (inertia_hbm, inertia),
                (dest_hbm, dest),
                (colors_hbm, colors),
                (pairs_hbm, pairs),
                (geo_hbm, geo),
            ]
        )
    ]
    for copy in copies:
        copy.start()
    count = geo.shape[2]
    tiles = count // TILE
    slots = place2.shape[0] // 10
    bodies = vel.shape[2]
    interface = exports.shape[2]
    sub, layer, sub_even, layer_even = parities()
    member = lax.rem(sub, WIN)
    start_own[...] = jnp.zeros_like(start_own)
    dense[...] = jnp.zeros_like(dense)
    for copy in copies[:6]:
        copy.wait()
    for r in range(6):
        start_own[r : r + 1, :] = vel[r]
    for r in range(4):
        start_own[8 + r : 9 + r, :] = inertia[r]
    listed[0:1, 0:interface] = exports[0]
    listed[0:1, interface : 2 * interface] = exports[1]
    listed[1:2, 0:interface] = exports[1]
    listed[1:2, interface : 2 * interface] = exports[0]
    listed[2:3, 0:interface] = exports[2]
    listed[2:3, interface : 2 * interface] = exports[3]
    listed[3:4, 0:interface] = exports[3]
    listed[3:4, interface : 2 * interface] = exports[2]
    row0 = jnp.where(sub_even, listed[1:2, :], listed[0:1, :])
    row1 = jnp.where(layer_even, listed[3:4, :], listed[2:3, :])
    idx0 = jnp.broadcast_to(row0, (8, LANES))
    idx1 = jnp.broadcast_to(row1, (8, LANES))
    export_index[0:8, :] = idx0
    export_index[8:16, :] = idx1
    blocks = bodies // LANES
    for base in (0, 8):
        tables = [
            start_own[base : base + 8, h * LANES : (h + 1) * LANES] for h in range(blocks)
        ]
        picked = pick(tables, idx0)
        out0[base : base + 8, :] = picked
        send0[10 * slots + base : 10 * slots + base + 8, :] = picked
        out1[base : base + 8, :] = pick(tables, idx1)
    rank = used.shape[0]
    for i in range(rank):
        scalars[i] = tiles
    for k in range(NCOLOR):
        scalars[FILLED + k] = 0
    colored, ranks = [], []
    for t in range(tiles):
        color = colors[0, t]
        rank_here = scalars[FILLED + color]
        scalars[FILLED + color] = rank_here + 1
        colored.append(color)
        ranks.append(rank_here)
    over = jnp.int32(0)
    for k in range(NCOLOR):
        scalars[OVER_BASE + k] = (NCOLOR + over) * GROUP - GROUP
        scalars[OVER_FROM + k] = over
        filled = scalars[FILLED + k]
        over = over + jnp.right_shift(jnp.maximum(filled - 1, GROUP - 1), GROUP.bit_length() - 1)
        scalars[OVER_TO + k] = over
    place = []
    for t in range(tiles):
        base = jnp.where(ranks[t] < GROUP, GROUP * colored[t], scalars[OVER_BASE + colored[t]])
        place.append(base + ranks[t])
        scalars[place[t]] = t
    index_out[...] = jnp.zeros_like(index_out)
    used[...] = jnp.zeros_like(used)
    flip_sub = jnp.where(sub_even, interface, 0)
    flip_layer = jnp.where(layer_even, interface, 0)
    for t in range(tiles):
        span = slice(t * TILE, (t + 1) * TILE)
        nearer = pairs[0, :, span]
        other = pairs[1, :, span]
        ghost = other - bodies
        turned = jnp.where(
            ghost < 2 * interface,
            jnp.bitwise_xor(ghost, flip_sub),
            jnp.bitwise_xor(ghost, flip_layer),
        )
        farther = jnp.where(ghost < 0, other, bodies + turned)
        scalars[TILE_SLOT + t] = place[t]
        ordered[t : t + 1, :] = nearer
        ordered[16 + t : 17 + t, :] = farther
        index_out[pl.ds(place[t], 1), :] = nearer
        index_out[pl.ds(rank + place[t], 1), :] = farther
        used[pl.ds(place[t], 1), :] = jnp.ones((1, LANES), F32)
    slot = dest[...] - (sub - member) * count
    target = jnp.zeros_like(slot)
    for m in range(1, WIN):
        target = target + jnp.where(slot >= m * count, 1, 0)
    within = slot - target * count
    row_id = jnp.bitwise_xor(target, member) * 8 + jnp.right_shift(within, 8)
    low = jnp.bitwise_and(within, WIDE - 1)
    paired = (16, TILE)
    ids = lax.broadcasted_iota(jnp.int32, paired, 0)
    ids = jnp.bitwise_and(ids, 7).astype(F32)
    one, zero = jnp.ones(paired, BF16), jnp.zeros(paired, BF16)
    for t in range(tiles):
        span = slice(t * TILE, (t + 1) * TILE)
        hot[:, span] = equal_rows(low[:, span], WIDE)
        here = jnp.broadcast_to(row_id[:, span].astype(F32), paired).astype(BF16)
        for k in range(WIN):
            chosen = jnp.where(here == (ids + 8.0 * k).astype(BF16), one, zero)
            if k == 0:
                own_mask[:, span] = chosen
            else:
                mask[16 * k - 16 : 16 * k, span] = chosen
    give = pltpu.make_async_copy(scalars, scalars_out, sems.at[7])
    give.start()
    copies[6].wait()
    for r in range(10):
        dense[r : r + 1, :] = geo[r]
    value = dense[...]
    first = value.astype(BF16).astype(F32)
    parts = [first, value - first]
    for p in range(2):
        for i in range(5):
            pair = jnp.concatenate(
                [jnp.broadcast_to(parts[p][r : r + 1, :], (8, count)) for r in (2 * i, 2 * i + 1)],
                axis=0,
            ).astype(BF16)
            tall[p, 16 * i : 16 * i + 16, :] = pair
            for k in range(1, WIN):
                at = 80 * (k - 1) + 16 * i
                lhs[p, at : at + 16, :] = mask[16 * k - 16 : 16 * k, :] * pair
    total = contract_lanes(lhs[0], hot[...]) + contract_lanes(lhs[1], hot[...])
    for k, out in enumerate((send0, place2, place3)):
        store_placed(out, total[80 * k : 80 * k + 80, :])
    give.wait()


def store_placed(out, total):
    for r in range(10):
        for side in range(2):
            out[16 * r + 8 * side : 16 * r + 8 * side + 8, :] = total[
                8 * r : 8 * r + 8, side * LANES : (side + 1) * LANES
            ]


def place_kernel(tall, own_mask, hot, out):
    left = [jnp.concatenate([own_mask[...]] * 5, axis=0) * tall[p] for p in range(2)]
    store_placed(out, contract_lanes(left[0], hot[...]) + contract_lanes(left[1], hot[...]))


TILE_SLOT, OVER_FROM, FILLED, OVER_TO, OVER_BASE = 32, 48, 52, 56, 60


def overflow_groups(tiles):
    most = 0
    for busy in range(1, NCOLOR + 1):
        spare = tiles - busy * (GROUP + 1)
        if spare >= 0:
            most = max(most, busy + spare // GROUP)
    return most


def slot_count(tiles):
    return -(-GROUP * (NCOLOR + overflow_groups(tiles)) // 8) * 8


def index_kernel(
    subs, layers, interface, bodies, ordered, export_index, own,
    hot, masks, export_hot, export_masks, mult, near_props, far_props,
):
    tiles = masks.shape[0] - 1
    blocks = bodies // LANES
    total = blocks + 4 * interface // LANES
    sub, layer, sub_even, layer_even = parities()
    props = [own[8:16, h * LANES : (h + 1) * LANES] for h in range(blocks)]
    for t in range(tiles):
        first = ordered[t : t + 1, :]
        second = ordered[16 + t : 17 + t, :]
        near_props[8 * t : 8 * t + 8, :] = pick(props, jnp.broadcast_to(first, (8, LANES)))
        far_props[8 * t : 8 * t + 8, :] = pick(props, jnp.broadcast_to(second, (8, LANES)))
        hot[:, 2 * t * TILE : (2 * t + 1) * TILE] = low_onehot(first)
        hot[:, (2 * t + 1) * TILE : (2 * t + 2) * TILE] = low_onehot(second)
        masks[t, : 16 * blocks, :] = high_masks(first, blocks)
        masks[t, 16 * blocks :, :] = high_masks(second, total)
    hot[:, 2 * tiles * TILE :] = jnp.zeros((LANES, 2 * TILE), BF16)
    masks[tiles] = jnp.zeros_like(masks[tiles])
    inner_sub = jnp.where(jnp.logical_and(sub > 0, sub < subs - 1), 1.0, 0.0)
    inner_layer = jnp.where(jnp.logical_and(layer > 0, layer < layers - 1), 1.0, 0.0)
    lane = lane_iota()
    weights = [
        jnp.where(lane < interface, 1.0, inner_sub),
        jnp.where(lane < interface, 1.0, inner_layer),
    ]
    left = []
    for i in range(2):
        row = export_index[8 * i : 8 * i + 1, :]
        export_hot[:, i * LANES : (i + 1) * LANES] = low_onehot(row)
        chosen = high_masks(row, blocks)
        export_masks[i] = chosen
        weight = jnp.concatenate([weights[i], jnp.zeros_like(weights[i])], axis=0).astype(BF16)
        left.append(jnp.concatenate([weight] * blocks, axis=0) * chosen)
    listed = contract_lanes(jnp.concatenate(left, axis=1), export_hot[...])
    for h in range(blocks):
        mult[:, h * LANES : (h + 1) * LANES] = 1.0 + listed[16 * h : 16 * h + 8]


STATE = 34


def contact_state(geo, first, second):
    raw = geo[0:3]
    length = jnp.sqrt(dot3(raw, raw))
    normal = [x / length for x in raw]
    side = jnp.sqrt(normal[1] * normal[1] + normal[2] * normal[2])
    tan_y = normal[2] / side
    tan_z = -normal[1] / side
    two = [
        normal[1] * tan_z - normal[2] * tan_y,
        -normal[0] * tan_z,
        normal[0] * tan_y,
    ]

    def arm(p, spin):
        return [
            spin[1] * p[2] * p[2] + spin[2] * p[1] * p[1],
            spin[0] * p[2] * p[2] + spin[2] * p[0] * p[0],
            spin[0] * p[1] * p[1] + spin[1] * p[0] * p[0],
            -spin[2] * p[0] * p[1],
            -spin[1] * p[0] * p[2],
            -spin[0] * p[1] * p[2],
        ]

    arm_a, arm_b = geo[3:6], geo[6:9]
    e = [x + y for x, y in zip(arm(arm_a, first[1:4]), arm(arm_b, second[1:4]))]
    mass = first[0] + second[0]
    xx, yy, zz = mass + e[0], mass + e[1], mass + e[2]
    xy, xz, yz = e[3], e[4], e[5]
    c_xx = yy * zz - yz * yz
    c_xy = xz * yz - xy * zz
    c_xz = xy * yz - xz * yy
    c_yy = xx * zz - xz * xz
    c_yz = xy * xz - xx * yz
    c_zz = xx * yy - xy * xy
    det = xx * c_xx + xy * c_xy + xz * c_xz
    inv = [
        [c_xx / det, c_xy / det, c_xz / det],
        [c_xy / det, c_yy / det, c_yz / det],
        [c_xz / det, c_yz / det, c_zz / det],
    ]
    solve = []
    for row in (normal, None, two):
        for j in range(3):
            if row is None:
                value = tan_y * inv[1][j] + tan_z * inv[2][j]
            else:
                value = row[0] * inv[0][j] + row[1] * inv[1][j] + row[2] * inv[2][j]
            solve.append(relaxation * value)
    bias = [geo[9] * dot3(solve[3 * i : 3 * i + 3], normal) for i in range(3)]
    return (
        solve + bias + normal + [tan_y, tan_z] + two + arm_a + arm_b + list(first) + list(second)
    )


def sweep_kernel(bodies, interface, first_sweep, *refs):
    scalars_in, index, used, hot, masks = refs[:5]
    refs = refs[5:]
    if first_sweep:
        own, g1, r1, r2, r3, g0, g2, g3, ordered, near_props, far_props, state = refs[:12]
        refs = refs[12:]
        r0 = g1.at[pl.ds(g0.shape[0], 16), :]
    else:
        own, r0, r1, r2, r3, state, impulse_in = refs[:7]
        refs = refs[7:]
    impulse, own_change, ghost0, ghost1 = refs[:4]
    got_a, got_b, push_a, push_b, acc, table, all_a, all_b, gathered, placed, scalars, sem = refs[4:]
    slots = used.shape[0]
    tiles = masks.shape[0] - 1
    blocks = bodies // LANES
    total = blocks + (4 * interface) // LANES
    fetch = pltpu.make_async_copy(scalars_in, scalars, sem)
    fetch.start()

    def ghost_blocks(base):
        return [
            halves(r0[base : base + 8, :], r1[base : base + 8, :], interface),
            halves(r2[base : base + 8, :], r3[base : base + 8, :], interface),
        ]

    start = [own[0:8, h * LANES : (h + 1) * LANES] for h in range(blocks)] + ghost_blocks(0)
    for h in range(total):
        table[8 * h : 8 * h + 8, :] = start[h]
    push_a[...] = jnp.zeros_like(push_a)
    push_b[...] = jnp.zeros_like(push_b)

    if first_sweep:
        ghost_props = ghost_blocks(8)
        far = []
        for t in range(tiles):
            ib = jnp.broadcast_to(ordered[16 + t : 17 + t, :], (8, LANES))
            low, high = jnp.bitwise_and(ib, LANES - 1), jnp.right_shift(ib, 7)
            value = far_props[8 * t : 8 * t + 8, :]
            for h, block in enumerate(ghost_props):
                value = jnp.where(
                    high == blocks + h, jnp.take_along_axis(block, low, axis=1), value
                )
            far.append(value)
        all_a[...] = jnp.ones_like(all_a)
        all_b[...] = jnp.ones_like(all_b)
        gathered[...] = (g0[...] + g1[0 : g0.shape[0], :]) + (g2[...] + g3[...])
        placed[...] = jnp.ones_like(placed)
        fetch.wait()
        rows = g0.shape[0] // 10
        for t in range(tiles):
            slot = scalars[TILE_SLOT + t]
            group_rows = pl.ds(pl.multiple_of(8 * slot, 8), 8)
            all_a[group_rows, :] = near_props[8 * t : 8 * t + 8, :]
            all_b[group_rows, :] = far[t]
            at = 8 * (t % 2) + t // 2
            for c in range(10):
                row = c * rows + at
                placed[pl.ds(c * slots + slot, 1), :] = gathered[row : row + 1, :]
        first = [all_a[pl.ds(c, slots, stride=8), :] for c in range(4)]
        second = [all_b[pl.ds(c, slots, stride=8), :] for c in range(4)]
        geo = [placed[c * slots : (c + 1) * slots, :] for c in range(10)]
        for c, value in enumerate(contact_state(geo, first, second)):
            state[c * slots : (c + 1) * slots, :] = value
        impulse[...] = jnp.zeros_like(impulse)
    else:
        impulse[...] = impulse_in[...]

    def held_at(base):
        return lambda c: state[pl.ds(c * slots + base, GROUP), :]

    def gather(base, room, now):
        for j in range(GROUP):
            ia = jnp.broadcast_to(index[pl.ds(base + j, 1), :], (8, LANES))
            ib = jnp.broadcast_to(index[pl.ds(slots + base + j, 1), :], (8, LANES))
            got_a[room + 8 * j : room + 8 * j + 8, :] = pick(now[:blocks], ia)
            got_b[room + 8 * j : room + 8 * j + 8, :] = pick(now, ib)

    def press(base, room):
        held = held_at(base)
        tile_rows = [pl.ds(room + c, GROUP, stride=8) for c in range(6)]
        va = [got_a[tile_rows[c], :] for c in range(6)]
        vb = [got_b[tile_rows[c], :] for c in range(6)]
        arm_a = [held(20 + c) for c in range(3)]
        arm_b = [held(23 + c) for c in range(3)]
        turn_a = cross(va[3:6], arm_a)
        turn_b = cross(vb[3:6], arm_b)
        rel = [((va[c] + turn_a[c]) - vb[c]) - turn_b[c] for c in range(3)]
        old = [impulse[pl.ds(c * slots + base, GROUP), :] for c in range(3)]
        trial = [
            old[c] - (dot3([held(3 * c + j) for j in range(3)], rel) + held(9 + c))
            for c in range(3)
        ]
        normal_part = jnp.maximum(trial[0], 0.0)
        slide = trial[1] * trial[1] + trial[2] * trial[2]
        shrink = lax.rsqrt(jnp.maximum(slide, tangent_floor * tangent_floor))
        factor = jnp.minimum(1.0, friction * normal_part * shrink)
        active = used[pl.ds(base, GROUP), :] > 0.5
        new = [
            jnp.where(active, normal_part, old[0]),
            jnp.where(active, trial[1] * factor, old[1]),
            jnp.where(active, trial[2] * factor, old[2]),
        ]
        change = [new[c] - old[c] for c in range(3)]
        for c in range(3):
            impulse[pl.ds(c * slots + base, GROUP), :] = new[c]
        force = [
            held(12) * change[0] + held(17) * change[2],
            held(13) * change[0] + held(15) * change[1] + held(18) * change[2],
            held(14) * change[0] + held(16) * change[1] + held(19) * change[2],
        ]
        spin_a = cross(arm_a, force)
        spin_b = cross(arm_b, force)
        for c in range(3):
            push_a[tile_rows[c], :] = held(26) * force[c]
            push_a[tile_rows[3 + c], :] = held(27 + c) * spin_a[c]
            push_b[tile_rows[c], :] = -(held(30) * force[c])
            push_b[tile_rows[3 + c], :] = -(held(31 + c) * spin_b[c])

    def sides(base, room):
        left, right = [], []
        empty = jnp.zeros((16 * (total - blocks), LANES), BF16)
        for j in range(GROUP):
            t = scalars[base + j]
            first = two_parts(push_a[room + 8 * j : room + 8 * j + 8, :])
            second = two_parts(push_b[room + 8 * j : room + 8 * j + 8, :])
            rows = [masks[t, 16 * m : 16 * m + 16, :] for m in range(blocks + total)]
            left.append(jnp.concatenate([first * m for m in rows[:blocks]] + [empty], axis=0))
            left.append(jnp.concatenate([second * m for m in rows[blocks:]], axis=0))
            right.append(hot[:, pl.ds(pl.multiple_of(2 * TILE * t, 2 * TILE), 2 * TILE)])
        return left, right

    def groups(bases, now, before=None):
        rooms = [8 * GROUP * i for i in range(len(bases))]
        for base, room in zip(bases, rooms):
            gather(base, room, now)
        for base, room in zip(bases, rooms):
            press(base, room)
        if before is not None:
            before()
        left, right = [], []
        for base, room in zip(bases, rooms):
            more_left, more_right = sides(base, room)
            left += more_left
            right += more_right
        return contract_lanes(jnp.concatenate(left, axis=1), jnp.concatenate(right, axis=1))

    def color_pass(k, before=None):
        now = [table[8 * h : 8 * h + 8, :] for h in range(total)]
        main = pl.multiple_of(GROUP * k, GROUP)

        def over(g):
            return pl.multiple_of(GROUP * (NCOLOR + g), GROUP)

        if before is not None:
            acc[...] = groups([main], now, before)
        begin, end = scalars[OVER_FROM + k], scalars[OVER_TO + k]
        if before is None:

            @pl.when(end > begin)
            def _():
                acc[...] = groups([main, over(begin)], now)

            @pl.when(end <= begin)
            def _():
                acc[...] = groups([main], now)

            begin = begin + 1

        def more(g, c):
            acc[...] += groups([over(g)], now)
            return c

        lax.fori_loop(begin, end, more, 0)
        for h in range(total):
            table[8 * h : 8 * h + 8, :] = now[h] + sum_parts(acc, h)

    def later_pass(k, carry):
        color_pass(k)
        return carry

    color_pass(0, None if first_sweep else fetch.wait)
    lax.fori_loop(1, NCOLOR, later_pass, 0)
    for h in range(blocks):
        own_change[:, h * LANES : (h + 1) * LANES] = table[8 * h : 8 * h + 8, :] - start[h]
    ghost0[...] = table[8 * blocks : 8 * blocks + 8, :] - start[blocks]
    ghost1[...] = table[8 * blocks + 8 : 8 * blocks + 16, :] - start[blocks + 1]


def impulse_kernel(scalars, held, impulse):
    slots = held.shape[0] // 3
    for t in range(impulse.shape[2] // TILE):
        slot = scalars[TILE_SLOT + t]
        for c in range(3):
            impulse[c, :, t * TILE : (t + 1) * TILE] = held[pl.ds(c * slots + slot, 1), :]


def merge_kernel(
    interface, last_sweep, own, change, c0, c1, c2, c3, mult, export_index, export_hot,
    export_masks, *refs,
):
    blocks = own.shape[1] // LANES
    came = [halves(c0[...], c1[...], interface), halves(c2[...], c3[...], interface)]
    left = jnp.concatenate(
        [
            jnp.concatenate([two_parts(came[i])] * blocks, axis=0) * export_masks[i]
            for i in range(2)
        ],
        axis=1,
    )
    incoming = contract_lanes(left, export_hot[...])
    fresh = []
    for h in range(blocks):
        span = slice(h * LANES, (h + 1) * LANES)
        fresh.append(
            own[0:8, span] + (change[:, span] + sum_parts(incoming, h)) / mult[:, span]
        )
    if last_sweep:
        (velocity,) = refs
        for r in range(6):
            for h in range(blocks):
                velocity[r, :, h * LANES : (h + 1) * LANES] = fresh[h][r : r + 1, :]
    else:
        fresh_own, out0, out1 = refs
        for h in range(blocks):
            fresh_own[:, h * LANES : (h + 1) * LANES] = fresh[h]
        out0[...] = pick(fresh, export_index[0:8, :])
        out1[...] = pick(fresh, export_index[8:16, :])


def in_hbm(array):
    return pltpu.with_memory_space_constraint(array, pltpu.HBM)


def shape(dims, dtype=F32):
    return jax.ShapeDtypeStruct(dims, dtype)


def make(subs, layers):
    matchings = neighbour_matchings(subs, layers)
    shuffles = [relay_shuffle(subs, layers, k) for k in range(WIN)]

    def trade(low, high):
        return [
            lax.ppermute(low if m < 2 else high, AXES, matchings[m]) for m in range(4)
        ]

    def on_device(geometry, dest_slot, pairs, colors, free_vel, inertia, exports):
        count = geometry.shape[2]
        bodies = free_vel.shape[2]
        interface = exports.shape[2]
        tiles = count // TILE
        slots = 16
        assert count % TILE == 0 and tiles < slots and 2 * interface == LANES
        assert bodies % LANES == 0
        blocks = bodies // LANES
        total = blocks + 2
        place = shape((10 * slots, LANES))
        small = shape((16, LANES))
        arguments = (geometry, dest_slot, free_vel, inertia, exports, pairs, colors)
        rows = slot_count(tiles)
        assert rows <= TILE_SLOT
        prepared = pl.pallas_call(
            prepare_kernel,
            out_shape=(
                shape((10 * slots + 16, LANES)), place, place, small, small,
                shape((16, bodies)),
                shape((16, LANES), jnp.int32),
                shape((WIDE, count), BF16),
                shape((16, count), BF16),
                shape((2, 80, count), BF16),
                shape((32, LANES), jnp.int32),
                shape((2 * rows, LANES), jnp.int32),
                shape((rows, LANES)),
                shape((64,), jnp.int32),
            ),
            in_specs=[pl.BlockSpec(memory_space=pltpu.HBM)] * 7,
            out_specs=(VMEM_SPEC,) * 14,
            scratch_shapes=[
                pltpu.VMEM(geometry.shape, F32),
                pltpu.VMEM(dest_slot.shape, jnp.int32),
                pltpu.VMEM(free_vel.shape, F32),
                pltpu.VMEM(inertia.shape, F32),
                pltpu.VMEM(exports.shape, jnp.int32),
                pltpu.VMEM(pairs.shape, jnp.int32),
                pltpu.SMEM(colors.shape, jnp.int32),
                pltpu.SMEM((64,), jnp.int32),
                pltpu.VMEM((8, LANES), jnp.int32),
                pltpu.VMEM((16, count), F32),
                pltpu.VMEM((16 * (WIN - 1), count), BF16),
                pltpu.VMEM((2, 80 * (WIN - 1), count), BF16),
                pltpu.SemaphoreType.DMA((8,)),
            ],
            compiler_params=PARAMS,
            name="prepare",
        )(*[in_hbm(x) for x in arguments])
        send0, place2, place3, out0, out1, own, export_index = prepared[:7]
        wide_hot, own_mask, tall, ordered, index, used, scalars = prepared[7:]
        came = [lax.ppermute(send0, AXES, matchings[0])]
        came.append(lax.ppermute(out0, AXES, matchings[1]))
        came.append(lax.ppermute(out1, AXES, matchings[2]))
        came.append(lax.ppermute(out1, AXES, matchings[3]))
        place0 = pl.pallas_call(
            place_kernel,
            out_shape=place,
            in_specs=[VMEM_SPEC] * 3,
            out_specs=VMEM_SPEC,
            compiler_params=PARAMS,
            name="place",
        )(tall, own_mask, wide_hot)
        placed = [place0]
        placed.append(lax.ppermute(place2, AXES, shuffles[2]))
        placed.append(lax.ppermute(place3, AXES, shuffles[3]))

        def indexing(*refs):
            index_kernel(subs, layers, interface, bodies, *refs)

        hot, masks, export_hot, export_masks, mult, near_props, far_props = pl.pallas_call(
            indexing,
            out_shape=(
                shape((LANES, 2 * TILE * (tiles + 1)), BF16),
                shape((tiles + 1, 16 * (blocks + total), LANES), BF16),
                shape((LANES, 2 * LANES), BF16),
                shape((2, 16 * blocks, LANES), BF16),
                shape((8, bodies)),
                shape((8 * tiles, LANES)),
                shape((8 * tiles, LANES)),
            ),
            in_specs=[VMEM_SPEC] * 3,
            out_specs=(VMEM_SPEC,) * 7,
            compiler_params=PARAMS,
            name="indexing",
        )(ordered, export_index, own)

        state = impulse = None
        for sweep in range(SWEEPS):
            first, last = sweep == 0, sweep == SWEEPS - 1

            def run(*refs, first=first):
                sweep_kernel(bodies, interface, first, *refs)

            outs = [
                shape((3 * rows, LANES)),
                shape((8, bodies)),
                shape((8, LANES)),
                shape((8, LANES)),
            ]
            operands = [scalars, index, used, hot, masks, own, *came]
            if first:
                outs = [shape((STATE * rows, LANES))] + outs
                operands += [*placed, ordered, near_props, far_props]
            else:
                operands += [state, impulse]
            result = pl.pallas_call(
                run,
                out_shape=tuple(outs),
                in_specs=[VMEM_SPEC] * len(operands),
                out_specs=(VMEM_SPEC,) * len(outs),
                scratch_shapes=[
                    pltpu.VMEM((16 * GROUP, LANES), F32),
                    pltpu.VMEM((16 * GROUP, LANES), F32),
                    pltpu.VMEM((16 * GROUP, LANES), F32),
                    pltpu.VMEM((16 * GROUP, LANES), F32),
                    pltpu.VMEM((16 * total, LANES), F32),
                    pltpu.VMEM((8 * total, LANES), F32),
                    pltpu.VMEM((8 * rows, LANES), F32),
                    pltpu.VMEM((8 * rows, LANES), F32),
                    pltpu.VMEM((10 * slots, LANES), F32),
                    pltpu.VMEM((10 * rows, LANES), F32),
                    pltpu.SMEM((64,), jnp.int32),
                    pltpu.SemaphoreType.DMA,
                ],
                compiler_params=PARAMS,
                name="sweep",
            )(*operands)
            if first:
                state, result = result[0], result[1:]
            impulse, change, ghost0, ghost1 = result
            sums = trade(ghost0, ghost1)

            def merge(*refs, last=last):
                merge_kernel(interface, last, *refs)

            operands = [own, change, *sums, mult, export_index, export_hot, export_masks]
            if last:
                outs = (shape((6, 1, bodies)),)
            else:
                outs = (shape((8, bodies)), shape((8, LANES)), shape((8, LANES)))
            merged = pl.pallas_call(
                merge,
                out_shape=outs,
                in_specs=[VMEM_SPEC] * len(operands),
                out_specs=(VMEM_SPEC,) * len(outs),
                compiler_params=PARAMS,
                name="merge",
            )(*operands)
            if last:
                in_order = pl.pallas_call(
                    impulse_kernel,
                    out_shape=shape((3, 1, count)),
                    in_specs=[SMEM_SPEC, VMEM_SPEC],
                    out_specs=VMEM_SPEC,
                    compiler_params=PARAMS,
                    name="impulse",
                )(scalars, impulse)
                return in_order, merged[0]
            own = merged[0]
            came = trade(merged[1], merged[2])

    return on_device


def solution(mesh):
    placed = (
        P(None, "layer", "sub"),
        P("layer", "sub"),
        P(None, "layer", "sub"),
        P("layer", "sub"),
        P(None, "layer", "sub"),
        P(None, "layer", "sub"),
        P(None, "layer", "sub"),
    )
    return jax.shard_map(
        make(mesh.shape["sub"], mesh.shape["layer"]),
        mesh=mesh,
        in_specs=placed,
        out_specs=(P(None, "layer", "sub"), P(None, "layer", "sub")),
        check_vma=False,
    )
```

```python
import jax
import jax.numpy as jnp
from jax import lax
from jax.experimental import pallas as pl
from jax.experimental.pallas import tpu as pltpu
from jax.sharding import PartitionSpec as P

WIN = 4
SWEEPS = 3
NCOLOR = 4
TILE = 128
LANES = 128
WIDE = 256
GROUP = 4

relaxation = 0.7
friction = 0.6
tangent_floor = 0.1

AXES = ("sub", "layer")
F32 = jnp.float32
BF16 = jnp.bfloat16
VMEM_SPEC = pl.BlockSpec(memory_space=pltpu.VMEM)
SMEM_SPEC = pl.BlockSpec(memory_space=pltpu.SMEM)
PARAMS = pltpu.CompilerParams(vmem_limit_bytes=16 << 20)


def neighbour_matchings(subs, layers):
    assert subs % 2 == 0 and layers % 2 == 0

    def shifted(i):
        return i - 1 if i % 2 == 0 else i + 1

    def partner(match, s, y):
        if match == 0:
            return s ^ 1, y
        if match == 1:
            return (s, y ^ 1) if s in (0, subs - 1) else (shifted(s), y)
        if match == 2:
            return s, y ^ 1
        return (s ^ 1, y) if y in (0, layers - 1) else (s, shifted(y))

    out = []
    for match in range(4):
        pairs = []
        for s in range(subs):
            for y in range(layers):
                ps, py = partner(match, s, y)
                pairs.append((s * layers + y, ps * layers + py))
        out.append(pairs)
    return out


def relay_shuffle(subs, layers, k):
    return [
        (s * layers + y, (s ^ k) * layers + y) for s in range(subs) for y in range(layers)
    ]


def lane_iota():
    return lax.broadcasted_iota(jnp.int32, (8, LANES), 1)


def pick(tables, index):
    low = jnp.bitwise_and(index, LANES - 1)
    high = jnp.right_shift(index, 7)
    out = jnp.take_along_axis(tables[0], low, axis=1)
    for h in range(1, len(tables)):
        out = jnp.where(high == h, jnp.take_along_axis(tables[h], low, axis=1), out)
    return out


def two_parts(value):
    first = value.astype(BF16).astype(F32)
    return jnp.concatenate([first, value - first], axis=0).astype(BF16)


def equal_rows(row, count):
    shape = (count, row.shape[1])
    ids = lax.broadcasted_iota(jnp.int32, shape, 0).astype(F32).astype(BF16)
    here = jnp.broadcast_to(row.astype(F32), shape).astype(BF16)
    return jnp.where(ids == here, jnp.ones(shape, BF16), jnp.zeros(shape, BF16))


def high_masks(index_row, highs):
    shape = (16, LANES)
    high = jnp.broadcast_to(jnp.right_shift(index_row, 7).astype(F32), shape).astype(BF16)
    one, zero = jnp.ones(shape, BF16), jnp.zeros(shape, BF16)
    return jnp.concatenate(
        [jnp.where(high == jnp.full(shape, h, BF16), one, zero) for h in range(highs)], axis=0
    )


def low_onehot(index_row):
    return equal_rows(jnp.bitwise_and(index_row, LANES - 1), LANES)


def contract_lanes(lhs, rhs):
    return lax.dot_general(
        lhs, rhs, (((1,), (1,)), ((), ())), preferred_element_type=F32
    )


def sum_parts(block, h):
    return block[16 * h : 16 * h + 8] + block[16 * h + 8 : 16 * h + 16]


def cross(u, v):
    return [
        u[1] * v[2] - u[2] * v[1],
        u[2] * v[0] - u[0] * v[2],
        u[0] * v[1] - u[1] * v[0],
    ]


def dot3(u, v):
    return u[0] * v[0] + u[1] * v[1] + u[2] * v[2]


def halves(low, high, half):
    return jnp.where(lane_iota() < half, low, high)


def parities():
    sub = lax.axis_index("sub")
    layer = lax.axis_index("layer")
    return sub, layer, lax.rem(sub, 2) == 0, lax.rem(layer, 2) == 0


def prepare_kernel(
    geo_hbm, dest_hbm, vel_hbm, inertia_hbm, exports_hbm, pairs_hbm, colors_hbm,
    send0, place2, place3, out0, out1, start_own, export_index, hot, own_mask, tall,
    ordered, index_out, used, scalars_out,
    geo, dest, vel, inertia, exports, pairs, colors, scalars, listed, dense, mask, lhs, sems,
):
    copies = [
        pltpu.make_async_copy(src, dst, sems.at[i])
        for i, (src, dst) in enumerate(
            [
                (exports_hbm, exports),
                (vel_hbm, vel),
                (inertia_hbm, inertia),
                (dest_hbm, dest),
                (colors_hbm, colors),
                (pairs_hbm, pairs),
                (geo_hbm, geo),
            ]
        )
    ]
    for copy in copies:
        copy.start()
    count = geo.shape[2]
    tiles = count // TILE
    slots = place2.shape[0] // 10
    bodies = vel.shape[2]
    interface = exports.shape[2]
    sub, layer, sub_even, layer_even = parities()
    member = lax.rem(sub, WIN)
    start_own[...] = jnp.zeros_like(start_own)
    dense[...] = jnp.zeros_like(dense)
    for copy in copies[:6]:
        copy.wait()
    for r in range(6):
        start_own[r : r + 1, :] = vel[r]
    for r in range(4):
        start_own[8 + r : 9 + r, :] = inertia[r]
    listed[0:1, 0:interface] = exports[0]
    listed[0:1, interface : 2 * interface] = exports[1]
    listed[1:2, 0:interface] = exports[1]
    listed[1:2, interface : 2 * interface] = exports[0]
    listed[2:3, 0:interface] = exports[2]
    listed[2:3, interface : 2 * interface] = exports[3]
    listed[3:4, 0:interface] = exports[3]
    listed[3:4, interface : 2 * interface] = exports[2]
    row0 = jnp.where(sub_even, listed[1:2, :], listed[0:1, :])
    row1 = jnp.where(layer_even, listed[3:4, :], listed[2:3, :])
    idx0 = jnp.broadcast_to(row0, (8, LANES))
    idx1 = jnp.broadcast_to(row1, (8, LANES))
    export_index[0:8, :] = idx0
    export_index[8:16, :] = idx1
    blocks = bodies // LANES
    for base in (0, 8):
        tables = [
            start_own[base : base + 8, h * LANES : (h + 1) * LANES] for h in range(blocks)
        ]
        picked = pick(tables, idx0)
        out0[base : base + 8, :] = picked
        send0[10 * slots + base : 10 * slots + base + 8, :] = picked
        out1[base : base + 8, :] = pick(tables, idx1)
    rank = used.shape[0]
    for i in range(rank):
        scalars[i] = tiles
    for k in range(NCOLOR):
        scalars[FILLED + k] = 0
    colored, ranks = [], []
    for t in range(tiles):
        color = colors[0, t]
        rank_here = scalars[FILLED + color]
        scalars[FILLED + color] = rank_here + 1
        colored.append(color)
        ranks.append(rank_here)
    over = jnp.int32(0)
    for k in range(NCOLOR):
        scalars[OVER_BASE + k] = (NCOLOR + over) * GROUP - GROUP
        scalars[OVER_FROM + k] = over
        filled = scalars[FILLED + k]
        over = over + jnp.right_shift(jnp.maximum(filled - 1, GROUP - 1), GROUP.bit_length() - 1)
        scalars[OVER_TO + k] = over
    place = []
    for t in range(tiles):
        base = jnp.where(ranks[t] < GROUP, GROUP * colored[t], scalars[OVER_BASE + colored[t]])
        place.append(base + ranks[t])
        scalars[place[t]] = t
    index_out[...] = jnp.zeros_like(index_out)
    ordered[...] = jnp.zeros_like(ordered)
    used[...] = jnp.zeros_like(used)
    flip_sub = jnp.where(sub_even, interface, 0)
    flip_layer = jnp.where(layer_even, interface, 0)
    for t in range(tiles):
        span = slice(t * TILE, (t + 1) * TILE)
        nearer = pairs[0, :, span]
        other = pairs[1, :, span]
        ghost = other - bodies
        turned = jnp.where(
            ghost < 2 * interface,
            jnp.bitwise_xor(ghost, flip_sub),
            jnp.bitwise_xor(ghost, flip_layer),
        )
        farther = jnp.where(ghost < 0, other, bodies + turned)
        scalars[TILE_SLOT + t] = place[t]
        ordered[t : t + 1, :] = nearer
        ordered[16 + t : 17 + t, :] = farther
        index_out[pl.ds(place[t], 1), :] = nearer
        index_out[pl.ds(rank + place[t], 1), :] = farther
        used[pl.ds(place[t], 1), :] = jnp.ones((1, LANES), F32)
    slot = dest[...] - (sub - member) * count
    target = jnp.zeros_like(slot)
    for m in range(1, WIN):
        target = target + jnp.where(slot >= m * count, 1, 0)
    within = slot - target * count
    row_id = jnp.bitwise_xor(target, member) * 8 + jnp.right_shift(within, 8)
    low = jnp.bitwise_and(within, WIDE - 1)
    paired = (16, TILE)
    ids = lax.broadcasted_iota(jnp.int32, paired, 0)
    ids = jnp.bitwise_and(ids, 7).astype(F32)
    one, zero = jnp.ones(paired, BF16), jnp.zeros(paired, BF16)
    for t in range(tiles):
        span = slice(t * TILE, (t + 1) * TILE)
        hot[:, span] = equal_rows(low[:, span], WIDE)
        here = jnp.broadcast_to(row_id[:, span].astype(F32), paired).astype(BF16)
        for k in range(WIN):
            chosen = jnp.where(here == (ids + 8.0 * k).astype(BF16), one, zero)
            if k == 0:
                own_mask[:, span] = chosen
            else:
                mask[16 * k - 16 : 16 * k, span] = chosen
    give = pltpu.make_async_copy(scalars, scalars_out, sems.at[7])
    give.start()
    copies[6].wait()
    for r in range(10):
        dense[r : r + 1, :] = geo[r]
    value = dense[...]
    first = value.astype(BF16).astype(F32)
    parts = [first, value - first]
    for p in range(2):
        for i in range(5):
            pair = jnp.concatenate(
                [jnp.broadcast_to(parts[p][r : r + 1, :], (8, count)) for r in (2 * i, 2 * i + 1)],
                axis=0,
            ).astype(BF16)
            tall[p, 16 * i : 16 * i + 16, :] = pair
            for k in range(1, WIN):
                at = 80 * (k - 1) + 16 * i
                lhs[p, at : at + 16, :] = mask[16 * k - 16 : 16 * k, :] * pair
    total = contract_lanes(lhs[0], hot[...]) + contract_lanes(lhs[1], hot[...])
    for k, out in enumerate((send0, place2, place3)):
        store_placed(out, total[80 * k : 80 * k + 80, :])
    give.wait()


def store_placed(out, total):
    for r in range(10):
        for side in range(2):
            out[16 * r + 8 * side : 16 * r + 8 * side + 8, :] = total[
                8 * r : 8 * r + 8, side * LANES : (side + 1) * LANES
            ]


def place_kernel(tall, own_mask, hot, out):
    left = [jnp.concatenate([own_mask[...]] * 5, axis=0) * tall[p] for p in range(2)]
    store_placed(out, contract_lanes(left[0], hot[...]) + contract_lanes(left[1], hot[...]))


TILE_SLOT, OVER_FROM, FILLED, OVER_TO, OVER_BASE = 32, 48, 52, 56, 60


def overflow_groups(tiles):
    most = 0
    for busy in range(1, NCOLOR + 1):
        spare = tiles - busy * (GROUP + 1)
        if spare >= 0:
            most = max(most, busy + spare // GROUP)
    return most


def slot_count(tiles):
    return -(-GROUP * (NCOLOR + overflow_groups(tiles)) // 8) * 8


def index_kernel(
    subs, layers, interface, bodies, ordered, export_index, own,
    hot, masks, export_hot, export_masks, mult, near_props, far_props,
):
    tiles = masks.shape[0] - 1
    blocks = bodies // LANES
    total = blocks + 4 * interface // LANES
    sub, layer, sub_even, layer_even = parities()
    props = [own[8:16, h * LANES : (h + 1) * LANES] for h in range(blocks)]
    square = (TILE, LANES)
    lane_ids = lax.broadcasted_iota(jnp.int32, square, 1)
    eye = jnp.where(lax.broadcasted_iota(jnp.int32, square, 0) == lane_ids, 1.0, 0.0)
    lane_ids = lane_ids.astype(F32)
    low_rows = jnp.bitwise_and(ordered[...], LANES - 1).astype(F32).astype(BF16)
    columns = contract_lanes(eye.astype(BF16), low_rows).astype(BF16)
    ids = lax.broadcasted_iota(jnp.int32, (32, 2 * TILE), 0)
    lanes = lax.broadcasted_iota(jnp.int32, (32, 2 * TILE), 1)
    for t in range(tiles):
        first = ordered[t : t + 1, :]
        second = ordered[16 + t : 17 + t, :]
        near_props[8 * t : 8 * t + 8, :] = pick(props, jnp.broadcast_to(first, (8, LANES)))
        far_props[8 * t : 8 * t + 8, :] = pick(props, jnp.broadcast_to(second, (8, LANES)))
        sides = jnp.where(lanes < TILE, t, 16 + t)
        chosen = jnp.where(ids == sides, 1.0, 0.0).astype(BF16)
        low = jnp.dot(columns, chosen, preferred_element_type=F32)
        for side in range(2):
            hit = low[:, side * TILE : (side + 1) * TILE] == lane_ids
            at = (2 * t + side) * TILE
            hot[at : at + TILE, :] = jnp.where(hit, 1.0, 0.0).astype(BF16)
        masks[t, : 16 * blocks, :] = high_masks(first, blocks)
        masks[t, 16 * blocks :, :] = high_masks(second, total)
    hot[2 * tiles * TILE :, :] = jnp.zeros((2 * TILE, LANES), BF16)
    masks[tiles] = jnp.zeros_like(masks[tiles])
    inner_sub = jnp.where(jnp.logical_and(sub > 0, sub < subs - 1), 1.0, 0.0)
    inner_layer = jnp.where(jnp.logical_and(layer > 0, layer < layers - 1), 1.0, 0.0)
    lane = lane_iota()
    weights = [
        jnp.where(lane < interface, 1.0, inner_sub),
        jnp.where(lane < interface, 1.0, inner_layer),
    ]
    left = []
    for i in range(2):
        row = export_index[8 * i : 8 * i + 1, :]
        export_hot[:, i * LANES : (i + 1) * LANES] = low_onehot(row)
        chosen = high_masks(row, blocks)
        export_masks[i] = chosen
        weight = jnp.concatenate([weights[i], jnp.zeros_like(weights[i])], axis=0).astype(BF16)
        left.append(jnp.concatenate([weight] * blocks, axis=0) * chosen)
    listed = contract_lanes(jnp.concatenate(left, axis=1), export_hot[...])
    for h in range(blocks):
        mult[:, h * LANES : (h + 1) * LANES] = 1.0 + listed[16 * h : 16 * h + 8]


STATE = 34


def contact_state(geo, first, second):
    raw = geo[0:3]
    length = jnp.sqrt(dot3(raw, raw))
    normal = [x / length for x in raw]
    side = jnp.sqrt(normal[1] * normal[1] + normal[2] * normal[2])
    tan_y = normal[2] / side
    tan_z = -normal[1] / side
    two = [
        normal[1] * tan_z - normal[2] * tan_y,
        -normal[0] * tan_z,
        normal[0] * tan_y,
    ]

    def arm(p, spin):
        return [
            spin[1] * p[2] * p[2] + spin[2] * p[1] * p[1],
            spin[0] * p[2] * p[2] + spin[2] * p[0] * p[0],
            spin[0] * p[1] * p[1] + spin[1] * p[0] * p[0],
            -spin[2] * p[0] * p[1],
            -spin[1] * p[0] * p[2],
            -spin[0] * p[1] * p[2],
        ]

    arm_a, arm_b = geo[3:6], geo[6:9]
    e = [x + y for x, y in zip(arm(arm_a, first[1:4]), arm(arm_b, second[1:4]))]
    mass = first[0] + second[0]
    xx, yy, zz = mass + e[0], mass + e[1], mass + e[2]
    xy, xz, yz = e[3], e[4], e[5]
    c_xx = yy * zz - yz * yz
    c_xy = xz * yz - xy * zz
    c_xz = xy * yz - xz * yy
    c_yy = xx * zz - xz * xz
    c_yz = xy * xz - xx * yz
    c_zz = xx * yy - xy * xy
    det = xx * c_xx + xy * c_xy + xz * c_xz
    inv = [
        [c_xx / det, c_xy / det, c_xz / det],
        [c_xy / det, c_yy / det, c_yz / det],
        [c_xz / det, c_yz / det, c_zz / det],
    ]
    solve = []
    for row in (normal, None, two):
        for j in range(3):
            if row is None:
                value = tan_y * inv[1][j] + tan_z * inv[2][j]
            else:
                value = row[0] * inv[0][j] + row[1] * inv[1][j] + row[2] * inv[2][j]
            solve.append(relaxation * value)
    bias = [geo[9] * dot3(solve[3 * i : 3 * i + 3], normal) for i in range(3)]
    return (
        solve + bias + normal + [tan_y, tan_z] + two + arm_a + arm_b + list(first) + list(second)
    )


def sweep_kernel(bodies, interface, first_sweep, *refs):
    scalars_in, index, used, hot, masks = refs[:5]
    refs = refs[5:]
    if first_sweep:
        own, g1, r1, r2, r3, g0, g2, g3, ordered, near_props, far_props, state = refs[:12]
        refs = refs[12:]
        r0 = g1.at[pl.ds(g0.shape[0], 16), :]
    else:
        own, r0, r1, r2, r3, state, impulse_in = refs[:7]
        refs = refs[7:]
    impulse, own_change, ghost0, ghost1 = refs[:4]
    got_a, got_b, push_a, push_b, acc, table, all_a, all_b, gathered, placed, scalars, sem = refs[4:]
    slots = used.shape[0]
    tiles = masks.shape[0] - 1
    blocks = bodies // LANES
    total = blocks + (4 * interface) // LANES
    fetch = pltpu.make_async_copy(scalars_in, scalars, sem)
    fetch.start()

    def ghost_blocks(base):
        return [
            halves(r0[base : base + 8, :], r1[base : base + 8, :], interface),
            halves(r2[base : base + 8, :], r3[base : base + 8, :], interface),
        ]

    start = [own[0:8, h * LANES : (h + 1) * LANES] for h in range(blocks)] + ghost_blocks(0)
    for h in range(total):
        table[8 * h : 8 * h + 8, :] = start[h]
    push_a[...] = jnp.zeros_like(push_a)
    push_b[...] = jnp.zeros_like(push_b)

    if first_sweep:
        ghost_props = ghost_blocks(8)
        far = []
        for t in range(tiles):
            ib = jnp.broadcast_to(ordered[16 + t : 17 + t, :], (8, LANES))
            low, high = jnp.bitwise_and(ib, LANES - 1), jnp.right_shift(ib, 7)
            value = far_props[8 * t : 8 * t + 8, :]
            for h, block in enumerate(ghost_props):
                value = jnp.where(
                    high == blocks + h, jnp.take_along_axis(block, low, axis=1), value
                )
            far.append(value)
        all_a[...] = jnp.ones_like(all_a)
        all_b[...] = jnp.ones_like(all_b)
        gathered[...] = (g0[...] + g1[0 : g0.shape[0], :]) + (g2[...] + g3[...])
        placed[...] = jnp.ones_like(placed)
        fetch.wait()
        rows = g0.shape[0] // 10
        for t in range(tiles):
            slot = scalars[TILE_SLOT + t]
            group_rows = pl.ds(pl.multiple_of(8 * slot, 8), 8)
            all_a[group_rows, :] = near_props[8 * t : 8 * t + 8, :]
            all_b[group_rows, :] = far[t]
            at = 8 * (t % 2) + t // 2
            for c in range(10):
                row = c * rows + at
                placed[pl.ds(c * slots + slot, 1), :] = gathered[row : row + 1, :]
        first = [all_a[pl.ds(c, slots, stride=8), :] for c in range(4)]
        second = [all_b[pl.ds(c, slots, stride=8), :] for c in range(4)]
        geo = [placed[c * slots : (c + 1) * slots, :] for c in range(10)]
        for c, value in enumerate(contact_state(geo, first, second)):
            state[c * slots : (c + 1) * slots, :] = value
        impulse[...] = jnp.zeros_like(impulse)
    else:
        impulse[...] = impulse_in[...]

    def held_at(base):
        return lambda c: state[pl.ds(c * slots + base, GROUP), :]

    def gather(base, room, now):
        for j in range(GROUP):
            ia = jnp.broadcast_to(index[pl.ds(base + j, 1), :], (8, LANES))
            ib = jnp.broadcast_to(index[pl.ds(slots + base + j, 1), :], (8, LANES))
            got_a[room + 8 * j : room + 8 * j + 8, :] = pick(now[:blocks], ia)
            got_b[room + 8 * j : room + 8 * j + 8, :] = pick(now, ib)

    def press(base, room):
        held = held_at(base)
        tile_rows = [pl.ds(room + c, GROUP, stride=8) for c in range(6)]
        va = [got_a[tile_rows[c], :] for c in range(6)]
        vb = [got_b[tile_rows[c], :] for c in range(6)]
        arm_a = [held(20 + c) for c in range(3)]
        arm_b = [held(23 + c) for c in range(3)]
        turn_a = cross(va[3:6], arm_a)
        turn_b = cross(vb[3:6], arm_b)
        rel = [((va[c] + turn_a[c]) - vb[c]) - turn_b[c] for c in range(3)]
        old = [impulse[pl.ds(c * slots + base, GROUP), :] for c in range(3)]
        trial = [
            old[c] - (dot3([held(3 * c + j) for j in range(3)], rel) + held(9 + c))
            for c in range(3)
        ]
        normal_part = jnp.maximum(trial[0], 0.0)
        slide = trial[1] * trial[1] + trial[2] * trial[2]
        shrink = lax.rsqrt(jnp.maximum(slide, tangent_floor * tangent_floor))
        factor = jnp.minimum(1.0, friction * normal_part * shrink)
        active = used[pl.ds(base, GROUP), :] > 0.5
        new = [
            jnp.where(active, normal_part, old[0]),
            jnp.where(active, trial[1] * factor, old[1]),
            jnp.where(active, trial[2] * factor, old[2]),
        ]
        change = [new[c] - old[c] for c in range(3)]
        for c in range(3):
            impulse[pl.ds(c * slots + base, GROUP), :] = new[c]
        force = [
            held(12) * change[0] + held(17) * change[2],
            held(13) * change[0] + held(15) * change[1] + held(18) * change[2],
            held(14) * change[0] + held(16) * change[1] + held(19) * change[2],
        ]
        spin_a = cross(arm_a, force)
        spin_b = cross(arm_b, force)
        for c in range(3):
            push_a[tile_rows[c], :] = held(26) * force[c]
            push_a[tile_rows[3 + c], :] = held(27 + c) * spin_a[c]
            push_b[tile_rows[c], :] = -(held(30) * force[c])
            push_b[tile_rows[3 + c], :] = -(held(31 + c) * spin_b[c])

    def sides(base, room):
        left, right = [], []
        empty = jnp.zeros((16 * (total - blocks), LANES), BF16)
        for j in range(GROUP):
            t = scalars[base + j]
            first = two_parts(push_a[room + 8 * j : room + 8 * j + 8, :])
            second = two_parts(push_b[room + 8 * j : room + 8 * j + 8, :])
            rows = [masks[t, 16 * m : 16 * m + 16, :] for m in range(blocks + total)]
            left.append(jnp.concatenate([first * m for m in rows[:blocks]] + [empty], axis=0))
            left.append(jnp.concatenate([second * m for m in rows[blocks:]], axis=0))
            right.append(hot[pl.ds(pl.multiple_of(2 * TILE * t, 2 * TILE), 2 * TILE), :])
        return left, right

    def groups(bases, now, before=None):
        rooms = [8 * GROUP * i for i in range(len(bases))]
        for base, room in zip(bases, rooms):
            gather(base, room, now)
        for base, room in zip(bases, rooms):
            press(base, room)
        if before is not None:
            before()
        left, right = [], []
        for base, room in zip(bases, rooms):
            more_left, more_right = sides(base, room)
            left += more_left
            right += more_right
        return jnp.dot(
            jnp.concatenate(left, axis=1),
            jnp.concatenate(right, axis=0),
            preferred_element_type=F32,
        )

    def color_pass(k, before=None):
        now = [table[8 * h : 8 * h + 8, :] for h in range(total)]
        main = pl.multiple_of(GROUP * k, GROUP)

        def over(g):
            return pl.multiple_of(GROUP * (NCOLOR + g), GROUP)

        if before is not None:
            acc[...] = groups([main], now, before)
        begin, end = scalars[OVER_FROM + k], scalars[OVER_TO + k]
        if before is None:

            @pl.when(end > begin)
            def _():
                acc[...] = groups([main, over(begin)], now)

            @pl.when(end <= begin)
            def _():
                acc[...] = groups([main], now)

            begin = begin + 1

        def more(g, c):
            acc[...] += groups([over(g)], now)
            return c

        lax.fori_loop(begin, end, more, 0)
        for h in range(total):
            table[8 * h : 8 * h + 8, :] = now[h] + sum_parts(acc, h)

    def later_pass(k, carry):
        color_pass(k)
        return carry

    color_pass(0, None if first_sweep else fetch.wait)
    lax.fori_loop(1, NCOLOR, later_pass, 0)
    for h in range(blocks):
        own_change[:, h * LANES : (h + 1) * LANES] = table[8 * h : 8 * h + 8, :] - start[h]
    ghost0[...] = table[8 * blocks : 8 * blocks + 8, :] - start[blocks]
    ghost1[...] = table[8 * blocks + 8 : 8 * blocks + 16, :] - start[blocks + 1]


def impulse_kernel(scalars, held, impulse):
    slots = held.shape[0] // 3
    for t in range(impulse.shape[2] // TILE):
        slot = scalars[TILE_SLOT + t]
        for c in range(3):
            impulse[c, :, t * TILE : (t + 1) * TILE] = held[pl.ds(c * slots + slot, 1), :]


def merge_kernel(
    interface, last_sweep, own, change, c0, c1, c2, c3, mult, export_index, export_hot,
    export_masks, *refs,
):
    blocks = own.shape[1] // LANES
    came = [halves(c0[...], c1[...], interface), halves(c2[...], c3[...], interface)]
    left = jnp.concatenate(
        [
            jnp.concatenate([two_parts(came[i])] * blocks, axis=0) * export_masks[i]
            for i in range(2)
        ],
        axis=1,
    )
    incoming = contract_lanes(left, export_hot[...])
    fresh = []
    for h in range(blocks):
        span = slice(h * LANES, (h + 1) * LANES)
        fresh.append(
            own[0:8, span] + (change[:, span] + sum_parts(incoming, h)) / mult[:, span]
        )
    if last_sweep:
        (velocity,) = refs
        for r in range(6):
            for h in range(blocks):
                velocity[r, :, h * LANES : (h + 1) * LANES] = fresh[h][r : r + 1, :]
    else:
        fresh_own, out0, out1 = refs
        for h in range(blocks):
            fresh_own[:, h * LANES : (h + 1) * LANES] = fresh[h]
        out0[...] = pick(fresh, export_index[0:8, :])
        out1[...] = pick(fresh, export_index[8:16, :])


def in_hbm(array):
    return pltpu.with_memory_space_constraint(array, pltpu.HBM)


def shape(dims, dtype=F32):
    return jax.ShapeDtypeStruct(dims, dtype)


def make(subs, layers):
    matchings = neighbour_matchings(subs, layers)
    shuffles = [relay_shuffle(subs, layers, k) for k in range(WIN)]

    def trade(low, high):
        return [
            lax.ppermute(low if m < 2 else high, AXES, matchings[m]) for m in range(4)
        ]

    def on_device(geometry, dest_slot, pairs, colors, free_vel, inertia, exports):
        count = geometry.shape[2]
        bodies = free_vel.shape[2]
        interface = exports.shape[2]
        tiles = count // TILE
        slots = 16
        assert count % TILE == 0 and tiles < slots and 2 * interface == LANES
        assert bodies % LANES == 0
        blocks = bodies // LANES
        total = blocks + 2
        place = shape((10 * slots, LANES))
        small = shape((16, LANES))
        arguments = (geometry, dest_slot, free_vel, inertia, exports, pairs, colors)
        rows = slot_count(tiles)
        assert rows <= TILE_SLOT
        prepared = pl.pallas_call(
            prepare_kernel,
            out_shape=(
                shape((10 * slots + 16, LANES)), place, place, small, small,
                shape((16, bodies)),
                shape((16, LANES), jnp.int32),
                shape((WIDE, count), BF16),
                shape((16, count), BF16),
                shape((2, 80, count), BF16),
                shape((32, LANES), jnp.int32),
                shape((2 * rows, LANES), jnp.int32),
                shape((rows, LANES)),
                shape((64,), jnp.int32),
            ),
            in_specs=[pl.BlockSpec(memory_space=pltpu.HBM)] * 7,
            out_specs=(VMEM_SPEC,) * 14,
            scratch_shapes=[
                pltpu.VMEM(geometry.shape, F32),
                pltpu.VMEM(dest_slot.shape, jnp.int32),
                pltpu.VMEM(free_vel.shape, F32),
                pltpu.VMEM(inertia.shape, F32),
                pltpu.VMEM(exports.shape, jnp.int32),
                pltpu.VMEM(pairs.shape, jnp.int32),
                pltpu.SMEM(colors.shape, jnp.int32),
                pltpu.SMEM((64,), jnp.int32),
                pltpu.VMEM((8, LANES), jnp.int32),
                pltpu.VMEM((16, count), F32),
                pltpu.VMEM((16 * (WIN - 1), count), BF16),
                pltpu.VMEM((2, 80 * (WIN - 1), count), BF16),
                pltpu.SemaphoreType.DMA((8,)),
            ],
            compiler_params=PARAMS,
            name="prepare",
        )(*[in_hbm(x) for x in arguments])
        send0, place2, place3, out0, out1, own, export_index = prepared[:7]
        wide_hot, own_mask, tall, ordered, index, used, scalars = prepared[7:]
        came = [lax.ppermute(send0, AXES, matchings[0])]
        came.append(lax.ppermute(out0, AXES, matchings[1]))
        came.append(lax.ppermute(out1, AXES, matchings[2]))
        came.append(lax.ppermute(out1, AXES, matchings[3]))
        place0 = pl.pallas_call(
            place_kernel,
            out_shape=place,
            in_specs=[VMEM_SPEC] * 3,
            out_specs=VMEM_SPEC,
            compiler_params=PARAMS,
            name="place",
        )(tall, own_mask, wide_hot)
        placed = [place0]
        placed.append(lax.ppermute(place2, AXES, shuffles[2]))
        placed.append(lax.ppermute(place3, AXES, shuffles[3]))

        def indexing(*refs):
            index_kernel(subs, layers, interface, bodies, *refs)

        hot, masks, export_hot, export_masks, mult, near_props, far_props = pl.pallas_call(
            indexing,
            out_shape=(
                shape((2 * TILE * (tiles + 1), LANES), BF16),
                shape((tiles + 1, 16 * (blocks + total), LANES), BF16),
                shape((LANES, 2 * LANES), BF16),
                shape((2, 16 * blocks, LANES), BF16),
                shape((8, bodies)),
                shape((8 * tiles, LANES)),
                shape((8 * tiles, LANES)),
            ),
            in_specs=[VMEM_SPEC] * 3,
            out_specs=(VMEM_SPEC,) * 7,
            compiler_params=PARAMS,
            name="indexing",
        )(ordered, export_index, own)

        state = impulse = None
        for sweep in range(SWEEPS):
            first, last = sweep == 0, sweep == SWEEPS - 1

            def run(*refs, first=first):
                sweep_kernel(bodies, interface, first, *refs)

            outs = [
                shape((3 * rows, LANES)),
                shape((8, bodies)),
                shape((8, LANES)),
                shape((8, LANES)),
            ]
            operands = [scalars, index, used, hot, masks, own, *came]
            if first:
                outs = [shape((STATE * rows, LANES))] + outs
                operands += [*placed, ordered, near_props, far_props]
            else:
                operands += [state, impulse]
            result = pl.pallas_call(
                run,
                out_shape=tuple(outs),
                in_specs=[VMEM_SPEC] * len(operands),
                out_specs=(VMEM_SPEC,) * len(outs),
                scratch_shapes=[
                    pltpu.VMEM((16 * GROUP, LANES), F32),
                    pltpu.VMEM((16 * GROUP, LANES), F32),
                    pltpu.VMEM((16 * GROUP, LANES), F32),
                    pltpu.VMEM((16 * GROUP, LANES), F32),
                    pltpu.VMEM((16 * total, LANES), F32),
                    pltpu.VMEM((8 * total, LANES), F32),
                    pltpu.VMEM((8 * rows, LANES), F32),
                    pltpu.VMEM((8 * rows, LANES), F32),
                    pltpu.VMEM((10 * slots, LANES), F32),
                    pltpu.VMEM((10 * rows, LANES), F32),
                    pltpu.SMEM((64,), jnp.int32),
                    pltpu.SemaphoreType.DMA,
                ],
                compiler_params=PARAMS,
                name="sweep",
            )(*operands)
            if first:
                state, result = result[0], result[1:]
            impulse, change, ghost0, ghost1 = result
            sums = trade(ghost0, ghost1)

            def merge(*refs, last=last):
                merge_kernel(interface, last, *refs)

            operands = [own, change, *sums, mult, export_index, export_hot, export_masks]
            if last:
                outs = (shape((6, 1, bodies)),)
            else:
                outs = (shape((8, bodies)), shape((8, LANES)), shape((8, LANES)))
            merged = pl.pallas_call(
                merge,
                out_shape=outs,
                in_specs=[VMEM_SPEC] * len(operands),
                out_specs=(VMEM_SPEC,) * len(outs),
                compiler_params=PARAMS,
                name="merge",
            )(*operands)
            if last:
                in_order = pl.pallas_call(
                    impulse_kernel,
                    out_shape=shape((3, 1, count)),
                    in_specs=[SMEM_SPEC, VMEM_SPEC],
                    out_specs=VMEM_SPEC,
                    compiler_params=PARAMS,
                    name="impulse",
                )(scalars, impulse)
                return in_order, merged[0]
            own = merged[0]
            came = trade(merged[1], merged[2])

    return on_device


def solution(mesh):
    placed = (
        P(None, "layer", "sub"),
        P("layer", "sub"),
        P(None, "layer", "sub"),
        P("layer", "sub"),
        P(None, "layer", "sub"),
        P(None, "layer", "sub"),
        P(None, "layer", "sub"),
    )
    return jax.shard_map(
        make(mesh.shape["sub"], mesh.shape["layer"]),
        mesh=mesh,
        in_specs=placed,
        out_specs=(P(None, "layer", "sub"), P(None, "layer", "sub")),
        check_vma=False,
    )
```

```python
import jax
import jax.numpy as jnp
from jax import lax
from jax.experimental import pallas as pl
from jax.experimental.pallas import tpu as pltpu
from jax.sharding import PartitionSpec as P

WIN = 4
SWEEPS = 3
NCOLOR = 4
TILE = 128
LANES = 128
WIDE = 256
GROUP = 4

relaxation = 0.7
friction = 0.6
tangent_floor = 0.1

AXES = ("sub", "layer")
F32 = jnp.float32
BF16 = jnp.bfloat16
VMEM_SPEC = pl.BlockSpec(memory_space=pltpu.VMEM)
SMEM_SPEC = pl.BlockSpec(memory_space=pltpu.SMEM)
PARAMS = pltpu.CompilerParams(vmem_limit_bytes=16 << 20)


def neighbour_matchings(subs, layers):
    assert subs % 2 == 0 and layers % 2 == 0

    def shifted(i):
        return i - 1 if i % 2 == 0 else i + 1

    def partner(match, s, y):
        if match == 0:
            return s ^ 1, y
        if match == 1:
            return (s, y ^ 1) if s in (0, subs - 1) else (shifted(s), y)
        if match == 2:
            return s, y ^ 1
        return (s ^ 1, y) if y in (0, layers - 1) else (s, shifted(y))

    out = []
    for match in range(4):
        pairs = []
        for s in range(subs):
            for y in range(layers):
                ps, py = partner(match, s, y)
                pairs.append((s * layers + y, ps * layers + py))
        out.append(pairs)
    return out


def relay_shuffle(subs, layers, k):
    return [
        (s * layers + y, (s ^ k) * layers + y) for s in range(subs) for y in range(layers)
    ]


def lane_iota():
    return lax.broadcasted_iota(jnp.int32, (8, LANES), 1)


def pick(tables, index):
    low = jnp.bitwise_and(index, LANES - 1)
    high = jnp.right_shift(index, 7)
    out = jnp.take_along_axis(tables[0], low, axis=1)
    for h in range(1, len(tables)):
        out = jnp.where(high == h, jnp.take_along_axis(tables[h], low, axis=1), out)
    return out


def two_parts(value):
    first = value.astype(BF16).astype(F32)
    return jnp.concatenate([first, value - first], axis=0).astype(BF16)


def equal_rows(row, count):
    shape = (count, row.shape[1])
    ids = lax.broadcasted_iota(jnp.int32, shape, 0).astype(F32).astype(BF16)
    here = jnp.broadcast_to(row.astype(F32), shape).astype(BF16)
    return jnp.where(ids == here, jnp.ones(shape, BF16), jnp.zeros(shape, BF16))


def high_masks(index_row, highs):
    shape = (16, LANES)
    high = jnp.broadcast_to(jnp.right_shift(index_row, 7).astype(F32), shape).astype(BF16)
    one, zero = jnp.ones(shape, BF16), jnp.zeros(shape, BF16)
    return jnp.concatenate(
        [jnp.where(high == jnp.full(shape, h, BF16), one, zero) for h in range(highs)], axis=0
    )


def low_onehot(index_row):
    return equal_rows(jnp.bitwise_and(index_row, LANES - 1), LANES)


def contract_lanes(lhs, rhs):
    return lax.dot_general(
        lhs, rhs, (((1,), (1,)), ((), ())), preferred_element_type=F32
    )


def sum_parts(block, h):
    return block[16 * h : 16 * h + 8] + block[16 * h + 8 : 16 * h + 16]


def cross(u, v):
    return [
        u[1] * v[2] - u[2] * v[1],
        u[2] * v[0] - u[0] * v[2],
        u[0] * v[1] - u[1] * v[0],
    ]


def dot3(u, v):
    return u[0] * v[0] + u[1] * v[1] + u[2] * v[2]


def halves(low, high, half):
    return jnp.where(lane_iota() < half, low, high)


def parities():
    sub = lax.axis_index("sub")
    layer = lax.axis_index("layer")
    return sub, layer, lax.rem(sub, 2) == 0, lax.rem(layer, 2) == 0


def prepare_kernel(
    geo_hbm, dest_hbm, vel_hbm, inertia_hbm, exports_hbm, pairs_hbm, colors_hbm,
    send0, place2, place3, out0, out1, start_own, export_index, hot, own_mask, tall,
    ordered, index_out, used, scalars_out,
    geo, dest, vel, inertia, exports, pairs, colors, scalars, listed, dense, mask, lhs, sems,
):
    copies = [
        pltpu.make_async_copy(src, dst, sems.at[i])
        for i, (src, dst) in enumerate(
            [
                (exports_hbm, exports),
                (vel_hbm, vel),
                (inertia_hbm, inertia),
                (dest_hbm, dest),
                (colors_hbm, colors),
                (pairs_hbm, pairs),
                (geo_hbm, geo),
            ]
        )
    ]
    for copy in copies:
        copy.start()
    count = geo.shape[2]
    tiles = count // TILE
    slots = place2.shape[0] // 10
    bodies = vel.shape[2]
    interface = exports.shape[2]
    sub, layer, sub_even, layer_even = parities()
    member = lax.rem(sub, WIN)
    start_own[...] = jnp.zeros_like(start_own)
    dense[...] = jnp.zeros_like(dense)
    for copy in copies[:6]:
        copy.wait()
    for r in range(6):
        start_own[r : r + 1, :] = vel[r]
    for r in range(4):
        start_own[8 + r : 9 + r, :] = inertia[r]
    listed[0:1, 0:interface] = exports[0]
    listed[0:1, interface : 2 * interface] = exports[1]
    listed[1:2, 0:interface] = exports[1]
    listed[1:2, interface : 2 * interface] = exports[0]
    listed[2:3, 0:interface] = exports[2]
    listed[2:3, interface : 2 * interface] = exports[3]
    listed[3:4, 0:interface] = exports[3]
    listed[3:4, interface : 2 * interface] = exports[2]
    row0 = jnp.where(sub_even, listed[1:2, :], listed[0:1, :])
    row1 = jnp.where(layer_even, listed[3:4, :], listed[2:3, :])
    idx0 = jnp.broadcast_to(row0, (8, LANES))
    idx1 = jnp.broadcast_to(row1, (8, LANES))
    export_index[0:8, :] = idx0
    export_index[8:16, :] = idx1
    blocks = bodies // LANES
    for base in (0, 8):
        tables = [
            start_own[base : base + 8, h * LANES : (h + 1) * LANES] for h in range(blocks)
        ]
        picked = pick(tables, idx0)
        out0[base : base + 8, :] = picked
        send0[10 * slots + base : 10 * slots + base + 8, :] = picked
        out1[base : base + 8, :] = pick(tables, idx1)
    rank = used.shape[0]
    for i in range(rank):
        scalars[0, i] = tiles
    for k in range(NCOLOR):
        scalars[0, FILLED + k] = 0
    colored, ranks = [], []
    for t in range(tiles):
        color = colors[0, t]
        rank_here = scalars[0, FILLED + color]
        scalars[0, FILLED + color] = rank_here + 1
        colored.append(color)
        ranks.append(rank_here)
    over = jnp.int32(0)
    for k in range(NCOLOR):
        scalars[0, OVER_BASE + k] = (NCOLOR + over) * GROUP - GROUP
        scalars[0, OVER_FROM + k] = over
        filled = scalars[0, FILLED + k]
        over = over + jnp.right_shift(jnp.maximum(filled - 1, GROUP - 1), GROUP.bit_length() - 1)
        scalars[0, OVER_TO + k] = over
    place = []
    for t in range(tiles):
        base = jnp.where(ranks[t] < GROUP, GROUP * colored[t], scalars[0, OVER_BASE + colored[t]])
        place.append(base + ranks[t])
        scalars[0, place[t]] = t
    index_out[...] = jnp.zeros_like(index_out)
    ordered[...] = jnp.zeros_like(ordered)
    used[...] = jnp.zeros_like(used)
    flip_sub = jnp.where(sub_even, interface, 0)
    flip_layer = jnp.where(layer_even, interface, 0)
    for t in range(tiles):
        span = slice(t * TILE, (t + 1) * TILE)
        nearer = pairs[0, :, span]
        other = pairs[1, :, span]
        ghost = other - bodies
        turned = jnp.where(
            ghost < 2 * interface,
            jnp.bitwise_xor(ghost, flip_sub),
            jnp.bitwise_xor(ghost, flip_layer),
        )
        farther = jnp.where(ghost < 0, other, bodies + turned)
        scalars[0, TILE_SLOT + t] = place[t]
        ordered[t : t + 1, :] = nearer
        ordered[16 + t : 17 + t, :] = farther
        index_out[pl.ds(place[t], 1), :] = nearer
        index_out[pl.ds(rank + place[t], 1), :] = farther
        used[pl.ds(place[t], 1), :] = jnp.ones((1, LANES), F32)
    slot = dest[...] - (sub - member) * count
    target = jnp.zeros_like(slot)
    for m in range(1, WIN):
        target = target + jnp.where(slot >= m * count, 1, 0)
    within = slot - target * count
    row_id = jnp.bitwise_xor(target, member) * 8 + jnp.right_shift(within, 8)
    low = jnp.bitwise_and(within, WIDE - 1)
    paired = (16, TILE)
    ids = lax.broadcasted_iota(jnp.int32, paired, 0)
    ids = jnp.bitwise_and(ids, 7).astype(F32)
    one, zero = jnp.ones(paired, BF16), jnp.zeros(paired, BF16)
    for t in range(tiles):
        span = slice(t * TILE, (t + 1) * TILE)
        hot[:, span] = equal_rows(low[:, span], WIDE)
        here = jnp.broadcast_to(row_id[:, span].astype(F32), paired).astype(BF16)
        for k in range(WIN):
            chosen = jnp.where(here == (ids + 8.0 * k).astype(BF16), one, zero)
            if k == 0:
                own_mask[:, span] = chosen
            else:
                mask[16 * k - 16 : 16 * k, span] = chosen
    give = pltpu.make_async_copy(scalars, scalars_out, sems.at[7])
    give.start()
    copies[6].wait()
    for r in range(10):
        dense[r : r + 1, :] = geo[r]
    value = dense[...]
    first = value.astype(BF16).astype(F32)
    parts = [first, value - first]
    for p in range(2):
        for i in range(5):
            pair = jnp.concatenate(
                [jnp.broadcast_to(parts[p][r : r + 1, :], (8, count)) for r in (2 * i, 2 * i + 1)],
                axis=0,
            ).astype(BF16)
            tall[p, 16 * i : 16 * i + 16, :] = pair
            for k in range(1, WIN):
                at = 80 * (k - 1) + 16 * i
                lhs[p, at : at + 16, :] = mask[16 * k - 16 : 16 * k, :] * pair
    total = contract_lanes(lhs[0], hot[...]) + contract_lanes(lhs[1], hot[...])
    for k, out in enumerate((send0, place2, place3)):
        store_placed(out, total[80 * k : 80 * k + 80, :])
    give.wait()


def store_placed(out, total):
    for r in range(10):
        for side in range(2):
            out[16 * r + 8 * side : 16 * r + 8 * side + 8, :] = total[
                8 * r : 8 * r + 8, side * LANES : (side + 1) * LANES
            ]


def place_kernel(tall, own_mask, hot, out):
    left = [jnp.concatenate([own_mask[...]] * 5, axis=0) * tall[p] for p in range(2)]
    store_placed(out, contract_lanes(left[0], hot[...]) + contract_lanes(left[1], hot[...]))


TILE_SLOT, OVER_FROM, FILLED, OVER_TO, OVER_BASE = 32, 48, 52, 56, 60


def overflow_groups(tiles):
    most = 0
    for busy in range(1, NCOLOR + 1):
        spare = tiles - busy * (GROUP + 1)
        if spare >= 0:
            most = max(most, busy + spare // GROUP)
    return most


def slot_count(tiles):
    return -(-GROUP * (NCOLOR + overflow_groups(tiles)) // 8) * 8


def index_kernel(
    subs, layers, interface, bodies, ordered, export_index, own,
    hot, masks, export_hot, export_masks, mult, near_props, far_props,
):
    tiles = masks.shape[0] - 1
    blocks = bodies // LANES
    total = blocks + 4 * interface // LANES
    sub, layer, sub_even, layer_even = parities()
    props = [own[8:16, h * LANES : (h + 1) * LANES] for h in range(blocks)]
    square = (TILE, LANES)
    lane_ids = lax.broadcasted_iota(jnp.int32, square, 1)
    eye = jnp.where(lax.broadcasted_iota(jnp.int32, square, 0) == lane_ids, 1.0, 0.0)
    lane_ids = lane_ids.astype(F32)
    low_rows = jnp.bitwise_and(ordered[...], LANES - 1).astype(F32).astype(BF16)
    columns = contract_lanes(eye.astype(BF16), low_rows).astype(BF16)
    ids = lax.broadcasted_iota(jnp.int32, (32, 2 * TILE), 0)
    lanes = lax.broadcasted_iota(jnp.int32, (32, 2 * TILE), 1)
    for t in range(tiles):
        first = ordered[t : t + 1, :]
        second = ordered[16 + t : 17 + t, :]
        near_props[8 * t : 8 * t + 8, :] = pick(props, jnp.broadcast_to(first, (8, LANES)))
        far_props[8 * t : 8 * t + 8, :] = pick(props, jnp.broadcast_to(second, (8, LANES)))
        sides = jnp.where(lanes < TILE, t, 16 + t)
        chosen = jnp.where(ids == sides, 1.0, 0.0).astype(BF16)
        low = jnp.dot(columns, chosen, preferred_element_type=F32)
        for side in range(2):
            hit = low[:, side * TILE : (side + 1) * TILE] == lane_ids
            at = (2 * t + side) * TILE
            hot[at : at + TILE, :] = jnp.where(hit, 1.0, 0.0).astype(BF16)
        masks[t, : 16 * blocks, :] = high_masks(first, blocks)
        masks[t, 16 * blocks :, :] = high_masks(second, total)
    hot[2 * tiles * TILE :, :] = jnp.zeros((2 * TILE, LANES), BF16)
    masks[tiles] = jnp.zeros_like(masks[tiles])
    inner_sub = jnp.where(jnp.logical_and(sub > 0, sub < subs - 1), 1.0, 0.0)
    inner_layer = jnp.where(jnp.logical_and(layer > 0, layer < layers - 1), 1.0, 0.0)
    lane = lane_iota()
    weights = [
        jnp.where(lane < interface, 1.0, inner_sub),
        jnp.where(lane < interface, 1.0, inner_layer),
    ]
    left = []
    for i in range(2):
        row = export_index[8 * i : 8 * i + 1, :]
        export_hot[:, i * LANES : (i + 1) * LANES] = low_onehot(row)
        chosen = high_masks(row, blocks)
        export_masks[i] = chosen
        weight = jnp.concatenate([weights[i], jnp.zeros_like(weights[i])], axis=0).astype(BF16)
        left.append(jnp.concatenate([weight] * blocks, axis=0) * chosen)
    listed = contract_lanes(jnp.concatenate(left, axis=1), export_hot[...])
    for h in range(blocks):
        mult[:, h * LANES : (h + 1) * LANES] = 1.0 + listed[16 * h : 16 * h + 8]


STATE = 34


def contact_state(geo, first, second):
    raw = geo[0:3]
    length = jnp.sqrt(dot3(raw, raw))
    normal = [x / length for x in raw]
    side = jnp.sqrt(normal[1] * normal[1] + normal[2] * normal[2])
    tan_y = normal[2] / side
    tan_z = -normal[1] / side
    two = [
        normal[1] * tan_z - normal[2] * tan_y,
        -normal[0] * tan_z,
        normal[0] * tan_y,
    ]

    def arm(p, spin):
        return [
            spin[1] * p[2] * p[2] + spin[2] * p[1] * p[1],
            spin[0] * p[2] * p[2] + spin[2] * p[0] * p[0],
            spin[0] * p[1] * p[1] + spin[1] * p[0] * p[0],
            -spin[2] * p[0] * p[1],
            -spin[1] * p[0] * p[2],
            -spin[0] * p[1] * p[2],
        ]

    arm_a, arm_b = geo[3:6], geo[6:9]
    e = [x + y for x, y in zip(arm(arm_a, first[1:4]), arm(arm_b, second[1:4]))]
    mass = first[0] + second[0]
    xx, yy, zz = mass + e[0], mass + e[1], mass + e[2]
    xy, xz, yz = e[3], e[4], e[5]
    c_xx = yy * zz - yz * yz
    c_xy = xz * yz - xy * zz
    c_xz = xy * yz - xz * yy
    c_yy = xx * zz - xz * xz
    c_yz = xy * xz - xx * yz
    c_zz = xx * yy - xy * xy
    det = xx * c_xx + xy * c_xy + xz * c_xz
    inv = [
        [c_xx / det, c_xy / det, c_xz / det],
        [c_xy / det, c_yy / det, c_yz / det],
        [c_xz / det, c_yz / det, c_zz / det],
    ]
    solve = []
    for row in (normal, None, two):
        for j in range(3):
            if row is None:
                value = tan_y * inv[1][j] + tan_z * inv[2][j]
            else:
                value = row[0] * inv[0][j] + row[1] * inv[1][j] + row[2] * inv[2][j]
            solve.append(relaxation * value)
    bias = [geo[9] * dot3(solve[3 * i : 3 * i + 3], normal) for i in range(3)]
    return (
        solve + bias + normal + [tan_y, tan_z] + two + arm_a + arm_b + list(first) + list(second)
    )


def sweep_kernel(bodies, interface, first_sweep, *refs):
    scalars_in, index, used, hot, masks = refs[:5]
    refs = refs[5:]
    if first_sweep:
        own, g1, r1, r2, r3, g0, g2, g3, ordered, near_props, far_props, state = refs[:12]
        refs = refs[12:]
        r0 = g1.at[pl.ds(g0.shape[0], 16), :]
    else:
        own, r0, r1, r2, r3, state, impulse_in = refs[:7]
        refs = refs[7:]
    impulse, own_change, ghost0, ghost1 = refs[:4]
    got_a, got_b, push_a, push_b, acc, table, all_a, all_b, gathered, placed, scalars = refs[4:]
    slots = used.shape[0]
    tiles = masks.shape[0] - 1
    blocks = bodies // LANES
    total = blocks + (4 * interface) // LANES
    values = scalars_in[...]
    wanted = list(range(slots)) + [OVER_FROM + k for k in range(NCOLOR)]
    wanted += [OVER_TO + k for k in range(NCOLOR)]
    if first_sweep:
        wanted += [TILE_SLOT + t for t in range(tiles)]
    for i in wanted:
        scalars[i] = values[0, i]

    def ghost_blocks(base):
        return [
            halves(r0[base : base + 8, :], r1[base : base + 8, :], interface),
            halves(r2[base : base + 8, :], r3[base : base + 8, :], interface),
        ]

    start = [own[0:8, h * LANES : (h + 1) * LANES] for h in range(blocks)] + ghost_blocks(0)
    for h in range(total):
        table[8 * h : 8 * h + 8, :] = start[h]
    push_a[...] = jnp.zeros_like(push_a)
    push_b[...] = jnp.zeros_like(push_b)

    if first_sweep:
        ghost_props = ghost_blocks(8)
        far = []
        for t in range(tiles):
            ib = jnp.broadcast_to(ordered[16 + t : 17 + t, :], (8, LANES))
            low, high = jnp.bitwise_and(ib, LANES - 1), jnp.right_shift(ib, 7)
            value = far_props[8 * t : 8 * t + 8, :]
            for h, block in enumerate(ghost_props):
                value = jnp.where(
                    high == blocks + h, jnp.take_along_axis(block, low, axis=1), value
                )
            far.append(value)
        all_a[...] = jnp.ones_like(all_a)
        all_b[...] = jnp.ones_like(all_b)
        gathered[...] = (g0[...] + g1[0 : g0.shape[0], :]) + (g2[...] + g3[...])
        placed[...] = jnp.ones_like(placed)
        rows = g0.shape[0] // 10
        for t in range(tiles):
            slot = scalars[TILE_SLOT + t]
            group_rows = pl.ds(pl.multiple_of(8 * slot, 8), 8)
            all_a[group_rows, :] = near_props[8 * t : 8 * t + 8, :]
            all_b[group_rows, :] = far[t]
            at = 8 * (t % 2) + t // 2
            for c in range(10):
                row = c * rows + at
                placed[pl.ds(c * slots + slot, 1), :] = gathered[row : row + 1, :]
        first = [all_a[pl.ds(c, slots, stride=8), :] for c in range(4)]
        second = [all_b[pl.ds(c, slots, stride=8), :] for c in range(4)]
        geo = [placed[c * slots : (c + 1) * slots, :] for c in range(10)]
        for c, value in enumerate(contact_state(geo, first, second)):
            state[c * slots : (c + 1) * slots, :] = value
        impulse[...] = jnp.zeros_like(impulse)
    else:
        impulse[...] = impulse_in[...]

    def held_at(base):
        return lambda c: state[pl.ds(c * slots + base, GROUP), :]

    def gather(base, room, now):
        for j in range(GROUP):
            ia = jnp.broadcast_to(index[pl.ds(base + j, 1), :], (8, LANES))
            ib = jnp.broadcast_to(index[pl.ds(slots + base + j, 1), :], (8, LANES))
            got_a[room + 8 * j : room + 8 * j + 8, :] = pick(now[:blocks], ia)
            got_b[room + 8 * j : room + 8 * j + 8, :] = pick(now, ib)

    def press(base, room):
        held = held_at(base)
        tile_rows = [pl.ds(room + c, GROUP, stride=8) for c in range(6)]
        va = [got_a[tile_rows[c], :] for c in range(6)]
        vb = [got_b[tile_rows[c], :] for c in range(6)]
        arm_a = [held(20 + c) for c in range(3)]
        arm_b = [held(23 + c) for c in range(3)]
        turn_a = cross(va[3:6], arm_a)
        turn_b = cross(vb[3:6], arm_b)
        rel = [((va[c] + turn_a[c]) - vb[c]) - turn_b[c] for c in range(3)]
        old = [impulse[pl.ds(c * slots + base, GROUP), :] for c in range(3)]
        trial = [
            old[c] - (dot3([held(3 * c + j) for j in range(3)], rel) + held(9 + c))
            for c in range(3)
        ]
        normal_part = jnp.maximum(trial[0], 0.0)
        slide = trial[1] * trial[1] + trial[2] * trial[2]
        shrink = lax.rsqrt(jnp.maximum(slide, tangent_floor * tangent_floor))
        factor = jnp.minimum(1.0, friction * normal_part * shrink)
        active = used[pl.ds(base, GROUP), :] > 0.5
        new = [
            jnp.where(active, normal_part, old[0]),
            jnp.where(active, trial[1] * factor, old[1]),
            jnp.where(active, trial[2] * factor, old[2]),
        ]
        change = [new[c] - old[c] for c in range(3)]
        for c in range(3):
            impulse[pl.ds(c * slots + base, GROUP), :] = new[c]
        force = [
            held(12) * change[0] + held(17) * change[2],
            held(13) * change[0] + held(15) * change[1] + held(18) * change[2],
            held(14) * change[0] + held(16) * change[1] + held(19) * change[2],
        ]
        spin_a = cross(arm_a, force)
        spin_b = cross(arm_b, force)
        for c in range(3):
            push_a[tile_rows[c], :] = held(26) * force[c]
            push_a[tile_rows[3 + c], :] = held(27 + c) * spin_a[c]
            push_b[tile_rows[c], :] = -(held(30) * force[c])
            push_b[tile_rows[3 + c], :] = -(held(31 + c) * spin_b[c])

    def sides(base, room):
        left, right = [], []
        empty = jnp.zeros((16 * (total - blocks), LANES), BF16)
        for j in range(GROUP):
            t = scalars[base + j]
            first = two_parts(push_a[room + 8 * j : room + 8 * j + 8, :])
            second = two_parts(push_b[room + 8 * j : room + 8 * j + 8, :])
            rows = [masks[t, 16 * m : 16 * m + 16, :] for m in range(blocks + total)]
            left.append(jnp.concatenate([first * m for m in rows[:blocks]] + [empty], axis=0))
            left.append(jnp.concatenate([second * m for m in rows[blocks:]], axis=0))
            right.append(hot[pl.ds(pl.multiple_of(2 * TILE * t, 2 * TILE), 2 * TILE), :])
        return left, right

    def groups(bases, now):
        rooms = [8 * GROUP * i for i in range(len(bases))]
        for base, room in zip(bases, rooms):
            gather(base, room, now)
        for base, room in zip(bases, rooms):
            press(base, room)
        left, right = [], []
        for base, room in zip(bases, rooms):
            more_left, more_right = sides(base, room)
            left += more_left
            right += more_right
        return jnp.dot(
            jnp.concatenate(left, axis=1),
            jnp.concatenate(right, axis=0),
            preferred_element_type=F32,
        )

    def color_pass(k):
        now = [table[8 * h : 8 * h + 8, :] for h in range(total)]
        main = pl.multiple_of(GROUP * k, GROUP)

        def over(g):
            return pl.multiple_of(GROUP * (NCOLOR + g), GROUP)

        begin, end = scalars[OVER_FROM + k], scalars[OVER_TO + k]

        @pl.when(end > begin)
        def _():
            acc[...] = groups([main, over(begin)], now)

        @pl.when(end <= begin)
        def _():
            acc[...] = groups([main], now)

        def more(g, c):
            acc[...] += groups([over(g)], now)
            return c

        lax.fori_loop(begin + 1, end, more, 0)
        for h in range(total):
            table[8 * h : 8 * h + 8, :] = now[h] + sum_parts(acc, h)

    def later_pass(k, carry):
        color_pass(k)
        return carry

    lax.fori_loop(0, NCOLOR, later_pass, 0)
    for h in range(blocks):
        own_change[:, h * LANES : (h + 1) * LANES] = table[8 * h : 8 * h + 8, :] - start[h]
    ghost0[...] = table[8 * blocks : 8 * blocks + 8, :] - start[blocks]
    ghost1[...] = table[8 * blocks + 8 : 8 * blocks + 16, :] - start[blocks + 1]


def impulse_kernel(scalars, held, impulse):
    slots = held.shape[0] // 3
    for t in range(impulse.shape[2] // TILE):
        slot = scalars[0, TILE_SLOT + t]
        for c in range(3):
            impulse[c, :, t * TILE : (t + 1) * TILE] = held[pl.ds(c * slots + slot, 1), :]


def merge_kernel(
    interface, last_sweep, own, change, c0, c1, c2, c3, mult, export_index, export_hot,
    export_masks, *refs,
):
    blocks = own.shape[1] // LANES
    came = [halves(c0[...], c1[...], interface), halves(c2[...], c3[...], interface)]
    left = jnp.concatenate(
        [
            jnp.concatenate([two_parts(came[i])] * blocks, axis=0) * export_masks[i]
            for i in range(2)
        ],
        axis=1,
    )
    incoming = contract_lanes(left, export_hot[...])
    fresh = []
    for h in range(blocks):
        span = slice(h * LANES, (h + 1) * LANES)
        fresh.append(
            own[0:8, span] + (change[:, span] + sum_parts(incoming, h)) / mult[:, span]
        )
    if last_sweep:
        (velocity,) = refs
        for r in range(6):
            for h in range(blocks):
                velocity[r, :, h * LANES : (h + 1) * LANES] = fresh[h][r : r + 1, :]
    else:
        fresh_own, out0, out1 = refs
        for h in range(blocks):
            fresh_own[:, h * LANES : (h + 1) * LANES] = fresh[h]
        out0[...] = pick(fresh, export_index[0:8, :])
        out1[...] = pick(fresh, export_index[8:16, :])


def in_hbm(array):
    return pltpu.with_memory_space_constraint(array, pltpu.HBM)


def shape(dims, dtype=F32):
    return jax.ShapeDtypeStruct(dims, dtype)


def make(subs, layers):
    matchings = neighbour_matchings(subs, layers)
    shuffles = [relay_shuffle(subs, layers, k) for k in range(WIN)]

    def trade(low, high):
        return [
            lax.ppermute(low if m < 2 else high, AXES, matchings[m]) for m in range(4)
        ]

    def on_device(geometry, dest_slot, pairs, colors, free_vel, inertia, exports):
        count = geometry.shape[2]
        bodies = free_vel.shape[2]
        interface = exports.shape[2]
        tiles = count // TILE
        slots = 16
        assert count % TILE == 0 and tiles < slots and 2 * interface == LANES
        assert bodies % LANES == 0
        blocks = bodies // LANES
        total = blocks + 2
        place = shape((10 * slots, LANES))
        small = shape((16, LANES))
        arguments = (geometry, dest_slot, free_vel, inertia, exports, pairs, colors)
        rows = slot_count(tiles)
        assert rows <= TILE_SLOT
        prepared = pl.pallas_call(
            prepare_kernel,
            out_shape=(
                shape((10 * slots + 16, LANES)), place, place, small, small,
                shape((16, bodies)),
                shape((16, LANES), jnp.int32),
                shape((WIDE, count), BF16),
                shape((16, count), BF16),
                shape((2, 80, count), BF16),
                shape((32, LANES), jnp.int32),
                shape((2 * rows, LANES), jnp.int32),
                shape((rows, LANES)),
                shape((1, LANES), jnp.int32),
            ),
            in_specs=[pl.BlockSpec(memory_space=pltpu.HBM)] * 7,
            out_specs=(VMEM_SPEC,) * 14,
            scratch_shapes=[
                pltpu.VMEM(geometry.shape, F32),
                pltpu.VMEM(dest_slot.shape, jnp.int32),
                pltpu.VMEM(free_vel.shape, F32),
                pltpu.VMEM(inertia.shape, F32),
                pltpu.VMEM(exports.shape, jnp.int32),
                pltpu.VMEM(pairs.shape, jnp.int32),
                pltpu.SMEM(colors.shape, jnp.int32),
                pltpu.SMEM((1, LANES), jnp.int32),
                pltpu.VMEM((8, LANES), jnp.int32),
                pltpu.VMEM((16, count), F32),
                pltpu.VMEM((16 * (WIN - 1), count), BF16),
                pltpu.VMEM((2, 80 * (WIN - 1), count), BF16),
                pltpu.SemaphoreType.DMA((8,)),
            ],
            compiler_params=PARAMS,
            name="prepare",
        )(*[in_hbm(x) for x in arguments])
        send0, place2, place3, out0, out1, own, export_index = prepared[:7]
        wide_hot, own_mask, tall, ordered, index, used, scalars = prepared[7:]
        came = [lax.ppermute(send0, AXES, matchings[0])]
        came.append(lax.ppermute(out0, AXES, matchings[1]))
        came.append(lax.ppermute(out1, AXES, matchings[2]))
        came.append(lax.ppermute(out1, AXES, matchings[3]))
        place0 = pl.pallas_call(
            place_kernel,
            out_shape=place,
            in_specs=[VMEM_SPEC] * 3,
            out_specs=VMEM_SPEC,
            compiler_params=PARAMS,
            name="place",
        )(tall, own_mask, wide_hot)
        placed = [place0]
        placed.append(lax.ppermute(place2, AXES, shuffles[2]))
        placed.append(lax.ppermute(place3, AXES, shuffles[3]))

        def indexing(*refs):
            index_kernel(subs, layers, interface, bodies, *refs)

        hot, masks, export_hot, export_masks, mult, near_props, far_props = pl.pallas_call(
            indexing,
            out_shape=(
                shape((2 * TILE * (tiles + 1), LANES), BF16),
                shape((tiles + 1, 16 * (blocks + total), LANES), BF16),
                shape((LANES, 2 * LANES), BF16),
                shape((2, 16 * blocks, LANES), BF16),
                shape((8, bodies)),
                shape((8 * tiles, LANES)),
                shape((8 * tiles, LANES)),
            ),
            in_specs=[VMEM_SPEC] * 3,
            out_specs=(VMEM_SPEC,) * 7,
            compiler_params=PARAMS,
            name="indexing",
        )(ordered, export_index, own)

        state = impulse = None
        for sweep in range(SWEEPS):
            first, last = sweep == 0, sweep == SWEEPS - 1

            def run(*refs, first=first):
                sweep_kernel(bodies, interface, first, *refs)

            outs = [
                shape((3 * rows, LANES)),
                shape((8, bodies)),
                shape((8, LANES)),
                shape((8, LANES)),
            ]
            operands = [scalars, index, used, hot, masks, own, *came]
            if first:
                outs = [shape((STATE * rows, LANES))] + outs
                operands += [*placed, ordered, near_props, far_props]
            else:
                operands += [state, impulse]
            result = pl.pallas_call(
                run,
                out_shape=tuple(outs),
                in_specs=[VMEM_SPEC] * len(operands),
                out_specs=(VMEM_SPEC,) * len(outs),
                scratch_shapes=[
                    pltpu.VMEM((16 * GROUP, LANES), F32),
                    pltpu.VMEM((16 * GROUP, LANES), F32),
                    pltpu.VMEM((16 * GROUP, LANES), F32),
                    pltpu.VMEM((16 * GROUP, LANES), F32),
                    pltpu.VMEM((16 * total, LANES), F32),
                    pltpu.VMEM((8 * total, LANES), F32),
                    pltpu.VMEM((8 * rows, LANES), F32),
                    pltpu.VMEM((8 * rows, LANES), F32),
                    pltpu.VMEM((10 * slots, LANES), F32),
                    pltpu.VMEM((10 * rows, LANES), F32),
                    pltpu.SMEM((64,), jnp.int32),
                ],
                compiler_params=PARAMS,
                name="sweep",
            )(*operands)
            if first:
                state, result = result[0], result[1:]
            impulse, change, ghost0, ghost1 = result
            sums = trade(ghost0, ghost1)

            def merge(*refs, last=last):
                merge_kernel(interface, last, *refs)

            operands = [own, change, *sums, mult, export_index, export_hot, export_masks]
            if last:
                outs = (shape((6, 1, bodies)),)
            else:
                outs = (shape((8, bodies)), shape((8, LANES)), shape((8, LANES)))
            merged = pl.pallas_call(
                merge,
                out_shape=outs,
                in_specs=[VMEM_SPEC] * len(operands),
                out_specs=(VMEM_SPEC,) * len(outs),
                compiler_params=PARAMS,
                name="merge",
            )(*operands)
            if last:
                in_order = pl.pallas_call(
                    impulse_kernel,
                    out_shape=shape((3, 1, count)),
                    in_specs=[SMEM_SPEC, VMEM_SPEC],
                    out_specs=VMEM_SPEC,
                    compiler_params=PARAMS,
                    name="impulse",
                )(scalars, impulse)
                return in_order, merged[0]
            own = merged[0]
            came = trade(merged[1], merged[2])

    return on_device


def solution(mesh):
    placed = (
        P(None, "layer", "sub"),
        P("layer", "sub"),
        P(None, "layer", "sub"),
        P("layer", "sub"),
        P(None, "layer", "sub"),
        P(None, "layer", "sub"),
        P(None, "layer", "sub"),
    )
    return jax.shard_map(
        make(mesh.shape["sub"], mesh.shape["layer"]),
        mesh=mesh,
        in_specs=placed,
        out_specs=(P(None, "layer", "sub"), P(None, "layer", "sub")),
        check_vma=False,
    )
```

```python
import jax
import jax.numpy as jnp
from jax import lax
from jax.experimental import pallas as pl
from jax.experimental.pallas import tpu as pltpu
from jax.sharding import PartitionSpec as P

WIN = 4
SWEEPS = 3
NCOLOR = 4
TILE = 128
LANES = 128
WIDE = 256
GROUP = 4

relaxation = 0.7
friction = 0.6
tangent_floor = 0.1

AXES = ("sub", "layer")
F32 = jnp.float32
BF16 = jnp.bfloat16
VMEM_SPEC = pl.BlockSpec(memory_space=pltpu.VMEM)
SMEM_SPEC = pl.BlockSpec(memory_space=pltpu.SMEM)
PARAMS = pltpu.CompilerParams(vmem_limit_bytes=16 << 20)


def neighbour_matchings(subs, layers):
    assert subs % 2 == 0 and layers % 2 == 0

    def shifted(i):
        return i - 1 if i % 2 == 0 else i + 1

    def partner(match, s, y):
        if match == 0:
            return s ^ 1, y
        if match == 1:
            return (s, y ^ 1) if s in (0, subs - 1) else (shifted(s), y)
        if match == 2:
            return s, y ^ 1
        return (s ^ 1, y) if y in (0, layers - 1) else (s, shifted(y))

    out = []
    for match in range(4):
        pairs = []
        for s in range(subs):
            for y in range(layers):
                ps, py = partner(match, s, y)
                pairs.append((s * layers + y, ps * layers + py))
        out.append(pairs)
    return out


def relay_shuffle(subs, layers, k):
    return [
        (s * layers + y, (s ^ k) * layers + y) for s in range(subs) for y in range(layers)
    ]


def lane_iota():
    return lax.broadcasted_iota(jnp.int32, (8, LANES), 1)


def pick(tables, index):
    low = jnp.bitwise_and(index, LANES - 1)
    high = jnp.right_shift(index, 7)
    out = jnp.take_along_axis(tables[0], low, axis=1)
    for h in range(1, len(tables)):
        out = jnp.where(high == h, jnp.take_along_axis(tables[h], low, axis=1), out)
    return out


def two_parts(value):
    first = value.astype(BF16).astype(F32)
    return jnp.concatenate([first, value - first], axis=0).astype(BF16)


def equal_rows(row, count):
    shape = (count, row.shape[1])
    ids = lax.broadcasted_iota(jnp.int32, shape, 0).astype(F32).astype(BF16)
    here = jnp.broadcast_to(row.astype(F32), shape).astype(BF16)
    return jnp.where(ids == here, jnp.ones(shape, BF16), jnp.zeros(shape, BF16))


def high_masks(index_row, highs):
    shape = (16, LANES)
    high = jnp.broadcast_to(jnp.right_shift(index_row, 7).astype(F32), shape).astype(BF16)
    one, zero = jnp.ones(shape, BF16), jnp.zeros(shape, BF16)
    return jnp.concatenate(
        [jnp.where(high == jnp.full(shape, h, BF16), one, zero) for h in range(highs)], axis=0
    )


def low_onehot(index_row):
    return equal_rows(jnp.bitwise_and(index_row, LANES - 1), LANES)


def contract_lanes(lhs, rhs):
    return lax.dot_general(
        lhs, rhs, (((1,), (1,)), ((), ())), preferred_element_type=F32
    )


def sum_parts(block, h):
    return block[16 * h : 16 * h + 8] + block[16 * h + 8 : 16 * h + 16]


def cross(u, v):
    return [
        u[1] * v[2] - u[2] * v[1],
        u[2] * v[0] - u[0] * v[2],
        u[0] * v[1] - u[1] * v[0],
    ]


def dot3(u, v):
    return u[0] * v[0] + u[1] * v[1] + u[2] * v[2]


def halves(low, high, half):
    return jnp.where(lane_iota() < half, low, high)


def parities():
    sub = lax.axis_index("sub")
    layer = lax.axis_index("layer")
    return sub, layer, lax.rem(sub, 2) == 0, lax.rem(layer, 2) == 0


def prepare_kernel(
    geo_hbm, dest_hbm, vel_hbm, inertia_hbm, exports_hbm, pairs_hbm, colors_hbm,
    send0, place2, place3, out0, out1, start_own, export_index, hot, own_mask, tall,
    ordered, index_out, used, scalars_out,
    geo, dest, vel, inertia, exports, pairs, colors, scalars, listed, dense, mask, lhs, sems,
):
    copies = [
        pltpu.make_async_copy(src, dst, sems.at[i])
        for i, (src, dst) in enumerate(
            [
                (exports_hbm, exports),
                (vel_hbm, vel),
                (inertia_hbm, inertia),
                (dest_hbm, dest),
                (colors_hbm, colors),
                (pairs_hbm, pairs),
                (geo_hbm, geo),
            ]
        )
    ]
    for copy in copies:
        copy.start()
    count = geo.shape[2]
    tiles = count // TILE
    slots = place2.shape[0] // 10
    bodies = vel.shape[2]
    interface = exports.shape[2]
    sub, layer, sub_even, layer_even = parities()
    member = lax.rem(sub, WIN)
    start_own[...] = jnp.zeros_like(start_own)
    dense[...] = jnp.zeros_like(dense)
    for copy in copies[:6]:
        copy.wait()
    for r in range(6):
        start_own[r : r + 1, :] = vel[r]
    for r in range(4):
        start_own[8 + r : 9 + r, :] = inertia[r]
    listed[0:1, 0:interface] = exports[0]
    listed[0:1, interface : 2 * interface] = exports[1]
    listed[1:2, 0:interface] = exports[1]
    listed[1:2, interface : 2 * interface] = exports[0]
    listed[2:3, 0:interface] = exports[2]
    listed[2:3, interface : 2 * interface] = exports[3]
    listed[3:4, 0:interface] = exports[3]
    listed[3:4, interface : 2 * interface] = exports[2]
    row0 = jnp.where(sub_even, listed[1:2, :], listed[0:1, :])
    row1 = jnp.where(layer_even, listed[3:4, :], listed[2:3, :])
    idx0 = jnp.broadcast_to(row0, (8, LANES))
    idx1 = jnp.broadcast_to(row1, (8, LANES))
    export_index[0:8, :] = idx0
    export_index[8:16, :] = idx1
    blocks = bodies // LANES
    for base in (0, 8):
        tables = [
            start_own[base : base + 8, h * LANES : (h + 1) * LANES] for h in range(blocks)
        ]
        picked = pick(tables, idx0)
        out0[base : base + 8, :] = picked
        send0[10 * slots + base : 10 * slots + base + 8, :] = picked
        out1[base : base + 8, :] = pick(tables, idx1)
    rank = used.shape[0]
    for i in range(rank):
        scalars[0, i] = tiles
    for k in range(NCOLOR):
        scalars[0, FILLED + k] = 0
    colored, ranks = [], []
    for t in range(tiles):
        color = colors[0, t]
        rank_here = scalars[0, FILLED + color]
        scalars[0, FILLED + color] = rank_here + 1
        colored.append(color)
        ranks.append(rank_here)
    over = jnp.int32(0)
    for k in range(NCOLOR):
        scalars[0, OVER_BASE + k] = (NCOLOR + over) * GROUP - GROUP
        scalars[0, OVER_FROM + k] = over
        filled = scalars[0, FILLED + k]
        over = over + jnp.right_shift(jnp.maximum(filled - 1, GROUP - 1), GROUP.bit_length() - 1)
        scalars[0, OVER_TO + k] = over
    place = []
    for t in range(tiles):
        base = jnp.where(ranks[t] < GROUP, GROUP * colored[t], scalars[0, OVER_BASE + colored[t]])
        place.append(base + ranks[t])
        scalars[0, place[t]] = t
    index_out[...] = jnp.zeros_like(index_out)
    ordered[...] = jnp.zeros_like(ordered)
    used[...] = jnp.zeros_like(used)
    flip_sub = jnp.where(sub_even, interface, 0)
    flip_layer = jnp.where(layer_even, interface, 0)
    for t in range(tiles):
        span = slice(t * TILE, (t + 1) * TILE)
        nearer = pairs[0, :, span]
        other = pairs[1, :, span]
        ghost = other - bodies
        turned = jnp.where(
            ghost < 2 * interface,
            jnp.bitwise_xor(ghost, flip_sub),
            jnp.bitwise_xor(ghost, flip_layer),
        )
        farther = jnp.where(ghost < 0, other, bodies + turned)
        scalars[0, TILE_SLOT + t] = place[t]
        ordered[t : t + 1, :] = nearer
        ordered[16 + t : 17 + t, :] = farther
        index_out[pl.ds(place[t], 1), :] = nearer
        index_out[pl.ds(rank + place[t], 1), :] = farther
        used[pl.ds(place[t], 1), :] = jnp.ones((1, LANES), F32)
    slot = dest[...] - (sub - member) * count
    target = jnp.zeros_like(slot)
    for m in range(1, WIN):
        target = target + jnp.where(slot >= m * count, 1, 0)
    within = slot - target * count
    row_id = jnp.bitwise_xor(target, member) * 8 + jnp.right_shift(within, 8)
    low = jnp.bitwise_and(within, WIDE - 1)
    paired = (16, TILE)
    ids = lax.broadcasted_iota(jnp.int32, paired, 0)
    ids = jnp.bitwise_and(ids, 7).astype(F32)
    one, zero = jnp.ones(paired, BF16), jnp.zeros(paired, BF16)
    for t in range(tiles):
        span = slice(t * TILE, (t + 1) * TILE)
        hot[:, span] = equal_rows(low[:, span], WIDE)
        here = jnp.broadcast_to(row_id[:, span].astype(F32), paired).astype(BF16)
        for k in range(WIN):
            chosen = jnp.where(here == (ids + 8.0 * k).astype(BF16), one, zero)
            if k == 0:
                own_mask[:, span] = chosen
            else:
                mask[16 * k - 16 : 16 * k, span] = chosen
    give = pltpu.make_async_copy(scalars, scalars_out, sems.at[7])
    give.start()
    copies[6].wait()
    for r in range(10):
        dense[r : r + 1, :] = geo[r]
    value = dense[...]
    first = value.astype(BF16).astype(F32)
    parts = [first, value - first]
    for p in range(2):
        for i in range(5):
            pair = jnp.concatenate(
                [jnp.broadcast_to(parts[p][r : r + 1, :], (8, count)) for r in (2 * i, 2 * i + 1)],
                axis=0,
            ).astype(BF16)
            tall[p, 16 * i : 16 * i + 16, :] = pair
            for k in range(1, WIN):
                at = 80 * (WIN - 1) * p + 80 * (k - 1) + 16 * i
                lhs[at : at + 16, :] = mask[16 * k - 16 : 16 * k, :] * pair
    both = contract_lanes(lhs[...], hot[...])
    total = both[: 80 * (WIN - 1)] + both[80 * (WIN - 1) :]
    for k, out in enumerate((send0, place2, place3)):
        store_placed(out, total[80 * k : 80 * k + 80, :])
    give.wait()


def store_placed(out, total):
    for r in range(10):
        for side in range(2):
            out[16 * r + 8 * side : 16 * r + 8 * side + 8, :] = total[
                8 * r : 8 * r + 8, side * LANES : (side + 1) * LANES
            ]


def place_kernel(tall, own_mask, hot, out):
    left = [jnp.concatenate([own_mask[...]] * 5, axis=0) * tall[p] for p in range(2)]
    both = contract_lanes(jnp.concatenate(left, axis=0), hot[...])
    store_placed(out, both[:80] + both[80:])


TILE_SLOT, OVER_FROM, FILLED, OVER_TO, OVER_BASE = 32, 48, 52, 56, 60


def overflow_groups(tiles):
    most = 0
    for busy in range(1, NCOLOR + 1):
        spare = tiles - busy * (GROUP + 1)
        if spare >= 0:
            most = max(most, busy + spare // GROUP)
    return most


def slot_count(tiles):
    return -(-GROUP * (NCOLOR + overflow_groups(tiles)) // 8) * 8


def index_kernel(
    subs, layers, interface, bodies, ordered, export_index, own,
    hot, masks, export_hot, export_masks, mult, near_props, far_props,
):
    tiles = masks.shape[0] - 1
    blocks = bodies // LANES
    total = blocks + 4 * interface // LANES
    sub, layer, sub_even, layer_even = parities()
    props = [own[8:16, h * LANES : (h + 1) * LANES] for h in range(blocks)]
    square = (TILE, LANES)
    lane_ids = lax.broadcasted_iota(jnp.int32, square, 1)
    eye = jnp.where(lax.broadcasted_iota(jnp.int32, square, 0) == lane_ids, 1.0, 0.0)
    lane_ids = lane_ids.astype(F32)
    low_rows = jnp.bitwise_and(ordered[...], LANES - 1).astype(F32).astype(BF16)
    columns = contract_lanes(eye.astype(BF16), low_rows).astype(BF16)
    ids = lax.broadcasted_iota(jnp.int32, (32, 2 * TILE), 0)
    lanes = lax.broadcasted_iota(jnp.int32, (32, 2 * TILE), 1)
    for t in range(tiles):
        first = ordered[t : t + 1, :]
        second = ordered[16 + t : 17 + t, :]
        near_props[8 * t : 8 * t + 8, :] = pick(props, jnp.broadcast_to(first, (8, LANES)))
        far_props[8 * t : 8 * t + 8, :] = pick(props, jnp.broadcast_to(second, (8, LANES)))
        sides = jnp.where(lanes < TILE, t, 16 + t)
        chosen = jnp.where(ids == sides, 1.0, 0.0).astype(BF16)
        low = jnp.dot(columns, chosen, preferred_element_type=F32)
        for side in range(2):
            hit = low[:, side * TILE : (side + 1) * TILE] == lane_ids
            at = (2 * t + side) * TILE
            hot[at : at + TILE, :] = jnp.where(hit, 1.0, 0.0).astype(BF16)
        masks[t, : 16 * blocks, :] = high_masks(first, blocks)
        masks[t, 16 * blocks :, :] = high_masks(second, total)
    hot[2 * tiles * TILE :, :] = jnp.zeros((2 * TILE, LANES), BF16)
    masks[tiles] = jnp.zeros_like(masks[tiles])
    inner_sub = jnp.where(jnp.logical_and(sub > 0, sub < subs - 1), 1.0, 0.0)
    inner_layer = jnp.where(jnp.logical_and(layer > 0, layer < layers - 1), 1.0, 0.0)
    lane = lane_iota()
    weights = [
        jnp.where(lane < interface, 1.0, inner_sub),
        jnp.where(lane < interface, 1.0, inner_layer),
    ]
    left = []
    for i in range(2):
        row = export_index[8 * i : 8 * i + 1, :]
        export_hot[:, i * LANES : (i + 1) * LANES] = low_onehot(row)
        chosen = high_masks(row, blocks)
        export_masks[i] = chosen
        weight = jnp.concatenate([weights[i], jnp.zeros_like(weights[i])], axis=0).astype(BF16)
        left.append(jnp.concatenate([weight] * blocks, axis=0) * chosen)
    listed = contract_lanes(jnp.concatenate(left, axis=1), export_hot[...])
    for h in range(blocks):
        mult[:, h * LANES : (h + 1) * LANES] = 1.0 + listed[16 * h : 16 * h + 8]


STATE = 34


def contact_state(geo, first, second):
    raw = geo[0:3]
    length = jnp.sqrt(dot3(raw, raw))
    normal = [x / length for x in raw]
    side = jnp.sqrt(normal[1] * normal[1] + normal[2] * normal[2])
    tan_y = normal[2] / side
    tan_z = -normal[1] / side
    two = [
        normal[1] * tan_z - normal[2] * tan_y,
        -normal[0] * tan_z,
        normal[0] * tan_y,
    ]

    def arm(p, spin):
        return [
            spin[1] * p[2] * p[2] + spin[2] * p[1] * p[1],
            spin[0] * p[2] * p[2] + spin[2] * p[0] * p[0],
            spin[0] * p[1] * p[1] + spin[1] * p[0] * p[0],
            -spin[2] * p[0] * p[1],
            -spin[1] * p[0] * p[2],
            -spin[0] * p[1] * p[2],
        ]

    arm_a, arm_b = geo[3:6], geo[6:9]
    e = [x + y for x, y in zip(arm(arm_a, first[1:4]), arm(arm_b, second[1:4]))]
    mass = first[0] + second[0]
    xx, yy, zz = mass + e[0], mass + e[1], mass + e[2]
    xy, xz, yz = e[3], e[4], e[5]
    c_xx = yy * zz - yz * yz
    c_xy = xz * yz - xy * zz
    c_xz = xy * yz - xz * yy
    c_yy = xx * zz - xz * xz
    c_yz = xy * xz - xx * yz
    c_zz = xx * yy - xy * xy
    det = xx * c_xx + xy * c_xy + xz * c_xz
    inv = [
        [c_xx / det, c_xy / det, c_xz / det],
        [c_xy / det, c_yy / det, c_yz / det],
        [c_xz / det, c_yz / det, c_zz / det],
    ]
    solve = []
    for row in (normal, None, two):
        for j in range(3):
            if row is None:
                value = tan_y * inv[1][j] + tan_z * inv[2][j]
            else:
                value = row[0] * inv[0][j] + row[1] * inv[1][j] + row[2] * inv[2][j]
            solve.append(relaxation * value)
    bias = [geo[9] * dot3(solve[3 * i : 3 * i + 3], normal) for i in range(3)]
    return (
        solve + bias + normal + [tan_y, tan_z] + two + arm_a + arm_b + list(first) + list(second)
    )


def sweep_kernel(bodies, interface, first_sweep, *refs):
    scalars_in, index, used, hot, masks = refs[:5]
    refs = refs[5:]
    if first_sweep:
        own, g1, r1, r2, r3, g0, g2, g3, ordered, near_props, far_props, state = refs[:12]
        refs = refs[12:]
        r0 = g1.at[pl.ds(g0.shape[0], 16), :]
    else:
        own, r0, r1, r2, r3, state, impulse_in = refs[:7]
        refs = refs[7:]
    impulse, own_change, ghost0, ghost1 = refs[:4]
    got_a, got_b, push_a, push_b, acc, table, all_a, all_b, gathered, placed, scalars = refs[4:]
    slots = used.shape[0]
    tiles = masks.shape[0] - 1
    blocks = bodies // LANES
    total = blocks + (4 * interface) // LANES
    values = scalars_in[...]
    wanted = list(range(slots)) + [OVER_FROM + k for k in range(NCOLOR)]
    wanted += [OVER_TO + k for k in range(NCOLOR)]
    if first_sweep:
        wanted += [TILE_SLOT + t for t in range(tiles)]
    for i in wanted:
        scalars[i] = values[0, i]

    def ghost_blocks(base):
        return [
            halves(r0[base : base + 8, :], r1[base : base + 8, :], interface),
            halves(r2[base : base + 8, :], r3[base : base + 8, :], interface),
        ]

    start = [own[0:8, h * LANES : (h + 1) * LANES] for h in range(blocks)] + ghost_blocks(0)
    for h in range(total):
        table[8 * h : 8 * h + 8, :] = start[h]
    push_a[...] = jnp.zeros_like(push_a)
    push_b[...] = jnp.zeros_like(push_b)

    if first_sweep:
        ghost_props = ghost_blocks(8)
        far = []
        for t in range(tiles):
            ib = jnp.broadcast_to(ordered[16 + t : 17 + t, :], (8, LANES))
            low, high = jnp.bitwise_and(ib, LANES - 1), jnp.right_shift(ib, 7)
            value = far_props[8 * t : 8 * t + 8, :]
            for h, block in enumerate(ghost_props):
                value = jnp.where(
                    high == blocks + h, jnp.take_along_axis(block, low, axis=1), value
                )
            far.append(value)
        all_a[...] = jnp.ones_like(all_a)
        all_b[...] = jnp.ones_like(all_b)
        gathered[...] = (g0[...] + g1[0 : g0.shape[0], :]) + (g2[...] + g3[...])
        placed[...] = jnp.ones_like(placed)
        rows = g0.shape[0] // 10
        for t in range(tiles):
            slot = scalars[TILE_SLOT + t]
            group_rows = pl.ds(pl.multiple_of(8 * slot, 8), 8)
            all_a[group_rows, :] = near_props[8 * t : 8 * t + 8, :]
            all_b[group_rows, :] = far[t]
            at = 8 * (t % 2) + t // 2
            for c in range(10):
                row = c * rows + at
                placed[pl.ds(c * slots + slot, 1), :] = gathered[row : row + 1, :]
        first = [all_a[pl.ds(c, slots, stride=8), :] for c in range(4)]
        second = [all_b[pl.ds(c, slots, stride=8), :] for c in range(4)]
        geo = [placed[c * slots : (c + 1) * slots, :] for c in range(10)]
        for c, value in enumerate(contact_state(geo, first, second)):
            state[c * slots : (c + 1) * slots, :] = value
        impulse[...] = jnp.zeros_like(impulse)
    else:
        impulse[...] = impulse_in[...]

    def held_at(base):
        return lambda c: state[pl.ds(c * slots + base, GROUP), :]

    def gather(base, room, now):
        for j in range(GROUP):
            ia = jnp.broadcast_to(index[pl.ds(base + j, 1), :], (8, LANES))
            ib = jnp.broadcast_to(index[pl.ds(slots + base + j, 1), :], (8, LANES))
            got_a[room + 8 * j : room + 8 * j + 8, :] = pick(now[:blocks], ia)
            got_b[room + 8 * j : room + 8 * j + 8, :] = pick(now, ib)

    def press(base, room):
        held = held_at(base)
        tile_rows = [pl.ds(room + c, GROUP, stride=8) for c in range(6)]
        va = [got_a[tile_rows[c], :] for c in range(6)]
        vb = [got_b[tile_rows[c], :] for c in range(6)]
        arm_a = [held(20 + c) for c in range(3)]
        arm_b = [held(23 + c) for c in range(3)]
        turn_a = cross(va[3:6], arm_a)
        turn_b = cross(vb[3:6], arm_b)
        rel = [((va[c] + turn_a[c]) - vb[c]) - turn_b[c] for c in range(3)]
        old = [impulse[pl.ds(c * slots + base, GROUP), :] for c in range(3)]
        trial = [
            old[c] - (dot3([held(3 * c + j) for j in range(3)], rel) + held(9 + c))
            for c in range(3)
        ]
        normal_part = jnp.maximum(trial[0], 0.0)
        slide = trial[1] * trial[1] + trial[2] * trial[2]
        shrink = lax.rsqrt(jnp.maximum(slide, tangent_floor * tangent_floor))
        factor = jnp.minimum(1.0, friction * normal_part * shrink)
        active = used[pl.ds(base, GROUP), :] > 0.5
        new = [
            jnp.where(active, normal_part, old[0]),
            jnp.where(active, trial[1] * factor, old[1]),
            jnp.where(active, trial[2] * factor, old[2]),
        ]
        change = [new[c] - old[c] for c in range(3)]
        for c in range(3):
            impulse[pl.ds(c * slots + base, GROUP), :] = new[c]
        force = [
            held(12) * change[0] + held(17) * change[2],
            held(13) * change[0] + held(15) * change[1] + held(18) * change[2],
            held(14) * change[0] + held(16) * change[1] + held(19) * change[2],
        ]
        spin_a = cross(arm_a, force)
        spin_b = cross(arm_b, force)
        for c in range(3):
            push_a[tile_rows[c], :] = held(26) * force[c]
            push_a[tile_rows[3 + c], :] = held(27 + c) * spin_a[c]
            push_b[tile_rows[c], :] = -(held(30) * force[c])
            push_b[tile_rows[3 + c], :] = -(held(31 + c) * spin_b[c])

    def sides(base, room):
        left, right = [], []
        empty = jnp.zeros((16 * (total - blocks), LANES), BF16)
        for j in range(GROUP):
            t = scalars[base + j]
            first = two_parts(push_a[room + 8 * j : room + 8 * j + 8, :])
            second = two_parts(push_b[room + 8 * j : room + 8 * j + 8, :])
            rows = [masks[t, 16 * m : 16 * m + 16, :] for m in range(blocks + total)]
            left.append(jnp.concatenate([first * m for m in rows[:blocks]] + [empty], axis=0))
            left.append(jnp.concatenate([second * m for m in rows[blocks:]], axis=0))
            right.append(hot[pl.ds(pl.multiple_of(2 * TILE * t, 2 * TILE), 2 * TILE), :])
        return left, right

    def groups(bases, now):
        rooms = [8 * GROUP * i for i in range(len(bases))]
        for base, room in zip(bases, rooms):
            gather(base, room, now)
        for base, room in zip(bases, rooms):
            press(base, room)
        left, right = [], []
        for base, room in zip(bases, rooms):
            more_left, more_right = sides(base, room)
            left += more_left
            right += more_right
        return jnp.dot(
            jnp.concatenate(left, axis=1),
            jnp.concatenate(right, axis=0),
            preferred_element_type=F32,
        )

    def color_pass(k):
        now = [table[8 * h : 8 * h + 8, :] for h in range(total)]
        main = pl.multiple_of(GROUP * k, GROUP)

        def over(g):
            return pl.multiple_of(GROUP * (NCOLOR + g), GROUP)

        begin, end = scalars[OVER_FROM + k], scalars[OVER_TO + k]

        @pl.when(end > begin)
        def _():
            acc[...] = groups([main, over(begin)], now)

        @pl.when(end <= begin)
        def _():
            acc[...] = groups([main], now)

        def more(g, c):
            acc[...] += groups([over(g)], now)
            return c

        lax.fori_loop(begin + 1, end, more, 0)
        for h in range(total):
            table[8 * h : 8 * h + 8, :] = now[h] + sum_parts(acc, h)

    def later_pass(k, carry):
        color_pass(k)
        return carry

    lax.fori_loop(0, NCOLOR, later_pass, 0)
    for h in range(blocks):
        own_change[:, h * LANES : (h + 1) * LANES] = table[8 * h : 8 * h + 8, :] - start[h]
    ghost0[...] = table[8 * blocks : 8 * blocks + 8, :] - start[blocks]
    ghost1[...] = table[8 * blocks + 8 : 8 * blocks + 16, :] - start[blocks + 1]


def impulse_kernel(scalars, held, impulse):
    slots = held.shape[0] // 3
    for t in range(impulse.shape[2] // TILE):
        slot = scalars[0, TILE_SLOT + t]
        for c in range(3):
            impulse[c, :, t * TILE : (t + 1) * TILE] = held[pl.ds(c * slots + slot, 1), :]


def merge_kernel(
    interface, last_sweep, own, change, c0, c1, c2, c3, mult, export_index, export_hot,
    export_masks, *refs,
):
    blocks = own.shape[1] // LANES
    came = [halves(c0[...], c1[...], interface), halves(c2[...], c3[...], interface)]
    left = jnp.concatenate(
        [
            jnp.concatenate([two_parts(came[i])] * blocks, axis=0) * export_masks[i]
            for i in range(2)
        ],
        axis=1,
    )
    incoming = contract_lanes(left, export_hot[...])
    fresh = []
    for h in range(blocks):
        span = slice(h * LANES, (h + 1) * LANES)
        fresh.append(
            own[0:8, span] + (change[:, span] + sum_parts(incoming, h)) / mult[:, span]
        )
    if last_sweep:
        (velocity,) = refs
        for r in range(6):
            for h in range(blocks):
                velocity[r, :, h * LANES : (h + 1) * LANES] = fresh[h][r : r + 1, :]
    else:
        fresh_own, out0, out1 = refs
        for h in range(blocks):
            fresh_own[:, h * LANES : (h + 1) * LANES] = fresh[h]
        out0[...] = pick(fresh, export_index[0:8, :])
        out1[...] = pick(fresh, export_index[8:16, :])


def in_hbm(array):
    return pltpu.with_memory_space_constraint(array, pltpu.HBM)


def shape(dims, dtype=F32):
    return jax.ShapeDtypeStruct(dims, dtype)


def make(subs, layers):
    matchings = neighbour_matchings(subs, layers)
    shuffles = [relay_shuffle(subs, layers, k) for k in range(WIN)]

    def trade(low, high):
        return [
            lax.ppermute(low if m < 2 else high, AXES, matchings[m]) for m in range(4)
        ]

    def on_device(geometry, dest_slot, pairs, colors, free_vel, inertia, exports):
        count = geometry.shape[2]
        bodies = free_vel.shape[2]
        interface = exports.shape[2]
        tiles = count // TILE
        slots = 16
        assert count % TILE == 0 and tiles < slots and 2 * interface == LANES
        assert bodies % LANES == 0
        blocks = bodies // LANES
        total = blocks + 2
        place = shape((10 * slots, LANES))
        small = shape((16, LANES))
        arguments = (geometry, dest_slot, free_vel, inertia, exports, pairs, colors)
        rows = slot_count(tiles)
        assert rows <= TILE_SLOT
        prepared = pl.pallas_call(
            prepare_kernel,
            out_shape=(
                shape((10 * slots + 16, LANES)), place, place, small, small,
                shape((16, bodies)),
                shape((16, LANES), jnp.int32),
                shape((WIDE, count), BF16),
                shape((16, count), BF16),
                shape((2, 80, count), BF16),
                shape((32, LANES), jnp.int32),
                shape((2 * rows, LANES), jnp.int32),
                shape((rows, LANES)),
                shape((1, LANES), jnp.int32),
            ),
            in_specs=[pl.BlockSpec(memory_space=pltpu.HBM)] * 7,
            out_specs=(VMEM_SPEC,) * 14,
            scratch_shapes=[
                pltpu.VMEM(geometry.shape, F32),
                pltpu.VMEM(dest_slot.shape, jnp.int32),
                pltpu.VMEM(free_vel.shape, F32),
                pltpu.VMEM(inertia.shape, F32),
                pltpu.VMEM(exports.shape, jnp.int32),
                pltpu.VMEM(pairs.shape, jnp.int32),
                pltpu.SMEM(colors.shape, jnp.int32),
                pltpu.SMEM((1, LANES), jnp.int32),
                pltpu.VMEM((8, LANES), jnp.int32),
                pltpu.VMEM((16, count), F32),
                pltpu.VMEM((16 * (WIN - 1), count), BF16),
                pltpu.VMEM((2 * 80 * (WIN - 1), count), BF16),
                pltpu.SemaphoreType.DMA((8,)),
            ],
            compiler_params=PARAMS,
            name="prepare",
        )(*[in_hbm(x) for x in arguments])
        send0, place2, place3, out0, out1, own, export_index = prepared[:7]
        wide_hot, own_mask, tall, ordered, index, used, scalars = prepared[7:]
        came = [lax.ppermute(send0, AXES, matchings[0])]
        came.append(lax.ppermute(out0, AXES, matchings[1]))
        came.append(lax.ppermute(out1, AXES, matchings[2]))
        came.append(lax.ppermute(out1, AXES, matchings[3]))
        place0 = pl.pallas_call(
            place_kernel,
            out_shape=place,
            in_specs=[VMEM_SPEC] * 3,
            out_specs=VMEM_SPEC,
            compiler_params=PARAMS,
            name="place",
        )(tall, own_mask, wide_hot)
        placed = [place0]
        placed.append(lax.ppermute(place2, AXES, shuffles[2]))
        placed.append(lax.ppermute(place3, AXES, shuffles[3]))

        def indexing(*refs):
            index_kernel(subs, layers, interface, bodies, *refs)

        hot, masks, export_hot, export_masks, mult, near_props, far_props = pl.pallas_call(
            indexing,
            out_shape=(
                shape((2 * TILE * (tiles + 1), LANES), BF16),
                shape((tiles + 1, 16 * (blocks + total), LANES), BF16),
                shape((LANES, 2 * LANES), BF16),
                shape((2, 16 * blocks, LANES), BF16),
                shape((8, bodies)),
                shape((8 * tiles, LANES)),
                shape((8 * tiles, LANES)),
            ),
            in_specs=[VMEM_SPEC] * 3,
            out_specs=(VMEM_SPEC,) * 7,
            compiler_params=PARAMS,
            name="indexing",
        )(ordered, export_index, own)

        state = impulse = None
        for sweep in range(SWEEPS):
            first, last = sweep == 0, sweep == SWEEPS - 1

            def run(*refs, first=first):
                sweep_kernel(bodies, interface, first, *refs)

            outs = [
                shape((3 * rows, LANES)),
                shape((8, bodies)),
                shape((8, LANES)),
                shape((8, LANES)),
            ]
            operands = [scalars, index, used, hot, masks, own, *came]
            if first:
                outs = [shape((STATE * rows, LANES))] + outs
                operands += [*placed, ordered, near_props, far_props]
            else:
                operands += [state, impulse]
            result = pl.pallas_call(
                run,
                out_shape=tuple(outs),
                in_specs=[VMEM_SPEC] * len(operands),
                out_specs=(VMEM_SPEC,) * len(outs),
                scratch_shapes=[
                    pltpu.VMEM((16 * GROUP, LANES), F32),
                    pltpu.VMEM((16 * GROUP, LANES), F32),
                    pltpu.VMEM((16 * GROUP, LANES), F32),
                    pltpu.VMEM((16 * GROUP, LANES), F32),
                    pltpu.VMEM((16 * total, LANES), F32),
                    pltpu.VMEM((8 * total, LANES), F32),
                    pltpu.VMEM((8 * rows, LANES), F32),
                    pltpu.VMEM((8 * rows, LANES), F32),
                    pltpu.VMEM((10 * slots, LANES), F32),
                    pltpu.VMEM((10 * rows, LANES), F32),
                    pltpu.SMEM((64,), jnp.int32),
                ],
                compiler_params=PARAMS,
                name="sweep",
            )(*operands)
            if first:
                state, result = result[0], result[1:]
            impulse, change, ghost0, ghost1 = result
            sums = trade(ghost0, ghost1)

            def merge(*refs, last=last):
                merge_kernel(interface, last, *refs)

            operands = [own, change, *sums, mult, export_index, export_hot, export_masks]
            if last:
                outs = (shape((6, 1, bodies)),)
            else:
                outs = (shape((8, bodies)), shape((8, LANES)), shape((8, LANES)))
            merged = pl.pallas_call(
                merge,
                out_shape=outs,
                in_specs=[VMEM_SPEC] * len(operands),
                out_specs=(VMEM_SPEC,) * len(outs),
                compiler_params=PARAMS,
                name="merge",
            )(*operands)
            if last:
                in_order = pl.pallas_call(
                    impulse_kernel,
                    out_shape=shape((3, 1, count)),
                    in_specs=[SMEM_SPEC, VMEM_SPEC],
                    out_specs=VMEM_SPEC,
                    compiler_params=PARAMS,
                    name="impulse",
                )(scalars, impulse)
                return in_order, merged[0]
            own = merged[0]
            came = trade(merged[1], merged[2])

    return on_device


def solution(mesh):
    placed = (
        P(None, "layer", "sub"),
        P("layer", "sub"),
        P(None, "layer", "sub"),
        P("layer", "sub"),
        P(None, "layer", "sub"),
        P(None, "layer", "sub"),
        P(None, "layer", "sub"),
    )
    return jax.shard_map(
        make(mesh.shape["sub"], mesh.shape["layer"]),
        mesh=mesh,
        in_specs=placed,
        out_specs=(P(None, "layer", "sub"), P(None, "layer", "sub")),
        check_vma=False,
    )
```

```python
import jax
import jax.numpy as jnp
from jax import lax
from jax.experimental import pallas as pl
from jax.experimental.pallas import tpu as pltpu
from jax.sharding import PartitionSpec as P

WIN = 4
SWEEPS = 3
NCOLOR = 4
TILE = 128
LANES = 128
WIDE = 256
GROUP = 4

relaxation = 0.7
friction = 0.6
tangent_floor = 0.1

AXES = ("sub", "layer")
F32 = jnp.float32
BF16 = jnp.bfloat16
VMEM_SPEC = pl.BlockSpec(memory_space=pltpu.VMEM)
SMEM_SPEC = pl.BlockSpec(memory_space=pltpu.SMEM)
PARAMS = pltpu.CompilerParams(vmem_limit_bytes=16 << 20)


def neighbour_matchings(subs, layers):
    assert subs % 2 == 0 and layers % 2 == 0

    def shifted(i):
        return i - 1 if i % 2 == 0 else i + 1

    def partner(match, s, y):
        if match == 0:
            return s ^ 1, y
        if match == 1:
            return (s, y ^ 1) if s in (0, subs - 1) else (shifted(s), y)
        if match == 2:
            return s, y ^ 1
        return (s ^ 1, y) if y in (0, layers - 1) else (s, shifted(y))

    out = []
    for match in range(4):
        pairs = []
        for s in range(subs):
            for y in range(layers):
                ps, py = partner(match, s, y)
                pairs.append((s * layers + y, ps * layers + py))
        out.append(pairs)
    return out


def relay_shuffle(subs, layers, k):
    return [
        (s * layers + y, (s ^ k) * layers + y) for s in range(subs) for y in range(layers)
    ]


def lane_iota():
    return lax.broadcasted_iota(jnp.int32, (8, LANES), 1)


def pick(tables, index):
    low = jnp.bitwise_and(index, LANES - 1)
    high = jnp.right_shift(index, 7)
    out = jnp.take_along_axis(tables[0], low, axis=1)
    for h in range(1, len(tables)):
        out = jnp.where(high == h, jnp.take_along_axis(tables[h], low, axis=1), out)
    return out


def two_parts(value):
    first = value.astype(BF16).astype(F32)
    return jnp.concatenate([first, value - first], axis=0).astype(BF16)


def equal_rows(row, count):
    shape = (count, row.shape[1])
    ids = lax.broadcasted_iota(jnp.int32, shape, 0).astype(F32).astype(BF16)
    here = jnp.broadcast_to(row.astype(F32), shape).astype(BF16)
    return jnp.where(ids == here, jnp.ones(shape, BF16), jnp.zeros(shape, BF16))


def high_masks(index_row, highs, shift=7):
    shape = (16, LANES)
    high = jnp.broadcast_to(jnp.right_shift(index_row, shift).astype(F32), shape).astype(BF16)
    one, zero = jnp.ones(shape, BF16), jnp.zeros(shape, BF16)
    return jnp.concatenate(
        [jnp.where(high == jnp.full(shape, h, BF16), one, zero) for h in range(highs)], axis=0
    )


def low_onehot(index_row):
    return equal_rows(jnp.bitwise_and(index_row, LANES - 1), LANES)


def contract_lanes(lhs, rhs):
    return lax.dot_general(
        lhs, rhs, (((1,), (1,)), ((), ())), preferred_element_type=F32
    )


def sum_parts(block, h):
    return block[16 * h : 16 * h + 8] + block[16 * h + 8 : 16 * h + 16]


def cross(u, v):
    return [
        u[1] * v[2] - u[2] * v[1],
        u[2] * v[0] - u[0] * v[2],
        u[0] * v[1] - u[1] * v[0],
    ]


def dot3(u, v):
    return u[0] * v[0] + u[1] * v[1] + u[2] * v[2]


def halves(low, high, half):
    return jnp.where(lane_iota() < half, low, high)


def parities():
    sub = lax.axis_index("sub")
    layer = lax.axis_index("layer")
    return sub, layer, lax.rem(sub, 2) == 0, lax.rem(layer, 2) == 0


def prepare_kernel(
    geo_hbm, dest_hbm, vel_hbm, inertia_hbm, exports_hbm, pairs_hbm, colors_hbm,
    send0, place2, place3, out0, out1, start_own, export_index, hot, own_mask, tall,
    ordered, index_out, used, scalars_out,
    geo, dest, vel, inertia, exports, pairs, colors, scalars, listed, dense, mask, lhs, sems,
):
    copies = [
        pltpu.make_async_copy(src, dst, sems.at[i])
        for i, (src, dst) in enumerate(
            [
                (exports_hbm, exports),
                (vel_hbm, vel),
                (inertia_hbm, inertia),
                (dest_hbm, dest),
                (colors_hbm, colors),
                (pairs_hbm, pairs),
                (geo_hbm, geo),
            ]
        )
    ]
    for copy in copies:
        copy.start()
    count = geo.shape[2]
    tiles = count // TILE
    slots = place2.shape[0] // 10
    bodies = vel.shape[2]
    interface = exports.shape[2]
    sub, layer, sub_even, layer_even = parities()
    member = lax.rem(sub, WIN)
    start_own[...] = jnp.zeros_like(start_own)
    dense[...] = jnp.zeros_like(dense)
    for copy in copies[:6]:
        copy.wait()
    for r in range(6):
        start_own[r : r + 1, :] = vel[r]
    for r in range(4):
        start_own[8 + r : 9 + r, :] = inertia[r]
    listed[0:1, 0:interface] = exports[0]
    listed[0:1, interface : 2 * interface] = exports[1]
    listed[1:2, 0:interface] = exports[1]
    listed[1:2, interface : 2 * interface] = exports[0]
    listed[2:3, 0:interface] = exports[2]
    listed[2:3, interface : 2 * interface] = exports[3]
    listed[3:4, 0:interface] = exports[3]
    listed[3:4, interface : 2 * interface] = exports[2]
    row0 = jnp.where(sub_even, listed[1:2, :], listed[0:1, :])
    row1 = jnp.where(layer_even, listed[3:4, :], listed[2:3, :])
    idx0 = jnp.broadcast_to(row0, (8, LANES))
    idx1 = jnp.broadcast_to(row1, (8, LANES))
    export_index[0:8, :] = idx0
    export_index[8:16, :] = idx1
    blocks = bodies // LANES
    for base in (0, 8):
        tables = [
            start_own[base : base + 8, h * LANES : (h + 1) * LANES] for h in range(blocks)
        ]
        picked = pick(tables, idx0)
        out0[base : base + 8, :] = picked
        send0[10 * slots + base : 10 * slots + base + 8, :] = picked
        out1[base : base + 8, :] = pick(tables, idx1)
    rank = used.shape[0]
    for i in range(rank):
        scalars[0, i] = tiles
    for k in range(NCOLOR):
        scalars[0, FILLED + k] = 0
    colored, ranks = [], []
    for t in range(tiles):
        color = colors[0, t]
        rank_here = scalars[0, FILLED + color]
        scalars[0, FILLED + color] = rank_here + 1
        colored.append(color)
        ranks.append(rank_here)
    over = jnp.int32(0)
    for k in range(NCOLOR):
        scalars[0, OVER_BASE + k] = (NCOLOR + over) * GROUP - GROUP
        scalars[0, OVER_FROM + k] = over
        filled = scalars[0, FILLED + k]
        over = over + jnp.right_shift(jnp.maximum(filled - 1, GROUP - 1), GROUP.bit_length() - 1)
        scalars[0, OVER_TO + k] = over
    place = []
    for t in range(tiles):
        base = jnp.where(ranks[t] < GROUP, GROUP * colored[t], scalars[0, OVER_BASE + colored[t]])
        place.append(base + ranks[t])
        scalars[0, place[t]] = t
    index_out[...] = jnp.zeros_like(index_out)
    ordered[...] = jnp.zeros_like(ordered)
    used[...] = jnp.zeros_like(used)
    flip_sub = jnp.where(sub_even, interface, 0)
    flip_layer = jnp.where(layer_even, interface, 0)
    for t in range(tiles):
        span = slice(t * TILE, (t + 1) * TILE)
        nearer = pairs[0, :, span]
        other = pairs[1, :, span]
        ghost = other - bodies
        turned = jnp.where(
            ghost < 2 * interface,
            jnp.bitwise_xor(ghost, flip_sub),
            jnp.bitwise_xor(ghost, flip_layer),
        )
        farther = jnp.where(ghost < 0, other, bodies + turned)
        scalars[0, TILE_SLOT + t] = place[t]
        ordered[t : t + 1, :] = nearer
        ordered[16 + t : 17 + t, :] = farther
        index_out[pl.ds(place[t], 1), :] = nearer
        index_out[pl.ds(rank + place[t], 1), :] = farther
        used[pl.ds(place[t], 1), :] = jnp.ones((1, LANES), F32)
    slot = dest[...] - (sub - member) * count
    target = jnp.zeros_like(slot)
    for m in range(1, WIN):
        target = target + jnp.where(slot >= m * count, 1, 0)
    within = slot - target * count
    row_id = jnp.bitwise_xor(target, member) * 8 + jnp.right_shift(within, 8)
    low = jnp.bitwise_and(within, WIDE - 1)
    paired = (16, TILE)
    ids = lax.broadcasted_iota(jnp.int32, paired, 0)
    ids = jnp.bitwise_and(ids, 7).astype(F32)
    one, zero = jnp.ones(paired, BF16), jnp.zeros(paired, BF16)
    for t in range(tiles):
        span = slice(t * TILE, (t + 1) * TILE)
        hot[:, span] = equal_rows(low[:, span], WIDE)
        here = jnp.broadcast_to(row_id[:, span].astype(F32), paired).astype(BF16)
        for k in range(WIN):
            chosen = jnp.where(here == (ids + 8.0 * k).astype(BF16), one, zero)
            if k == 0:
                own_mask[:, span] = chosen
            else:
                mask[16 * k - 16 : 16 * k, span] = chosen
    give = pltpu.make_async_copy(scalars, scalars_out, sems.at[7])
    give.start()
    copies[6].wait()
    for r in range(10):
        dense[r : r + 1, :] = geo[r]
    value = dense[...]
    first = value.astype(BF16).astype(F32)
    parts = [first, value - first]
    for p in range(2):
        for i in range(5):
            pair = jnp.concatenate(
                [jnp.broadcast_to(parts[p][r : r + 1, :], (8, count)) for r in (2 * i, 2 * i + 1)],
                axis=0,
            ).astype(BF16)
            tall[p, 16 * i : 16 * i + 16, :] = pair
            for k in range(1, WIN):
                at = 80 * (WIN - 1) * p + 80 * (k - 1) + 16 * i
                lhs[at : at + 16, :] = mask[16 * k - 16 : 16 * k, :] * pair
    both = contract_lanes(lhs[...], hot[...])
    total = both[: 80 * (WIN - 1)] + both[80 * (WIN - 1) :]
    for k, out in enumerate((send0, place2, place3)):
        store_placed(out, total[80 * k : 80 * k + 80, :])
    give.wait()


def store_placed(out, total):
    for r in range(10):
        for side in range(2):
            out[16 * r + 8 * side : 16 * r + 8 * side + 8, :] = total[
                8 * r : 8 * r + 8, side * LANES : (side + 1) * LANES
            ]


def place_kernel(tall, own_mask, hot, out):
    left = [jnp.concatenate([own_mask[...]] * 5, axis=0) * tall[p] for p in range(2)]
    both = contract_lanes(jnp.concatenate(left, axis=0), hot[...])
    store_placed(out, both[:80] + both[80:])


TILE_SLOT, OVER_FROM, FILLED, OVER_TO, OVER_BASE = 32, 48, 52, 56, 60


def overflow_groups(tiles):
    most = 0
    for busy in range(1, NCOLOR + 1):
        spare = tiles - busy * (GROUP + 1)
        if spare >= 0:
            most = max(most, busy + spare // GROUP)
    return most


def slot_count(tiles):
    return -(-GROUP * (NCOLOR + overflow_groups(tiles)) // 8) * 8


def index_kernel(
    subs, layers, interface, bodies, ordered, export_index, own,
    hot, masks, export_hot, export_masks, mult, near_props, far_props,
):
    tiles = masks.shape[0] - 1
    blocks = bodies // LANES
    total = blocks + 4 * interface // LANES
    sub, layer, sub_even, layer_even = parities()
    props = [own[8:16, h * LANES : (h + 1) * LANES] for h in range(blocks)]
    square = (TILE, LANES)
    lane_ids = lax.broadcasted_iota(jnp.int32, square, 1)
    eye = jnp.where(lax.broadcasted_iota(jnp.int32, square, 0) == lane_ids, 1.0, 0.0)
    lane_ids = lax.broadcasted_iota(jnp.int32, (TILE, WIDE), 1).astype(F32)
    low_rows = jnp.bitwise_and(ordered[...], WIDE - 1).astype(F32).astype(BF16)
    columns = contract_lanes(eye.astype(BF16), low_rows).astype(BF16)
    ids = lax.broadcasted_iota(jnp.int32, (32, 2 * TILE), 0)
    lanes = lax.broadcasted_iota(jnp.int32, (32, 2 * TILE), 1)
    for t in range(tiles):
        first = ordered[t : t + 1, :]
        second = ordered[16 + t : 17 + t, :]
        near_props[8 * t : 8 * t + 8, :] = pick(props, jnp.broadcast_to(first, (8, LANES)))
        far_props[8 * t : 8 * t + 8, :] = pick(props, jnp.broadcast_to(second, (8, LANES)))
        sides = jnp.where(lanes < TILE, t, 16 + t)
        chosen = jnp.where(ids == sides, 1.0, 0.0).astype(BF16)
        low = jnp.dot(columns, chosen, preferred_element_type=F32)
        for side in range(2):
            here = low[:, side * TILE : (side + 1) * TILE]
            hit = jnp.concatenate([here, here], axis=1) == lane_ids
            at = (2 * t + side) * TILE
            hot[at : at + TILE, :] = jnp.where(hit, 1.0, 0.0).astype(BF16)
        masks[t, : 8 * blocks, :] = high_masks(first, blocks // 2, 8)
        masks[t, 8 * blocks :, :] = high_masks(second, total // 2, 8)
    hot[2 * tiles * TILE :, :] = jnp.zeros((2 * TILE, WIDE), BF16)
    masks[tiles] = jnp.zeros_like(masks[tiles])
    inner_sub = jnp.where(jnp.logical_and(sub > 0, sub < subs - 1), 1.0, 0.0)
    inner_layer = jnp.where(jnp.logical_and(layer > 0, layer < layers - 1), 1.0, 0.0)
    lane = lane_iota()
    weights = [
        jnp.where(lane < interface, 1.0, inner_sub),
        jnp.where(lane < interface, 1.0, inner_layer),
    ]
    left = []
    for i in range(2):
        row = export_index[8 * i : 8 * i + 1, :]
        export_hot[:, i * LANES : (i + 1) * LANES] = low_onehot(row)
        chosen = high_masks(row, blocks)
        export_masks[i] = chosen
        weight = jnp.concatenate([weights[i], jnp.zeros_like(weights[i])], axis=0).astype(BF16)
        left.append(jnp.concatenate([weight] * blocks, axis=0) * chosen)
    listed = contract_lanes(jnp.concatenate(left, axis=1), export_hot[...])
    for h in range(blocks):
        mult[:, h * LANES : (h + 1) * LANES] = 1.0 + listed[16 * h : 16 * h + 8]


STATE = 34


def contact_state(geo, first, second):
    raw = geo[0:3]
    length = jnp.sqrt(dot3(raw, raw))
    normal = [x / length for x in raw]
    side = jnp.sqrt(normal[1] * normal[1] + normal[2] * normal[2])
    tan_y = normal[2] / side
    tan_z = -normal[1] / side
    two = [
        normal[1] * tan_z - normal[2] * tan_y,
        -normal[0] * tan_z,
        normal[0] * tan_y,
    ]

    def arm(p, spin):
        return [
            spin[1] * p[2] * p[2] + spin[2] * p[1] * p[1],
            spin[0] * p[2] * p[2] + spin[2] * p[0] * p[0],
            spin[0] * p[1] * p[1] + spin[1] * p[0] * p[0],
            -spin[2] * p[0] * p[1],
            -spin[1] * p[0] * p[2],
            -spin[0] * p[1] * p[2],
        ]

    arm_a, arm_b = geo[3:6], geo[6:9]
    e = [x + y for x, y in zip(arm(arm_a, first[1:4]), arm(arm_b, second[1:4]))]
    mass = first[0] + second[0]
    xx, yy, zz = mass + e[0], mass + e[1], mass + e[2]
    xy, xz, yz = e[3], e[4], e[5]
    c_xx = yy * zz - yz * yz
    c_xy = xz * yz - xy * zz
    c_xz = xy * yz - xz * yy
    c_yy = xx * zz - xz * xz
    c_yz = xy * xz - xx * yz
    c_zz = xx * yy - xy * xy
    det = xx * c_xx + xy * c_xy + xz * c_xz
    inv = [
        [c_xx / det, c_xy / det, c_xz / det],
        [c_xy / det, c_yy / det, c_yz / det],
        [c_xz / det, c_yz / det, c_zz / det],
    ]
    solve = []
    for row in (normal, None, two):
        for j in range(3):
            if row is None:
                value = tan_y * inv[1][j] + tan_z * inv[2][j]
            else:
                value = row[0] * inv[0][j] + row[1] * inv[1][j] + row[2] * inv[2][j]
            solve.append(relaxation * value)
    bias = [geo[9] * dot3(solve[3 * i : 3 * i + 3], normal) for i in range(3)]
    return (
        solve + bias + normal + [tan_y, tan_z] + two + arm_a + arm_b + list(first) + list(second)
    )


def sweep_kernel(bodies, interface, first_sweep, *refs):
    scalars_in, index, used, hot, masks = refs[:5]
    refs = refs[5:]
    if first_sweep:
        own, g1, r1, r2, r3, g0, g2, g3, ordered, near_props, far_props, state = refs[:12]
        refs = refs[12:]
        r0 = g1.at[pl.ds(g0.shape[0], 16), :]
    else:
        own, r0, r1, r2, r3, state, impulse_in = refs[:7]
        refs = refs[7:]
    impulse, own_change, ghost0, ghost1 = refs[:4]
    got_a, got_b, push_a, push_b, acc, table, all_a, all_b, gathered, placed, scalars = refs[4:]
    slots = used.shape[0]
    tiles = masks.shape[0] - 1
    blocks = bodies // LANES
    total = blocks + (4 * interface) // LANES
    values = scalars_in[...]
    wanted = list(range(slots)) + [OVER_FROM + k for k in range(NCOLOR)]
    wanted += [OVER_TO + k for k in range(NCOLOR)]
    if first_sweep:
        wanted += [TILE_SLOT + t for t in range(tiles)]
    for i in wanted:
        scalars[i] = values[0, i]

    def ghost_blocks(base):
        return [
            halves(r0[base : base + 8, :], r1[base : base + 8, :], interface),
            halves(r2[base : base + 8, :], r3[base : base + 8, :], interface),
        ]

    start = [own[0:8, h * LANES : (h + 1) * LANES] for h in range(blocks)] + ghost_blocks(0)
    for h in range(total):
        table[8 * h : 8 * h + 8, :] = start[h]
    push_a[...] = jnp.zeros_like(push_a)
    push_b[...] = jnp.zeros_like(push_b)

    if first_sweep:
        ghost_props = ghost_blocks(8)
        far = []
        for t in range(tiles):
            ib = jnp.broadcast_to(ordered[16 + t : 17 + t, :], (8, LANES))
            low, high = jnp.bitwise_and(ib, LANES - 1), jnp.right_shift(ib, 7)
            value = far_props[8 * t : 8 * t + 8, :]
            for h, block in enumerate(ghost_props):
                value = jnp.where(
                    high == blocks + h, jnp.take_along_axis(block, low, axis=1), value
                )
            far.append(value)
        all_a[...] = jnp.ones_like(all_a)
        all_b[...] = jnp.ones_like(all_b)
        gathered[...] = (g0[...] + g1[0 : g0.shape[0], :]) + (g2[...] + g3[...])
        placed[...] = jnp.ones_like(placed)
        rows = g0.shape[0] // 10
        for t in range(tiles):
            slot = scalars[TILE_SLOT + t]
            group_rows = pl.ds(pl.multiple_of(8 * slot, 8), 8)
            all_a[group_rows, :] = near_props[8 * t : 8 * t + 8, :]
            all_b[group_rows, :] = far[t]
            at = 8 * (t % 2) + t // 2
            for c in range(10):
                row = c * rows + at
                placed[pl.ds(c * slots + slot, 1), :] = gathered[row : row + 1, :]
        first = [all_a[pl.ds(c, slots, stride=8), :] for c in range(4)]
        second = [all_b[pl.ds(c, slots, stride=8), :] for c in range(4)]
        geo = [placed[c * slots : (c + 1) * slots, :] for c in range(10)]
        for c, value in enumerate(contact_state(geo, first, second)):
            state[c * slots : (c + 1) * slots, :] = value
        impulse[...] = jnp.zeros_like(impulse)
    else:
        impulse[...] = impulse_in[...]

    def held_at(base):
        return lambda c: state[pl.ds(c * slots + base, GROUP), :]

    def gather(base, room, now):
        for j in range(GROUP):
            ia = jnp.broadcast_to(index[pl.ds(base + j, 1), :], (8, LANES))
            ib = jnp.broadcast_to(index[pl.ds(slots + base + j, 1), :], (8, LANES))
            got_a[room + 8 * j : room + 8 * j + 8, :] = pick(now[:blocks], ia)
            got_b[room + 8 * j : room + 8 * j + 8, :] = pick(now, ib)

    def press(base, room):
        held = held_at(base)
        tile_rows = [pl.ds(room + c, GROUP, stride=8) for c in range(6)]
        va = [got_a[tile_rows[c], :] for c in range(6)]
        vb = [got_b[tile_rows[c], :] for c in range(6)]
        arm_a = [held(20 + c) for c in range(3)]
        arm_b = [held(23 + c) for c in range(3)]
        turn_a = cross(va[3:6], arm_a)
        turn_b = cross(vb[3:6], arm_b)
        rel = [((va[c] + turn_a[c]) - vb[c]) - turn_b[c] for c in range(3)]
        old = [impulse[pl.ds(c * slots + base, GROUP), :] for c in range(3)]
        trial = [
            old[c] - (dot3([held(3 * c + j) for j in range(3)], rel) + held(9 + c))
            for c in range(3)
        ]
        normal_part = jnp.maximum(trial[0], 0.0)
        slide = trial[1] * trial[1] + trial[2] * trial[2]
        shrink = lax.rsqrt(jnp.maximum(slide, tangent_floor * tangent_floor))
        factor = jnp.minimum(1.0, friction * normal_part * shrink)
        active = used[pl.ds(base, GROUP), :] > 0.5
        new = [
            jnp.where(active, normal_part, old[0]),
            jnp.where(active, trial[1] * factor, old[1]),
            jnp.where(active, trial[2] * factor, old[2]),
        ]
        change = [new[c] - old[c] for c in range(3)]
        for c in range(3):
            impulse[pl.ds(c * slots + base, GROUP), :] = new[c]
        force = [
            held(12) * change[0] + held(17) * change[2],
            held(13) * change[0] + held(15) * change[1] + held(18) * change[2],
            held(14) * change[0] + held(16) * change[1] + held(19) * change[2],
        ]
        spin_a = cross(arm_a, force)
        spin_b = cross(arm_b, force)
        for c in range(3):
            push_a[tile_rows[c], :] = held(26) * force[c]
            push_a[tile_rows[3 + c], :] = held(27 + c) * spin_a[c]
            push_b[tile_rows[c], :] = -(held(30) * force[c])
            push_b[tile_rows[3 + c], :] = -(held(31 + c) * spin_b[c])

    def sides(base, room):
        left, right = [], []
        near = blocks // 2
        empty = jnp.zeros((8 * (total - blocks), LANES), BF16)
        for j in range(GROUP):
            t = scalars[base + j]
            first = two_parts(push_a[room + 8 * j : room + 8 * j + 8, :])
            second = two_parts(push_b[room + 8 * j : room + 8 * j + 8, :])
            rows = [masks[t, 16 * m : 16 * m + 16, :] for m in range(near + total // 2)]
            left.append(jnp.concatenate([first * m for m in rows[:near]] + [empty], axis=0))
            left.append(jnp.concatenate([second * m for m in rows[near:]], axis=0))
            right.append(hot[pl.ds(pl.multiple_of(2 * TILE * t, 2 * TILE), 2 * TILE), :])
        return left, right

    def groups(bases, now):
        rooms = [8 * GROUP * i for i in range(len(bases))]
        for base, room in zip(bases, rooms):
            gather(base, room, now)
        for base, room in zip(bases, rooms):
            press(base, room)
        left, right = [], []
        for base, room in zip(bases, rooms):
            more_left, more_right = sides(base, room)
            left += more_left
            right += more_right
        return jnp.dot(
            jnp.concatenate(left, axis=1),
            jnp.concatenate(right, axis=0),
            preferred_element_type=F32,
        )

    def color_pass(k):
        now = [table[8 * h : 8 * h + 8, :] for h in range(total)]
        main = pl.multiple_of(GROUP * k, GROUP)

        def over(g):
            return pl.multiple_of(GROUP * (NCOLOR + g), GROUP)

        begin, end = scalars[OVER_FROM + k], scalars[OVER_TO + k]

        @pl.when(end > begin)
        def _():
            acc[...] = groups([main, over(begin)], now)

        @pl.when(end <= begin)
        def _():
            acc[...] = groups([main], now)

        def more(g, c):
            acc[...] += groups([over(g)], now)
            return c

        lax.fori_loop(begin + 1, end, more, 0)
        for h in range(total):
            side = slice((h % 2) * LANES, (h % 2 + 1) * LANES)
            at = 16 * (h // 2)
            table[8 * h : 8 * h + 8, :] = now[h] + (
                acc[at : at + 8, side] + acc[at + 8 : at + 16, side]
            )

    def later_pass(k, carry):
        color_pass(k)
        return carry

    lax.fori_loop(0, NCOLOR, later_pass, 0)
    for h in range(blocks):
        own_change[:, h * LANES : (h + 1) * LANES] = table[8 * h : 8 * h + 8, :] - start[h]
    ghost0[...] = table[8 * blocks : 8 * blocks + 8, :] - start[blocks]
    ghost1[...] = table[8 * blocks + 8 : 8 * blocks + 16, :] - start[blocks + 1]


def impulse_kernel(scalars, held, impulse):
    slots = held.shape[0] // 3
    for t in range(impulse.shape[2] // TILE):
        slot = scalars[0, TILE_SLOT + t]
        for c in range(3):
            impulse[c, :, t * TILE : (t + 1) * TILE] = held[pl.ds(c * slots + slot, 1), :]


def merge_kernel(
    interface, last_sweep, own, change, c0, c1, c2, c3, mult, export_index, export_hot,
    export_masks, *refs,
):
    blocks = own.shape[1] // LANES
    came = [halves(c0[...], c1[...], interface), halves(c2[...], c3[...], interface)]
    left = jnp.concatenate(
        [
            jnp.concatenate([two_parts(came[i])] * blocks, axis=0) * export_masks[i]
            for i in range(2)
        ],
        axis=1,
    )
    incoming = contract_lanes(left, export_hot[...])
    fresh = []
    for h in range(blocks):
        span = slice(h * LANES, (h + 1) * LANES)
        fresh.append(
            own[0:8, span] + (change[:, span] + sum_parts(incoming, h)) / mult[:, span]
        )
    if last_sweep:
        (velocity,) = refs
        for r in range(6):
            for h in range(blocks):
                velocity[r, :, h * LANES : (h + 1) * LANES] = fresh[h][r : r + 1, :]
    else:
        fresh_own, out0, out1 = refs
        for h in range(blocks):
            fresh_own[:, h * LANES : (h + 1) * LANES] = fresh[h]
        out0[...] = pick(fresh, export_index[0:8, :])
        out1[...] = pick(fresh, export_index[8:16, :])


def in_hbm(array):
    return pltpu.with_memory_space_constraint(array, pltpu.HBM)


def shape(dims, dtype=F32):
    return jax.ShapeDtypeStruct(dims, dtype)


def make(subs, layers):
    matchings = neighbour_matchings(subs, layers)
    shuffles = [relay_shuffle(subs, layers, k) for k in range(WIN)]

    def trade(low, high):
        return [
            lax.ppermute(low if m < 2 else high, AXES, matchings[m]) for m in range(4)
        ]

    def on_device(geometry, dest_slot, pairs, colors, free_vel, inertia, exports):
        count = geometry.shape[2]
        bodies = free_vel.shape[2]
        interface = exports.shape[2]
        tiles = count // TILE
        slots = 16
        assert count % TILE == 0 and tiles < slots and 2 * interface == LANES
        assert bodies % WIDE == 0
        blocks = bodies // LANES
        total = blocks + 2
        place = shape((10 * slots, LANES))
        small = shape((16, LANES))
        arguments = (geometry, dest_slot, free_vel, inertia, exports, pairs, colors)
        rows = slot_count(tiles)
        assert rows <= TILE_SLOT
        prepared = pl.pallas_call(
            prepare_kernel,
            out_shape=(
                shape((10 * slots + 16, LANES)), place, place, small, small,
                shape((16, bodies)),
                shape((16, LANES), jnp.int32),
                shape((WIDE, count), BF16),
                shape((16, count), BF16),
                shape((2, 80, count), BF16),
                shape((32, LANES), jnp.int32),
                shape((2 * rows, LANES), jnp.int32),
                shape((rows, LANES)),
                shape((1, LANES), jnp.int32),
            ),
            in_specs=[pl.BlockSpec(memory_space=pltpu.HBM)] * 7,
            out_specs=(VMEM_SPEC,) * 14,
            scratch_shapes=[
                pltpu.VMEM(geometry.shape, F32),
                pltpu.VMEM(dest_slot.shape, jnp.int32),
                pltpu.VMEM(free_vel.shape, F32),
                pltpu.VMEM(inertia.shape, F32),
                pltpu.VMEM(exports.shape, jnp.int32),
                pltpu.VMEM(pairs.shape, jnp.int32),
                pltpu.SMEM(colors.shape, jnp.int32),
                pltpu.SMEM((1, LANES), jnp.int32),
                pltpu.VMEM((8, LANES), jnp.int32),
                pltpu.VMEM((16, count), F32),
                pltpu.VMEM((16 * (WIN - 1), count), BF16),
                pltpu.VMEM((2 * 80 * (WIN - 1), count), BF16),
                pltpu.SemaphoreType.DMA((8,)),
            ],
            compiler_params=PARAMS,
            name="prepare",
        )(*[in_hbm(x) for x in arguments])
        send0, place2, place3, out0, out1, own, export_index = prepared[:7]
        wide_hot, own_mask, tall, ordered, index, used, scalars = prepared[7:]
        came = [lax.ppermute(send0, AXES, matchings[0])]
        came.append(lax.ppermute(out0, AXES, matchings[1]))
        came.append(lax.ppermute(out1, AXES, matchings[2]))
        came.append(lax.ppermute(out1, AXES, matchings[3]))
        place0 = pl.pallas_call(
            place_kernel,
            out_shape=place,
            in_specs=[VMEM_SPEC] * 3,
            out_specs=VMEM_SPEC,
            compiler_params=PARAMS,
            name="place",
        )(tall, own_mask, wide_hot)
        placed = [place0]
        placed.append(lax.ppermute(place2, AXES, shuffles[2]))
        placed.append(lax.ppermute(place3, AXES, shuffles[3]))

        def indexing(*refs):
            index_kernel(subs, layers, interface, bodies, *refs)

        hot, masks, export_hot, export_masks, mult, near_props, far_props = pl.pallas_call(
            indexing,
            out_shape=(
                shape((2 * TILE * (tiles + 1), WIDE), BF16),
                shape((tiles + 1, 8 * (blocks + total), LANES), BF16),
                shape((LANES, 2 * LANES), BF16),
                shape((2, 16 * blocks, LANES), BF16),
                shape((8, bodies)),
                shape((8 * tiles, LANES)),
                shape((8 * tiles, LANES)),
            ),
            in_specs=[VMEM_SPEC] * 3,
            out_specs=(VMEM_SPEC,) * 7,
            compiler_params=PARAMS,
            name="indexing",
        )(ordered, export_index, own)

        state = impulse = None
        for sweep in range(SWEEPS):
            first, last = sweep == 0, sweep == SWEEPS - 1

            def run(*refs, first=first):
                sweep_kernel(bodies, interface, first, *refs)

            outs = [
                shape((3 * rows, LANES)),
                shape((8, bodies)),
                shape((8, LANES)),
                shape((8, LANES)),
            ]
            operands = [scalars, index, used, hot, masks, own, *came]
            if first:
                outs = [shape((STATE * rows, LANES))] + outs
                operands += [*placed, ordered, near_props, far_props]
            else:
                operands += [state, impulse]
            result = pl.pallas_call(
                run,
                out_shape=tuple(outs),
                in_specs=[VMEM_SPEC] * len(operands),
                out_specs=(VMEM_SPEC,) * len(outs),
                scratch_shapes=[
                    pltpu.VMEM((16 * GROUP, LANES), F32),
                    pltpu.VMEM((16 * GROUP, LANES), F32),
                    pltpu.VMEM((16 * GROUP, LANES), F32),
                    pltpu.VMEM((16 * GROUP, LANES), F32),
                    pltpu.VMEM((8 * total, WIDE), F32),
                    pltpu.VMEM((8 * total, LANES), F32),
                    pltpu.VMEM((8 * rows, LANES), F32),
                    pltpu.VMEM((8 * rows, LANES), F32),
                    pltpu.VMEM((10 * slots, LANES), F32),
                    pltpu.VMEM((10 * rows, LANES), F32),
                    pltpu.SMEM((64,), jnp.int32),
                ],
                compiler_params=PARAMS,
                name="sweep",
            )(*operands)
            if first:
                state, result = result[0], result[1:]
            impulse, change, ghost0, ghost1 = result
            sums = trade(ghost0, ghost1)

            def merge(*refs, last=last):
                merge_kernel(interface, last, *refs)

            operands = [own, change, *sums, mult, export_index, export_hot, export_masks]
            if last:
                outs = (shape((6, 1, bodies)),)
            else:
                outs = (shape((8, bodies)), shape((8, LANES)), shape((8, LANES)))
            merged = pl.pallas_call(
                merge,
                out_shape=outs,
                in_specs=[VMEM_SPEC] * len(operands),
                out_specs=(VMEM_SPEC,) * len(outs),
                compiler_params=PARAMS,
                name="merge",
            )(*operands)
            if last:
                in_order = pl.pallas_call(
                    impulse_kernel,
                    out_shape=shape((3, 1, count)),
                    in_specs=[SMEM_SPEC, VMEM_SPEC],
                    out_specs=VMEM_SPEC,
                    compiler_params=PARAMS,
                    name="impulse",
                )(scalars, impulse)
                return in_order, merged[0]
            own = merged[0]
            came = trade(merged[1], merged[2])

    return on_device


def solution(mesh):
    placed = (
        P(None, "layer", "sub"),
        P("layer", "sub"),
        P(None, "layer", "sub"),
        P("layer", "sub"),
        P(None, "layer", "sub"),
        P(None, "layer", "sub"),
        P(None, "layer", "sub"),
    )
    return jax.shard_map(
        make(mesh.shape["sub"], mesh.shape["layer"]),
        mesh=mesh,
        in_specs=placed,
        out_specs=(P(None, "layer", "sub"), P(None, "layer", "sub")),
        check_vma=False,
    )
```

```python
import jax
import jax.numpy as jnp
from jax import lax
from jax.experimental import pallas as pl
from jax.experimental.pallas import tpu as pltpu
from jax.sharding import PartitionSpec as P


WIN = 4
SWEEPS = 3
NCOLOR = 4
TILE = 128
LANES = 128
WIDE = 256
GROUP = 4

relaxation = 0.7
friction = 0.6
tangent_floor = 0.1

AXES = ("sub", "layer")
ORDER = (1, 0, 2, 3)
F32 = jnp.float32
BF16 = jnp.bfloat16
VMEM_SPEC = pl.BlockSpec(memory_space=pltpu.VMEM)
SMEM_SPEC = pl.BlockSpec(memory_space=pltpu.SMEM)
PARAMS = pltpu.CompilerParams(vmem_limit_bytes=16 << 20)


def neighbour_matchings(subs, layers):
    assert subs % 2 == 0 and layers % 2 == 0

    def shifted(i):
        return i - 1 if i % 2 == 0 else i + 1

    def partner(match, s, y):
        if match == 0:
            return s ^ 1, y
        if match == 1:
            return (s, y ^ 1) if s in (0, subs - 1) else (shifted(s), y)
        if match == 2:
            return s, y ^ 1
        return (s ^ 1, y) if y in (0, layers - 1) else (s, shifted(y))

    out = []
    for match in range(4):
        pairs = []
        for s in range(subs):
            for y in range(layers):
                ps, py = partner(match, s, y)
                pairs.append((s * layers + y, ps * layers + py))
        out.append(pairs)
    return out


def relay_shuffle(subs, layers, k):
    return [
        (s * layers + y, (s ^ k) * layers + y) for s in range(subs) for y in range(layers)
    ]


def lane_iota():
    return lax.broadcasted_iota(jnp.int32, (8, LANES), 1)


def pick(tables, index):
    low = jnp.bitwise_and(index, LANES - 1)
    high = jnp.right_shift(index, 7)
    out = jnp.take_along_axis(tables[0], low, axis=1)
    for h in range(1, len(tables)):
        out = jnp.where(high == h, jnp.take_along_axis(tables[h], low, axis=1), out)
    return out


def two_parts(value):
    first = value.astype(BF16).astype(F32)
    return jnp.concatenate([first, value - first], axis=0).astype(BF16)


def equal_rows(row, count):
    shape = (count, row.shape[1])
    ids = lax.broadcasted_iota(jnp.int32, shape, 0).astype(F32).astype(BF16)
    here = jnp.broadcast_to(row.astype(F32), shape).astype(BF16)
    return jnp.where(ids == here, jnp.ones(shape, BF16), jnp.zeros(shape, BF16))


def high_masks(index_row, highs, shift=7):
    shape = (16, LANES)
    high = jnp.broadcast_to(jnp.right_shift(index_row, shift).astype(F32), shape).astype(BF16)
    one, zero = jnp.ones(shape, BF16), jnp.zeros(shape, BF16)
    return jnp.concatenate(
        [jnp.where(high == jnp.full(shape, h, BF16), one, zero) for h in range(highs)], axis=0
    )


def low_onehot(index_row):
    return equal_rows(jnp.bitwise_and(index_row, LANES - 1), LANES)


def contract_lanes(lhs, rhs):
    return lax.dot_general(
        lhs, rhs, (((1,), (1,)), ((), ())), preferred_element_type=F32
    )


def sum_parts(block, h):
    return block[16 * h : 16 * h + 8] + block[16 * h + 8 : 16 * h + 16]


def cross(u, v):
    return [
        u[1] * v[2] - u[2] * v[1],
        u[2] * v[0] - u[0] * v[2],
        u[0] * v[1] - u[1] * v[0],
    ]


def dot3(u, v):
    return u[0] * v[0] + u[1] * v[1] + u[2] * v[2]


def halves(low, high, half):
    return jnp.where(lane_iota() < half, low, high)


def parities():
    sub = lax.axis_index("sub")
    layer = lax.axis_index("layer")
    return sub, layer, lax.rem(sub, 2) == 0, lax.rem(layer, 2) == 0


def prepare_kernel(
    geo_hbm, dest_hbm, vel_hbm, inertia_hbm, exports_hbm, pairs_hbm, colors_hbm,
    send0, place2, place3, out0, out1, start_own, export_index, hot, own_mask, tall,
    ordered, index_out, used, scalars_out,
    geo, dest, vel, inertia, exports, pairs, colors, scalars, listed, dense, mask, lhs, sems,
):
    copies = [
        pltpu.make_async_copy(src, dst, sems.at[i])
        for i, (src, dst) in enumerate(
            [
                (exports_hbm, exports),
                (vel_hbm, vel),
                (inertia_hbm, inertia),
                (dest_hbm, dest),
                (colors_hbm, colors),
                (pairs_hbm, pairs),
                (geo_hbm, geo),
            ]
        )
    ]
    for copy in copies:
        copy.start()
    count = geo.shape[2]
    tiles = count // TILE
    slots = place2.shape[0] // 10
    bodies = vel.shape[2]
    interface = exports.shape[2]
    sub, _, sub_even, layer_even = parities()
    member = lax.rem(sub, WIN)
    start_own[...] = jnp.zeros_like(start_own)
    dense[...] = jnp.zeros_like(dense)
    for copy in copies[:6]:
        copy.wait()
    for r in range(6):
        start_own[r : r + 1, :] = vel[r]
    for r in range(4):
        start_own[8 + r : 9 + r, :] = inertia[r]
    listed[0:1, 0:interface] = exports[0]
    listed[0:1, interface : 2 * interface] = exports[1]
    listed[1:2, 0:interface] = exports[1]
    listed[1:2, interface : 2 * interface] = exports[0]
    listed[2:3, 0:interface] = exports[2]
    listed[2:3, interface : 2 * interface] = exports[3]
    listed[3:4, 0:interface] = exports[3]
    listed[3:4, interface : 2 * interface] = exports[2]
    row0 = jnp.where(sub_even, listed[1:2, :], listed[0:1, :])
    row1 = jnp.where(layer_even, listed[3:4, :], listed[2:3, :])
    idx0 = jnp.broadcast_to(row0, (8, LANES))
    idx1 = jnp.broadcast_to(row1, (8, LANES))
    export_index[0:8, :] = idx0
    export_index[8:16, :] = idx1
    blocks = bodies // LANES
    for base in (0, 8):
        tables = [
            start_own[base : base + 8, h * LANES : (h + 1) * LANES] for h in range(blocks)
        ]
        picked = pick(tables, idx0)
        out0[base : base + 8, :] = picked
        send0[10 * slots + base : 10 * slots + base + 8, :] = picked
        out1[base : base + 8, :] = pick(tables, idx1)
    rank = used.shape[0]
    for i in range(rank):
        scalars[0, i] = tiles
    for k in range(NCOLOR):
        scalars[0, FILLED + k] = 0
    colored, ranks = [], []
    for t in range(tiles):
        color = colors[0, t]
        rank_here = scalars[0, FILLED + color]
        scalars[0, FILLED + color] = rank_here + 1
        colored.append(color)
        ranks.append(rank_here)
    over = jnp.int32(0)
    for k in range(NCOLOR):
        scalars[0, OVER_BASE + k] = (NCOLOR + over) * GROUP - GROUP
        scalars[0, OVER_FROM + k] = over
        filled = scalars[0, FILLED + k]
        over = over + jnp.right_shift(jnp.maximum(filled - 1, GROUP - 1), GROUP.bit_length() - 1)
        scalars[0, OVER_TO + k] = over
    place = []
    for t in range(tiles):
        base = jnp.where(ranks[t] < GROUP, GROUP * colored[t], scalars[0, OVER_BASE + colored[t]])
        place.append(base + ranks[t])
        scalars[0, place[t]] = t
    index_out[...] = jnp.zeros_like(index_out)
    ordered[...] = jnp.zeros_like(ordered)
    used[...] = jnp.zeros_like(used)
    flip_sub = jnp.where(sub_even, interface, 0)
    flip_layer = jnp.where(layer_even, interface, 0)
    for t in range(tiles):
        span = slice(t * TILE, (t + 1) * TILE)
        nearer = pairs[0, :, span]
        other = pairs[1, :, span]
        ghost = other - bodies
        turned = jnp.where(
            ghost < 2 * interface,
            jnp.bitwise_xor(ghost, flip_sub),
            jnp.bitwise_xor(ghost, flip_layer),
        )
        farther = jnp.where(ghost < 0, other, bodies + turned)
        scalars[0, TILE_SLOT + t] = place[t]
        ordered[t : t + 1, :] = nearer
        ordered[16 + t : 17 + t, :] = farther
        index_out[pl.ds(place[t], 1), :] = nearer
        index_out[pl.ds(rank + place[t], 1), :] = farther
        used[pl.ds(place[t], 1), :] = jnp.ones((1, LANES), F32)
    slot = dest[...] - (sub - member) * count
    target = jnp.zeros_like(slot)
    for m in range(1, WIN):
        target = target + jnp.where(slot >= m * count, 1, 0)
    within = slot - target * count
    row_id = jnp.bitwise_xor(target, member) * 8 + jnp.right_shift(within, 8)
    low = jnp.bitwise_and(within, WIDE - 1)
    paired = (16, TILE)
    ids = lax.broadcasted_iota(jnp.int32, paired, 0)
    ids = jnp.bitwise_and(ids, 7).astype(F32)
    one, zero = jnp.ones(paired, BF16), jnp.zeros(paired, BF16)
    for t in range(tiles):
        span = slice(t * TILE, (t + 1) * TILE)
        hot[:, span] = equal_rows(low[:, span], WIDE)
        here = jnp.broadcast_to(row_id[:, span].astype(F32), paired).astype(BF16)
        for k in range(WIN):
            chosen = jnp.where(here == (ids + 8.0 * k).astype(BF16), one, zero)
            if k == 0:
                own_mask[:, span] = chosen
            else:
                mask[16 * k - 16 : 16 * k, span] = chosen
    give = pltpu.make_async_copy(scalars, scalars_out, sems.at[7])
    give.start()
    copies[6].wait()
    for r in range(10):
        dense[r : r + 1, :] = geo[r]
    value = dense[...]
    first = value.astype(BF16).astype(F32)
    parts = [first, value - first]
    for p in range(2):
        for i in range(5):
            pair = jnp.concatenate(
                [jnp.broadcast_to(parts[p][r : r + 1, :], (8, count)) for r in (2 * i, 2 * i + 1)],
                axis=0,
            ).astype(BF16)
            tall[p, 16 * i : 16 * i + 16, :] = pair
            for k in range(1, WIN):
                at = 80 * (WIN - 1) * p + 80 * (k - 1) + 16 * i
                lhs[at : at + 16, :] = mask[16 * k - 16 : 16 * k, :] * pair
    both = contract_lanes(lhs[...], hot[...])
    total = both[: 80 * (WIN - 1)] + both[80 * (WIN - 1) :]
    for k, out in enumerate((send0, place2, place3)):
        store_placed(out, total[80 * k : 80 * k + 80, :])
    give.wait()


def store_placed(out, total):
    for r in range(10):
        for side in range(2):
            out[16 * r + 8 * side : 16 * r + 8 * side + 8, :] = total[
                8 * r : 8 * r + 8, side * LANES : (side + 1) * LANES
            ]


def place_kernel(tall, own_mask, hot, out):
    left = [jnp.concatenate([own_mask[...]] * 5, axis=0) * tall[p] for p in range(2)]
    both = contract_lanes(jnp.concatenate(left, axis=0), hot[...])
    store_placed(out, both[:80] + both[80:])


TILE_SLOT, OVER_FROM, FILLED, OVER_TO, OVER_BASE = 32, 48, 52, 56, 60


def overflow_groups(tiles):
    most = 0
    for busy in range(1, NCOLOR + 1):
        spare = tiles - busy * (GROUP + 1)
        if spare >= 0:
            most = max(most, busy + spare // GROUP)
    return most


def slot_count(tiles):
    return -(-GROUP * (NCOLOR + overflow_groups(tiles)) // 8) * 8


def index_kernel(
    subs, layers, interface, bodies, ordered, export_index, own,
    hot, masks, export_hot, export_masks, mult, near_props, far_props,
):
    tiles = masks.shape[0] - 1
    blocks = bodies // LANES
    total = blocks + 4 * interface // LANES
    sub, layer, _, _ = parities()
    props = [own[8:16, h * LANES : (h + 1) * LANES] for h in range(blocks)]
    square = (TILE, LANES)
    lane_ids = lax.broadcasted_iota(jnp.int32, square, 1)
    eye = jnp.where(lax.broadcasted_iota(jnp.int32, square, 0) == lane_ids, 1.0, 0.0)
    lane_ids = lax.broadcasted_iota(jnp.int32, (TILE, WIDE), 1).astype(F32)
    low_rows = jnp.bitwise_and(ordered[...], WIDE - 1).astype(F32).astype(BF16)
    columns = contract_lanes(eye.astype(BF16), low_rows).astype(BF16)
    ids = lax.broadcasted_iota(jnp.int32, (32, 2 * TILE), 0)
    lanes = lax.broadcasted_iota(jnp.int32, (32, 2 * TILE), 1)
    for t in range(tiles):
        first = ordered[t : t + 1, :]
        second = ordered[16 + t : 17 + t, :]
        near_props[8 * t : 8 * t + 8, :] = pick(props, jnp.broadcast_to(first, (8, LANES)))
        far_props[8 * t : 8 * t + 8, :] = pick(props, jnp.broadcast_to(second, (8, LANES)))
        sides = jnp.where(lanes < TILE, t, 16 + t)
        chosen = jnp.where(ids == sides, 1.0, 0.0).astype(BF16)
        low = jnp.dot(columns, chosen, preferred_element_type=F32)
        for side in range(2):
            here = low[:, side * TILE : (side + 1) * TILE]
            hit = jnp.concatenate([here, here], axis=1) == lane_ids
            at = (2 * t + side) * TILE
            hot[at : at + TILE, :] = jnp.where(hit, 1.0, 0.0).astype(BF16)
        masks[t, : 8 * blocks, :] = high_masks(first, blocks // 2, 8)
        masks[t, 8 * blocks :, :] = high_masks(second, total // 2, 8)
    hot[2 * tiles * TILE :, :] = jnp.zeros((2 * TILE, WIDE), BF16)
    masks[tiles] = jnp.zeros_like(masks[tiles])
    inner_sub = jnp.where(jnp.logical_and(sub > 0, sub < subs - 1), 1.0, 0.0)
    inner_layer = jnp.where(jnp.logical_and(layer > 0, layer < layers - 1), 1.0, 0.0)
    lane = lane_iota()
    weights = [
        jnp.where(lane < interface, 1.0, inner_sub),
        jnp.where(lane < interface, 1.0, inner_layer),
    ]
    left = []
    for i in range(2):
        row = export_index[8 * i : 8 * i + 1, :]
        export_hot[:, i * LANES : (i + 1) * LANES] = low_onehot(row)
        chosen = high_masks(row, blocks)
        export_masks[i] = chosen
        weight = jnp.concatenate([weights[i], jnp.zeros_like(weights[i])], axis=0).astype(BF16)
        left.append(jnp.concatenate([weight] * blocks, axis=0) * chosen)
    listed = contract_lanes(jnp.concatenate(left, axis=1), export_hot[...])
    for h in range(blocks):
        mult[:, h * LANES : (h + 1) * LANES] = 1.0 + listed[16 * h : 16 * h + 8]


STATE = 34


def contact_state(geo, first, second):
    raw = geo[0:3]
    length = jnp.sqrt(dot3(raw, raw))
    normal = [x / length for x in raw]
    side = jnp.sqrt(normal[1] * normal[1] + normal[2] * normal[2])
    tan_y = normal[2] / side
    tan_z = -normal[1] / side
    two = [
        normal[1] * tan_z - normal[2] * tan_y,
        -normal[0] * tan_z,
        normal[0] * tan_y,
    ]

    def arm(p, spin):
        return [
            spin[1] * p[2] * p[2] + spin[2] * p[1] * p[1],
            spin[0] * p[2] * p[2] + spin[2] * p[0] * p[0],
            spin[0] * p[1] * p[1] + spin[1] * p[0] * p[0],
            -spin[2] * p[0] * p[1],
            -spin[1] * p[0] * p[2],
            -spin[0] * p[1] * p[2],
        ]

    arm_a, arm_b = geo[3:6], geo[6:9]
    e = [x + y for x, y in zip(arm(arm_a, first[1:4]), arm(arm_b, second[1:4]))]
    mass = first[0] + second[0]
    xx, yy, zz = mass + e[0], mass + e[1], mass + e[2]
    xy, xz, yz = e[3], e[4], e[5]
    c_xx = yy * zz - yz * yz
    c_xy = xz * yz - xy * zz
    c_xz = xy * yz - xz * yy
    c_yy = xx * zz - xz * xz
    c_yz = xy * xz - xx * yz
    c_zz = xx * yy - xy * xy
    det = xx * c_xx + xy * c_xy + xz * c_xz
    inv = [
        [c_xx / det, c_xy / det, c_xz / det],
        [c_xy / det, c_yy / det, c_yz / det],
        [c_xz / det, c_yz / det, c_zz / det],
    ]
    solve = []
    for row in (normal, None, two):
        for j in range(3):
            if row is None:
                value = tan_y * inv[1][j] + tan_z * inv[2][j]
            else:
                value = row[0] * inv[0][j] + row[1] * inv[1][j] + row[2] * inv[2][j]
            solve.append(relaxation * value)
    bias = [geo[9] * dot3(solve[3 * i : 3 * i + 3], normal) for i in range(3)]
    return (
        solve + bias + normal + [tan_y, tan_z] + two + arm_a + arm_b + list(first) + list(second)
    )


def sweep_kernel(bodies, interface, first_sweep, *refs):
    scalars_in, index, used, hot, masks = refs[:5]
    refs = refs[5:]
    if first_sweep:
        own, g1, r1, r2, r3, g0, g2, g3, ordered, near_props, far_props, state = refs[:12]
        refs = refs[12:]
        r0 = g1.at[pl.ds(g0.shape[0], 16), :]
    else:
        own, r0, r1, r2, r3, state, impulse_in = refs[:7]
        refs = refs[7:]
    impulse, own_change, ghost0, ghost1 = refs[:4]
    got_a, got_b, push_a, push_b, acc, table, all_a, all_b, gathered, placed, scalars = refs[4:]
    slots = used.shape[0]
    tiles = masks.shape[0] - 1
    blocks = bodies // LANES
    total = blocks + (4 * interface) // LANES
    values = scalars_in[...]
    wanted = list(range(slots)) + [OVER_FROM + k for k in range(NCOLOR)]
    wanted += [OVER_TO + k for k in range(NCOLOR)]
    if first_sweep:
        wanted += [TILE_SLOT + t for t in range(tiles)]
    for i in wanted:
        scalars[i] = values[0, i]

    def ghost_blocks(base):
        return [
            halves(r0[base : base + 8, :], r1[base : base + 8, :], interface),
            halves(r2[base : base + 8, :], r3[base : base + 8, :], interface),
        ]

    start = [own[0:8, h * LANES : (h + 1) * LANES] for h in range(blocks)] + ghost_blocks(0)
    for h in range(total):
        table[8 * h : 8 * h + 8, :] = start[h]
    push_a[...] = jnp.zeros_like(push_a)
    push_b[...] = jnp.zeros_like(push_b)

    if first_sweep:
        ghost_props = ghost_blocks(8)
        far = []
        for t in range(tiles):
            ib = jnp.broadcast_to(ordered[16 + t : 17 + t, :], (8, LANES))
            low, high = jnp.bitwise_and(ib, LANES - 1), jnp.right_shift(ib, 7)
            value = far_props[8 * t : 8 * t + 8, :]
            for h, block in enumerate(ghost_props):
                value = jnp.where(
                    high == blocks + h, jnp.take_along_axis(block, low, axis=1), value
                )
            far.append(value)
        all_a[...] = jnp.ones_like(all_a)
        all_b[...] = jnp.ones_like(all_b)
        gathered[...] = (g0[...] + g1[0 : g0.shape[0], :]) + (g2[...] + g3[...])
        placed[...] = jnp.ones_like(placed)
        rows = g0.shape[0] // 10
        for t in range(tiles):
            slot = scalars[TILE_SLOT + t]
            group_rows = pl.ds(pl.multiple_of(8 * slot, 8), 8)
            all_a[group_rows, :] = near_props[8 * t : 8 * t + 8, :]
            all_b[group_rows, :] = far[t]
            at = 8 * (t % 2) + t // 2
            for c in range(10):
                row = c * rows + at
                placed[pl.ds(c * slots + slot, 1), :] = gathered[row : row + 1, :]
        first = [all_a[pl.ds(c, slots, stride=8), :] for c in range(4)]
        second = [all_b[pl.ds(c, slots, stride=8), :] for c in range(4)]
        geo = [placed[c * slots : (c + 1) * slots, :] for c in range(10)]
        for c, value in enumerate(contact_state(geo, first, second)):
            state[c * slots : (c + 1) * slots, :] = value
        impulse[...] = jnp.zeros_like(impulse)
    else:
        impulse[...] = impulse_in[...]

    def held_at(base):
        return lambda c: state[pl.ds(c * slots + base, GROUP), :]

    def gather(base, room, now):
        for j in range(GROUP):
            ia = jnp.broadcast_to(index[pl.ds(base + j, 1), :], (8, LANES))
            ib = jnp.broadcast_to(index[pl.ds(slots + base + j, 1), :], (8, LANES))
            got_a[room + 8 * j : room + 8 * j + 8, :] = pick(now[:blocks], ia)
            got_b[room + 8 * j : room + 8 * j + 8, :] = pick(now, ib)

    def press(base, room):
        held = held_at(base)
        tile_rows = [pl.ds(room + c, GROUP, stride=8) for c in range(6)]
        va = [got_a[tile_rows[c], :] for c in range(6)]
        vb = [got_b[tile_rows[c], :] for c in range(6)]
        arm_a = [held(20 + c) for c in range(3)]
        arm_b = [held(23 + c) for c in range(3)]
        turn_a = cross(va[3:6], arm_a)
        turn_b = cross(vb[3:6], arm_b)
        rel = [((va[c] + turn_a[c]) - vb[c]) - turn_b[c] for c in range(3)]
        old = [impulse[pl.ds(c * slots + base, GROUP), :] for c in range(3)]
        trial = [
            old[c] - (dot3([held(3 * c + j) for j in range(3)], rel) + held(9 + c))
            for c in range(3)
        ]
        normal_part = jnp.maximum(trial[0], 0.0)
        slide = trial[1] * trial[1] + trial[2] * trial[2]
        shrink = lax.rsqrt(jnp.maximum(slide, tangent_floor * tangent_floor))
        factor = jnp.minimum(1.0, friction * normal_part * shrink)
        active = used[pl.ds(base, GROUP), :] > 0.5
        new = [
            jnp.where(active, normal_part, old[0]),
            jnp.where(active, trial[1] * factor, old[1]),
            jnp.where(active, trial[2] * factor, old[2]),
        ]
        change = [new[c] - old[c] for c in range(3)]
        for c in range(3):
            impulse[pl.ds(c * slots + base, GROUP), :] = new[c]
        force = [
            held(12) * change[0] + held(17) * change[2],
            held(13) * change[0] + held(15) * change[1] + held(18) * change[2],
            held(14) * change[0] + held(16) * change[1] + held(19) * change[2],
        ]
        spin_a = cross(arm_a, force)
        spin_b = cross(arm_b, force)
        for c in range(3):
            push_a[tile_rows[c], :] = held(26) * force[c]
            push_a[tile_rows[3 + c], :] = held(27 + c) * spin_a[c]
            push_b[tile_rows[c], :] = -(held(30) * force[c])
            push_b[tile_rows[3 + c], :] = -(held(31 + c) * spin_b[c])

    def sides(base, room):
        left, right = [], []
        near = blocks // 2
        empty = jnp.zeros((8 * (total - blocks), LANES), BF16)
        for j in range(GROUP):
            t = scalars[base + j]
            first = two_parts(push_a[room + 8 * j : room + 8 * j + 8, :])
            second = two_parts(push_b[room + 8 * j : room + 8 * j + 8, :])
            rows = [masks[t, 16 * m : 16 * m + 16, :] for m in range(near + total // 2)]
            left.append(jnp.concatenate([first * m for m in rows[:near]] + [empty], axis=0))
            left.append(jnp.concatenate([second * m for m in rows[near:]], axis=0))
            right.append(hot[pl.ds(pl.multiple_of(2 * TILE * t, 2 * TILE), 2 * TILE), :])
        return left, right

    def groups(bases, now):
        rooms = [8 * GROUP * i for i in range(len(bases))]
        for base, room in zip(bases, rooms):
            gather(base, room, now)
        for base, room in zip(bases, rooms):
            press(base, room)
        left, right = [], []
        for base, room in zip(bases, rooms):
            more_left, more_right = sides(base, room)
            left += more_left
            right += more_right
        return jnp.dot(
            jnp.concatenate(left, axis=1),
            jnp.concatenate(right, axis=0),
            preferred_element_type=F32,
        )

    def color_pass(k):
        now = [table[8 * h : 8 * h + 8, :] for h in range(total)]
        main = pl.multiple_of(GROUP * k, GROUP)

        def over(g):
            return pl.multiple_of(GROUP * (NCOLOR + g), GROUP)

        begin, end = scalars[OVER_FROM + k], scalars[OVER_TO + k]

        @pl.when(end > begin)
        def _():
            acc[...] = groups([main, over(begin)], now)

        @pl.when(end <= begin)
        def _():
            acc[...] = groups([main], now)

        def more(g, c):
            acc[...] += groups([over(g)], now)
            return c

        lax.fori_loop(begin + 1, end, more, 0)
        for h in range(total):
            side = slice((h % 2) * LANES, (h % 2 + 1) * LANES)
            at = 16 * (h // 2)
            table[8 * h : 8 * h + 8, :] = now[h] + (
                acc[at : at + 8, side] + acc[at + 8 : at + 16, side]
            )

    def later_pass(k, carry):
        color_pass(k)
        return carry

    lax.fori_loop(0, NCOLOR, later_pass, 0)
    for h in range(blocks):
        own_change[:, h * LANES : (h + 1) * LANES] = table[8 * h : 8 * h + 8, :] - start[h]
    ghost0[...] = table[8 * blocks : 8 * blocks + 8, :] - start[blocks]
    ghost1[...] = table[8 * blocks + 8 : 8 * blocks + 16, :] - start[blocks + 1]


def impulse_kernel(scalars, held, impulse):
    slots = held.shape[0] // 3
    for t in range(impulse.shape[2] // TILE):
        slot = scalars[0, TILE_SLOT + t]
        for c in range(3):
            impulse[c, :, t * TILE : (t + 1) * TILE] = held[pl.ds(c * slots + slot, 1), :]


def merge_kernel(
    interface, last_sweep, own, change, c0, c1, c2, c3, mult, export_index, export_hot,
    export_masks, *refs,
):
    blocks = own.shape[1] // LANES
    came = [halves(c0[...], c1[...], interface), halves(c2[...], c3[...], interface)]
    left = jnp.concatenate(
        [
            jnp.concatenate([two_parts(came[i])] * blocks, axis=0) * export_masks[i]
            for i in range(2)
        ],
        axis=1,
    )
    incoming = contract_lanes(left, export_hot[...])
    fresh = []
    for h in range(blocks):
        span = slice(h * LANES, (h + 1) * LANES)
        fresh.append(
            own[0:8, span] + (change[:, span] + sum_parts(incoming, h)) / mult[:, span]
        )
    if last_sweep:
        (velocity,) = refs
        for r in range(6):
            for h in range(blocks):
                velocity[r, :, h * LANES : (h + 1) * LANES] = fresh[h][r : r + 1, :]
    else:
        fresh_own, out0, out1 = refs
        for h in range(blocks):
            fresh_own[:, h * LANES : (h + 1) * LANES] = fresh[h]
        out0[...] = pick(fresh, export_index[0:8, :])
        out1[...] = pick(fresh, export_index[8:16, :])


def in_hbm(array):
    return pltpu.with_memory_space_constraint(array, pltpu.HBM)


def shape(dims, dtype=F32):
    return jax.ShapeDtypeStruct(dims, dtype)


def make(subs, layers):
    matchings = neighbour_matchings(subs, layers)
    shuffles = [relay_shuffle(subs, layers, k) for k in range(WIN)]

    def trade(low, high):
        came = [None] * 4
        for m in ORDER:
            came[m] = lax.ppermute(low if m < 2 else high, AXES, matchings[m])
        return came

    def on_device(geometry, dest_slot, pairs, colors, free_vel, inertia, exports):
        count = geometry.shape[2]
        bodies = free_vel.shape[2]
        interface = exports.shape[2]
        tiles = count // TILE
        slots = 16
        assert count % TILE == 0 and tiles < slots and 2 * interface == LANES
        assert bodies % WIDE == 0
        blocks = bodies // LANES
        total = blocks + 2
        place = shape((10 * slots, LANES))
        small = shape((16, LANES))
        arguments = (geometry, dest_slot, free_vel, inertia, exports, pairs, colors)
        rows = slot_count(tiles)
        assert rows <= TILE_SLOT
        prepared = pl.pallas_call(
            prepare_kernel,
            out_shape=(
                shape((10 * slots + 16, LANES)), place, place, small, small,
                shape((16, bodies)),
                shape((16, LANES), jnp.int32),
                shape((WIDE, count), BF16),
                shape((16, count), BF16),
                shape((2, 80, count), BF16),
                shape((32, LANES), jnp.int32),
                shape((2 * rows, LANES), jnp.int32),
                shape((rows, LANES)),
                shape((1, LANES), jnp.int32),
            ),
            in_specs=[pl.BlockSpec(memory_space=pltpu.HBM)] * 7,
            out_specs=(VMEM_SPEC,) * 14,
            scratch_shapes=[
                pltpu.VMEM(geometry.shape, F32),
                pltpu.VMEM(dest_slot.shape, jnp.int32),
                pltpu.VMEM(free_vel.shape, F32),
                pltpu.VMEM(inertia.shape, F32),
                pltpu.VMEM(exports.shape, jnp.int32),
                pltpu.VMEM(pairs.shape, jnp.int32),
                pltpu.SMEM(colors.shape, jnp.int32),
                pltpu.SMEM((1, LANES), jnp.int32),
                pltpu.VMEM((8, LANES), jnp.int32),
                pltpu.VMEM((16, count), F32),
                pltpu.VMEM((16 * (WIN - 1), count), BF16),
                pltpu.VMEM((2 * 80 * (WIN - 1), count), BF16),
                pltpu.SemaphoreType.DMA((8,)),
            ],
            compiler_params=PARAMS,
            name="prepare",
        )(*[in_hbm(x) for x in arguments])
        send0, place2, place3, out0, out1, own, export_index = prepared[:7]
        wide_hot, own_mask, tall, ordered, index, used, scalars = prepared[7:]
        came = [lax.ppermute(send0, AXES, matchings[0])]
        came.append(lax.ppermute(out0, AXES, matchings[1]))
        came.append(lax.ppermute(out1, AXES, matchings[2]))
        came.append(lax.ppermute(out1, AXES, matchings[3]))
        place0 = pl.pallas_call(
            place_kernel,
            out_shape=place,
            in_specs=[VMEM_SPEC] * 3,
            out_specs=VMEM_SPEC,
            compiler_params=PARAMS,
            name="place",
        )(tall, own_mask, wide_hot)
        placed = [place0]
        placed.append(lax.ppermute(place2, AXES, shuffles[2]))
        placed.append(lax.ppermute(place3, AXES, shuffles[3]))

        def indexing(*refs):
            index_kernel(subs, layers, interface, bodies, *refs)

        hot, masks, export_hot, export_masks, mult, near_props, far_props = pl.pallas_call(
            indexing,
            out_shape=(
                shape((2 * TILE * (tiles + 1), WIDE), BF16),
                shape((tiles + 1, 8 * (blocks + total), LANES), BF16),
                shape((LANES, 2 * LANES), BF16),
                shape((2, 16 * blocks, LANES), BF16),
                shape((8, bodies)),
                shape((8 * tiles, LANES)),
                shape((8 * tiles, LANES)),
            ),
            in_specs=[VMEM_SPEC] * 3,
            out_specs=(VMEM_SPEC,) * 7,
            compiler_params=PARAMS,
            name="indexing",
        )(ordered, export_index, own)

        state = impulse = None
        for sweep in range(SWEEPS):
            first, last = sweep == 0, sweep == SWEEPS - 1

            def run(*refs, first=first):
                sweep_kernel(bodies, interface, first, *refs)

            outs = [
                shape((3 * rows, LANES)),
                shape((8, bodies)),
                shape((8, LANES)),
                shape((8, LANES)),
            ]
            operands = [scalars, index, used, hot, masks, own, *came]
            if first:
                outs = [shape((STATE * rows, LANES))] + outs
                operands += [*placed, ordered, near_props, far_props]
            else:
                operands += [state, impulse]
            result = pl.pallas_call(
                run,
                out_shape=tuple(outs),
                in_specs=[VMEM_SPEC] * len(operands),
                out_specs=(VMEM_SPEC,) * len(outs),
                scratch_shapes=[
                    pltpu.VMEM((16 * GROUP, LANES), F32),
                    pltpu.VMEM((16 * GROUP, LANES), F32),
                    pltpu.VMEM((16 * GROUP, LANES), F32),
                    pltpu.VMEM((16 * GROUP, LANES), F32),
                    pltpu.VMEM((8 * total, WIDE), F32),
                    pltpu.VMEM((8 * total, LANES), F32),
                    pltpu.VMEM((8 * rows, LANES), F32),
                    pltpu.VMEM((8 * rows, LANES), F32),
                    pltpu.VMEM((10 * slots, LANES), F32),
                    pltpu.VMEM((10 * rows, LANES), F32),
                    pltpu.SMEM((64,), jnp.int32),
                ],
                compiler_params=PARAMS,
                name="sweep",
            )(*operands)
            if first:
                state, result = result[0], result[1:]
            impulse, change, ghost0, ghost1 = result
            sums = trade(ghost0, ghost1)

            def merge(*refs, last=last):
                merge_kernel(interface, last, *refs)

            operands = [own, change, *sums, mult, export_index, export_hot, export_masks]
            if last:
                outs = (shape((6, 1, bodies)),)
            else:
                outs = (shape((8, bodies)), shape((8, LANES)), shape((8, LANES)))
            merged = pl.pallas_call(
                merge,
                out_shape=outs,
                in_specs=[VMEM_SPEC] * len(operands),
                out_specs=(VMEM_SPEC,) * len(outs),
                compiler_params=PARAMS,
                name="merge",
            )(*operands)
            if last:
                in_order = pl.pallas_call(
                    impulse_kernel,
                    out_shape=shape((3, 1, count)),
                    in_specs=[SMEM_SPEC, VMEM_SPEC],
                    out_specs=VMEM_SPEC,
                    compiler_params=PARAMS,
                    name="impulse",
                )(scalars, impulse)
                return in_order, merged[0]
            own = merged[0]
            came = trade(merged[1], merged[2])

    return on_device


def solution(mesh):
    placed = (
        P(None, "layer", "sub"),
        P("layer", "sub"),
        P(None, "layer", "sub"),
        P("layer", "sub"),
        P(None, "layer", "sub"),
        P(None, "layer", "sub"),
        P(None, "layer", "sub"),
    )
    return jax.shard_map(
        make(mesh.shape["sub"], mesh.shape["layer"]),
        mesh=mesh,
        in_specs=placed,
        out_specs=(P(None, "layer", "sub"), P(None, "layer", "sub")),
        check_vma=False,
    )
```

```python
import jax
import jax.numpy as jnp
from jax import lax
from jax.experimental import pallas as pl
from jax.experimental.pallas import tpu as pltpu
from jax.sharding import PartitionSpec as P

WIN = 4
SWEEPS = 3
NCOLOR = 4
TILE = 128
LANES = 128
WIDE = 256
GROUP = 4

relaxation = 0.7
friction = 0.6
tangent_floor = 0.1

AXES = ("sub", "layer")
F32 = jnp.float32
BF16 = jnp.bfloat16
VMEM_SPEC = pl.BlockSpec(memory_space=pltpu.VMEM)
SMEM_SPEC = pl.BlockSpec(memory_space=pltpu.SMEM)
PARAMS = pltpu.CompilerParams(vmem_limit_bytes=16 << 20)


def neighbour_matchings(subs, layers):
    assert subs % 2 == 0 and layers % 2 == 0

    def shifted(i):
        return i - 1 if i % 2 == 0 else i + 1

    def partner(match, s, y):
        if match == 0:
            return s ^ 1, y
        if match == 1:
            return (s, y ^ 1) if s in (0, subs - 1) else (shifted(s), y)
        if match == 2:
            return s, y ^ 1
        return (s ^ 1, y) if y in (0, layers - 1) else (s, shifted(y))

    out = []
    for match in range(4):
        pairs = []
        for s in range(subs):
            for y in range(layers):
                ps, py = partner(match, s, y)
                pairs.append((s * layers + y, ps * layers + py))
        out.append(pairs)
    return out


def relay_shuffle(subs, layers, k):
    return [
        (s * layers + y, (s ^ k) * layers + y) for s in range(subs) for y in range(layers)
    ]


def lane_iota():
    return lax.broadcasted_iota(jnp.int32, (8, LANES), 1)


def pick(tables, index):
    low = jnp.bitwise_and(index, LANES - 1)
    high = jnp.right_shift(index, 7)
    out = jnp.take_along_axis(tables[0], low, axis=1)
    for h in range(1, len(tables)):
        out = jnp.where(high == h, jnp.take_along_axis(tables[h], low, axis=1), out)
    return out


def two_parts(value):
    first = value.astype(BF16).astype(F32)
    return jnp.concatenate([first, value - first], axis=0).astype(BF16)


def equal_rows(row, count):
    shape = (count, row.shape[1])
    ids = lax.broadcasted_iota(jnp.int32, shape, 0).astype(F32).astype(BF16)
    here = jnp.broadcast_to(row.astype(F32), shape).astype(BF16)
    return jnp.where(ids == here, jnp.ones(shape, BF16), jnp.zeros(shape, BF16))


def high_masks(index_row, highs, shift=7):
    shape = (16, LANES)
    high = jnp.broadcast_to(jnp.right_shift(index_row, shift).astype(F32), shape).astype(BF16)
    one, zero = jnp.ones(shape, BF16), jnp.zeros(shape, BF16)
    return jnp.concatenate(
        [jnp.where(high == jnp.full(shape, h, BF16), one, zero) for h in range(highs)], axis=0
    )


def low_onehot(index_row):
    return equal_rows(jnp.bitwise_and(index_row, LANES - 1), LANES)


def contract_lanes(lhs, rhs):
    return lax.dot_general(
        lhs, rhs, (((1,), (1,)), ((), ())), preferred_element_type=F32
    )


def sum_parts(block, h):
    return block[16 * h : 16 * h + 8] + block[16 * h + 8 : 16 * h + 16]


def cross(u, v):
    return [
        u[1] * v[2] - u[2] * v[1],
        u[2] * v[0] - u[0] * v[2],
        u[0] * v[1] - u[1] * v[0],
    ]


def dot3(u, v):
    return u[0] * v[0] + u[1] * v[1] + u[2] * v[2]


def halves(low, high, half):
    return jnp.where(lane_iota() < half, low, high)


def parities():
    sub = lax.axis_index("sub")
    layer = lax.axis_index("layer")
    return sub, layer, lax.rem(sub, 2) == 0, lax.rem(layer, 2) == 0


def prepare_kernel(
    geo_hbm, dest_hbm, vel_hbm, inertia_hbm, exports_hbm, pairs_hbm, colors_hbm,
    send0, place2, place3, out0, out1, start_own, export_index, hot, own_mask, tall,
    ordered, index_out, used, scalars_out,
    geo, dest, vel, inertia, exports, pairs, colors, scalars, listed, dense, mask, lhs, sems,
):
    copies = [
        pltpu.make_async_copy(src, dst, sems.at[i])
        for i, (src, dst) in enumerate(
            [
                (exports_hbm, exports),
                (vel_hbm, vel),
                (inertia_hbm, inertia),
                (dest_hbm, dest),
                (colors_hbm, colors),
                (pairs_hbm, pairs),
                (geo_hbm, geo),
            ]
        )
    ]
    for copy in copies:
        copy.start()
    count = geo.shape[2]
    tiles = count // TILE
    slots = place2.shape[0] // 10
    bodies = vel.shape[2]
    interface = exports.shape[2]
    sub, layer, sub_even, layer_even = parities()
    member = lax.rem(sub, WIN)
    start_own[...] = jnp.zeros_like(start_own)
    dense[...] = jnp.zeros_like(dense)
    for copy in copies[:6]:
        copy.wait()
    for r in range(6):
        start_own[r : r + 1, :] = vel[r]
    for r in range(4):
        start_own[8 + r : 9 + r, :] = inertia[r]
    listed[0:1, 0:interface] = exports[0]
    listed[0:1, interface : 2 * interface] = exports[1]
    listed[1:2, 0:interface] = exports[1]
    listed[1:2, interface : 2 * interface] = exports[0]
    listed[2:3, 0:interface] = exports[2]
    listed[2:3, interface : 2 * interface] = exports[3]
    listed[3:4, 0:interface] = exports[3]
    listed[3:4, interface : 2 * interface] = exports[2]
    row0 = jnp.where(sub_even, listed[1:2, :], listed[0:1, :])
    row1 = jnp.where(layer_even, listed[3:4, :], listed[2:3, :])
    idx0 = jnp.broadcast_to(row0, (8, LANES))
    idx1 = jnp.broadcast_to(row1, (8, LANES))
    export_index[0:8, :] = idx0
    export_index[8:16, :] = idx1
    blocks = bodies // LANES
    for base in (0, 8):
        tables = [
            start_own[base : base + 8, h * LANES : (h + 1) * LANES] for h in range(blocks)
        ]
        picked = pick(tables, idx0)
        out0[base : base + 8, :] = picked
        send0[10 * slots + base : 10 * slots + base + 8, :] = picked
        out1[base : base + 8, :] = pick(tables, idx1)
    rank = used.shape[0]
    for i in range(rank):
        scalars[0, i] = tiles
    for k in range(NCOLOR):
        scalars[0, FILLED + k] = 0
    colored, ranks = [], []
    for t in range(tiles):
        color = colors[0, t]
        rank_here = scalars[0, FILLED + color]
        scalars[0, FILLED + color] = rank_here + 1
        colored.append(color)
        ranks.append(rank_here)
    over = jnp.int32(0)
    for k in range(NCOLOR):
        scalars[0, OVER_BASE + k] = (NCOLOR + over) * GROUP - GROUP
        scalars[0, OVER_FROM + k] = over
        filled = scalars[0, FILLED + k]
        over = over + jnp.right_shift(jnp.maximum(filled - 1, GROUP - 1), GROUP.bit_length() - 1)
        scalars[0, OVER_TO + k] = over
    place = []
    for t in range(tiles):
        base = jnp.where(ranks[t] < GROUP, GROUP * colored[t], scalars[0, OVER_BASE + colored[t]])
        place.append(base + ranks[t])
        scalars[0, place[t]] = t
    index_out[...] = jnp.zeros_like(index_out)
    ordered[...] = jnp.zeros_like(ordered)
    used[...] = jnp.zeros_like(used)
    flip_sub = jnp.where(sub_even, interface, 0)
    flip_layer = jnp.where(layer_even, interface, 0)
    for t in range(tiles):
        span = slice(t * TILE, (t + 1) * TILE)
        nearer = pairs[0, :, span]
        other = pairs[1, :, span]
        ghost = other - bodies
        turned = jnp.where(
            ghost < 2 * interface,
            jnp.bitwise_xor(ghost, flip_sub),
            jnp.bitwise_xor(ghost, flip_layer),
        )
        farther = jnp.where(ghost < 0, other, bodies + turned)
        scalars[0, TILE_SLOT + t] = place[t]
        ordered[t : t + 1, :] = nearer
        ordered[16 + t : 17 + t, :] = farther
        index_out[pl.ds(place[t], 1), :] = nearer
        index_out[pl.ds(rank + place[t], 1), :] = farther
        used[pl.ds(place[t], 1), :] = jnp.ones((1, LANES), F32)
    slot = dest[...] - (sub - member) * count
    target = jnp.zeros_like(slot)
    for m in range(1, WIN):
        target = target + jnp.where(slot >= m * count, 1, 0)
    within = slot - target * count
    row_id = jnp.bitwise_xor(target, member) * 8 + jnp.right_shift(within, 8)
    low = jnp.bitwise_and(within, WIDE - 1)
    paired = (16, TILE)
    ids = lax.broadcasted_iota(jnp.int32, paired, 0)
    ids = jnp.bitwise_and(ids, 7).astype(F32)
    one, zero = jnp.ones(paired, BF16), jnp.zeros(paired, BF16)
    for t in range(tiles):
        span = slice(t * TILE, (t + 1) * TILE)
        hot[:, span] = equal_rows(low[:, span], WIDE)
        here = jnp.broadcast_to(row_id[:, span].astype(F32), paired).astype(BF16)
        for k in range(WIN):
            chosen = jnp.where(here == (ids + 8.0 * k).astype(BF16), one, zero)
            if k == 0:
                own_mask[:, span] = chosen
            else:
                mask[16 * k - 16 : 16 * k, span] = chosen
    give = pltpu.make_async_copy(scalars, scalars_out, sems.at[7])
    give.start()
    copies[6].wait()
    for r in range(10):
        dense[r : r + 1, :] = geo[r]
    value = dense[...]
    first = value.astype(BF16).astype(F32)
    parts = [first, value - first]
    for p in range(2):
        for i in range(5):
            pair = jnp.concatenate(
                [jnp.broadcast_to(parts[p][r : r + 1, :], (8, count)) for r in (2 * i, 2 * i + 1)],
                axis=0,
            ).astype(BF16)
            tall[p, 16 * i : 16 * i + 16, :] = pair
            for k in range(1, WIN):
                at = 80 * (WIN - 1) * p + 80 * (k - 1) + 16 * i
                lhs[at : at + 16, :] = mask[16 * k - 16 : 16 * k, :] * pair
    both = contract_lanes(lhs[...], hot[...])
    total = both[: 80 * (WIN - 1)] + both[80 * (WIN - 1) :]
    for k, out in enumerate((send0, place2, place3)):
        store_placed(out, total[80 * k : 80 * k + 80, :])
    give.wait()


def store_placed(out, total):
    for r in range(10):
        for side in range(2):
            out[16 * r + 8 * side : 16 * r + 8 * side + 8, :] = total[
                8 * r : 8 * r + 8, side * LANES : (side + 1) * LANES
            ]


def place_kernel(tall, own_mask, hot, out):
    left = [jnp.concatenate([own_mask[...]] * 5, axis=0) * tall[p] for p in range(2)]
    both = contract_lanes(jnp.concatenate(left, axis=0), hot[...])
    store_placed(out, both[:80] + both[80:])


TILE_SLOT, OVER_FROM, FILLED, OVER_TO, OVER_BASE = 32, 48, 52, 56, 60


def overflow_groups(tiles):
    most = 0
    for busy in range(1, NCOLOR + 1):
        spare = tiles - busy * (GROUP + 1)
        if spare >= 0:
            most = max(most, busy + spare // GROUP)
    return most


def slot_count(tiles):
    return -(-GROUP * (NCOLOR + overflow_groups(tiles)) // 8) * 8


def index_kernel(
    subs, layers, interface, bodies, ordered, export_index, own,
    hot, masks, export_hot, export_masks, mult, near_props, far_props,
):
    tiles = masks.shape[0] - 1
    blocks = bodies // LANES
    total = blocks + 4 * interface // LANES
    sub, layer, sub_even, layer_even = parities()
    props = [own[8:16, h * LANES : (h + 1) * LANES] for h in range(blocks)]
    square = (TILE, LANES)
    lane_ids = lax.broadcasted_iota(jnp.int32, square, 1)
    eye = jnp.where(lax.broadcasted_iota(jnp.int32, square, 0) == lane_ids, 1.0, 0.0)
    lane_ids = lax.broadcasted_iota(jnp.int32, (TILE, WIDE), 1).astype(F32)
    low_rows = jnp.bitwise_and(ordered[...], WIDE - 1).astype(F32).astype(BF16)
    columns = contract_lanes(eye.astype(BF16), low_rows).astype(BF16)
    ids = lax.broadcasted_iota(jnp.int32, (32, 2 * TILE), 0)
    lanes = lax.broadcasted_iota(jnp.int32, (32, 2 * TILE), 1)
    for t in range(tiles):
        first = ordered[t : t + 1, :]
        second = ordered[16 + t : 17 + t, :]
        near_props[8 * t : 8 * t + 8, :] = pick(props, jnp.broadcast_to(first, (8, LANES)))
        far_props[8 * t : 8 * t + 8, :] = pick(props, jnp.broadcast_to(second, (8, LANES)))
        sides = jnp.where(lanes < TILE, t, 16 + t)
        chosen = jnp.where(ids == sides, 1.0, 0.0).astype(BF16)
        low = jnp.dot(columns, chosen, preferred_element_type=F32)
        for side in range(2):
            here = low[:, side * TILE : (side + 1) * TILE]
            hit = jnp.concatenate([here, here], axis=1) == lane_ids
            at = (2 * t + side) * TILE
            hot[at : at + TILE, :] = jnp.where(hit, 1.0, 0.0).astype(BF16)
        masks[t, : 8 * blocks, :] = high_masks(first, blocks // 2, 8)
        masks[t, 8 * blocks :, :] = high_masks(second, total // 2, 8)
    hot[2 * tiles * TILE :, :] = jnp.zeros((2 * TILE, WIDE), BF16)
    masks[tiles] = jnp.zeros_like(masks[tiles])
    inner_sub = jnp.where(jnp.logical_and(sub > 0, sub < subs - 1), 1.0, 0.0)
    inner_layer = jnp.where(jnp.logical_and(layer > 0, layer < layers - 1), 1.0, 0.0)
    lane = lane_iota()
    weights = [
        jnp.where(lane < interface, 1.0, inner_sub),
        jnp.where(lane < interface, 1.0, inner_layer),
    ]
    left = []
    for i in range(2):
        row = export_index[8 * i : 8 * i + 1, :]
        export_hot[:, i * LANES : (i + 1) * LANES] = low_onehot(row)
        chosen = high_masks(row, blocks)
        export_masks[i] = chosen
        weight = jnp.concatenate([weights[i], jnp.zeros_like(weights[i])], axis=0).astype(BF16)
        left.append(jnp.concatenate([weight] * blocks, axis=0) * chosen)
    listed = contract_lanes(jnp.concatenate(left, axis=1), export_hot[...])
    for h in range(blocks):
        mult[:, h * LANES : (h + 1) * LANES] = 1.0 + listed[16 * h : 16 * h + 8]


STATE = 34


def contact_state(geo, first, second):
    raw = geo[0:3]
    length = jnp.sqrt(dot3(raw, raw))
    normal = [x / length for x in raw]
    side = jnp.sqrt(normal[1] * normal[1] + normal[2] * normal[2])
    tan_y = normal[2] / side
    tan_z = -normal[1] / side
    two = [
        normal[1] * tan_z - normal[2] * tan_y,
        -normal[0] * tan_z,
        normal[0] * tan_y,
    ]

    def arm(p, spin):
        return [
            spin[1] * p[2] * p[2] + spin[2] * p[1] * p[1],
            spin[0] * p[2] * p[2] + spin[2] * p[0] * p[0],
            spin[0] * p[1] * p[1] + spin[1] * p[0] * p[0],
            -spin[2] * p[0] * p[1],
            -spin[1] * p[0] * p[2],
            -spin[0] * p[1] * p[2],
        ]

    arm_a, arm_b = geo[3:6], geo[6:9]
    e = [x + y for x, y in zip(arm(arm_a, first[1:4]), arm(arm_b, second[1:4]))]
    mass = first[0] + second[0]
    xx, yy, zz = mass + e[0], mass + e[1], mass + e[2]
    xy, xz, yz = e[3], e[4], e[5]
    c_xx = yy * zz - yz * yz
    c_xy = xz * yz - xy * zz
    c_xz = xy * yz - xz * yy
    c_yy = xx * zz - xz * xz
    c_yz = xy * xz - xx * yz
    c_zz = xx * yy - xy * xy
    det = xx * c_xx + xy * c_xy + xz * c_xz
    inv = [
        [c_xx / det, c_xy / det, c_xz / det],
        [c_xy / det, c_yy / det, c_yz / det],
        [c_xz / det, c_yz / det, c_zz / det],
    ]
    solve = []
    for row in (normal, None, two):
        for j in range(3):
            if row is None:
                value = tan_y * inv[1][j] + tan_z * inv[2][j]
            else:
                value = row[0] * inv[0][j] + row[1] * inv[1][j] + row[2] * inv[2][j]
            solve.append(relaxation * value)
    bias = [geo[9] * dot3(solve[3 * i : 3 * i + 3], normal) for i in range(3)]
    return (
        solve + bias + normal + [tan_y, tan_z] + two + arm_a + arm_b + list(first) + list(second)
    )


def sweep_kernel(bodies, interface, first_sweep, *refs):
    scalars_in, index, used, hot, masks = refs[:5]
    refs = refs[5:]
    if first_sweep:
        own, g1, r1, r2, r3, g0, g2, g3, ordered, near_props, far_props, state = refs[:12]
        refs = refs[12:]
        r0 = g1.at[pl.ds(g0.shape[0], 16), :]
    else:
        own, r0, r1, r2, r3, state, impulse_in = refs[:7]
        refs = refs[7:]
    impulse, own_change, ghost0, ghost1 = refs[:4]
    got_a, got_b, push_a, push_b, acc, table, all_a, all_b, gathered, placed, scalars = refs[4:]
    slots = used.shape[0]
    tiles = masks.shape[0] - 1
    blocks = bodies // LANES
    total = blocks + (4 * interface) // LANES
    values = scalars_in[...]
    wanted = list(range(slots)) + [OVER_FROM + k for k in range(NCOLOR)]
    wanted += [OVER_TO + k for k in range(NCOLOR)]
    if first_sweep:
        wanted += [TILE_SLOT + t for t in range(tiles)]
    for i in wanted:
        scalars[i] = values[0, i]

    def ghost_blocks(base):
        return [
            halves(r0[base : base + 8, :], r1[base : base + 8, :], interface),
            halves(r2[base : base + 8, :], r3[base : base + 8, :], interface),
        ]

    start = [own[0:8, h * LANES : (h + 1) * LANES] for h in range(blocks)] + ghost_blocks(0)
    for h in range(total):
        table[8 * h : 8 * h + 8, :] = start[h]
    push_a[...] = jnp.zeros_like(push_a)
    push_b[...] = jnp.zeros_like(push_b)

    if first_sweep:
        ghost_props = ghost_blocks(8)
        far = []
        for t in range(tiles):
            ib = jnp.broadcast_to(ordered[16 + t : 17 + t, :], (8, LANES))
            low, high = jnp.bitwise_and(ib, LANES - 1), jnp.right_shift(ib, 7)
            value = far_props[8 * t : 8 * t + 8, :]
            for h, block in enumerate(ghost_props):
                value = jnp.where(
                    high == blocks + h, jnp.take_along_axis(block, low, axis=1), value
                )
            far.append(value)
        all_a[...] = jnp.ones_like(all_a)
        all_b[...] = jnp.ones_like(all_b)
        gathered[...] = (g0[...] + g1[0 : g0.shape[0], :]) + (g2[...] + g3[...])
        placed[...] = jnp.ones_like(placed)
        rows = g0.shape[0] // 10
        for t in range(tiles):
            slot = scalars[TILE_SLOT + t]
            group_rows = pl.ds(pl.multiple_of(8 * slot, 8), 8)
            all_a[group_rows, :] = near_props[8 * t : 8 * t + 8, :]
            all_b[group_rows, :] = far[t]
            at = 8 * (t % 2) + t // 2
            for c in range(10):
                row = c * rows + at
                placed[pl.ds(c * slots + slot, 1), :] = gathered[row : row + 1, :]
        first = [all_a[pl.ds(c, slots, stride=8), :] for c in range(4)]
        second = [all_b[pl.ds(c, slots, stride=8), :] for c in range(4)]
        geo = [placed[c * slots : (c + 1) * slots, :] for c in range(10)]
        for c, value in enumerate(contact_state(geo, first, second)):
            state[c * slots : (c + 1) * slots, :] = value
        impulse[...] = jnp.zeros_like(impulse)
    else:
        impulse[...] = impulse_in[...]

    def held_at(base):
        return lambda c: state[pl.ds(c * slots + base, GROUP), :]

    def gather(base, room, now):
        for j in range(GROUP):
            ia = jnp.broadcast_to(index[pl.ds(base + j, 1), :], (8, LANES))
            ib = jnp.broadcast_to(index[pl.ds(slots + base + j, 1), :], (8, LANES))
            got_a[room + 8 * j : room + 8 * j + 8, :] = pick(now[:blocks], ia)
            got_b[room + 8 * j : room + 8 * j + 8, :] = pick(now, ib)

    def press(base, room):
        held = held_at(base)
        tile_rows = [pl.ds(room + c, GROUP, stride=8) for c in range(6)]
        va = [got_a[tile_rows[c], :] for c in range(6)]
        vb = [got_b[tile_rows[c], :] for c in range(6)]
        arm_a = [held(20 + c) for c in range(3)]
        arm_b = [held(23 + c) for c in range(3)]
        turn_a = cross(va[3:6], arm_a)
        turn_b = cross(vb[3:6], arm_b)
        rel = [((va[c] + turn_a[c]) - vb[c]) - turn_b[c] for c in range(3)]
        old = [impulse[pl.ds(c * slots + base, GROUP), :] for c in range(3)]
        trial = [
            old[c] - (dot3([held(3 * c + j) for j in range(3)], rel) + held(9 + c))
            for c in range(3)
        ]
        normal_part = jnp.maximum(trial[0], 0.0)
        slide = trial[1] * trial[1] + trial[2] * trial[2]
        shrink = lax.rsqrt(jnp.maximum(slide, tangent_floor * tangent_floor))
        factor = jnp.minimum(1.0, friction * normal_part * shrink)
        active = used[pl.ds(base, GROUP), :] > 0.5
        new = [
            jnp.where(active, normal_part, old[0]),
            jnp.where(active, trial[1] * factor, old[1]),
            jnp.where(active, trial[2] * factor, old[2]),
        ]
        change = [new[c] - old[c] for c in range(3)]
        for c in range(3):
            impulse[pl.ds(c * slots + base, GROUP), :] = new[c]
        force = [
            held(12) * change[0] + held(17) * change[2],
            held(13) * change[0] + held(15) * change[1] + held(18) * change[2],
            held(14) * change[0] + held(16) * change[1] + held(19) * change[2],
        ]
        spin_a = cross(arm_a, force)
        spin_b = cross(arm_b, force)
        for c in range(3):
            push_a[tile_rows[c], :] = held(26) * force[c]
            push_a[tile_rows[3 + c], :] = held(27 + c) * spin_a[c]
            push_b[tile_rows[c], :] = -(held(30) * force[c])
            push_b[tile_rows[3 + c], :] = -(held(31 + c) * spin_b[c])

    def sides(base, room):
        left, right = [], []
        near = blocks // 2
        empty = jnp.zeros((8 * (total - blocks), LANES), BF16)
        for j in range(GROUP):
            t = scalars[base + j]
            first = two_parts(push_a[room + 8 * j : room + 8 * j + 8, :])
            second = two_parts(push_b[room + 8 * j : room + 8 * j + 8, :])
            rows = [masks[t, 16 * m : 16 * m + 16, :] for m in range(near + total // 2)]
            left.append(jnp.concatenate([first * m for m in rows[:near]] + [empty], axis=0))
            left.append(jnp.concatenate([second * m for m in rows[near:]], axis=0))
            right.append(hot[pl.ds(pl.multiple_of(2 * TILE * t, 2 * TILE), 2 * TILE), :])
        return left, right

    def groups(bases, now):
        rooms = [8 * GROUP * i for i in range(len(bases))]
        for base, room in zip(bases, rooms):
            gather(base, room, now)
        for base, room in zip(bases, rooms):
            press(base, room)
        left, right = [], []
        for base, room in zip(bases, rooms):
            more_left, more_right = sides(base, room)
            left += more_left
            right += more_right
        return jnp.dot(
            jnp.concatenate(left, axis=1),
            jnp.concatenate(right, axis=0),
            preferred_element_type=F32,
        )

    def color_pass(k):
        now = [table[8 * h : 8 * h + 8, :] for h in range(total)]
        main = GROUP * k

        def over(g):
            return pl.multiple_of(GROUP * (NCOLOR + g), GROUP)

        begin, end = scalars[OVER_FROM + k], scalars[OVER_TO + k]

        @pl.when(end > begin)
        def _():
            acc[...] = groups([main, over(begin)], now)

        @pl.when(end <= begin)
        def _():
            acc[...] = groups([main], now)

        def more(g, c):
            acc[...] += groups([over(g)], now)
            return c

        lax.fori_loop(begin + 1, end, more, 0)
        for h in range(total):
            side = slice((h % 2) * LANES, (h % 2 + 1) * LANES)
            at = 16 * (h // 2)
            table[8 * h : 8 * h + 8, :] = now[h] + (
                acc[at : at + 8, side] + acc[at + 8 : at + 16, side]
            )

    for k in range(NCOLOR):
        color_pass(k)
    for h in range(blocks):
        own_change[:, h * LANES : (h + 1) * LANES] = table[8 * h : 8 * h + 8, :] - start[h]
    ghost0[...] = table[8 * blocks : 8 * blocks + 8, :] - start[blocks]
    ghost1[...] = table[8 * blocks + 8 : 8 * blocks + 16, :] - start[blocks + 1]


def impulse_kernel(scalars, held, impulse):
    slots = held.shape[0] // 3
    for t in range(impulse.shape[2] // TILE):
        slot = scalars[0, TILE_SLOT + t]
        for c in range(3):
            impulse[c, :, t * TILE : (t + 1) * TILE] = held[pl.ds(c * slots + slot, 1), :]


def merge_kernel(
    interface, last_sweep, own, change, c0, c1, c2, c3, mult, export_index, export_hot,
    export_masks, *refs,
):
    blocks = own.shape[1] // LANES
    came = [halves(c0[...], c1[...], interface), halves(c2[...], c3[...], interface)]
    left = jnp.concatenate(
        [
            jnp.concatenate([two_parts(came[i])] * blocks, axis=0) * export_masks[i]
            for i in range(2)
        ],
        axis=1,
    )
    incoming = contract_lanes(left, export_hot[...])
    fresh = []
    for h in range(blocks):
        span = slice(h * LANES, (h + 1) * LANES)
        fresh.append(
            own[0:8, span] + (change[:, span] + sum_parts(incoming, h)) / mult[:, span]
        )
    if last_sweep:
        (velocity,) = refs
        for r in range(6):
            for h in range(blocks):
                velocity[r, :, h * LANES : (h + 1) * LANES] = fresh[h][r : r + 1, :]
    else:
        fresh_own, out0, out1 = refs
        for h in range(blocks):
            fresh_own[:, h * LANES : (h + 1) * LANES] = fresh[h]
        out0[...] = pick(fresh, export_index[0:8, :])
        out1[...] = pick(fresh, export_index[8:16, :])


def in_hbm(array):
    return pltpu.with_memory_space_constraint(array, pltpu.HBM)


def shape(dims, dtype=F32):
    return jax.ShapeDtypeStruct(dims, dtype)


def make(subs, layers):
    matchings = neighbour_matchings(subs, layers)
    shuffles = [relay_shuffle(subs, layers, k) for k in range(WIN)]

    def trade(low, high):
        return [
            lax.ppermute(low if m < 2 else high, AXES, matchings[m]) for m in range(4)
        ]

    def on_device(geometry, dest_slot, pairs, colors, free_vel, inertia, exports):
        count = geometry.shape[2]
        bodies = free_vel.shape[2]
        interface = exports.shape[2]
        tiles = count // TILE
        slots = 16
        assert count % TILE == 0 and tiles < slots and 2 * interface == LANES
        assert bodies % WIDE == 0
        blocks = bodies // LANES
        total = blocks + 2
        place = shape((10 * slots, LANES))
        small = shape((16, LANES))
        arguments = (geometry, dest_slot, free_vel, inertia, exports, pairs, colors)
        rows = slot_count(tiles)
        assert rows <= TILE_SLOT
        prepared = pl.pallas_call(
            prepare_kernel,
            out_shape=(
                shape((10 * slots + 16, LANES)), place, place, small, small,
                shape((16, bodies)),
                shape((16, LANES), jnp.int32),
                shape((WIDE, count), BF16),
                shape((16, count), BF16),
                shape((2, 80, count), BF16),
                shape((32, LANES), jnp.int32),
                shape((2 * rows, LANES), jnp.int32),
                shape((rows, LANES)),
                shape((1, LANES), jnp.int32),
            ),
            in_specs=[pl.BlockSpec(memory_space=pltpu.HBM)] * 7,
            out_specs=(VMEM_SPEC,) * 14,
            scratch_shapes=[
                pltpu.VMEM(geometry.shape, F32),
                pltpu.VMEM(dest_slot.shape, jnp.int32),
                pltpu.VMEM(free_vel.shape, F32),
                pltpu.VMEM(inertia.shape, F32),
                pltpu.VMEM(exports.shape, jnp.int32),
                pltpu.VMEM(pairs.shape, jnp.int32),
                pltpu.SMEM(colors.shape, jnp.int32),
                pltpu.SMEM((1, LANES), jnp.int32),
                pltpu.VMEM((8, LANES), jnp.int32),
                pltpu.VMEM((16, count), F32),
                pltpu.VMEM((16 * (WIN - 1), count), BF16),
                pltpu.VMEM((2 * 80 * (WIN - 1), count), BF16),
                pltpu.SemaphoreType.DMA((8,)),
            ],
            compiler_params=PARAMS,
            name="prepare",
        )(*[in_hbm(x) for x in arguments])
        send0, place2, place3, out0, out1, own, export_index = prepared[:7]
        wide_hot, own_mask, tall, ordered, index, used, scalars = prepared[7:]
        came = [lax.ppermute(send0, AXES, matchings[0])]
        came.append(lax.ppermute(out0, AXES, matchings[1]))
        came.append(lax.ppermute(out1, AXES, matchings[2]))
        came.append(lax.ppermute(out1, AXES, matchings[3]))
        place0 = pl.pallas_call(
            place_kernel,
            out_shape=place,
            in_specs=[VMEM_SPEC] * 3,
            out_specs=VMEM_SPEC,
            compiler_params=PARAMS,
            name="place",
        )(tall, own_mask, wide_hot)
        placed = [place0]
        placed.append(lax.ppermute(place2, AXES, shuffles[2]))
        placed.append(lax.ppermute(place3, AXES, shuffles[3]))

        def indexing(*refs):
            index_kernel(subs, layers, interface, bodies, *refs)

        hot, masks, export_hot, export_masks, mult, near_props, far_props = pl.pallas_call(
            indexing,
            out_shape=(
                shape((2 * TILE * (tiles + 1), WIDE), BF16),
                shape((tiles + 1, 8 * (blocks + total), LANES), BF16),
                shape((LANES, 2 * LANES), BF16),
                shape((2, 16 * blocks, LANES), BF16),
                shape((8, bodies)),
                shape((8 * tiles, LANES)),
                shape((8 * tiles, LANES)),
            ),
            in_specs=[VMEM_SPEC] * 3,
            out_specs=(VMEM_SPEC,) * 7,
            compiler_params=PARAMS,
            name="indexing",
        )(ordered, export_index, own)

        state = impulse = None
        for sweep in range(SWEEPS):
            first, last = sweep == 0, sweep == SWEEPS - 1

            def run(*refs, first=first):
                sweep_kernel(bodies, interface, first, *refs)

            outs = [
                shape((3 * rows, LANES)),
                shape((8, bodies)),
                shape((8, LANES)),
                shape((8, LANES)),
            ]
            operands = [scalars, index, used, hot, masks, own, *came]
            if first:
                outs = [shape((STATE * rows, LANES))] + outs
                operands += [*placed, ordered, near_props, far_props]
            else:
                operands += [state, impulse]
            result = pl.pallas_call(
                run,
                out_shape=tuple(outs),
                in_specs=[VMEM_SPEC] * len(operands),
                out_specs=(VMEM_SPEC,) * len(outs),
                scratch_shapes=[
                    pltpu.VMEM((16 * GROUP, LANES), F32),
                    pltpu.VMEM((16 * GROUP, LANES), F32),
                    pltpu.VMEM((16 * GROUP, LANES), F32),
                    pltpu.VMEM((16 * GROUP, LANES), F32),
                    pltpu.VMEM((8 * total, WIDE), F32),
                    pltpu.VMEM((8 * total, LANES), F32),
                    pltpu.VMEM((8 * rows, LANES), F32),
                    pltpu.VMEM((8 * rows, LANES), F32),
                    pltpu.VMEM((10 * slots, LANES), F32),
                    pltpu.VMEM((10 * rows, LANES), F32),
                    pltpu.SMEM((64,), jnp.int32),
                ],
                compiler_params=PARAMS,
                name="sweep",
            )(*operands)
            if first:
                state, result = result[0], result[1:]
            impulse, change, ghost0, ghost1 = result
            sums = trade(ghost0, ghost1)

            def merge(*refs, last=last):
                merge_kernel(interface, last, *refs)

            operands = [own, change, *sums, mult, export_index, export_hot, export_masks]
            if last:
                outs = (shape((6, 1, bodies)),)
            else:
                outs = (shape((8, bodies)), shape((8, LANES)), shape((8, LANES)))
            merged = pl.pallas_call(
                merge,
                out_shape=outs,
                in_specs=[VMEM_SPEC] * len(operands),
                out_specs=(VMEM_SPEC,) * len(outs),
                compiler_params=PARAMS,
                name="merge",
            )(*operands)
            if last:
                in_order = pl.pallas_call(
                    impulse_kernel,
                    out_shape=shape((3, 1, count)),
                    in_specs=[SMEM_SPEC, VMEM_SPEC],
                    out_specs=VMEM_SPEC,
                    compiler_params=PARAMS,
                    name="impulse",
                )(scalars, impulse)
                return in_order, merged[0]
            own = merged[0]
            came = trade(merged[1], merged[2])

    return on_device


def solution(mesh):
    placed = (
        P(None, "layer", "sub"),
        P("layer", "sub"),
        P(None, "layer", "sub"),
        P("layer", "sub"),
        P(None, "layer", "sub"),
        P(None, "layer", "sub"),
        P(None, "layer", "sub"),
    )
    return jax.shard_map(
        make(mesh.shape["sub"], mesh.shape["layer"]),
        mesh=mesh,
        in_specs=placed,
        out_specs=(P(None, "layer", "sub"), P(None, "layer", "sub")),
        check_vma=False,
    )
```
